32 devices in a mesh: blk: 16 (over z, y, core), grp: 2 (over x).
Axes of the slice: x: 2, y: 2, z: 4, core: 2. Of those that a mesh axis runs over, the one named last changes fastest.
Arguments:
- tokens: bfloat16 [2, 2048, 1024], P('grp', 'blk'), may hold values from -6 to 6
- qkv_weight: bfloat16 [2, 1024, 3072], replicated, may hold values from -0.1875 to 0.1875
- out_weight: bfloat16 [2, 1024, 1024], replicated, may hold values from -0.75 to 0.75
- up_weight: bfloat16 [2, 1024, 4096], replicated, may hold values from -0.1875 to 0.1875
- down_weight: bfloat16 [2, 4096, 1024], replicated, may hold values from -0.09375 to 0.09375
- vectors: float32 [2, 11, 1024], replicated, may hold values from -0.5 to 1.5, as said below
- up_bias: float32 [2, 4096], replicated, may hold values from -1.2 to 1.2
- head_norm: float32 [2, 192], replicated, may hold values from -0.3 to 1.7, as said below
- token_valid: int32 [2, 16, 128], P('grp', 'blk'), may hold values 0 or 1
- frame_scene: int32 [2, 16], P('grp', 'blk'), may hold values from 0 to 1
- cotangent: bfloat16 [2, 2048, 1024], P('grp', 'blk'), may hold values from -6 to 6
Outputs:
- output: bfloat16 [2, 2048, 1024], P('grp', 'blk')
- input_grad: bfloat16 [2, 2048, 1024], P('grp', 'blk')
- qkv_grad: float32 [2, 1024, 3072], P(None, 'blk')
- out_grad: float32 [2, 1024, 1024], P(None, 'blk')
- up_grad: float32 [2, 1024, 4096], P(None, 'blk')
- down_grad: float32 [2, 4096, 1024], P(None, 'blk')
- vector_grad: float32 [2, 11, 1024], P(None, None, 'blk')
- up_bias_grad: float32 [2, 4096], P(None, 'blk')
- head_norm_grad: float32 [2, 192], replicated
The draws below stay inside these ranges and needn't reach their ends.
Inputs may be any that keep to these rules, and one draw needn't show every extreme that they name: `vectors`: gains and layer scales about one, biases and shifts about zero. `head_norm`: gains about one, shifts about zero.
All inputs are finite; a program needn't handle non-finite values. No bound on the sum of `token_valid` on one device may be relied on, other than what follows from the above.
Results may differ from the reference program's by a relative error of at most 0.018.
Values may be sent and summed in bfloat16 or wider, within the bound.
A program may use at most 320 MiB of HBM per device.

```python
import math
import jax
import jax.numpy as jnp
from jax import lax

D = 1024
HEADS = 16
FF = 4096
HD = 64
VEC = 11
SPECIAL = 5
FTOK = 128
SCENES = 2
FRAMES = 16
SCENE_TOK = 2048
N_GRP = 2


def draw_vectors(key, part):
    uniform_draw = jax.random.uniform(jax.random.fold_in(key, 11), (2, VEC, D), jnp.float32, -1.0, 1.0)
    row_index = lax.broadcasted_iota(jnp.int32, (2, VEC, D), 1)
    gain_rows = (row_index == 0) | (row_index == 7)
    scale_rows = (row_index == 6) | (row_index == 10)
    return jnp.where(gain_rows, 1.0 + 0.3 * uniform_draw, jnp.where(scale_rows, 1.0 + 0.5 * uniform_draw, 0.3 * uniform_draw))


def draw_head_norm(key, part):
    uniform_draw = jax.random.uniform(jax.random.fold_in(key, 23), (2, 3 * HD), jnp.float32, -1.0, 1.0)
    column = lax.broadcasted_iota(jnp.int32, (2, 3 * HD), 1)
    shift_cols = (column >= HD) & (column < 2 * HD)
    return jnp.where(shift_cols, 0.3 * uniform_draw, 1.25 + 0.45 * uniform_draw)


def draw_frame_scene(key, part):
    drawn = jax.random.randint(jax.random.fold_in(key, 37), (N_GRP, FRAMES), 0, SCENES, dtype=jnp.int32)
    first_scene = drawn[:, :1]
    second_scene = (first_scene + 1) % SCENES
    column = lax.broadcasted_iota(jnp.int32, (N_GRP, FRAMES), 1)
    drawn = jnp.where(column == FRAMES - 1, first_scene, drawn)
    return jnp.where(column == 1, second_scene, drawn).astype(jnp.int32)


def with_ends(result, rng, least, largest):
    dims = result.shape
    place = [jax.random.randint(jax.random.fold_in(rng, axis), (), 0, dims[axis]) for axis in range(len(dims))]
    result = result.at[tuple(place)].set(least)
    longest = dims.index(max(dims))
    place[longest] = (place[longest] + 1) % dims[longest]
    return result.at[tuple(place)].set(largest)


def block_scale(key, shape, pieces, least, largest):
    gain = 1.0
    for axis_at, shards_of in pieces:
        draws = jax.random.uniform(jax.random.fold_in(jax.random.fold_in(key, 6), axis_at), (shards_of,), jnp.float32, least / len(pieces), largest / len(pieces))
        gain = gain * jnp.repeat(jnp.exp(draws), shape[axis_at] // shards_of).reshape((-1,) + (1,) * (len(shape) - 1 - axis_at))
    return gain


def noise(own_key, extent, spread, most, cuts=(), kind=jnp.bfloat16):
    loudness = block_scale(own_key, extent, cuts, -0.22, 0.18) if cuts else 1.0
    values = jax.random.normal(own_key, extent, jnp.float32) * spread * loudness
    return jnp.minimum(jnp.maximum(values, -most), most).astype(kind)


def setup_inputs(seed: int = 0) -> dict:
    splits = jax.random.split(jax.random.key(seed), 12)
    tokens = noise(splits[0], (N_GRP, SCENE_TOK, D), 1.0, 6.0, ((0, 2), (1, 16)))
    qkv_weight = noise(splits[1], (2, D, 3 * D), D ** -0.5, 0.1875)
    out_weight = noise(splits[2], (2, D, D), (D // 16) ** -0.5, 0.75)
    up_weight = noise(splits[3], (2, D, FF), D ** -0.5, 0.1875)
    down_weight = noise(splits[4], (2, FF, D), FF ** -0.5, 0.09375)
    vectors = draw_vectors(jax.random.fold_in(splits[11], 71), 0)
    up_bias = noise(splits[6], (2, FF), 0.2, 1.2, (), jnp.float32)
    head_norm = draw_head_norm(jax.random.fold_in(splits[11], 71), 0)
    token_valid = with_ends((jax.random.randint(splits[8], (N_GRP, FRAMES, FTOK), 0, 4) < 3).astype(jnp.int32), jax.random.fold_in(splits[8], 1), 0, 1)
    frame_scene = draw_frame_scene(jax.random.fold_in(splits[11], 71), 0)
    cotangent = noise(splits[10], (N_GRP, SCENE_TOK, D), 1.0, 6.0, ((0, 2), (1, 16)))
    return {"tokens": tokens, "qkv_weight": qkv_weight, "out_weight": out_weight, "up_weight": up_weight, "down_weight": down_weight, "vectors": vectors, "up_bias": up_bias, "head_norm": head_norm, "token_valid": token_valid, "frame_scene": frame_scene, "cotangent": cotangent}


EPS = 1e-06
NEG = -1e+30

@jax.custom_vjp
def low(v):
    return lax.optimization_barrier(v.astype(jnp.bfloat16)).astype(jnp.float32)

@jax.custom_vjp
def low_back(v):
    return v

def low_keep(v):
    return (low(v), None)

def low_pass(kept, grad):
    return (grad,)

def back_keep(v):
    return (v, None)

def back_low(kept, grad):
    return (low(grad),)
low.defvjp(low_keep, low_pass)
low_back.defvjp(back_keep, back_low)

def norm_rows(values, scaling, offset):
    average = lax.optimization_barrier(jnp.mean(values, axis=-1, keepdims=True))
    centered = values - average
    variance = lax.optimization_barrier(jnp.mean(centered * centered, axis=-1, keepdims=True))
    return centered * lax.rsqrt(variance + EPS) * scaling + offset

def product(left_side, right_side):
    return jnp.dot(left_side, right_side, precision=lax.Precision.HIGHEST)

def attend(queries, key_rows, values, allowed):
    scores = jnp.einsum('qhd,khd->hqk', queries, key_rows, precision=lax.Precision.HIGHEST) * HD ** (-0.5)
    scores = jnp.where(allowed[None], low_back(scores), NEG)
    shares = low(jax.nn.softmax(scores, axis=-1))
    return jnp.einsum('hqk,khd->qhd', shares, values, precision=lax.Precision.HIGHEST)

def frame_attention(usable):

    def compute(queries, key_rows, values):

        def one_frame(frame_items):
            frame_query, frame_key, frame_value, frame_usable = frame_items
            allowed = jnp.broadcast_to(frame_usable[None, :], (FTOK, FTOK))
            return attend(frame_query, frame_key, frame_value, allowed)
        shaped = (queries.reshape(FRAMES, FTOK, HEADS, HD), key_rows.reshape(FRAMES, FTOK, HEADS, HD), values.reshape(FRAMES, FTOK, HEADS, HD), usable)
        return lax.map(jax.checkpoint(one_frame), shaped).reshape(SCENE_TOK, HEADS, HD)
    return compute

def global_attention(query_scene, key_tags):
    block_rows = math.gcd(SCENE_TOK, 512)
    block_count = SCENE_TOK // block_rows

    def compute(queries, key_rows, values):

        def one_block(block_items):
            block_query, block_scene = block_items
            allowed = block_scene[:, None] == key_tags[None, :]
            return attend(block_query, key_rows, values, allowed)
        shaped = (queries.reshape(block_count, block_rows, HEADS, HD), query_scene.reshape(block_count, block_rows))
        return lax.map(jax.checkpoint(one_block), shaped).reshape(SCENE_TOK, HEADS, HD)
    return compute

def run_block(residual, layer_index, params, attention):
    qkv_matrix, out_matrix, up_matrix, down_matrix, vectors, up_bias, head_norm = params
    vector_rows = vectors[layer_index]
    head_gains = head_norm[layer_index]
    row_count = residual.shape[0]
    normed = low(norm_rows(residual, vector_rows[0], vector_rows[1]))
    projected = low_back(product(normed, qkv_matrix[layer_index]) + jnp.concatenate([vector_rows[2], vector_rows[3], vector_rows[4]]))
    query_pre = projected[:, :D].reshape(row_count, HEADS, HD)
    key_pre = projected[:, D:2 * D].reshape(row_count, HEADS, HD)
    value_pre = projected[:, 2 * D:].reshape(row_count, HEADS, HD)
    queries = low(norm_rows(query_pre, head_gains[:HD], head_gains[HD:2 * HD]))
    key_rows = low(norm_rows(key_pre, head_gains[2 * HD:], 0.0))
    values = low(value_pre)
    attended = low(low_back(attention(queries, key_rows, values).reshape(row_count, D)))
    mixed = low_back(product(attended, out_matrix[layer_index]) + vector_rows[5])
    middle = residual + vector_rows[6] * mixed
    lifted = low(norm_rows(middle, vector_rows[7], vector_rows[8]))
    hidden = low_back(product(lifted, up_matrix[layer_index]) + up_bias[layer_index])
    active = low(jax.nn.gelu(hidden, approximate=False))
    feed = low_back(product(active, down_matrix[layer_index]) + vector_rows[9])
    return middle + vector_rows[10] * feed

def reference(tokens, qkv_weight, out_weight, up_weight, down_weight, vectors, up_bias, head_norm, token_valid, frame_scene, cotangent):
    position = jnp.arange(FTOK).astype(jnp.int32)[None, None, :]
    usable = (token_valid == 1) | (position < SPECIAL)
    scene_rows = jnp.broadcast_to(frame_scene[:, :, None], usable.shape)
    key_tags = jnp.where(usable, scene_rows, -1).reshape(N_GRP, SCENE_TOK)
    query_scene = scene_rows.reshape(N_GRP, SCENE_TOK)
    params = (qkv_weight.astype(jnp.float32), out_weight.astype(jnp.float32), up_weight.astype(jnp.float32), down_weight.astype(jnp.float32), vectors, up_bias, head_norm)

    def forward(residual, weights):
        results = []
        for group_index in range(N_GRP):
            middle = run_block(residual[group_index], 0, weights, frame_attention(usable[group_index]))
            results.append(run_block(middle, 1, weights, global_attention(query_scene[group_index], key_tags[group_index])))
        return jnp.stack(results)
    output, pullback = jax.vjp(forward, tokens.astype(jnp.float32), params)
    input_grad, grads = pullback(cotangent.astype(jnp.float32))
    return (output.astype(jnp.bfloat16), input_grad.astype(jnp.bfloat16), grads[0], grads[1], grads[2], grads[3], grads[4], grads[5], grads[6])
```

```python
import functools

import jax
import jax.numpy as jnp
from jax import lax
from jax.experimental import pallas as pl
from jax.experimental.pallas import tpu as pltpu
from jax.sharding import PartitionSpec as P

HEADS = 16
HD = 64
SPECIAL = 5
PAIRS = HEADS // 2
LANES = 2 * HD
FRAME = 128
KEEP = 16
EPS = 1e-06
NEG = -1e30
SCALE = HD**-0.5
BF = jnp.bfloat16
F32 = jnp.float32


def norm_rows(values, scaling, offset):
    average = jnp.mean(values, axis=-1, keepdims=True)
    centered = values - average
    variance = jnp.mean(centered * centered, axis=-1, keepdims=True)
    return centered * lax.rsqrt(variance + EPS) * scaling + offset


def product(left_side, right_side):
    return jnp.dot(left_side, right_side, preferred_element_type=F32)


def product_left(left_side, right_side):
    return lax.dot_general(
        left_side, right_side, (((0,), (0,)), ((), ())), preferred_element_type=F32
    )


def product_right(left_side, right_side):
    return lax.dot_general(
        left_side, right_side, (((1,), (1,)), ((), ())), preferred_element_type=F32
    )


def head_norms(query_pre, key_pre, head_gains):
    query_norm = norm_rows(query_pre, head_gains[:HD], head_gains[HD : 2 * HD])
    key_norm = norm_rows(key_pre, head_gains[2 * HD :], 0.0)
    return (query_norm, key_norm)


def gelu_exact(values):
    return jax.nn.gelu(values, approximate=False)


def column_sum(values):
    return jnp.sum(values.astype(F32), axis=0)


def lane_masks(dtype):
    lane = lax.broadcasted_iota(jnp.int32, (1, LANES), 1)
    first = (lane < HD).astype(dtype)
    return (first, 1 - first)


def as_column(row):
    size = row.shape[1]
    return jnp.transpose(jnp.broadcast_to(row, (LANES, size)))[:, :1]


def as_row(column):
    size = column.shape[0]
    return jnp.transpose(jnp.broadcast_to(column, (size, LANES)))[:1, :]


def flat(ref):
    block = ref[...]
    return block.reshape(block.shape[0] * block.shape[1], block.shape[2])


def attend_kernel(blocks, q_ref, k_ref, v_ref, tag_ref, scene_ref, o_ref, lse_ref, m_sc, l_sc, a_sc):
    step = pl.program_id(1)
    keys, values = flat(k_ref), flat(v_ref)
    allowed = tag_ref[...] == scene_ref[:1, :1]
    queries = q_ref[...]
    pieces = []
    for index, mask in enumerate(lane_masks(BF)):
        scores = product_right(queries * mask, keys) * SCALE
        scores = jnp.where(allowed, scores, NEG)
        top = jnp.max(scores, axis=-1, keepdims=True)

        if blocks > 1:

            @pl.when(step == 0)
            def _():
                m_sc[index] = jnp.full_like(m_sc[index], NEG)
                l_sc[index] = jnp.zeros_like(l_sc[index])
                a_sc[index] = jnp.zeros_like(a_sc[index])

            old = m_sc[index][:, :1]
            top = jnp.maximum(top, old)
            keep = jnp.exp(old - top)
        shares = jnp.where(allowed, jnp.exp(scores - top), 0.0)
        total = jnp.sum(shares, axis=-1, keepdims=True)
        weighted = product(shares.astype(BF), values)
        if blocks > 1:
            total = total + keep * l_sc[index][:, :1]
            weighted = weighted + keep * a_sc[index]
            m_sc[index] = jnp.broadcast_to(top, m_sc[index].shape)
            l_sc[index] = jnp.broadcast_to(total, l_sc[index].shape)
            a_sc[index] = weighted
        pieces.append(weighted / total)
        lse_ref[0, index : index + 1, :] = as_row(top + jnp.log(total))
    first, second = lane_masks(F32)
    o_ref[...] = jnp.where(first > 0, pieces[0], pieces[1])


def key_block(count):
    for size in (16, 8, 4, 2, 1):
        if count % size == 0:
            return size


def global_attend(queries, pairs, tags, scene):
    frames = pairs.shape[0]
    group = key_block(frames)
    blocks = frames // group
    return pl.pallas_call(
        functools.partial(attend_kernel, blocks),
        grid=(PAIRS, blocks),
        in_specs=[
            pl.BlockSpec((FRAME, LANES), lambda p, k: (0, p)),
            pl.BlockSpec((group, FRAME, LANES), lambda p, k: (k, 0, p)),
            pl.BlockSpec((group, FRAME, LANES), lambda p, k: (k, 0, PAIRS + p)),
            pl.BlockSpec((1, group * FRAME), lambda p, k: (0, k)),
            pl.BlockSpec((8, LANES), lambda p, k: (0, 0)),
        ],
        out_specs=[
            pl.BlockSpec((FRAME, LANES), lambda p, k: (0, p)),
            pl.BlockSpec((1, 2, FRAME), lambda p, k: (p, 0, 0)),
        ],
        out_shape=[
            jax.ShapeDtypeStruct((FRAME, PAIRS * LANES), F32),
            jax.ShapeDtypeStruct((PAIRS, 2, FRAME), F32),
        ],
        scratch_shapes=[pltpu.VMEM((2, FRAME, LANES), F32)] * 3,
        compiler_params=pltpu.CompilerParams(vmem_limit_bytes=48 * 2**20),
        cost_estimate=pl.CostEstimate(
            flops=4 * FRAME * frames * FRAME * LANES * HEADS,
            bytes_accessed=frames * FRAME * 4096,
            transcendentals=FRAME * frames * FRAME * HEADS,
        ),
        name="global_attend",
    )(queries, pairs, pairs, tags, scene)


def query_grad_kernel(
    q_ref, k_ref, v_ref, tag_ref, scene_ref, do_ref, lse_ref, delta_ref, dq_ref
):
    step = pl.program_id(1)
    keys, values = flat(k_ref), flat(v_ref)
    allowed = tag_ref[...] == scene_ref[:1, :1]
    queries, outs = q_ref[...], do_ref[...]
    pieces = []
    for index, mask in enumerate(lane_masks(BF)):
        scores = product_right(queries * mask, keys) * SCALE
        top = as_column(lse_ref[0, index : index + 1, :])
        delta = as_column(delta_ref[0, index : index + 1, :])
        shares = jnp.where(allowed, jnp.exp(scores - top), 0.0)
        share_grad = product_right(outs * mask, values)
        score_grad = (shares * (share_grad - delta)).astype(BF)
        pieces.append(product(score_grad, keys) * SCALE)
    first, second = lane_masks(F32)
    piece = jnp.where(first > 0, pieces[0], pieces[1])

    @pl.when(step == 0)
    def _():
        dq_ref[...] = piece

    @pl.when(step > 0)
    def _():
        dq_ref[...] += piece


def global_query_grad(queries, pairs, tags, scene, outs, lse, delta):
    frames = pairs.shape[0]
    group = key_block(frames)
    blocks = frames // group
    return pl.pallas_call(
        query_grad_kernel,
        grid=(PAIRS, blocks),
        in_specs=[
            pl.BlockSpec((FRAME, LANES), lambda p, k: (0, p)),
            pl.BlockSpec((group, FRAME, LANES), lambda p, k: (k, 0, p)),
            pl.BlockSpec((group, FRAME, LANES), lambda p, k: (k, 0, PAIRS + p)),
            pl.BlockSpec((1, group * FRAME), lambda p, k: (0, k)),
            pl.BlockSpec((8, LANES), lambda p, k: (0, 0)),
            pl.BlockSpec((FRAME, LANES), lambda p, k: (0, p)),
            pl.BlockSpec((1, 2, FRAME), lambda p, k: (p, 0, 0)),
            pl.BlockSpec((1, 2, FRAME), lambda p, k: (p, 0, 0)),
        ],
        out_specs=pl.BlockSpec((FRAME, LANES), lambda p, k: (0, p)),
        out_shape=jax.ShapeDtypeStruct((FRAME, PAIRS * LANES), F32),
        compiler_params=pltpu.CompilerParams(vmem_limit_bytes=48 * 2**20),
        cost_estimate=pl.CostEstimate(
            flops=6 * FRAME * frames * FRAME * LANES * HEADS,
            bytes_accessed=frames * FRAME * 4096,
            transcendentals=FRAME * frames * FRAME * HEADS,
        ),
        name="global_query_grad",
    )(queries, pairs, pairs, tags, scene, outs, lse, delta)


def key_grad_kernel(
    k_ref, v_ref, tag_ref, scene_ref, q_ref, do_ref, lse_ref, delta_ref, dk_ref, dv_ref
):
    step = pl.program_id(1)
    keys, values = k_ref[...], v_ref[...]
    queries, outs = flat(q_ref), flat(do_ref)
    allowed = as_column(tag_ref[...]) == scene_ref[...]
    key_pieces, value_pieces = [], []
    for index, mask in enumerate(lane_masks(BF)):
        scores = product_right(keys * mask, queries) * SCALE
        top = lse_ref[0, index : index + 1, :]
        delta = delta_ref[0, index : index + 1, :]
        shares = jnp.where(allowed, jnp.exp(scores - top), 0.0)
        share_grad = product_right(values * mask, outs)
        score_grad = (shares * (share_grad - delta)).astype(BF)
        key_pieces.append(product(score_grad, queries) * SCALE)
        value_pieces.append(product(shares.astype(BF), outs))
    first, second = lane_masks(F32)
    key_piece = jnp.where(first > 0, key_pieces[0], key_pieces[1])
    value_piece = jnp.where(first > 0, value_pieces[0], value_pieces[1])

    @pl.when(step == 0)
    def _():
        dk_ref[...] = key_piece
        dv_ref[...] = value_piece

    @pl.when(step > 0)
    def _():
        dk_ref[...] += key_piece
        dv_ref[...] += value_piece


def global_key_grad(keys, values, tags, scenes, queries, outs, lse, delta):
    frames = queries.shape[0]
    group = key_block(frames)
    blocks = frames // group
    return pl.pallas_call(
        key_grad_kernel,
        grid=(PAIRS, blocks),
        in_specs=[
            pl.BlockSpec((FRAME, LANES), lambda p, k: (0, p)),
            pl.BlockSpec((FRAME, LANES), lambda p, k: (0, p)),
            pl.BlockSpec((1, FRAME), lambda p, k: (0, 0)),
            pl.BlockSpec((1, group * FRAME), lambda p, k: (0, k)),
            pl.BlockSpec((group, FRAME, LANES), lambda p, k: (k, 0, p)),
            pl.BlockSpec((group, FRAME, LANES), lambda p, k: (k, 0, p)),
            pl.BlockSpec((1, 2, group * FRAME), lambda p, k: (p, 0, k)),
            pl.BlockSpec((1, 2, group * FRAME), lambda p, k: (p, 0, k)),
        ],
        out_specs=[pl.BlockSpec((FRAME, LANES), lambda p, k: (0, p))] * 2,
        out_shape=[jax.ShapeDtypeStruct((FRAME, PAIRS * LANES), F32)] * 2,
        compiler_params=pltpu.CompilerParams(vmem_limit_bytes=48 * 2**20),
        cost_estimate=pl.CostEstimate(
            flops=8 * FRAME * frames * FRAME * LANES * HEADS,
            bytes_accessed=frames * FRAME * 4096,
            transcendentals=FRAME * frames * FRAME * HEADS,
        ),
        name="global_key_grad",
    )(keys, values, tags, scenes, queries, outs, lse, delta)


def split_three(values):
    high = values.astype(BF)
    rest = values - high.astype(F32)
    middle = rest.astype(BF)
    return jnp.stack([high, middle, (rest - middle.astype(F32)).astype(BF)])


def with_rows(body, statistic):
    width = body.shape[1]
    extra = split_three(statistic).reshape(-1, width)
    pad = jnp.zeros((KEEP - extra.shape[0], width), BF)
    return jnp.concatenate([body, extra, pad], axis=0)


def rows_of(gathered, width):
    frames = gathered.shape[0]
    used = 3 * HEADS * FRAME // width
    terms = gathered[:, FRAME : FRAME + used].reshape(frames, 3, HEADS, FRAME).astype(F32)
    total = terms[:, 0] + terms[:, 1] + terms[:, 2]
    return total.transpose(1, 0, 2).reshape(PAIRS, 2, frames * FRAME)


def per_device(
    tokens,
    qkv_weight,
    out_weight,
    up_weight,
    down_weight,
    vectors,
    up_bias,
    head_norm,
    token_valid,
    frame_scene,
    cotangent,
):
    count = lax.axis_size("blk")
    outer = count // 4
    me = lax.axis_index("blk")
    x_at = lax.axis_index("grp")
    c_at = lax.rem(me, 2)
    y_at = lax.rem(me // 2, 2)
    c_pairs = [(i, i ^ 1) for i in range(count)]
    y_pairs = [(i, i ^ 2) for i in range(count)]
    z_groups = [[4 * o + k for o in range(outer)] for k in range(4)]

    def swap_x(value):
        return lax.ppermute(value, "grp", [(0, 1), (1, 0)])

    def swap_c(value):
        return lax.ppermute(value, "blk", c_pairs)

    def swap_y(value):
        return lax.ppermute(value, "blk", y_pairs)

    def part(value, index, parts, axis):
        size = value.shape[axis] // parts
        return lax.dynamic_slice_in_dim(value, index * size, size, axis)

    def gather_left(value):
        two = jnp.concatenate([value, swap_x(value)], axis=0)
        return jnp.concatenate([two, swap_c(two)], axis=0)

    def gather_right(value):
        two = jnp.concatenate(
            [part(value, x_at, 2, 1), swap_x(part(value, 1 - x_at, 2, 1))], axis=0
        )
        return jnp.concatenate(
            [part(two, c_at, 2, 1), swap_c(part(two, 1 - c_at, 2, 1))], axis=0
        )

    def reduced(left, right):
        left, right = gather_left(left), gather_right(right)
        tokens_here, rows = left.shape
        size = rows // (2 * outer)
        lefts = left.reshape(tokens_here, outer, 2, size)

        def rows_for(index):
            chosen = lax.dynamic_index_in_dim(lefts, index, 2, keepdims=False)
            return chosen.reshape(tokens_here, outer * size)

        arrived = swap_y(product_left(rows_for(1 - y_at), right).astype(BF))
        own = (product_left(rows_for(y_at), right) + arrived.astype(F32)).astype(BF)
        total = lax.psum_scatter(
            own, "blk", scatter_dimension=0, tiled=True, axis_index_groups=z_groups
        )
        mine = part(total, c_at, 2, 0)
        other = swap_c(part(total, 1 - c_at, 2, 0))
        half = jnp.concatenate(
            [jnp.where(c_at == 0, mine, other), jnp.where(c_at == 0, other, mine)], axis=1
        )
        far = swap_x(half)
        return jnp.concatenate(
            [jnp.where(x_at == 0, half, far), jnp.where(x_at == 0, far, half)], axis=1
        ).astype(F32)

    row_count = tokens.shape[1]
    model_width = tokens.shape[2]
    position = lax.broadcasted_iota(jnp.int32, (row_count,), 0)
    usable = (token_valid[0, 0] == 1) | (position < SPECIAL)
    scene = frame_scene[0, 0].astype(F32)
    tag_rows = jnp.where(usable, scene, -1.0)
    scene_tile = jnp.full((8, LANES), scene)

    def block_forward(residual, layer_weights, attention):
        qkv_matrix, out_matrix, up_matrix, down_matrix, vector_rows, up_offset, head_gains = (
            layer_weights
        )
        normed_low = norm_rows(residual, vector_rows[0], vector_rows[1]).astype(BF)
        projected = product(normed_low, qkv_matrix) + jnp.concatenate(
            [vector_rows[2], vector_rows[3], vector_rows[4]]
        )
        query_pre = projected[:, :model_width].reshape(row_count, HEADS, HD)
        key_pre = projected[:, model_width : 2 * model_width].reshape(row_count, HEADS, HD)
        query_norm, key_norm = head_norms(query_pre, key_pre, head_gains)
        query_low = query_norm.astype(BF)
        key_low = key_norm.astype(BF)
        value_low = projected[:, 2 * model_width :].astype(BF).reshape(row_count, HEADS, HD)
        attended, kept = attention(query_low, key_low, value_low)
        attended_low = attended.astype(BF)
        mixed_heads = product(attended_low, out_matrix) + vector_rows[5]
        middle = residual + vector_rows[6] * mixed_heads
        normed_two = norm_rows(middle, vector_rows[7], vector_rows[8]).astype(BF)
        hidden = product(normed_two, up_matrix) + up_offset
        activated = gelu_exact(hidden).astype(BF)
        feed_out = product(activated, down_matrix) + vector_rows[9]
        stored = (
            residual,
            normed_low,
            query_pre,
            key_pre,
            query_low,
            key_low,
            value_low,
            attended,
            kept,
            attended_low,
            mixed_heads,
            middle,
            normed_two,
            hidden,
            activated,
            feed_out,
        )
        return (middle + vector_rows[10] * feed_out, stored)

    def block_backward(grad_out, layer_weights, stored, attention_back):
        qkv_matrix, out_matrix, up_matrix, down_matrix, vector_rows, up_offset, head_gains = (
            layer_weights
        )
        (
            residual,
            normed_low,
            query_pre,
            key_pre,
            query_low,
            key_low,
            value_low,
            attended,
            kept,
            attended_low,
            mixed_heads,
            middle,
            normed_two,
            hidden,
            activated,
            feed_out,
        ) = stored
        feed_grad = (vector_rows[10] * grad_out).astype(BF)
        scale_two_grad = jnp.sum(grad_out * feed_out, axis=0)
        down_offset_grad = column_sum(feed_grad)
        down_grad = reduced(activated, feed_grad)
        active_grad = product_right(feed_grad, down_matrix)
        gelu_value, gelu_pull = jax.vjp(gelu_exact, hidden)
        hidden_grad = gelu_pull(active_grad)[0].astype(BF)
        up_offset_grad = column_sum(hidden_grad)
        up_grad = reduced(normed_two, hidden_grad)
        norm_value, norm_pull = jax.vjp(norm_rows, middle, vector_rows[7], vector_rows[8])
        middle_part, gain_two_grad, shift_two_grad = norm_pull(
            product_right(hidden_grad, up_matrix)
        )
        middle_grad = grad_out + middle_part
        mixed_grad = (vector_rows[6] * middle_grad).astype(BF)
        scale_one_grad = jnp.sum(middle_grad * mixed_heads, axis=0)
        out_offset_grad = column_sum(mixed_grad)
        out_grad = reduced(attended_low, mixed_grad)
        attended_grad = product_right(mixed_grad, out_matrix).astype(BF)
        query_grad, key_grad, value_grad = attention_back(
            query_low, key_low, value_low, attended, kept, attended_grad
        )
        head_value, head_pull = jax.vjp(head_norms, query_pre, key_pre, head_gains)
        query_part, key_part, head_grad = head_pull((query_grad, key_grad))
        projected_grad = jnp.concatenate(
            [
                query_part.reshape(row_count, model_width),
                key_part.reshape(row_count, model_width),
                value_grad.reshape(row_count, model_width),
            ],
            axis=1,
        ).astype(BF)
        qkv_offset_grad = column_sum(projected_grad)
        qkv_grad = reduced(normed_low, projected_grad)
        first_value, first_pull = jax.vjp(norm_rows, residual, vector_rows[0], vector_rows[1])
        residual_part, gain_one_grad, shift_one_grad = first_pull(
            product_right(projected_grad, qkv_matrix)
        )
        vector_grad = jnp.stack(
            [
                gain_one_grad,
                shift_one_grad,
                qkv_offset_grad[:model_width],
                qkv_offset_grad[model_width : 2 * model_width],
                qkv_offset_grad[2 * model_width :],
                out_offset_grad,
                scale_one_grad,
                gain_two_grad,
                shift_two_grad,
                down_offset_grad,
                scale_two_grad,
            ]
        )
        return (
            middle_grad + residual_part,
            (qkv_grad, out_grad, up_grad, down_grad),
            (vector_grad, up_offset_grad, head_grad),
        )

    def frame_shares(query_low, key_low):
        scores = (
            jnp.einsum("qhd,khd->hqk", query_low, key_low, preferred_element_type=F32) * SCALE
        )
        return jax.nn.softmax(jnp.where(usable[None, None, :], scores, NEG), axis=-1)

    def frame_forward(query_low, key_low, value_low):
        shares = frame_shares(query_low, key_low)
        attended = jnp.einsum(
            "hqk,khd->qhd", shares.astype(BF), value_low, preferred_element_type=F32
        )
        return (attended.reshape(row_count, model_width), None)

    def frame_back(query_low, key_low, value_low, attended, kept, attended_grad):
        attended_grad = attended_grad.reshape(row_count, HEADS, HD)
        shares = frame_shares(query_low, key_low)
        value_grad = jnp.einsum(
            "hqk,qhd->khd", shares.astype(BF), attended_grad, preferred_element_type=F32
        )
        share_grad = jnp.einsum(
            "qhd,khd->hqk", attended_grad, value_low, preferred_element_type=F32
        )
        delta_rows = jnp.sum(shares * share_grad, axis=-1, keepdims=True)
        score_grad = (shares * (share_grad - delta_rows)).astype(BF)
        query_grad = (
            jnp.einsum("hqk,khd->qhd", score_grad, key_low, preferred_element_type=F32) * SCALE
        )
        key_grad = (
            jnp.einsum("hqk,qhd->khd", score_grad, query_low, preferred_element_type=F32) * SCALE
        )
        return (query_grad, key_grad, value_grad)

    def everywhere(value):
        return lax.all_gather(value, "blk", axis=0, tiled=False)

    def global_forward(query_low, key_low, value_low):
        query_low = query_low.reshape(row_count, model_width)
        marks = jnp.zeros((KEEP, 2 * model_width), BF)
        marks = marks.at[0, :row_count].set(tag_rows.astype(BF))
        marks = marks.at[1, :row_count].set(jnp.full((row_count,), scene).astype(BF))
        outgoing = jnp.concatenate(
            [
                jnp.concatenate(
                    [
                        key_low.reshape(row_count, model_width),
                        value_low.reshape(row_count, model_width),
                    ],
                    axis=1,
                ),
                marks,
            ],
            axis=0,
        )
        pairs = everywhere(outgoing)
        tags = pairs[:, FRAME, :FRAME].astype(F32).reshape(1, -1)
        scenes = pairs[:, FRAME + 1, :FRAME].astype(F32).reshape(1, -1)
        attended, lse = global_attend(query_low, pairs, tags, scene_tile)
        every_query = everywhere(with_rows(query_low, lse.reshape(HEADS, row_count)))
        return (attended, (pairs, tags, scenes, lse, every_query))

    def global_back(query_low, key_low, value_low, attended, kept, attended_grad):
        pairs, tags, scenes, lse, every_query = kept
        delta = jnp.sum(
            (attended_grad.astype(F32) * attended).reshape(row_count, HEADS, HD), axis=-1
        ).T
        every_grad = everywhere(with_rows(attended_grad, delta))
        query_grad = global_query_grad(
            query_low.reshape(row_count, model_width),
            pairs,
            tags,
            scene_tile,
            attended_grad,
            lse,
            delta.reshape(PAIRS, 2, row_count),
        )
        key_grad, value_grad = global_key_grad(
            key_low.reshape(row_count, model_width),
            value_low.reshape(row_count, model_width),
            tag_rows.reshape(1, row_count),
            scenes,
            every_query,
            every_grad,
            rows_of(every_query, model_width),
            rows_of(every_grad, model_width),
        )
        shape = (row_count, HEADS, HD)
        return (query_grad.reshape(shape), key_grad.reshape(shape), value_grad)

    weight_sets = (qkv_weight, out_weight, up_weight, down_weight, vectors, up_bias, head_norm)
    layers = [
        tuple((weight_set[layer_index] for weight_set in weight_sets)) for layer_index in range(2)
    ]
    first_out, stored_one = block_forward(tokens[0].astype(F32), layers[0], frame_forward)
    second_out, stored_two = block_forward(first_out, layers[1], global_forward)
    grad_middle, grads_two, small_two = block_backward(
        cotangent[0].astype(F32), layers[1], stored_two, global_back
    )
    grad_input, grads_one, small_one = block_backward(
        grad_middle, layers[0], stored_one, frame_back
    )
    weight_grads = [jnp.stack([one, two]) for one, two in zip(grads_one, grads_two)]
    small = [jnp.stack([one, two]) for one, two in zip(small_one, small_two)]
    packed = lax.psum(jnp.concatenate([s.reshape(-1) for s in small]), ("blk", "grp"))
    pieces, start = [], 0
    for s in small:
        pieces.append(packed[start : start + s.size].reshape(s.shape))
        start += s.size
    return (
        second_out.astype(BF)[None],
        grad_input.astype(BF)[None],
        *weight_grads,
        part(pieces[0], me, count, 2),
        part(pieces[1], me, count, 1),
        pieces[2],
    )


def solution(mesh):
    return jax.shard_map(
        per_device,
        mesh=mesh,
        in_specs=(
            P("grp", "blk", None),
            P(),
            P(),
            P(),
            P(),
            P(),
            P(),
            P(),
            P("grp", "blk", None),
            P("grp", "blk"),
            P("grp", "blk", None),
        ),
        out_specs=(
            P("grp", "blk", None),
            P("grp", "blk", None),
            P(None, "blk", None),
            P(None, "blk", None),
            P(None, "blk", None),
            P(None, "blk", None),
            P(None, None, "blk"),
            P(None, "blk"),
            P(),
        ),
        check_vma=False,
    )
```

```python
import functools

import jax
import jax.numpy as jnp
from jax import lax
from jax.experimental import pallas as pl
from jax.experimental.pallas import tpu as pltpu
from jax.sharding import PartitionSpec as P

HEADS = 16
HD = 64
SPECIAL = 5
PAIRS = HEADS // 2
LANES = 2 * HD
FRAME = 128
KEEP = 16
EPS = 1e-06
NEG = -1e30
SCALE = HD**-0.5
BF = jnp.bfloat16
F32 = jnp.float32


def product(left_side, right_side):
    return jnp.dot(left_side, right_side, preferred_element_type=F32)


def product_left(left_side, right_side):
    return lax.dot_general(
        left_side, right_side, (((0,), (0,)), ((), ())), preferred_element_type=F32
    )


def product_right(left_side, right_side):
    return lax.dot_general(
        left_side, right_side, (((1,), (1,)), ((), ())), preferred_element_type=F32
    )


def lane_masks(dtype):
    lane = lax.broadcasted_iota(jnp.int32, (1, LANES), 1)
    first = (lane < HD).astype(dtype)
    return (first, 1 - first)


def as_column(row):
    size = row.shape[1]
    return jnp.transpose(jnp.broadcast_to(row, (LANES, size)))[:, :1]


def as_row(column):
    size = column.shape[0]
    return jnp.transpose(jnp.broadcast_to(column, (size, LANES)))[:1, :]


def flat(ref):
    block = ref[...]
    return block.reshape(block.shape[0] * block.shape[1], block.shape[2])


def attend_kernel(blocks, q_ref, k_ref, v_ref, tag_ref, scene_ref, o_ref, lse_ref, m_sc, l_sc, a_sc):
    step = pl.program_id(1)
    keys, values = flat(k_ref), flat(v_ref)
    allowed = tag_ref[...] == scene_ref[:1, :1]
    queries = q_ref[...]
    pieces = []
    for index, mask in enumerate(lane_masks(BF)):
        scores = product_right(queries * mask, keys) * SCALE
        scores = jnp.where(allowed, scores, NEG)
        top = jnp.max(scores, axis=-1, keepdims=True)

        if blocks > 1:

            @pl.when(step == 0)
            def _():
                m_sc[index] = jnp.full_like(m_sc[index], NEG)
                l_sc[index] = jnp.zeros_like(l_sc[index])
                a_sc[index] = jnp.zeros_like(a_sc[index])

            old = m_sc[index][:, :1]
            top = jnp.maximum(top, old)
            keep = jnp.exp(old - top)
        shares = jnp.where(allowed, jnp.exp(scores - top), 0.0)
        total = jnp.sum(shares, axis=-1, keepdims=True)
        weighted = product(shares.astype(BF), values)
        if blocks > 1:
            total = total + keep * l_sc[index][:, :1]
            weighted = weighted + keep * a_sc[index]
            m_sc[index] = jnp.broadcast_to(top, m_sc[index].shape)
            l_sc[index] = jnp.broadcast_to(total, l_sc[index].shape)
            a_sc[index] = weighted
        pieces.append(weighted / total)
        lse_ref[0, index : index + 1, :] = as_row(top + jnp.log(total))
    first, second = lane_masks(F32)
    o_ref[...] = jnp.where(first > 0, pieces[0], pieces[1])


def key_block(count):
    for size in (16, 8, 4, 2, 1):
        if count % size == 0:
            return size


def global_attend(queries, pairs, tags, scene):
    frames = pairs.shape[0]
    group = key_block(frames)
    blocks = frames // group
    return pl.pallas_call(
        functools.partial(attend_kernel, blocks),
        grid=(PAIRS, blocks),
        in_specs=[
            pl.BlockSpec((FRAME, LANES), lambda p, k: (0, p)),
            pl.BlockSpec((group, FRAME, LANES), lambda p, k: (k, 0, p)),
            pl.BlockSpec((group, FRAME, LANES), lambda p, k: (k, 0, PAIRS + p)),
            pl.BlockSpec((1, group * FRAME), lambda p, k: (0, k)),
            pl.BlockSpec((8, LANES), lambda p, k: (0, 0)),
        ],
        out_specs=[
            pl.BlockSpec((FRAME, LANES), lambda p, k: (0, p)),
            pl.BlockSpec((1, 2, FRAME), lambda p, k: (p, 0, 0)),
        ],
        out_shape=[
            jax.ShapeDtypeStruct((FRAME, PAIRS * LANES), F32),
            jax.ShapeDtypeStruct((PAIRS, 2, FRAME), F32),
        ],
        scratch_shapes=[pltpu.VMEM((2, FRAME, LANES), F32)] * 3,
        compiler_params=pltpu.CompilerParams(vmem_limit_bytes=48 * 2**20),
        cost_estimate=pl.CostEstimate(
            flops=4 * FRAME * frames * FRAME * LANES * HEADS,
            bytes_accessed=frames * FRAME * 4096,
            transcendentals=FRAME * frames * FRAME * HEADS,
        ),
        name="global_attend",
    )(queries, pairs, pairs, tags, scene)


def query_grad_kernel(
    q_ref, k_ref, v_ref, tag_ref, scene_ref, do_ref, lse_ref, delta_ref, dq_ref
):
    step = pl.program_id(1)
    keys, values = flat(k_ref), flat(v_ref)
    allowed = tag_ref[...] == scene_ref[:1, :1]
    queries, outs = q_ref[...], do_ref[...]
    pieces = []
    for index, mask in enumerate(lane_masks(BF)):
        scores = product_right(queries * mask, keys) * SCALE
        top = as_column(lse_ref[0, index : index + 1, :])
        delta = as_column(delta_ref[0, index : index + 1, :])
        shares = jnp.where(allowed, jnp.exp(scores - top), 0.0)
        share_grad = product_right(outs * mask, values)
        score_grad = (shares * (share_grad - delta)).astype(BF)
        pieces.append(product(score_grad, keys) * SCALE)
    first, second = lane_masks(F32)
    piece = jnp.where(first > 0, pieces[0], pieces[1])

    @pl.when(step == 0)
    def _():
        dq_ref[...] = piece

    @pl.when(step > 0)
    def _():
        dq_ref[...] += piece


def global_query_grad(queries, pairs, tags, scene, outs, lse, delta):
    frames = pairs.shape[0]
    group = key_block(frames)
    blocks = frames // group
    return pl.pallas_call(
        query_grad_kernel,
        grid=(PAIRS, blocks),
        in_specs=[
            pl.BlockSpec((FRAME, LANES), lambda p, k: (0, p)),
            pl.BlockSpec((group, FRAME, LANES), lambda p, k: (k, 0, p)),
            pl.BlockSpec((group, FRAME, LANES), lambda p, k: (k, 0, PAIRS + p)),
            pl.BlockSpec((1, group * FRAME), lambda p, k: (0, k)),
            pl.BlockSpec((8, LANES), lambda p, k: (0, 0)),
            pl.BlockSpec((FRAME, LANES), lambda p, k: (0, p)),
            pl.BlockSpec((1, 2, FRAME), lambda p, k: (p, 0, 0)),
            pl.BlockSpec((1, 2, FRAME), lambda p, k: (p, 0, 0)),
        ],
        out_specs=pl.BlockSpec((FRAME, LANES), lambda p, k: (0, p)),
        out_shape=jax.ShapeDtypeStruct((FRAME, PAIRS * LANES), F32),
        compiler_params=pltpu.CompilerParams(vmem_limit_bytes=48 * 2**20),
        cost_estimate=pl.CostEstimate(
            flops=6 * FRAME * frames * FRAME * LANES * HEADS,
            bytes_accessed=frames * FRAME * 4096,
            transcendentals=FRAME * frames * FRAME * HEADS,
        ),
        name="global_query_grad",
    )(queries, pairs, pairs, tags, scene, outs, lse, delta)


def key_grad_kernel(
    k_ref, v_ref, tag_ref, scene_ref, q_ref, do_ref, lse_ref, delta_ref, dk_ref, dv_ref
):
    step = pl.program_id(1)
    keys, values = k_ref[...], v_ref[...]
    queries, outs = flat(q_ref), flat(do_ref)
    allowed = as_column(tag_ref[...]) == scene_ref[...]
    key_pieces, value_pieces = [], []
    for index, mask in enumerate(lane_masks(BF)):
        scores = product_right(keys * mask, queries) * SCALE
        top = lse_ref[0, index : index + 1, :]
        delta = delta_ref[0, index : index + 1, :]
        shares = jnp.where(allowed, jnp.exp(scores - top), 0.0)
        share_grad = product_right(values * mask, outs)
        score_grad = (shares * (share_grad - delta)).astype(BF)
        key_pieces.append(product(score_grad, queries) * SCALE)
        value_pieces.append(product(shares.astype(BF), outs))
    first, second = lane_masks(F32)
    key_piece = jnp.where(first > 0, key_pieces[0], key_pieces[1])
    value_piece = jnp.where(first > 0, value_pieces[0], value_pieces[1])

    @pl.when(step == 0)
    def _():
        dk_ref[...] = key_piece
        dv_ref[...] = value_piece

    @pl.when(step > 0)
    def _():
        dk_ref[...] += key_piece
        dv_ref[...] += value_piece


def global_key_grad(keys, values, tags, scenes, queries, outs, lse, delta):
    frames = queries.shape[0]
    group = key_block(frames)
    blocks = frames // group
    return pl.pallas_call(
        key_grad_kernel,
        grid=(PAIRS, blocks),
        in_specs=[
            pl.BlockSpec((FRAME, LANES), lambda p, k: (0, p)),
            pl.BlockSpec((FRAME, LANES), lambda p, k: (0, p)),
            pl.BlockSpec((1, FRAME), lambda p, k: (0, 0)),
            pl.BlockSpec((1, group * FRAME), lambda p, k: (0, k)),
            pl.BlockSpec((group, FRAME, LANES), lambda p, k: (k, 0, p)),
            pl.BlockSpec((group, FRAME, LANES), lambda p, k: (k, 0, p)),
            pl.BlockSpec((1, 2, group * FRAME), lambda p, k: (p, 0, k)),
            pl.BlockSpec((1, 2, group * FRAME), lambda p, k: (p, 0, k)),
        ],
        out_specs=[pl.BlockSpec((FRAME, LANES), lambda p, k: (0, p))] * 2,
        out_shape=[jax.ShapeDtypeStruct((FRAME, PAIRS * LANES), F32)] * 2,
        compiler_params=pltpu.CompilerParams(vmem_limit_bytes=48 * 2**20),
        cost_estimate=pl.CostEstimate(
            flops=8 * FRAME * frames * FRAME * LANES * HEADS,
            bytes_accessed=frames * FRAME * 4096,
            transcendentals=FRAME * frames * FRAME * HEADS,
        ),
        name="global_key_grad",
    )(keys, values, tags, scenes, queries, outs, lse, delta)


def split_three(values):
    high = values.astype(BF)
    rest = values - high.astype(F32)
    middle = rest.astype(BF)
    return jnp.stack([high, middle, (rest - middle.astype(F32)).astype(BF)])


def with_rows(body, statistic):
    width = body.shape[1]
    extra = split_three(statistic).reshape(-1, width)
    pad = jnp.zeros((KEEP - extra.shape[0], width), BF)
    return jnp.concatenate([body, extra, pad], axis=0)


def rows_of(gathered, width):
    frames = gathered.shape[0]
    used = 3 * HEADS * FRAME // width
    terms = gathered[:, FRAME : FRAME + used].reshape(frames, 3, HEADS, FRAME).astype(F32)
    total = terms[:, 0] + terms[:, 1] + terms[:, 2]
    return total.transpose(1, 0, 2).reshape(PAIRS, 2, frames * FRAME)


VMEM_MIB = 2**20
WIDE = 256
ROOT_HALF = 0.7071067811865476
ROOT_TWO_PI = 0.3989422804014327


def whole(space=pltpu.VMEM):
    return pl.BlockSpec(memory_space=space)


def terms_of(values):
    high = values.astype(BF)
    rest = values - high.astype(F32)
    middle = rest.astype(BF)
    return (high, middle, (rest - middle.astype(F32)).astype(BF))


def head_averager():
    row = lax.broadcasted_iota(jnp.int32, (WIDE, WIDE), 0) // HD
    col = lax.broadcasted_iota(jnp.int32, (WIDE, WIDE), 1) // HD
    return jnp.where(row == col, 1.0 / HD, 0.0).astype(BF)


def head_mean(values, averager):
    high, middle, least = terms_of(values)
    return product(high, averager) + product(middle, averager) + product(least, averager)


def standard(values):
    centered = values - jnp.mean(values, axis=-1, keepdims=True)
    scale = lax.rsqrt(jnp.mean(centered * centered, axis=-1, keepdims=True) + EPS)
    return centered * scale, scale


def standard_heads(values, averager):
    centered = values - head_mean(values, averager)
    scale = lax.rsqrt(head_mean(centered * centered, averager) + EPS)
    return centered * scale, scale


def norm_pull(values, gain, grad):
    unit, scale = standard(values)
    scaled = grad * gain
    spread = jnp.mean(scaled * unit, axis=-1, keepdims=True)
    result = scale * (scaled - jnp.mean(scaled, axis=-1, keepdims=True) - unit * spread)
    return (
        result,
        jnp.sum(grad * unit, axis=0, keepdims=True),
        jnp.sum(grad, axis=0, keepdims=True),
    )


def weight_copies(sources, targets, sems):
    copies = [
        pltpu.make_async_copy(source, target, sems.at[index])
        for index, (source, target) in enumerate(zip(sources, targets))
    ]
    for copy in copies:
        copy.start()
    return copies


def column_pieces(ref, parts):
    size = ref.shape[-1] // parts
    return [ref.at[:, i * size : (i + 1) * size] for i in range(parts)]


def row_pieces(ref, parts):
    size = ref.shape[0] // parts
    return [ref.at[i * size : (i + 1) * size] for i in range(parts)]


def project(layer, residual, vec_ref, head_ref, w_ref, copies, normed_ref, pre_ref, qkv_ref):
    width = residual.shape[1]
    unit, _ = standard(residual)
    normed = (unit * vec_ref[layer, 0:1] + vec_ref[layer, 1:2]).astype(BF)
    normed_ref[...] = normed
    averager = head_averager()
    for part in range(3):
        copies[part].wait()
        bias = vec_ref[layer, 2 + part : 3 + part]
        for j in range(width // WIDE):
            at = slice(part * width + j * WIDE, part * width + (j + 1) * WIDE)
            value = product(normed, w_ref[:, at]) + bias[:, j * WIDE : (j + 1) * WIDE]
            if part < 2:
                pre_ref[:, at] = value
                unit, _ = standard_heads(value, averager)
                value = unit * head_ref[layer, 2 * part : 2 * part + 1]
                if part == 0:
                    value = value + head_ref[layer, 1:2]
            qkv_ref[:, at] = value.astype(BF)


def frame_attend(usable, qkv_ref, att_ref):
    width = att_ref.shape[1]
    first, _ = lane_masks(F32)
    for pair in range(width // LANES):
        q, k, v = [
            qkv_ref[:, part * width + pair * LANES : part * width + (pair + 1) * LANES]
            for part in range(3)
        ]
        pieces = []
        for mask in lane_masks(BF):
            shares = frame_shares(q * mask, k, usable)
            pieces.append(product(shares.astype(BF), v))
        at = slice(pair * LANES, (pair + 1) * LANES)
        att_ref[:, at] = jnp.where(first > 0, pieces[0], pieces[1]).astype(att_ref.dtype)


def frame_shares(queries, keys, usable):
    scores = jnp.where(usable > 0, product_right(queries, keys) * SCALE, NEG)
    shares = jnp.exp(scores - jnp.max(scores, axis=-1, keepdims=True))
    return shares / jnp.sum(shares, axis=-1, keepdims=True)


def feed_forward(
    layer, att, residual, vec_ref, bias_ref, w_out, w_up, w_down, copies, mixed_ref, middle_ref,
    lifted_ref, slope_ref, active_ref, feed_ref,
):
    chunks = w_up.shape[1] // 512
    copies[0].wait()
    mixed = product(att, w_out[...]) + vec_ref[layer, 5:6]
    mixed_ref[...] = mixed
    middle = residual + vec_ref[layer, 6:7] * mixed
    middle_ref[...] = middle
    unit, _ = standard(middle)
    lifted = (unit * vec_ref[layer, 7:8] + vec_ref[layer, 8:9]).astype(BF)
    lifted_ref[...] = lifted
    feed = None
    for j in range(chunks):
        at = slice(j * 512, (j + 1) * 512)
        if j % 2 == 0:
            copies[1 + j].wait()
            copies[2 + j].wait()
        hidden = product(lifted, w_up[:, at]) + bias_ref[layer : layer + 1, at]
        bell = 0.5 * (1.0 + lax.erf(hidden * ROOT_HALF))
        slope_ref[:, at] = bell + hidden * jnp.exp(-0.5 * hidden * hidden) * ROOT_TWO_PI
        active = (hidden * bell).astype(BF)
        active_ref[:, at] = active
        piece = product(active, w_down[at])
        feed = piece if feed is None else feed + piece
    feed = feed + vec_ref[layer, 9:10]
    feed_ref[...] = feed
    return middle + vec_ref[layer, 10:11] * feed


def split_columns(value_refs, x_at, keep_ref, send_ref):
    start = 0
    for value_ref in value_refs:
        half = value_ref.shape[1] // 2
        to = slice(start, start + half)
        keep_ref[:, to] = value_ref[:, pl.ds(pl.multiple_of(x_at * half, LANES), half)]
        send_ref[:, to] = value_ref[:, pl.ds(pl.multiple_of((1 - x_at) * half, LANES), half)]
        start += half


def feed_backward(
    layer, grad, feed, middle, mixed, slope_ref, vec_ref, w_up, w_down, copies, feed_grad_ref,
    hidden_grad_ref, mixed_grad_ref, bias_out, rows_ref, row0,
):
    chunks = w_up.shape[1] // 512
    feed_grad = (vec_ref[layer, 10:11] * grad).astype(BF)
    feed_grad_ref[...] = feed_grad
    rows_ref[row0 + 4 : row0 + 5] = jnp.sum(feed_grad.astype(F32), axis=0, keepdims=True)
    rows_ref[row0 + 5 : row0 + 6] = jnp.sum(grad * feed, axis=0, keepdims=True)
    lifted_grad = None
    for j in range(chunks):
        at = slice(j * 512, (j + 1) * 512)
        if copies is not None and j % 2 == 0:
            copies[j].wait()
            copies[j + 1].wait()
        hidden_grad = (slope_ref[:, at] * product_right(feed_grad, w_down[at])).astype(BF)
        hidden_grad_ref[:, at] = hidden_grad
        bias_out[:, at] = jnp.sum(hidden_grad.astype(F32), axis=0, keepdims=True)
        piece = product_right(hidden_grad, w_up[:, at])
        lifted_grad = piece if lifted_grad is None else lifted_grad + piece
    part, gain_grad, shift_grad = norm_pull(middle, vec_ref[layer, 7:8], lifted_grad)
    middle_grad = grad + part
    mixed_grad = (vec_ref[layer, 6:7] * middle_grad).astype(BF)
    mixed_grad_ref[...] = mixed_grad
    rows_ref[row0 : row0 + 1] = jnp.sum(mixed_grad.astype(F32), axis=0, keepdims=True)
    rows_ref[row0 + 1 : row0 + 2] = jnp.sum(middle_grad * mixed, axis=0, keepdims=True)
    rows_ref[row0 + 2 : row0 + 3] = gain_grad
    rows_ref[row0 + 3 : row0 + 4] = shift_grad
    return middle_grad


def project_backward(
    layer, residual, dqkv_ref, pre_ref, vec_ref, head_ref, w_ref, copies, pg_ref, rows_ref, head_out
):
    width = residual.shape[1]
    averager = head_averager()
    sums = [None, None, None]
    for part in range(3):
        for j in range(width // WIDE):
            at = slice(part * width + j * WIDE, part * width + (j + 1) * WIDE)
            value = dqkv_ref[:, at].astype(F32)
            if part < 2:
                unit, scale = standard_heads(pre_ref[:, at], averager)
                news = [(2 * part, jnp.sum(value * unit, axis=0, keepdims=True))]
                if part == 0:
                    news.append((1, jnp.sum(value, axis=0, keepdims=True)))
                for index, new in news:
                    sums[index] = new if sums[index] is None else sums[index] + new
                scaled = value * head_ref[layer, 2 * part : 2 * part + 1]
                value = scale * (
                    scaled
                    - head_mean(scaled, averager)
                    - unit * head_mean(scaled * unit, averager)
                )
            low = value.astype(BF)
            pg_ref[:, at] = low
            rows_ref[2 + part : 3 + part, j * WIDE : (j + 1) * WIDE] = jnp.sum(
                low.astype(F32), axis=0, keepdims=True
            )
    head_out[...] = jnp.concatenate(sums + [jnp.zeros((5, WIDE), F32)], axis=0)
    normed_grad = None
    for part in range(3):
        copies[part].wait()
        at = slice(part * width, (part + 1) * width)
        piece = product_right(pg_ref[:, at], w_ref[:, at])
        normed_grad = piece if normed_grad is None else normed_grad + piece
    part, gain_grad, shift_grad = norm_pull(residual, vec_ref[layer, 0:1], normed_grad)
    rows_ref[0:1] = gain_grad
    rows_ref[1:2] = shift_grad
    return part


def interleaved(one, two):
    return [piece for pair in zip(one, two) for piece in pair]


def front_kernel(
    tok_ref, usable_ref, vec_ref, bias_ref, head_ref, qkv_w, out_w, up_w, down_w,
    left_pack, pre0, qkv0, mixed0, middle0, slope0, feed0, res1, pre1, qkv1,
    w_qkv, w_out, w_up, w_down, w_next, sems,
):
    width, units = tok_ref.shape[1], up_w.shape[2]
    lifted0 = left_pack.at[:, :width]
    active0 = left_pack.at[:, width : width + units]
    normed0, att0, normed1 = [
        left_pack.at[:, units + i * width : units + (i + 1) * width] for i in (1, 2, 3)
    ]
    copies = weight_copies(
        column_pieces(qkv_w.at[0], 3)
        + [out_w.at[0]]
        + interleaved(column_pieces(up_w.at[0], 4), row_pieces(down_w.at[0], 4))
        + column_pieces(qkv_w.at[1], 3),
        column_pieces(w_qkv, 3)
        + [w_out]
        + interleaved(column_pieces(w_up, 4), row_pieces(w_down, 4))
        + column_pieces(w_next, 3),
        sems,
    )
    residual = tok_ref[...].astype(F32)
    project(0, residual, vec_ref, head_ref, w_qkv, copies[:3], normed0, pre0, qkv0)
    frame_attend(usable_ref[...], qkv0, att0)
    result = feed_forward(
        0, att0[...], residual, vec_ref, bias_ref, w_out, w_up, w_down, copies[3:12], mixed0,
        middle0, lifted0, slope0, active0, feed0,
    )
    res1[...] = result
    project(1, result, vec_ref, head_ref, w_next, copies[12:], normed1, pre1, qkv1)


def front(tokens, usable, vectors, up_bias, head_rows, qkv_weight, out_weight, up_weight, down_weight):
    rows, width = tokens.shape
    hidden = up_weight.shape[2]
    shapes = [
        ((rows, hidden + 4 * width), BF),
        ((rows, 2 * width), F32),
        ((rows, 3 * width), BF),
        ((rows, width), F32),
        ((rows, width), F32),
        ((rows, hidden), F32),
        ((rows, width), F32),
        ((rows, width), F32),
        ((rows, 2 * width), F32),
        ((rows, 3 * width), BF),
    ]
    return pl.pallas_call(
        front_kernel,
        in_specs=[whole()] * 5 + [whole(pl.ANY)] * 4,
        out_specs=[whole()] * len(shapes),
        out_shape=[jax.ShapeDtypeStruct(*shape) for shape in shapes],
        scratch_shapes=[
            pltpu.VMEM((width, 3 * width), BF),
            pltpu.VMEM((width, width), BF),
            pltpu.VMEM((width, hidden), BF),
            pltpu.VMEM((hidden, width), BF),
            pltpu.VMEM((width, 3 * width), BF),
            pltpu.SemaphoreType.DMA((15,)),
        ],
        compiler_params=pltpu.CompilerParams(vmem_limit_bytes=58 * VMEM_MIB),
        cost_estimate=pl.CostEstimate(
            flops=2 * rows * width * (7 * width + 2 * hidden),
            bytes_accessed=2 * width * (7 * width + 2 * hidden),
            transcendentals=2 * rows * hidden,
        ),
        name="front",
    )(tokens, usable, vectors, up_bias, head_rows, qkv_weight, out_weight, up_weight, down_weight)


def turn_kernel(
    x_ref, att_ref, res_ref, cot_ref, vec_ref, bias_ref, out_w, up_w, down_w,
    left_pack, output, right_keep, right_send, att_grad, middle_grad, bias_out, rows_out,
    w_out, w_up, w_down, mixed_sc, middle_sc, slope_sc, feed_sc, fg_sc, hg_sc, mg_sc, sems,
):
    width, units = att_ref.shape[1], up_w.shape[2]
    lifted = left_pack.at[:, :width]
    active = left_pack.at[:, width : width + units]
    left_pack[:, width + units :] = att_ref[...]
    copies = weight_copies(
        [out_w.at[1]] + interleaved(column_pieces(up_w.at[1], 4), row_pieces(down_w.at[1], 4)),
        [w_out] + interleaved(column_pieces(w_up, 4), row_pieces(w_down, 4)),
        sems,
    )
    result = feed_forward(
        1, att_ref[...], res_ref[...], vec_ref, bias_ref, w_out, w_up, w_down, copies, mixed_sc,
        middle_sc, lifted, slope_sc, active, feed_sc,
    )
    output[...] = result.astype(BF)
    grad = feed_backward(
        1, cot_ref[...].astype(F32), feed_sc[...], middle_sc[...], mixed_sc[...], slope_sc, vec_ref,
        w_up, w_down, None, fg_sc, hg_sc, mg_sc, bias_out, rows_out, 0,
    )
    middle_grad[...] = grad
    att_grad[...] = product_right(mg_sc[...], w_out[...]).astype(BF)
    split_columns([hg_sc, fg_sc, mg_sc], x_ref[0], right_keep, right_send)


def turn(x_at, att, res, cotangent, vectors, up_bias, out_weight, up_weight, down_weight):
    rows, width = res.shape
    hidden = up_weight.shape[2]
    shapes = [
        ((rows, hidden + 2 * width), BF),
        ((rows, width), BF),
        ((rows, hidden // 2 + width), BF),
        ((rows, hidden // 2 + width), BF),
        ((rows, width), BF),
        ((rows, width), F32),
        ((1, hidden), F32),
        ((8, width), F32),
    ]
    return pl.pallas_call(
        turn_kernel,
        in_specs=[whole(pltpu.SMEM)] + [whole()] * 5 + [whole(pl.ANY)] * 3,
        out_specs=[whole()] * len(shapes),
        out_shape=[jax.ShapeDtypeStruct(*shape) for shape in shapes],
        scratch_shapes=[
            pltpu.VMEM((width, width), BF),
            pltpu.VMEM((width, hidden), BF),
            pltpu.VMEM((hidden, width), BF),
            pltpu.VMEM((rows, width), F32),
            pltpu.VMEM((rows, width), F32),
            pltpu.VMEM((rows, hidden), F32),
            pltpu.VMEM((rows, width), F32),
            pltpu.VMEM((rows, width), BF),
            pltpu.VMEM((rows, hidden), BF),
            pltpu.VMEM((rows, width), BF),
            pltpu.SemaphoreType.DMA((9,)),
        ],
        compiler_params=pltpu.CompilerParams(vmem_limit_bytes=58 * VMEM_MIB),
        cost_estimate=pl.CostEstimate(
            flops=4 * rows * width * (width + 2 * hidden),
            bytes_accessed=2 * width * (width + 2 * hidden),
            transcendentals=2 * rows * hidden,
        ),
        name="turn",
    )(x_at, att, res, cotangent, vectors, up_bias, out_weight, up_weight, down_weight)


def back_one_kernel(
    x_ref, dqkv_ref, pre_ref, res_ref, grad_ref, feed_ref, middle_ref, mixed_ref, slope_ref,
    vec_ref, head_ref, qkv_w, up_w, down_w,
    pg_keep, pg_send, right_keep, right_send, mixed_grad, middle_grad, bias_out, rows_out, head_out,
    w_qkv, w_up, w_down, pg_sc, fg_sc, hg_sc, sems,
):
    copies = weight_copies(
        column_pieces(qkv_w.at[1], 3)
        + interleaved(column_pieces(up_w.at[0], 4), row_pieces(down_w.at[0], 4)),
        column_pieces(w_qkv, 3) + interleaved(column_pieces(w_up, 4), row_pieces(w_down, 4)),
        sems,
    )
    part = project_backward(
        1, res_ref[...], dqkv_ref, pre_ref, vec_ref, head_ref, w_qkv, copies[:3], pg_sc,
        rows_out, head_out,
    )
    split_columns([pg_sc], x_ref[0], pg_keep, pg_send)
    middle_grad[...] = feed_backward(
        0, grad_ref[...] + part, feed_ref[...], middle_ref[...], mixed_ref[...], slope_ref, vec_ref,
        w_up, w_down, copies[3:], fg_sc, hg_sc, mixed_grad, bias_out, rows_out, 8,
    )
    split_columns([hg_sc, fg_sc, mixed_grad], x_ref[0], right_keep, right_send)


def back_one(
    x_at, dqkv, pre, res, grad, feed, middle, mixed, slope, vectors, head_rows, qkv_weight,
    up_weight, down_weight,
):
    rows, width = res.shape
    hidden = up_weight.shape[2]
    shapes = [
        ((rows, 3 * width // 2), BF),
        ((rows, 3 * width // 2), BF),
        ((rows, hidden // 2 + width), BF),
        ((rows, hidden // 2 + width), BF),
        ((rows, width), BF),
        ((rows, width), F32),
        ((1, hidden), F32),
        ((16, width), F32),
        ((8, WIDE), F32),
    ]
    return pl.pallas_call(
        back_one_kernel,
        in_specs=[whole(pltpu.SMEM)] + [whole()] * 10 + [whole(pl.ANY)] * 3,
        out_specs=[whole()] * len(shapes),
        out_shape=[jax.ShapeDtypeStruct(*shape) for shape in shapes],
        scratch_shapes=[
            pltpu.VMEM((width, 3 * width), BF),
            pltpu.VMEM((width, hidden), BF),
            pltpu.VMEM((hidden, width), BF),
            pltpu.VMEM((rows, 3 * width), BF),
            pltpu.VMEM((rows, width), BF),
            pltpu.VMEM((rows, hidden), BF),
            pltpu.SemaphoreType.DMA((11,)),
        ],
        compiler_params=pltpu.CompilerParams(vmem_limit_bytes=58 * VMEM_MIB),
        cost_estimate=pl.CostEstimate(
            flops=2 * rows * width * (3 * width + 2 * hidden),
            bytes_accessed=2 * width * (3 * width + 2 * hidden),
            transcendentals=0,
        ),
        name="back_one",
    )(
        x_at, dqkv, pre, res, grad, feed, middle, mixed, slope, vectors, head_rows, qkv_weight,
        up_weight, down_weight,
    )


def back_two_kernel(
    x_ref, mixed_ref, grad_ref, qkv_ref, pre_ref, tok_ref, usable_ref, vec_ref, head_ref, out_w,
    qkv_w, pg_keep, pg_send, input_grad, rows_out, head_out, w_out, w_qkv, dqkv_sc, pg_sc, sems,
):
    width = tok_ref.shape[1]
    copies = weight_copies(
        [out_w.at[0]] + column_pieces(qkv_w.at[0], 3), [w_out] + column_pieces(w_qkv, 3), sems
    )
    copies[0].wait()
    att_grad = product_right(mixed_ref[...], w_out[...]).astype(BF)
    first, _ = lane_masks(F32)
    usable = usable_ref[...]
    for pair in range(width // LANES):
        q, k, v = [
            qkv_ref[:, part * width + pair * LANES : part * width + (pair + 1) * LANES]
            for part in range(3)
        ]
        out = att_grad[:, pair * LANES : (pair + 1) * LANES]
        pieces = []
        for mask in lane_masks(BF):
            shares = frame_shares(q * mask, k, usable)
            share_grad = product_right(out * mask, v)
            delta = jnp.sum(shares * share_grad, axis=-1, keepdims=True)
            score_grad = (shares * (share_grad - delta)).astype(BF)
            pieces.append(
                (
                    product(score_grad, k) * SCALE,
                    product_left(score_grad, q) * SCALE,
                    product_left(shares.astype(BF), out),
                )
            )
        for part in range(3):
            dqkv_sc[:, part * width + pair * LANES : part * width + (pair + 1) * LANES] = jnp.where(
                first > 0, pieces[0][part], pieces[1][part]
            )
    part = project_backward(
        0, tok_ref[...].astype(F32), dqkv_sc, pre_ref, vec_ref, head_ref, w_qkv, copies[1:], pg_sc,
        rows_out, head_out,
    )
    split_columns([pg_sc], x_ref[0], pg_keep, pg_send)
    input_grad[...] = (grad_ref[...] + part).astype(BF)


def back_two(
    x_at, mixed_grad, grad, qkv, pre, tokens, usable, vectors, head_rows, out_weight, qkv_weight
):
    rows, width = tokens.shape
    shapes = [
        ((rows, 3 * width // 2), BF),
        ((rows, 3 * width // 2), BF),
        ((rows, width), BF),
        ((8, width), F32),
        ((8, WIDE), F32),
    ]
    return pl.pallas_call(
        back_two_kernel,
        in_specs=[whole(pltpu.SMEM)] + [whole()] * 8 + [whole(pl.ANY)] * 2,
        out_specs=[whole()] * len(shapes),
        out_shape=[jax.ShapeDtypeStruct(*shape) for shape in shapes],
        scratch_shapes=[
            pltpu.VMEM((width, width), BF),
            pltpu.VMEM((width, 3 * width), BF),
            pltpu.VMEM((rows, 3 * width), F32),
            pltpu.VMEM((rows, 3 * width), BF),
            pltpu.SemaphoreType.DMA((4,)),
        ],
        compiler_params=pltpu.CompilerParams(vmem_limit_bytes=48 * VMEM_MIB),
        cost_estimate=pl.CostEstimate(
            flops=2 * rows * width * 4 * width,
            bytes_accessed=2 * width * 4 * width,
            transcendentals=HEADS * rows * rows,
        ),
        name="back_two",
    )(x_at, mixed_grad, grad, qkv, pre, tokens, usable, vectors, head_rows, out_weight, qkv_weight)


def weight_grad_kernel(outer, tall, starts, at_ref, *refs):
    count = len(tall)
    lefts, rights = refs[: 4 * count], refs[4 * count : 8 * count]
    keep, send = refs[8 * count : 8 * count + 2]
    left_sc = refs[8 * count + 2 : 9 * count + 2]
    right_sc = refs[9 * count + 2 : 10 * count + 2]
    sems = refs[10 * count + 2]
    c_at, y_at = at_ref[0], at_ref[1]
    rows = lefts[0].shape[0]
    group = keep.shape[0] // outer
    copies = []
    for w in range(count):
        cols, left_cols = right_sc[w].shape[1], left_sc[w].shape[1]
        left_start, right_start = starts[w]
        for s in range(4):
            at = pl.ds(pl.multiple_of(right_start + c_at * cols, LANES), cols)
            copies.append(
                pltpu.make_async_copy(
                    rights[4 * w + s].at[:, at],
                    right_sc[w].at[s * rows : (s + 1) * rows],
                    sems.at[len(copies)],
                )
            )
            copies.append(
                pltpu.make_async_copy(
                    lefts[4 * w + s].at[:, left_start : left_start + left_cols],
                    left_sc[w].at[s * rows : (s + 1) * rows],
                    sems.at[len(copies)],
                )
            )
    for copy in copies:
        copy.start()
    start = 0
    for w in range(count):
        for copy in copies[8 * w : 8 * w + 8]:
            copy.wait()
        cols = right_sc[w].shape[1]
        right = right_sc[w][...]
        for block in range(left_sc[w].shape[1] // 512):
            result = product_left(left_sc[w][:, block * 512 : (block + 1) * 512], right).astype(BF)
            targets = {0: [], 1: []}
            if tall[w]:
                size, part = 4 * group, group // 2
                for piece in range(512 // part):
                    row = block * 512 + piece * part
                    o, y = row // (2 * size), (row // size) % 2
                    core, t = (row % size) // (size // 2), (row % (size // 2)) // part
                    targets[y].append(
                        (piece * part, part, o * group + core * part, start + t * cols)
                    )
            else:
                for piece in range(512 // group):
                    row = block * 512 + piece * group
                    o, y = row // (2 * group), (row // group) % 2
                    targets[y].append((piece * group, group, o * group, start))
            for y in range(2):
                if not targets[y]:
                    continue

                def store(ref, y=y):
                    for source, size, row, col in targets[y]:
                        ref[row : row + size, col : col + cols] = result[source : source + size]

                @pl.when(y_at == y)
                def _():
                    store(keep)

                @pl.when(y_at != y)
                def _():
                    store(send)

        start += cols * (4 if tall[w] else 1)


def weight_grads(name, outer, width, places, products):
    rows = products[0][0][0].shape[0]
    group = width // (2 * outer)
    lefts, left_starts, left_cols, rights, right_starts, halves, tall = zip(*products)
    columns = [half // 2 for half in halves]
    total = sum(c * (4 if t else 1) for c, t in zip(columns, tall))
    shape = jax.ShapeDtypeStruct((outer * group, total), BF)
    count = len(products)
    return pl.pallas_call(
        functools.partial(
            weight_grad_kernel, outer, tall, tuple(zip(left_starts, right_starts))
        ),
        in_specs=[whole(pltpu.SMEM)] + [whole(pl.ANY)] * (8 * count),
        out_specs=[whole()] * 2,
        out_shape=[shape] * 2,
        scratch_shapes=[pltpu.VMEM((4 * rows, c), BF) for c in left_cols]
        + [pltpu.VMEM((4 * rows, c), BF) for c in columns]
        + [pltpu.SemaphoreType.DMA((8 * count,))],
        compiler_params=pltpu.CompilerParams(vmem_limit_bytes=48 * VMEM_MIB),
        cost_estimate=pl.CostEstimate(
            flops=16 * rows * outer * group * total,
            bytes_accessed=8 * outer * group * total,
            transcendentals=0,
        ),
        name=name,
    )(places, *[a for l in lefts for a in l], *[a for r in rights for a in r])


def assemble_kernel(at_ref, *refs):
    pieces, outs = refs[:8], refs[8:]
    qkv_out, out_out, up_out, down_out = outs
    x_at, c_at = at_ref[2], at_ref[0]
    part = qkv_out.shape[1]
    for layer in range(2):
        for source in range(4):
            feed, att = [
                pieces[layer * 4 + kind * 2 + source // 2].at[source % 2] for kind in range(2)
            ]
            x = x_at if source < 2 else 1 - x_at
            c = c_at if source % 2 == 0 else 1 - c_at
            place = 2 * x + c

            def put(ref, values, row=0, layer=layer, place=place):
                cols = values.shape[1]
                at = pl.ds(pl.multiple_of(place * cols, LANES), cols)
                ref[layer, row : row + values.shape[0], at] = values.astype(F32)

            up_cols = up_out.shape[2] // 4
            down_cols = down_out.shape[2] // 4
            qkv_cols = qkv_out.shape[2] // 4
            put(up_out, feed[:, :up_cols])
            for t in range(4):
                put(
                    down_out,
                    feed[:, up_cols + t * down_cols : up_cols + (t + 1) * down_cols],
                    t * part,
                )
            put(qkv_out, att[:, :qkv_cols])
            put(out_out, att[:, qkv_cols:])


def assemble(places, pieces, shapes):
    return pl.pallas_call(
        assemble_kernel,
        in_specs=[whole(pltpu.SMEM)] + [whole()] * 8,
        out_specs=[whole()] * 4,
        out_shape=[jax.ShapeDtypeStruct(shape, F32) for shape in shapes],
        compiler_params=pltpu.CompilerParams(vmem_limit_bytes=40 * VMEM_MIB),
        name="assemble",
    )(places, *pieces)


PEERS = HEADS
FOLD = FRAME // 2
EXTRA = 16
MESH = pl.DeviceIdType.MESH


def fold_pair(values):
    lane = lax.broadcasted_iota(jnp.int32, (FOLD, LANES), 1)
    top, bottom = values[:FOLD], values[FOLD:]
    one = jnp.where(lane < HD, top, pltpu.roll(bottom, HD, 1))
    two = jnp.where(lane < HD, pltpu.roll(top, HD, 1), bottom)
    return one, two


def unfold_pair(one, two):
    lane = lax.broadcasted_iota(jnp.int32, (FOLD, LANES), 1)
    top = jnp.where(lane < HD, one, pltpu.roll(two, HD, 1))
    bottom = jnp.where(lane < HD, pltpu.roll(one, HD, 1), two)
    return top, bottom


def unfold_head(folded):
    lane = lax.broadcasted_iota(jnp.int32, (FOLD, LANES), 1)
    folded = folded.astype(F32)
    top = jnp.where(lane < HD, folded, 0.0)
    bottom = jnp.where(lane < HD, pltpu.roll(folded, HD, 1), 0.0)
    return top.astype(BF), bottom.astype(BF)


def fold_head(values):
    lane = lax.broadcasted_iota(jnp.int32, (FOLD, LANES), 1)
    return jnp.where(lane < HD, values[:FOLD], pltpu.roll(values[FOLD:], HD, 1))


def greet(me):
    barrier = pltpu.get_barrier_semaphore()
    for k in range(1, PEERS):
        pl.semaphore_signal(barrier, 1, device_id={"blk": me ^ k}, device_id_type=MESH)
    pl.semaphore_wait(barrier, PEERS - 1)


def exchange(me, k, source, target, send_sems, recv_sems):
    return pltpu.make_async_remote_copy(
        src_ref=source,
        dst_ref=target,
        send_sem=send_sems.at[k],
        recv_sem=recv_sems.at[k],
        device_id={"blk": me ^ k},
        device_id_type=MESH,
    )


GROUPS = 4
PER = PEERS // GROUPS


def head_forward_kernel(
    qkv_ref, tag_ref, att_ref, q_out, k_out, v_out, o_out, lse_ref, marks_ref,
    pack, got, outs, back, local, send, recv, back_send, back_recv,
):
    me = lax.axis_index("blk")
    width = att_ref.shape[1]
    for pair in range(width // LANES):
        for part in range(3):
            block = qkv_ref[:, part * width + pair * LANES : part * width + (pair + 1) * LANES]
            one, two = fold_pair(block.astype(F32))
            pack[2 * pair, part * FOLD : (part + 1) * FOLD] = one.astype(BF)
            pack[2 * pair + 1, part * FOLD : (part + 1) * FOLD] = two.astype(BF)
    for head in range(HEADS):
        pack[head, 3 * FOLD :] = tag_ref[...]
    greet(me)
    copies = [
        exchange(me, k, pack.at[me ^ k], got.at[me], send, recv) for k in range(PEERS - 1, 0, -1)
    ]
    for copy in copies:
        copy.start()
    own = pltpu.make_async_copy(pack.at[me], got.at[me], local.at[0])
    own.start()
    own.wait()
    for copy in copies:
        copy.wait()
    for s in range(PEERS):
        for part, target in enumerate((q_out, k_out, v_out)):
            top, bottom = unfold_head(got[s, part * FOLD : (part + 1) * FOLD])
            target[s * FRAME : s * FRAME + FOLD] = top
            target[s * FRAME + FOLD : (s + 1) * FRAME] = bottom
        marks_ref[s : s + 1] = got[s, 3 * FOLD : 3 * FOLD + 1].astype(F32)
        marks_ref[PEERS + s : PEERS + s + 1] = got[s, 3 * FOLD + 1 : 3 * FOLD + 2].astype(F32)
    keys, values = k_out[...], v_out[...]
    tags = jnp.concatenate([marks_ref[s : s + 1] for s in range(PEERS)], axis=1)
    sends = []
    for g in range(GROUPS):
        at = slice(g * PER * FRAME, (g + 1) * PER * FRAME)
        scores = product_right(q_out[at], keys) * SCALE
        scenes = jnp.concatenate(
            [
                jnp.broadcast_to(marks_ref[PEERS + s : PEERS + s + 1, :1], (FRAME, 1))
                for s in range(g * PER, (g + 1) * PER)
            ],
            axis=0,
        )
        allowed = tags == scenes
        scores = jnp.where(allowed, scores, NEG)
        top = jnp.max(scores, axis=-1, keepdims=True)
        shares = jnp.exp(scores - top)
        total = jnp.sum(shares, axis=-1, keepdims=True)
        result = product(shares.astype(BF), values) / total
        o_out[at] = result
        lse_ref[g : g + 1] = as_row(top + jnp.log(total))
        for s in range(PER):
            outs[g * PER + s] = fold_head(result[s * FRAME : (s + 1) * FRAME]).astype(BF)
    sends = [
        exchange(me, k, outs.at[me ^ k], back.at[me], back_send, back_recv)
        for k in range(PEERS - 1, 0, -1)
    ]
    for copy in sends:
        copy.start()
    own = pltpu.make_async_copy(outs.at[me], back.at[me], local.at[1])
    own.start()
    own.wait()
    for copy in sends:
        copy.wait()
    for pair in range(width // LANES):
        top, bottom = unfold_pair(back[2 * pair].astype(F32), back[2 * pair + 1].astype(F32))
        att_ref[:FOLD, pair * LANES : (pair + 1) * LANES] = top.astype(BF)
        att_ref[FOLD:, pair * LANES : (pair + 1) * LANES] = bottom.astype(BF)


def head_forward(qkv, marks):
    width = qkv.shape[1] // 3
    every = PEERS * FRAME
    shapes = [
        ((FRAME, width), BF),
        ((every, LANES), BF),
        ((every, LANES), BF),
        ((every, LANES), BF),
        ((every, LANES), F32),
        ((GROUPS, PER * FRAME), F32),
        ((2 * PEERS, LANES), F32),
    ]
    return pl.pallas_call(
        head_forward_kernel,
        in_specs=[whole()] * 2,
        out_specs=[whole()] * len(shapes),
        out_shape=[jax.ShapeDtypeStruct(*shape) for shape in shapes],
        scratch_shapes=[
            pltpu.VMEM((PEERS, 3 * FOLD + EXTRA, LANES), BF),
            pltpu.VMEM((PEERS, 3 * FOLD + EXTRA, LANES), BF),
            pltpu.VMEM((PEERS, FOLD, LANES), BF),
            pltpu.VMEM((PEERS, FOLD, LANES), BF),
            pltpu.SemaphoreType.DMA((2,)),
        ]
        + [pltpu.SemaphoreType.DMA((PEERS,))] * 4,
        compiler_params=pltpu.CompilerParams(
            vmem_limit_bytes=48 * VMEM_MIB, collective_id=1, has_side_effects=True
        ),
        cost_estimate=pl.CostEstimate(
            flops=4 * every * every * LANES, bytes_accessed=2**22, transcendentals=every * every
        ),
        name="head_forward",
    )(qkv, marks)


def head_backward_kernel(
    grad_ref, q_ref, k_ref, v_ref, o_ref, lse_ref, marks_ref, dqkv_ref,
    pack, got, grads, pairs_out, queries_out, pairs_in, queries_in, local,
    send, recv, pair_send, pair_recv, query_send, query_recv,
):
    me = lax.axis_index("blk")
    width = grad_ref.shape[1]
    for pair in range(width // LANES):
        one, two = fold_pair(grad_ref[:, pair * LANES : (pair + 1) * LANES].astype(F32))
        pack[2 * pair] = one.astype(BF)
        pack[2 * pair + 1] = two.astype(BF)
    greet(me)
    copies = [
        exchange(me, k, pack.at[me ^ k], got.at[me], send, recv) for k in range(PEERS - 1, 0, -1)
    ]
    for copy in copies:
        copy.start()
    own = pltpu.make_async_copy(pack.at[me], got.at[me], local.at[0])
    own.start()
    own.wait()
    for copy in copies:
        copy.wait()
    for s in range(PEERS):
        top, bottom = unfold_head(got[s])
        grads[s * FRAME : s * FRAME + FOLD] = top
        grads[s * FRAME + FOLD : (s + 1) * FRAME] = bottom
    queries, outs = q_ref[...], grads[...]
    deltas = []
    for s in range(PEERS):
        at = slice(s * FRAME, (s + 1) * FRAME)
        weighted = grads[at].astype(F32) * o_ref[at]
        deltas.append(jnp.sum(jnp.transpose(weighted), axis=0, keepdims=True))
    delta = jnp.concatenate(deltas, axis=1)
    lse = jnp.concatenate([lse_ref[g : g + 1] for g in range(GROUPS)], axis=1)
    scenes = jnp.concatenate([marks_ref[PEERS + s : PEERS + s + 1] for s in range(PEERS)], axis=1)
    query_grad = None
    for g in range(GROUPS):
        at = slice(g * PER * FRAME, (g + 1) * PER * FRAME)
        keys, values = k_ref[at], v_ref[at]
        tags = jnp.concatenate(
            [as_column(marks_ref[s : s + 1]) for s in range(g * PER, (g + 1) * PER)], axis=0
        )
        scores = product_right(keys, queries) * SCALE
        shares = jnp.where(tags == scenes, jnp.exp(scores - lse), 0.0)
        share_grad = product_right(values, outs)
        score_grad = (shares * (share_grad - delta)).astype(BF)
        value_grad = product(shares.astype(BF), outs)
        key_grad = product(score_grad, queries) * SCALE
        turned = jnp.transpose(keys.astype(F32)).astype(BF)[:HD]
        piece = product(turned, score_grad)
        query_grad = piece if query_grad is None else query_grad + piece
        for s in range(PER):
            part = slice(s * FRAME, (s + 1) * FRAME)
            pairs_out[g * PER + s, :FOLD] = fold_head(key_grad[part]).astype(BF)
            pairs_out[g * PER + s, FOLD:] = fold_head(value_grad[part]).astype(BF)
    sends = [
        exchange(me, k, pairs_out.at[me ^ k], pairs_in.at[me], pair_send, pair_recv)
        for k in range(PEERS - 1, 0, -1)
    ]
    for copy in sends:
        copy.start()
    own_pair = pltpu.make_async_copy(pairs_out.at[me], pairs_in.at[me], local.at[1])
    own_pair.start()
    padded = jnp.concatenate([query_grad * SCALE, jnp.zeros_like(query_grad)], axis=0)
    for s in range(PEERS):
        block = jnp.transpose(padded[:, s * FRAME : (s + 1) * FRAME])
        queries_out[s] = fold_head(block).astype(BF)
    more = [
        exchange(me, k, queries_out.at[me ^ k], queries_in.at[me], query_send, query_recv)
        for k in range(PEERS - 1, 0, -1)
    ]
    for copy in more:
        copy.start()
    own_query = pltpu.make_async_copy(queries_out.at[me], queries_in.at[me], local.at[2])
    own_query.start()
    own_pair.wait()
    own_query.wait()
    for copy in sends + more:
        copy.wait()
    for pair in range(width // LANES):
        for part in range(3):
            if part == 0:
                one, two = queries_in[2 * pair], queries_in[2 * pair + 1]
            else:
                rows = slice((part - 1) * FOLD, part * FOLD)
                one, two = pairs_in[2 * pair, rows], pairs_in[2 * pair + 1, rows]
            top, bottom = unfold_pair(one.astype(F32), two.astype(F32))
            cols = slice(part * width + pair * LANES, part * width + (pair + 1) * LANES)
            dqkv_ref[:FOLD, cols] = top.astype(BF)
            dqkv_ref[FOLD:, cols] = bottom.astype(BF)


def head_backward(grad, queries, keys, values, outs, lse, marks):
    width = grad.shape[1]
    every = PEERS * FRAME
    return pl.pallas_call(
        head_backward_kernel,
        in_specs=[whole()] * 7,
        out_specs=whole(),
        out_shape=jax.ShapeDtypeStruct((FRAME, 3 * width), BF),
        scratch_shapes=[
            pltpu.VMEM((PEERS, FOLD, LANES), BF),
            pltpu.VMEM((PEERS, FOLD, LANES), BF),
            pltpu.VMEM((every, LANES), BF),
            pltpu.VMEM((PEERS, 2 * FOLD, LANES), BF),
            pltpu.VMEM((PEERS, FOLD, LANES), BF),
            pltpu.VMEM((PEERS, 2 * FOLD, LANES), BF),
            pltpu.VMEM((PEERS, FOLD, LANES), BF),
            pltpu.SemaphoreType.DMA((3,)),
        ]
        + [pltpu.SemaphoreType.DMA((PEERS,))] * 6,
        compiler_params=pltpu.CompilerParams(
            vmem_limit_bytes=56 * VMEM_MIB, collective_id=2, has_side_effects=True
        ),
        cost_estimate=pl.CostEstimate(
            flops=10 * every * every * LANES, bytes_accessed=2**22, transcendentals=every * every
        ),
        name="head_backward",
    )(grad, queries, keys, values, outs, lse, marks)


def per_device(
    tokens,
    qkv_weight,
    out_weight,
    up_weight,
    down_weight,
    vectors,
    up_bias,
    head_norm,
    token_valid,
    frame_scene,
    cotangent,
):
    count = lax.axis_size("blk")
    outer = count // 4
    me = lax.axis_index("blk")
    x_at = lax.axis_index("grp")
    c_at = lax.rem(me, 2)
    y_at = lax.rem(me // 2, 2)
    c_pairs = [(i, i ^ 1) for i in range(count)]
    y_pairs = [(i, i ^ 2) for i in range(count)]
    z_groups = [[4 * o + k for o in range(outer)] for k in range(4)]
    places = jnp.stack([c_at, y_at, x_at]).astype(jnp.int32)
    x_place = x_at.reshape(1).astype(jnp.int32)

    def swap_x(value):
        return lax.ppermute(value, "grp", [(0, 1), (1, 0)])

    def swap_c(value):
        return lax.ppermute(value, "blk", c_pairs)

    def swap_y(value):
        return lax.ppermute(value, "blk", y_pairs)

    def part(value, index, parts, axis):
        size = value.shape[axis] // parts
        return lax.dynamic_slice_in_dim(value, index * size, size, axis)

    def tied(value, *others):
        return lax.optimization_barrier((value, *others))

    def ready_sum(keep, arrived):
        return (keep.astype(F32) + arrived.astype(F32)).astype(BF)

    def scattered(own):
        return lax.psum_scatter(
            own, "blk", scatter_dimension=0, tiled=True, axis_index_groups=z_groups
        )

    def finished(total):
        mine = part(total, c_at, 2, 0)
        near = swap_c(part(total, 1 - c_at, 2, 0))
        pair = jnp.stack([mine, near])
        return (pair, swap_x(pair))

    def total_of(value):
        value = value + swap_x(value)
        step = 1
        while step < count:
            pairs = [(i, i ^ step) for i in range(count)]
            value = value + lax.ppermute(value, "blk", pairs)
            step *= 2
        return value

    row_count, width = tokens.shape[1:]
    position = lax.broadcasted_iota(jnp.int32, (row_count,), 0)
    usable = (token_valid[0, 0] == 1) | (position < SPECIAL)
    usable_row = usable.astype(F32).reshape(1, row_count)
    scene = frame_scene[0, 0].astype(F32)
    tag_rows = jnp.where(usable, scene, -1.0)
    head_rows = jnp.tile(head_norm.reshape(2, 3, HD), (1, 1, WIDE // HD))
    head_rows = jnp.concatenate([head_rows, jnp.zeros((2, 5, WIDE), F32)], axis=1)

    hidden = up_weight.shape[2]
    left0, pre0, qkv0, mixed0, middle0, slope0, feed0, res1, pre1, qkv1 = front(
        tokens[0], usable_row, vectors, up_bias, head_rows, qkv_weight, out_weight, up_weight,
        down_weight,
    )
    left0_x = swap_x(left0)
    if count == HEADS:
        marks = jnp.concatenate(
            [
                tag_rows.reshape(1, row_count),
                jnp.full((1, row_count), scene),
                jnp.zeros((EXTRA - 2, row_count), F32),
            ],
            axis=0,
        ).astype(BF)
        att1, *kept = head_forward(qkv1, marks)
    else:
        att1, kept = gathered_forward(qkv1, tag_rows, scene)

    left0_c = swap_c(left0)
    res1, left0_x = tied(res1, left0_x)
    left1, output, right1, right1_send, att_grad1, middle_grad1, bias1, rows1 = turn(
        x_place, att1, res1, cotangent[0], vectors, up_bias, out_weight, up_weight, down_weight
    )
    left0_xc = swap_c(left0_x)
    att_grad1, left0_c, left0_xc = tied(att_grad1, left0_c, left0_xc)

    left1_x, left1_c, right1_x, right1_c = (
        swap_x(left1), swap_c(left1), swap_x(right1_send), swap_c(right1)
    )
    if count == HEADS:
        dqkv1 = head_backward(att_grad1, *kept)
    else:
        dqkv1 = gathered_backward(att_grad1, kept, tag_rows, scene)
    dqkv1, left1_x, left1_c, right1_x, right1_c = tied(
        dqkv1, left1_x, left1_c, right1_x, right1_c
    )
    left1_xc, right1_xc = swap_c(left1_x), swap_c(right1_x)
    left0_all = (left0, left0_x, left0_c, left0_xc)
    left1_all = (left1, left1_x, left1_c, left1_xc)
    right1_all = (right1, right1_x, right1_c, right1_xc)

    def feed_grads(name, lefts, rights):
        return weight_grads(
            name,
            outer,
            width,
            places,
            [
                (lefts, 0, width, rights, 0, hidden // 2, False),
                (lefts, width, hidden, rights, hidden // 2, width // 2, True),
            ],
        )

    def att_grads(name, normed, normed_at, att, att_at, projected, rights):
        return weight_grads(
            name,
            outer,
            width,
            places,
            [
                (normed, normed_at, width, projected, 0, 3 * width // 2, False),
                (att, att_at, width, rights, (hidden + width) // 2, width // 2, False),
            ],
        )

    feed1_keep, feed1_send = feed_grads("feed_grads1", left1_all, right1_all)
    dqkv1, feed1_send = tied(dqkv1, feed1_send)
    feed1_y = swap_y(feed1_send)
    (
        pg1, pg1_send, right0, right0_send, mixed_grad0, middle_grad0, bias0, rows10, heads1,
    ) = back_one(
        x_place, dqkv1, pre1, res1, middle_grad1, feed0, middle0, mixed0, slope0, vectors,
        head_rows, qkv_weight, up_weight, down_weight,
    )
    pg1_x, pg1_c, right0_x, right0_c = (
        swap_x(pg1_send), swap_c(pg1), swap_x(right0_send), swap_c(right0)
    )
    pg0, pg0_send, input_grad, rows0, heads0 = back_two(
        x_place, mixed_grad0, middle_grad0, qkv0, pre0, tokens[0], usable_row, vectors, head_rows,
        out_weight, qkv_weight,
    )
    pg0_send, pg1_x, pg1_c, right0_x, right0_c = tied(pg0_send, pg1_x, pg1_c, right0_x, right0_c)
    pg1_xc, right0_xc = swap_c(pg1_x), swap_c(right0_x)
    pg0_x, pg0_c = swap_x(pg0_send), swap_c(pg0)
    right0_all = (right0, right0_x, right0_c, right0_xc)
    att1_keep, att1_send = att_grads(
        "att_grads1", left0_all, hidden + 3 * width, left1_all, hidden + width,
        (pg1, pg1_x, pg1_c, pg1_xc), right1_all,
    )
    pg0_xc = swap_c(pg0_x)
    feed0_keep, feed0_send = feed_grads("feed_grads0", left0_all, right0_all)
    att0_keep, att0_send = att_grads(
        "att_grads0", left0_all, hidden + width, left0_all, hidden + 2 * width,
        (pg0, pg0_x, pg0_c, pg0_xc), right0_all,
    )
    att1_y = swap_y(att1_send)
    feed0_y = swap_y(feed0_send)
    att0_y = swap_y(att0_send)
    pieces = []
    for keep, arrived in (
        (feed0_keep, feed0_y), (att0_keep, att0_y), (feed1_keep, feed1_y), (att1_keep, att1_y)
    ):
        pieces += finished(scattered(ready_sum(keep, arrived)))
    weight_shapes = [
        (2, width // count, 3 * width),
        (2, width // count, width),
        (2, width // count, up_weight.shape[2]),
        (2, up_weight.shape[2] // count, width),
    ]
    qkv_grad, out_grad, up_grad, down_grad = assemble(
        places, pieces, weight_shapes
    )

    small = [
        jnp.stack(
            [
                jnp.concatenate([rows0[0:5], rows10[8:14]], axis=0),
                jnp.concatenate([rows10[0:5], rows1[0:6]], axis=0),
            ]
        ),
        jnp.concatenate([bias0, bias1], axis=0),
        jnp.stack(
            [
                jnp.sum(h[:3].reshape(3, WIDE // HD, HD), axis=1).reshape(3 * HD)
                for h in (heads0, heads1)
            ]
        ),
    ]
    packed = total_of(jnp.concatenate([s.reshape(-1) for s in small]))
    pieces, start = [], 0
    for s in small:
        pieces.append(packed[start : start + s.size].reshape(s.shape))
        start += s.size
    return (
        output[None],
        input_grad[None],
        qkv_grad,
        out_grad,
        up_grad,
        down_grad,
        part(pieces[0], me, count, 2),
        part(pieces[1], me, count, 1),
        pieces[2],
    )


def gathered_forward(qkv, tag_rows, scene):
    rows, width = qkv.shape[0], qkv.shape[1] // 3
    marks = jnp.zeros((KEEP, 2 * width), BF)
    marks = marks.at[0, :rows].set(tag_rows.astype(BF))
    marks = marks.at[1, :rows].set(jnp.full((rows,), scene).astype(BF))
    pairs = lax.all_gather(
        jnp.concatenate([qkv[:, width:], marks], axis=0), "blk", axis=0, tiled=False
    )
    tags = pairs[:, FRAME, :FRAME].astype(F32).reshape(1, -1)
    scenes = pairs[:, FRAME + 1, :FRAME].astype(F32).reshape(1, -1)
    queries = qkv[:, :width]
    attended, lse = global_attend(queries, pairs, tags, jnp.full((8, LANES), scene))
    every_query = lax.all_gather(
        with_rows(queries, lse.reshape(HEADS, rows)), "blk", axis=0, tiled=False
    )
    return attended.astype(BF), (qkv, pairs, tags, scenes, attended, lse, every_query)


def gathered_backward(attended_grad, kept, tag_rows, scene):
    qkv, pairs, tags, scenes, attended, lse, every_query = kept
    rows, width = attended_grad.shape
    delta = jnp.sum(
        (attended_grad.astype(F32) * attended).reshape(rows, HEADS, HD), axis=-1
    ).T
    every_grad = lax.all_gather(with_rows(attended_grad, delta), "blk", axis=0, tiled=False)
    query_grad = global_query_grad(
        qkv[:, :width],
        pairs,
        tags,
        jnp.full((8, LANES), scene),
        attended_grad,
        lse,
        delta.reshape(PAIRS, 2, rows),
    )
    key_grad, value_grad = global_key_grad(
        qkv[:, width : 2 * width],
        qkv[:, 2 * width :],
        tag_rows.reshape(1, rows),
        scenes,
        every_query,
        every_grad,
        rows_of(every_query, width),
        rows_of(every_grad, width),
    )
    return jnp.concatenate([query_grad, key_grad, value_grad], axis=1).astype(BF)


def solution(mesh):
    return jax.shard_map(
        per_device,
        mesh=mesh,
        in_specs=(
            P("grp", "blk", None),
            P(),
            P(),
            P(),
            P(),
            P(),
            P(),
            P(),
            P("grp", "blk", None),
            P("grp", "blk"),
            P("grp", "blk", None),
        ),
        out_specs=(
            P("grp", "blk", None),
            P("grp", "blk", None),
            P(None, "blk", None),
            P(None, "blk", None),
            P(None, "blk", None),
            P(None, "blk", None),
            P(None, None, "blk"),
            P(None, "blk"),
            P(),
        ),
        check_vma=False,
    )
```

```python
import functools
import types

import jax
import jax.numpy as jnp
from jax import lax
from jax.experimental import pallas as pl
from jax.experimental.pallas import tpu as pltpu
from jax.sharding import PartitionSpec as P

HEADS = 16
HD = 64
SPECIAL = 5
PAIRS = HEADS // 2
LANES = 2 * HD
FRAME = 128
KEEP = 16
EPS = 1e-06
NEG = -1e30
SCALE = HD**-0.5
BF = jnp.bfloat16
F32 = jnp.float32


def product(left_side, right_side):
    return jnp.dot(left_side, right_side, preferred_element_type=F32)


def product_left(left_side, right_side):
    return lax.dot_general(
        left_side, right_side, (((0,), (0,)), ((), ())), preferred_element_type=F32
    )


def product_right(left_side, right_side):
    return lax.dot_general(
        left_side, right_side, (((1,), (1,)), ((), ())), preferred_element_type=F32
    )


def lane_masks(dtype):
    lane = lax.broadcasted_iota(jnp.int32, (1, LANES), 1)
    first = (lane < HD).astype(dtype)
    return (first, 1 - first)


def as_column(row):
    size = row.shape[1]
    return jnp.transpose(jnp.broadcast_to(row, (LANES, size)))[:, :1]


def as_row(column):
    size = column.shape[0]
    return jnp.transpose(jnp.broadcast_to(column, (size, LANES)))[:1, :]


def flat(ref):
    block = ref[...]
    return block.reshape(block.shape[0] * block.shape[1], block.shape[2])


def attend_kernel(blocks, q_ref, k_ref, v_ref, tag_ref, scene_ref, o_ref, lse_ref, m_sc, l_sc, a_sc):
    step = pl.program_id(1)
    keys, values = flat(k_ref), flat(v_ref)
    allowed = tag_ref[...] == scene_ref[:1, :1]
    queries = q_ref[...]
    pieces = []
    for index, mask in enumerate(lane_masks(BF)):
        scores = product_right(queries * mask, keys) * SCALE
        scores = jnp.where(allowed, scores, NEG)
        top = jnp.max(scores, axis=-1, keepdims=True)

        if blocks > 1:

            @pl.when(step == 0)
            def _():
                m_sc[index] = jnp.full_like(m_sc[index], NEG)
                l_sc[index] = jnp.zeros_like(l_sc[index])
                a_sc[index] = jnp.zeros_like(a_sc[index])

            old = m_sc[index][:, :1]
            top = jnp.maximum(top, old)
            keep = jnp.exp(old - top)
        shares = jnp.where(allowed, jnp.exp(scores - top), 0.0)
        total = jnp.sum(shares, axis=-1, keepdims=True)
        weighted = product(shares.astype(BF), values)
        if blocks > 1:
            total = total + keep * l_sc[index][:, :1]
            weighted = weighted + keep * a_sc[index]
            m_sc[index] = jnp.broadcast_to(top, m_sc[index].shape)
            l_sc[index] = jnp.broadcast_to(total, l_sc[index].shape)
            a_sc[index] = weighted
        pieces.append(weighted / total)
        lse_ref[0, index : index + 1, :] = as_row(top + jnp.log(total))
    first, second = lane_masks(F32)
    o_ref[...] = jnp.where(first > 0, pieces[0], pieces[1])


def key_block(count):
    for size in (16, 8, 4, 2, 1):
        if count % size == 0:
            return size


def global_attend(queries, pairs, tags, scene):
    frames = pairs.shape[0]
    group = key_block(frames)
    blocks = frames // group
    return pl.pallas_call(
        functools.partial(attend_kernel, blocks),
        grid=(PAIRS, blocks),
        in_specs=[
            pl.BlockSpec((FRAME, LANES), lambda p, k: (0, p)),
            pl.BlockSpec((group, FRAME, LANES), lambda p, k: (k, 0, p)),
            pl.BlockSpec((group, FRAME, LANES), lambda p, k: (k, 0, PAIRS + p)),
            pl.BlockSpec((1, group * FRAME), lambda p, k: (0, k)),
            pl.BlockSpec((8, LANES), lambda p, k: (0, 0)),
        ],
        out_specs=[
            pl.BlockSpec((FRAME, LANES), lambda p, k: (0, p)),
            pl.BlockSpec((1, 2, FRAME), lambda p, k: (p, 0, 0)),
        ],
        out_shape=[
            jax.ShapeDtypeStruct((FRAME, PAIRS * LANES), F32),
            jax.ShapeDtypeStruct((PAIRS, 2, FRAME), F32),
        ],
        scratch_shapes=[pltpu.VMEM((2, FRAME, LANES), F32)] * 3,
        compiler_params=pltpu.CompilerParams(vmem_limit_bytes=48 * 2**20),
        cost_estimate=pl.CostEstimate(
            flops=4 * FRAME * frames * FRAME * LANES * HEADS,
            bytes_accessed=frames * FRAME * 4096,
            transcendentals=FRAME * frames * FRAME * HEADS,
        ),
        name="global_attend",
    )(queries, pairs, pairs, tags, scene)


def query_grad_kernel(
    q_ref, k_ref, v_ref, tag_ref, scene_ref, do_ref, lse_ref, delta_ref, dq_ref
):
    step = pl.program_id(1)
    keys, values = flat(k_ref), flat(v_ref)
    allowed = tag_ref[...] == scene_ref[:1, :1]
    queries, outs = q_ref[...], do_ref[...]
    pieces = []
    for index, mask in enumerate(lane_masks(BF)):
        scores = product_right(queries * mask, keys) * SCALE
        top = as_column(lse_ref[0, index : index + 1, :])
        delta = as_column(delta_ref[0, index : index + 1, :])
        shares = jnp.where(allowed, jnp.exp(scores - top), 0.0)
        share_grad = product_right(outs * mask, values)
        score_grad = (shares * (share_grad - delta)).astype(BF)
        pieces.append(product(score_grad, keys) * SCALE)
    first, second = lane_masks(F32)
    piece = jnp.where(first > 0, pieces[0], pieces[1])

    @pl.when(step == 0)
    def _():
        dq_ref[...] = piece

    @pl.when(step > 0)
    def _():
        dq_ref[...] += piece


def global_query_grad(queries, pairs, tags, scene, outs, lse, delta):
    frames = pairs.shape[0]
    group = key_block(frames)
    blocks = frames // group
    return pl.pallas_call(
        query_grad_kernel,
        grid=(PAIRS, blocks),
        in_specs=[
            pl.BlockSpec((FRAME, LANES), lambda p, k: (0, p)),
            pl.BlockSpec((group, FRAME, LANES), lambda p, k: (k, 0, p)),
            pl.BlockSpec((group, FRAME, LANES), lambda p, k: (k, 0, PAIRS + p)),
            pl.BlockSpec((1, group * FRAME), lambda p, k: (0, k)),
            pl.BlockSpec((8, LANES), lambda p, k: (0, 0)),
            pl.BlockSpec((FRAME, LANES), lambda p, k: (0, p)),
            pl.BlockSpec((1, 2, FRAME), lambda p, k: (p, 0, 0)),
            pl.BlockSpec((1, 2, FRAME), lambda p, k: (p, 0, 0)),
        ],
        out_specs=pl.BlockSpec((FRAME, LANES), lambda p, k: (0, p)),
        out_shape=jax.ShapeDtypeStruct((FRAME, PAIRS * LANES), F32),
        compiler_params=pltpu.CompilerParams(vmem_limit_bytes=48 * 2**20),
        cost_estimate=pl.CostEstimate(
            flops=6 * FRAME * frames * FRAME * LANES * HEADS,
            bytes_accessed=frames * FRAME * 4096,
            transcendentals=FRAME * frames * FRAME * HEADS,
        ),
        name="global_query_grad",
    )(queries, pairs, pairs, tags, scene, outs, lse, delta)


def key_grad_kernel(
    k_ref, v_ref, tag_ref, scene_ref, q_ref, do_ref, lse_ref, delta_ref, dk_ref, dv_ref
):
    step = pl.program_id(1)
    keys, values = k_ref[...], v_ref[...]
    queries, outs = flat(q_ref), flat(do_ref)
    allowed = as_column(tag_ref[...]) == scene_ref[...]
    key_pieces, value_pieces = [], []
    for index, mask in enumerate(lane_masks(BF)):
        scores = product_right(keys * mask, queries) * SCALE
        top = lse_ref[0, index : index + 1, :]
        delta = delta_ref[0, index : index + 1, :]
        shares = jnp.where(allowed, jnp.exp(scores - top), 0.0)
        share_grad = product_right(values * mask, outs)
        score_grad = (shares * (share_grad - delta)).astype(BF)
        key_pieces.append(product(score_grad, queries) * SCALE)
        value_pieces.append(product(shares.astype(BF), outs))
    first, second = lane_masks(F32)
    key_piece = jnp.where(first > 0, key_pieces[0], key_pieces[1])
    value_piece = jnp.where(first > 0, value_pieces[0], value_pieces[1])

    @pl.when(step == 0)
    def _():
        dk_ref[...] = key_piece
        dv_ref[...] = value_piece

    @pl.when(step > 0)
    def _():
        dk_ref[...] += key_piece
        dv_ref[...] += value_piece


def global_key_grad(keys, values, tags, scenes, queries, outs, lse, delta):
    frames = queries.shape[0]
    group = key_block(frames)
    blocks = frames // group
    return pl.pallas_call(
        key_grad_kernel,
        grid=(PAIRS, blocks),
        in_specs=[
            pl.BlockSpec((FRAME, LANES), lambda p, k: (0, p)),
            pl.BlockSpec((FRAME, LANES), lambda p, k: (0, p)),
            pl.BlockSpec((1, FRAME), lambda p, k: (0, 0)),
            pl.BlockSpec((1, group * FRAME), lambda p, k: (0, k)),
            pl.BlockSpec((group, FRAME, LANES), lambda p, k: (k, 0, p)),
            pl.BlockSpec((group, FRAME, LANES), lambda p, k: (k, 0, p)),
            pl.BlockSpec((1, 2, group * FRAME), lambda p, k: (p, 0, k)),
            pl.BlockSpec((1, 2, group * FRAME), lambda p, k: (p, 0, k)),
        ],
        out_specs=[pl.BlockSpec((FRAME, LANES), lambda p, k: (0, p))] * 2,
        out_shape=[jax.ShapeDtypeStruct((FRAME, PAIRS * LANES), F32)] * 2,
        compiler_params=pltpu.CompilerParams(vmem_limit_bytes=48 * 2**20),
        cost_estimate=pl.CostEstimate(
            flops=8 * FRAME * frames * FRAME * LANES * HEADS,
            bytes_accessed=frames * FRAME * 4096,
            transcendentals=FRAME * frames * FRAME * HEADS,
        ),
        name="global_key_grad",
    )(keys, values, tags, scenes, queries, outs, lse, delta)


def split_three(values):
    high = values.astype(BF)
    rest = values - high.astype(F32)
    middle = rest.astype(BF)
    return jnp.stack([high, middle, (rest - middle.astype(F32)).astype(BF)])


def with_rows(body, statistic):
    width = body.shape[1]
    extra = split_three(statistic).reshape(-1, width)
    pad = jnp.zeros((KEEP - extra.shape[0], width), BF)
    return jnp.concatenate([body, extra, pad], axis=0)


def rows_of(gathered, width):
    frames = gathered.shape[0]
    used = 3 * HEADS * FRAME // width
    terms = gathered[:, FRAME : FRAME + used].reshape(frames, 3, HEADS, FRAME).astype(F32)
    total = terms[:, 0] + terms[:, 1] + terms[:, 2]
    return total.transpose(1, 0, 2).reshape(PAIRS, 2, frames * FRAME)


VMEM_MIB = 2**20
WIDE = 256
ROOT_HALF = 0.7071067811865476
ROOT_TWO_PI = 0.3989422804014327


def whole(space=pltpu.VMEM):
    return pl.BlockSpec(memory_space=space)


def terms_of(values):
    high = values.astype(BF)
    rest = values - high.astype(F32)
    middle = rest.astype(BF)
    return (high, middle, (rest - middle.astype(F32)).astype(BF))


def head_averager():
    row = lax.broadcasted_iota(jnp.int32, (WIDE, WIDE), 0) // HD
    col = lax.broadcasted_iota(jnp.int32, (WIDE, WIDE), 1) // HD
    return jnp.where(row == col, 1.0 / HD, 0.0).astype(BF)


def head_mean(values, averager):
    high, middle, least = terms_of(values)
    return product(high, averager) + product(middle, averager) + product(least, averager)


def standard(values):
    centered = values - jnp.mean(values, axis=-1, keepdims=True)
    scale = lax.rsqrt(jnp.mean(centered * centered, axis=-1, keepdims=True) + EPS)
    return centered * scale, scale


def standard_heads(values, averager):
    centered = values - head_mean(values, averager)
    scale = lax.rsqrt(head_mean(centered * centered, averager) + EPS)
    return centered * scale, scale


def norm_pull(values, gain, grad):
    unit, scale = standard(values)
    scaled = grad * gain
    spread = jnp.mean(scaled * unit, axis=-1, keepdims=True)
    result = scale * (scaled - jnp.mean(scaled, axis=-1, keepdims=True) - unit * spread)
    return (
        result,
        jnp.sum(grad * unit, axis=0, keepdims=True),
        jnp.sum(grad, axis=0, keepdims=True),
    )


def weight_copies(sources, targets, sems):
    copies = [
        pltpu.make_async_copy(source, target, sems.at[index])
        for index, (source, target) in enumerate(zip(sources, targets))
    ]
    for copy in copies:
        copy.start()
    return copies


def column_pieces(ref, parts):
    size = ref.shape[-1] // parts
    return [ref.at[:, i * size : (i + 1) * size] for i in range(parts)]


def row_pieces(ref, parts):
    size = ref.shape[0] // parts
    return [ref.at[i * size : (i + 1) * size] for i in range(parts)]


def project(layer, residual, vec_ref, head_ref, w_ref, copies, normed_ref, pre_ref, qkv_ref):
    width = residual.shape[1]
    unit, _ = standard(residual)
    normed = (unit * vec_ref[layer, 0:1] + vec_ref[layer, 1:2]).astype(BF)
    normed_ref[...] = normed
    averager = head_averager()
    for part in range(3):
        copies[part].wait()
        bias = vec_ref[layer, 2 + part : 3 + part]
        for j in range(width // WIDE):
            at = slice(part * width + j * WIDE, part * width + (j + 1) * WIDE)
            value = product(normed, w_ref[:, at]) + bias[:, j * WIDE : (j + 1) * WIDE]
            if part < 2:
                pre_ref[:, at] = value
                unit, _ = standard_heads(value, averager)
                value = unit * head_ref[layer, 2 * part : 2 * part + 1]
                if part == 0:
                    value = value + head_ref[layer, 1:2]
            qkv_ref[:, at] = value.astype(BF)


def frame_attend(usable, qkv_ref, att_ref):
    width = att_ref.shape[1]
    first, _ = lane_masks(F32)
    for pair in range(width // LANES):
        q, k, v = [
            qkv_ref[:, part * width + pair * LANES : part * width + (pair + 1) * LANES]
            for part in range(3)
        ]
        pieces = []
        for mask in lane_masks(BF):
            shares = frame_shares(q * mask, k, usable)
            pieces.append(product(shares.astype(BF), v))
        at = slice(pair * LANES, (pair + 1) * LANES)
        att_ref[:, at] = jnp.where(first > 0, pieces[0], pieces[1]).astype(att_ref.dtype)


def frame_shares(queries, keys, usable):
    scores = jnp.where(usable > 0, product_right(queries, keys) * SCALE, NEG)
    shares = jnp.exp(scores - jnp.max(scores, axis=-1, keepdims=True))
    return shares / jnp.sum(shares, axis=-1, keepdims=True)


def feed_forward(
    layer, att, residual, vec_ref, bias_ref, w_out, w_up, w_down, copies, mixed_ref, middle_ref,
    lifted_ref, slope_ref, active_ref, feed_ref,
):
    chunks = w_up.shape[1] // 512
    copies[0].wait()
    mixed = product(att, w_out[...]) + vec_ref[layer, 5:6]
    mixed_ref[...] = mixed
    middle = residual + vec_ref[layer, 6:7] * mixed
    middle_ref[...] = middle
    unit, _ = standard(middle)
    lifted = (unit * vec_ref[layer, 7:8] + vec_ref[layer, 8:9]).astype(BF)
    lifted_ref[...] = lifted
    feed = None
    for j in range(chunks):
        at = slice(j * 512, (j + 1) * 512)
        if j % 2 == 0:
            copies[1 + j].wait()
            copies[2 + j].wait()
        hidden = product(lifted, w_up[:, at]) + bias_ref[layer : layer + 1, at]
        bell = 0.5 * (1.0 + lax.erf(hidden * ROOT_HALF))
        slope_ref[:, at] = bell + hidden * jnp.exp(-0.5 * hidden * hidden) * ROOT_TWO_PI
        active = (hidden * bell).astype(BF)
        active_ref[:, at] = active
        piece = product(active, w_down[at])
        feed = piece if feed is None else feed + piece
    feed = feed + vec_ref[layer, 9:10]
    feed_ref[...] = feed
    return middle + vec_ref[layer, 10:11] * feed


def split_columns(value_refs, x_at, keep_ref, send_ref):
    start = 0
    for value_ref in value_refs:
        half = value_ref.shape[1] // 2
        to = slice(start, start + half)
        keep_ref[:, to] = value_ref[:, pl.ds(pl.multiple_of(x_at * half, LANES), half)]
        send_ref[:, to] = value_ref[:, pl.ds(pl.multiple_of((1 - x_at) * half, LANES), half)]
        start += half


def feed_backward(
    layer, grad, feed, middle, mixed, slope_ref, vec_ref, w_up, w_down, copies, feed_grad_ref,
    hidden_grad_ref, mixed_grad_ref, bias_out, rows_ref, row0,
):
    chunks = w_up.shape[1] // 512
    feed_grad = (vec_ref[layer, 10:11] * grad).astype(BF)
    feed_grad_ref[...] = feed_grad
    rows_ref[row0 + 4 : row0 + 5] = jnp.sum(feed_grad.astype(F32), axis=0, keepdims=True)
    rows_ref[row0 + 5 : row0 + 6] = jnp.sum(grad * feed, axis=0, keepdims=True)
    lifted_grad = None
    for j in range(chunks):
        at = slice(j * 512, (j + 1) * 512)
        if copies is not None and j % 2 == 0:
            copies[j].wait()
            copies[j + 1].wait()
        hidden_grad = (slope_ref[:, at] * product_right(feed_grad, w_down[at])).astype(BF)
        hidden_grad_ref[:, at] = hidden_grad
        bias_out[:, at] = jnp.sum(hidden_grad.astype(F32), axis=0, keepdims=True)
        piece = product_right(hidden_grad, w_up[:, at])
        lifted_grad = piece if lifted_grad is None else lifted_grad + piece
    part, gain_grad, shift_grad = norm_pull(middle, vec_ref[layer, 7:8], lifted_grad)
    middle_grad = grad + part
    mixed_grad = (vec_ref[layer, 6:7] * middle_grad).astype(BF)
    mixed_grad_ref[...] = mixed_grad
    rows_ref[row0 : row0 + 1] = jnp.sum(mixed_grad.astype(F32), axis=0, keepdims=True)
    rows_ref[row0 + 1 : row0 + 2] = jnp.sum(middle_grad * mixed, axis=0, keepdims=True)
    rows_ref[row0 + 2 : row0 + 3] = gain_grad
    rows_ref[row0 + 3 : row0 + 4] = shift_grad
    return middle_grad


def project_backward(
    layer, residual, dqkv_ref, pre_ref, vec_ref, head_ref, w_ref, copies, pg_ref, rows_ref, head_out
):
    width = residual.shape[1]
    averager = head_averager()
    sums = [None, None, None]
    for part in range(3):
        for j in range(width // WIDE):
            at = slice(part * width + j * WIDE, part * width + (j + 1) * WIDE)
            value = dqkv_ref[:, at].astype(F32)
            if part < 2:
                unit, scale = standard_heads(pre_ref[:, at], averager)
                news = [(2 * part, jnp.sum(value * unit, axis=0, keepdims=True))]
                if part == 0:
                    news.append((1, jnp.sum(value, axis=0, keepdims=True)))
                for index, new in news:
                    sums[index] = new if sums[index] is None else sums[index] + new
                scaled = value * head_ref[layer, 2 * part : 2 * part + 1]
                value = scale * (
                    scaled
                    - head_mean(scaled, averager)
                    - unit * head_mean(scaled * unit, averager)
                )
            low = value.astype(BF)
            pg_ref[:, at] = low
            rows_ref[2 + part : 3 + part, j * WIDE : (j + 1) * WIDE] = jnp.sum(
                low.astype(F32), axis=0, keepdims=True
            )
    head_out[...] = jnp.concatenate(sums + [jnp.zeros((5, WIDE), F32)], axis=0)
    normed_grad = None
    for part in range(3):
        copies[part].wait()
        at = slice(part * width, (part + 1) * width)
        piece = product_right(pg_ref[:, at], w_ref[:, at])
        normed_grad = piece if normed_grad is None else normed_grad + piece
    part, gain_grad, shift_grad = norm_pull(residual, vec_ref[layer, 0:1], normed_grad)
    rows_ref[0:1] = gain_grad
    rows_ref[1:2] = shift_grad
    return part


def named_call(kernel, inputs, outputs, scratch, vmem_mib, cost, name, collective_id=None):
    names = [*inputs, *outputs, *scratch]

    def body(*refs):
        kernel(types.SimpleNamespace(**dict(zip(names, refs))))

    more = {}
    if collective_id is not None:
        more = {"collective_id": collective_id, "has_side_effects": True}
    results = pl.pallas_call(
        body,
        in_specs=[
            whole(pltpu.SMEM) if key.startswith("smem") else whole(pl.ANY) for key in inputs
        ],
        out_specs=[whole(pl.ANY if value[2] else pltpu.VMEM) for value in outputs.values()],
        out_shape=[jax.ShapeDtypeStruct(value[0], value[1]) for value in outputs.values()],
        scratch_shapes=list(scratch.values()),
        compiler_params=pltpu.CompilerParams(vmem_limit_bytes=vmem_mib * VMEM_MIB, **more),
        cost_estimate=cost,
        name=name,
    )(*inputs.values())
    return types.SimpleNamespace(**dict(zip(outputs, results)))


def low(*shape):
    return pltpu.VMEM(shape, BF)


def full(*shape):
    return pltpu.VMEM(shape, F32)


class Mover:
    def __init__(self, sems):
        self.sems, self.count, self.open = sems, 0, []

    def start(self, source, target):
        copy = pltpu.make_async_copy(source, target, self.sems.at[self.count])
        copy.start()
        self.count += 1
        return copy

    def flush(self, source, target):
        self.open.append(self.start(source, target))

    def finish(self):
        assert self.count == self.sems.shape[0]
        for copy in self.open:
            copy.wait()


def interleaved(one, two):
    return [piece for pair in zip(one, two) for piece in pair]


def front_kernel(
    tok_ref, usable_ref, vec_ref, bias_ref, head_ref, qkv_w, out_w, up_w, down_w,
    left_pack, att_pack, pre0, qkv0, mixed0, middle0, slope0, feed0, res1, normed1, pre1, qkv1,
    w_qkv, w_out, w_up, w_down, w_next, sems,
):
    width, units = tok_ref.shape[1], up_w.shape[2]
    lifted0 = left_pack.at[:, :width]
    active0 = left_pack.at[:, width : width + units]
    normed0, att0 = att_pack.at[:, :width], att_pack.at[:, width:]
    copies = weight_copies(
        column_pieces(qkv_w.at[0], 3)
        + [out_w.at[0]]
        + interleaved(column_pieces(up_w.at[0], 4), row_pieces(down_w.at[0], 4))
        + column_pieces(qkv_w.at[1], 3),
        column_pieces(w_qkv, 3)
        + [w_out]
        + interleaved(column_pieces(w_up, 4), row_pieces(w_down, 4))
        + column_pieces(w_next, 3),
        sems,
    )
    residual = tok_ref[...].astype(F32)
    project(0, residual, vec_ref, head_ref, w_qkv, copies[:3], normed0, pre0, qkv0)
    frame_attend(usable_ref[...], qkv0, att0)
    result = feed_forward(
        0, att0[...], residual, vec_ref, bias_ref, w_out, w_up, w_down, copies[3:12], mixed0,
        middle0, lifted0, slope0, active0, feed0,
    )
    res1[...] = result
    project(1, result, vec_ref, head_ref, w_next, copies[12:], normed1, pre1, qkv1)


def front(tokens, usable, vectors, up_bias, head_rows, qkv_weight, out_weight, up_weight, down_weight):
    rows, width = tokens.shape
    hidden = up_weight.shape[2]
    shapes = [
        ((rows, hidden + width), BF),
        ((rows, 2 * width), BF),
        ((rows, 2 * width), F32),
        ((rows, 3 * width), BF),
        ((rows, width), F32),
        ((rows, width), F32),
        ((rows, hidden), F32),
        ((rows, width), F32),
        ((rows, width), F32),
        ((rows, width), BF),
        ((rows, 2 * width), F32),
        ((rows, 3 * width), BF),
    ]
    return pl.pallas_call(
        front_kernel,
        in_specs=[whole()] * 5 + [whole(pl.ANY)] * 4,
        out_specs=[whole()] * len(shapes),
        out_shape=[jax.ShapeDtypeStruct(*shape) for shape in shapes],
        scratch_shapes=[
            pltpu.VMEM((width, 3 * width), BF),
            pltpu.VMEM((width, width), BF),
            pltpu.VMEM((width, hidden), BF),
            pltpu.VMEM((hidden, width), BF),
            pltpu.VMEM((width, 3 * width), BF),
            pltpu.SemaphoreType.DMA((15,)),
        ],
        compiler_params=pltpu.CompilerParams(vmem_limit_bytes=58 * VMEM_MIB),
        cost_estimate=pl.CostEstimate(
            flops=2 * rows * width * (7 * width + 2 * hidden),
            bytes_accessed=2 * width * (7 * width + 2 * hidden),
            transcendentals=2 * rows * hidden,
        ),
        name="front",
    )(tokens, usable, vectors, up_bias, head_rows, qkv_weight, out_weight, up_weight, down_weight)


def turn_kernel(
    x_ref, att_ref, normed_ref, res_ref, cot_ref, vec_ref, bias_ref, out_w, up_w, down_w,
    left_pack, att_pack, output, right_keep, right_send, att_grad, middle_grad, bias_out, rows_out,
    w_out, w_up, w_down, mixed_sc, middle_sc, slope_sc, feed_sc, fg_sc, hg_sc, mg_sc, sems,
):
    width, units = att_ref.shape[1], up_w.shape[2]
    lifted = left_pack.at[:, :width]
    active = left_pack.at[:, width : width + units]
    att_pack[:, :width] = normed_ref[...]
    att_pack[:, width:] = att_ref[...]
    copies = weight_copies(
        [out_w.at[1]] + interleaved(column_pieces(up_w.at[1], 4), row_pieces(down_w.at[1], 4)),
        [w_out] + interleaved(column_pieces(w_up, 4), row_pieces(w_down, 4)),
        sems,
    )
    result = feed_forward(
        1, att_ref[...], res_ref[...], vec_ref, bias_ref, w_out, w_up, w_down, copies, mixed_sc,
        middle_sc, lifted, slope_sc, active, feed_sc,
    )
    output[...] = result.astype(BF)
    grad = feed_backward(
        1, cot_ref[...].astype(F32), feed_sc[...], middle_sc[...], mixed_sc[...], slope_sc, vec_ref,
        w_up, w_down, None, fg_sc, hg_sc, mg_sc, bias_out, rows_out, 0,
    )
    middle_grad[...] = grad
    att_grad[...] = product_right(mg_sc[...], w_out[...]).astype(BF)
    split_columns([hg_sc, fg_sc, mg_sc], x_ref[0], right_keep, right_send)


def turn(x_at, att, normed, res, cotangent, vectors, up_bias, out_weight, up_weight, down_weight):
    rows, width = res.shape
    hidden = up_weight.shape[2]
    shapes = [
        ((rows, hidden + width), BF),
        ((rows, 2 * width), BF),
        ((rows, width), BF),
        ((rows, hidden // 2 + width), BF),
        ((rows, hidden // 2 + width), BF),
        ((rows, width), BF),
        ((rows, width), F32),
        ((1, hidden), F32),
        ((8, width), F32),
    ]
    return pl.pallas_call(
        turn_kernel,
        in_specs=[whole(pltpu.SMEM)] + [whole()] * 6 + [whole(pl.ANY)] * 3,
        out_specs=[whole()] * len(shapes),
        out_shape=[jax.ShapeDtypeStruct(*shape) for shape in shapes],
        scratch_shapes=[
            pltpu.VMEM((width, width), BF),
            pltpu.VMEM((width, hidden), BF),
            pltpu.VMEM((hidden, width), BF),
            pltpu.VMEM((rows, width), F32),
            pltpu.VMEM((rows, width), F32),
            pltpu.VMEM((rows, hidden), F32),
            pltpu.VMEM((rows, width), F32),
            pltpu.VMEM((rows, width), BF),
            pltpu.VMEM((rows, hidden), BF),
            pltpu.VMEM((rows, width), BF),
            pltpu.SemaphoreType.DMA((9,)),
        ],
        compiler_params=pltpu.CompilerParams(vmem_limit_bytes=58 * VMEM_MIB),
        cost_estimate=pl.CostEstimate(
            flops=4 * rows * width * (width + 2 * hidden),
            bytes_accessed=2 * width * (width + 2 * hidden),
            transcendentals=2 * rows * hidden,
        ),
        name="turn",
    )(x_at, att, normed, res, cotangent, vectors, up_bias, out_weight, up_weight, down_weight)


def back_one_kernel(r):
    mover = Mover(r.moves)
    loads = {}
    for key in ("vectors", "head_rows", "dqkv", "pre", "res", "grad"):
        loads[key] = mover.start(getattr(r, key), getattr(r, key + "_sc"))
    copies = weight_copies(column_pieces(r.qkv_w.at[1], 3), column_pieces(r.w_qkv, 3), r.sems)
    for key in ("feed", "middle", "mixed", "slope"):
        loads[key] = mover.start(getattr(r, key), getattr(r, key + "_sc"))
    copies = copies + weight_copies(
        interleaved(column_pieces(r.up_w.at[0], 4), row_pieces(r.down_w.at[0], 4)),
        interleaved(column_pieces(r.w_up, 4), row_pieces(r.w_down, 4)),
        r.more_sems,
    )
    for key in ("vectors", "head_rows", "dqkv", "pre", "res", "grad"):
        loads[key].wait()
    part = project_backward(
        1, r.res_sc[...], r.dqkv_sc, r.pre_sc, r.vectors_sc, r.head_rows_sc, r.w_qkv, copies[:3],
        r.pg_sc, r.rows_out, r.head_out,
    )
    split_columns([r.pg_sc], r.smem_at[0], r.pg_keep_sc, r.pg_send_sc)
    mover.flush(r.pg_send_sc, r.pg_send)
    mover.flush(r.pg_keep_sc, r.pg_keep)
    for key in ("feed", "middle", "mixed", "slope"):
        loads[key].wait()
    r.middle_grad_sc[...] = feed_backward(
        0, r.grad_sc[...] + part, r.feed_sc[...], r.middle_sc[...], r.mixed_sc[...], r.slope_sc,
        r.vectors_sc, r.w_up, r.w_down, copies[3:], r.fg_sc, r.hg_sc, r.mixed_grad_sc, r.bias_out,
        r.rows_out, 8,
    )
    mover.flush(r.middle_grad_sc, r.middle_grad)
    mover.flush(r.mixed_grad_sc, r.mixed_grad)
    split_columns([r.hg_sc, r.fg_sc], r.smem_at[1], r.right_keep_sc, r.right_send_sc)
    mover.flush(r.right_send_sc, r.right_send)
    mover.flush(r.right_keep_sc, r.right_keep)
    mover.finish()


def back_one(
    places, dqkv, pre, res, grad, feed, middle, mixed, slope, vectors, head_rows, qkv_weight,
    up_weight, down_weight,
):
    rows, width = res.shape
    hidden = up_weight.shape[2]
    loaded = {
        "vectors": vectors, "head_rows": head_rows, "dqkv": dqkv, "pre": pre, "res": res,
        "grad": grad, "feed": feed, "middle": middle, "mixed": mixed, "slope": slope,
    }
    stored = {
        "pg_keep": ((rows, 3 * width // 2), BF),
        "pg_send": ((rows, 3 * width // 2), BF),
        "right_keep": ((rows, (hidden + width) // 2), BF),
        "right_send": ((rows, (hidden + width) // 2), BF),
        "mixed_grad": ((rows, width), BF),
        "middle_grad": ((rows, width), F32),
    }
    return named_call(
        back_one_kernel,
        {"smem_at": places, **loaded, "qkv_w": qkv_weight, "up_w": up_weight, "down_w": down_weight},
        {
            **{key: (*value, True) for key, value in stored.items()},
            "bias_out": ((1, hidden), F32, False),
            "rows_out": ((16, width), F32, False),
            "head_out": ((8, WIDE), F32, False),
        },
        {
            **{key + "_sc": pltpu.VMEM(value.shape, value.dtype) for key, value in loaded.items()},
            **{key + "_sc": pltpu.VMEM(*value) for key, value in stored.items()},
            "w_qkv": low(width, 3 * width),
            "w_up": low(width, hidden),
            "w_down": low(hidden, width),
            "pg_sc": low(rows, 3 * width),
            "fg_sc": low(rows, width),
            "hg_sc": low(rows, hidden),
            "sems": pltpu.SemaphoreType.DMA((3,)),
            "more_sems": pltpu.SemaphoreType.DMA((8,)),
            "moves": pltpu.SemaphoreType.DMA((16,)),
        },
        56,
        pl.CostEstimate(
            flops=2 * rows * width * (3 * width + 2 * hidden),
            bytes_accessed=2 * width * (3 * width + 2 * hidden),
            transcendentals=0,
        ),
        "back_one",
    )


def frame_backward(att_grad, usable, qkv_ref, dqkv_ref):
    width = att_grad.shape[1]
    first, _ = lane_masks(F32)
    for pair in range(width // LANES):
        q, k, v = [
            qkv_ref[:, part * width + pair * LANES : part * width + (pair + 1) * LANES]
            for part in range(3)
        ]
        out = att_grad[:, pair * LANES : (pair + 1) * LANES]
        pieces = []
        for mask in lane_masks(BF):
            shares = frame_shares(q * mask, k, usable)
            share_grad = product_right(out * mask, v)
            delta = jnp.sum(shares * share_grad, axis=-1, keepdims=True)
            score_grad = (shares * (share_grad - delta)).astype(BF)
            pieces.append(
                (
                    product(score_grad, k) * SCALE,
                    product_left(score_grad, q) * SCALE,
                    product_left(shares.astype(BF), out),
                )
            )
        for part in range(3):
            dqkv_ref[:, part * width + pair * LANES : part * width + (pair + 1) * LANES] = jnp.where(
                first > 0, pieces[0][part], pieces[1][part]
            )


def back_two_kernel(r):
    width = r.tok.shape[1]
    mover = Mover(r.moves)
    loads = {}
    early = ("mixed_grad", "usable", "qkv")
    later = (
        "vectors", "head_rows", "pre", "tok", "grad", "rows10", "rows1", "bias0", "bias1", "heads1",
    )
    for key in early:
        loads[key] = mover.start(getattr(r, key), getattr(r, key + "_sc"))
    copies = weight_copies(
        [r.out_w.at[0]] + column_pieces(r.qkv_w.at[0], 3), [r.w_out] + column_pieces(r.w_qkv, 3),
        r.sems,
    )
    for key in later:
        loads[key] = mover.start(getattr(r, key), getattr(r, key + "_sc"))
    for key in early:
        loads[key].wait()
    copies[0].wait()
    att_grad = product_right(r.mixed_grad_sc[...], r.w_out[...]).astype(BF)
    frame_backward(att_grad, r.usable_sc[...], r.qkv_sc, r.dqkv_sc)
    for key in later:
        loads[key].wait()
    part = project_backward(
        0, r.tok_sc[...].astype(F32), r.dqkv_sc, r.pre_sc, r.vectors_sc, r.head_rows_sc, r.w_qkv,
        copies[1:], r.pg_sc, r.rows_sc, r.heads_sc,
    )
    split_columns([r.pg_sc, r.mixed_grad_sc], r.smem_at[0], r.pg_keep_sc, r.pg_send_sc)
    mover.flush(r.pg_send_sc, r.pg_send)
    mover.flush(r.pg_keep_sc, r.pg_keep)
    r.input_grad_sc[...] = (r.grad_sc[...] + part).astype(BF)
    mover.flush(r.input_grad_sc, r.input_grad)
    small = r.small_sc
    small[0:5] = r.rows_sc[0:5]
    small[5:11] = r.rows10_sc[8:14]
    small[11:16] = r.rows10_sc[0:5]
    small[16:22] = r.rows1_sc[0:6]
    at = 22
    for bias in (r.bias0_sc, r.bias1_sc):
        for j in range(bias.shape[1] // width):
            small[at : at + 1] = bias[:, j * width : (j + 1) * width]
            at += 1
    place = lax.broadcasted_iota(jnp.int32, (1, width), 1) // HD
    row = jnp.zeros((1, width), F32)
    for index, heads in enumerate((r.heads_sc, r.heads1_sc)):
        total = heads[...]
        total = total + pltpu.roll(total, WIDE // 2, 1)
        total = total + pltpu.roll(total, HD, 1)
        for j in range(3):
            many = jnp.concatenate([total[j : j + 1]] * (width // WIDE), axis=1)
            row = jnp.where(place == 3 * index + j, many, row)
    small[at : at + 1] = row
    small[at + 1 :] = jnp.zeros((small.shape[0] - at - 1, width), F32)
    mover.flush(r.small_sc, r.small)
    mover.finish()


def back_two(
    places, mixed_grad, grad, qkv, pre, tokens, usable, vectors, head_rows, rows10, rows1, bias0,
    bias1, heads1, out_weight, qkv_weight,
):
    rows, width = tokens.shape
    loaded = {
        "mixed_grad": mixed_grad, "usable": usable, "qkv": qkv, "vectors": vectors,
        "head_rows": head_rows, "pre": pre, "tok": tokens, "grad": grad, "rows10": rows10,
        "rows1": rows1, "bias0": bias0, "bias1": bias1, "heads1": heads1,
    }
    small_rows = 2 * vectors.shape[1] + 2 * bias0.shape[1] // width + 2
    stored = {
        "pg_keep": ((rows, 2 * width), BF),
        "pg_send": ((rows, 2 * width), BF),
        "input_grad": ((rows, width), BF),
        "small": ((small_rows, width), F32),
    }
    return named_call(
        back_two_kernel,
        {"smem_at": places, **loaded, "out_w": out_weight, "qkv_w": qkv_weight},
        {key: (*value, True) for key, value in stored.items()},
        {
            **{key + "_sc": pltpu.VMEM(value.shape, value.dtype) for key, value in loaded.items()},
            **{key + "_sc": pltpu.VMEM(*value) for key, value in stored.items()},
            "w_out": low(width, width),
            "w_qkv": low(width, 3 * width),
            "dqkv_sc": full(rows, 3 * width),
            "pg_sc": low(rows, 3 * width),
            "rows_sc": full(8, width),
            "heads_sc": full(8, WIDE),
            "sems": pltpu.SemaphoreType.DMA((4,)),
            "moves": pltpu.SemaphoreType.DMA((17,)),
        },
        48,
        pl.CostEstimate(
            flops=2 * rows * width * 4 * width,
            bytes_accessed=2 * width * 4 * width,
            transcendentals=HEADS * rows * rows,
        ),
        "back_two",
    )


def weight_grad_kernel(outer, tall, starts, at_ref, *refs):
    count = len(tall)
    lefts, rights = refs[: 4 * count], refs[4 * count : 8 * count]
    keep, send = refs[8 * count : 8 * count + 2]
    left_sc = refs[8 * count + 2 : 9 * count + 2]
    right_sc = refs[9 * count + 2 : 10 * count + 2]
    sems = refs[10 * count + 2]
    c_at, y_at = at_ref[0], at_ref[1]
    rows = lefts[0].shape[0]
    group = keep.shape[0] // outer
    copies = []
    for w in range(count):
        cols, left_cols = right_sc[w].shape[1], left_sc[w].shape[1]
        left_start, right_start = starts[w]
        for s in range(4):
            at = pl.ds(pl.multiple_of(right_start + c_at * cols, LANES), cols)
            copies.append(
                pltpu.make_async_copy(
                    rights[4 * w + s].at[:, at],
                    right_sc[w].at[s * rows : (s + 1) * rows],
                    sems.at[len(copies)],
                )
            )
            copies.append(
                pltpu.make_async_copy(
                    lefts[4 * w + s].at[:, left_start : left_start + left_cols],
                    left_sc[w].at[s * rows : (s + 1) * rows],
                    sems.at[len(copies)],
                )
            )
    for copy in copies:
        copy.start()
    start = 0
    for w in range(count):
        for copy in copies[8 * w : 8 * w + 8]:
            copy.wait()
        cols = right_sc[w].shape[1]
        right = right_sc[w][...]
        for block in range(left_sc[w].shape[1] // 512):
            result = product_left(left_sc[w][:, block * 512 : (block + 1) * 512], right).astype(BF)
            targets = {0: [], 1: []}
            if tall[w]:
                size, part = 4 * group, group // 2
                for piece in range(512 // part):
                    row = block * 512 + piece * part
                    o, y = row // (2 * size), (row // size) % 2
                    core, t = (row % size) // (size // 2), (row % (size // 2)) // part
                    targets[y].append(
                        (piece * part, part, o * group + core * part, start + t * cols)
                    )
            else:
                for piece in range(512 // group):
                    row = block * 512 + piece * group
                    o, y = row // (2 * group), (row // group) % 2
                    targets[y].append((piece * group, group, o * group, start))
            for y in range(2):
                if not targets[y]:
                    continue

                def store(ref, y=y):
                    for source, size, row, col in targets[y]:
                        ref[row : row + size, col : col + cols] = result[source : source + size]

                @pl.when(y_at == y)
                def _():
                    store(keep)

                @pl.when(y_at != y)
                def _():
                    store(send)

        start += cols * (4 if tall[w] else 1)


def weight_grads(name, outer, width, places, products):
    rows = products[0][0][0].shape[0]
    group = width // (2 * outer)
    lefts, left_starts, left_cols, rights, right_starts, halves, tall = zip(*products)
    columns = [half // 2 for half in halves]
    total = sum(c * (4 if t else 1) for c, t in zip(columns, tall))
    shape = jax.ShapeDtypeStruct((outer * group, total), BF)
    count = len(products)
    return pl.pallas_call(
        functools.partial(
            weight_grad_kernel, outer, tall, tuple(zip(left_starts, right_starts))
        ),
        in_specs=[whole(pltpu.SMEM)] + [whole(pl.ANY)] * (8 * count),
        out_specs=[whole()] * 2,
        out_shape=[shape] * 2,
        scratch_shapes=[pltpu.VMEM((4 * rows, c), BF) for c in left_cols]
        + [pltpu.VMEM((4 * rows, c), BF) for c in columns]
        + [pltpu.SemaphoreType.DMA((8 * count,))],
        compiler_params=pltpu.CompilerParams(vmem_limit_bytes=48 * VMEM_MIB),
        cost_estimate=pl.CostEstimate(
            flops=16 * rows * outer * group * total,
            bytes_accessed=8 * outer * group * total,
            transcendentals=0,
        ),
        name=name,
    )(places, *[a for l in lefts for a in l], *[a for r in rights for a in r])


def assemble_kernel(at_ref, *refs):
    sources, outs, pieces, sems = refs[:4], refs[4:8], refs[8:12], refs[12]
    copies = [
        pltpu.make_async_copy(source, piece, sems.at[index])
        for index, (source, piece) in enumerate(zip(sources, pieces))
    ]
    for copy in copies:
        copy.start()
    for copy in copies:
        copy.wait()
    qkv_out, out_out, up_out, down_out = outs
    c_at, x_at = at_ref[0], at_ref[2]
    half_at = (at_ref[5], x_at)
    part = qkv_out.shape[1]
    for layer in range(2):
        for source in range(4):
            feed, att = pieces[2 * layer].at[source], pieces[2 * layer + 1].at[source]
            c = c_at if source % 2 == 0 else 1 - c_at
            feed_place, att_place = [
                2 * (half if source < 2 else 1 - half) + c for half in (half_at[layer], x_at)
            ]

            def put(ref, values, place, row=0, layer=layer):
                cols = values.shape[1]
                at = pl.ds(pl.multiple_of(place * cols, LANES), cols)
                ref[layer, row : row + values.shape[0], at] = values.astype(F32)

            up_cols = up_out.shape[2] // 4
            down_cols = down_out.shape[2] // 4
            qkv_cols = qkv_out.shape[2] // 4
            put(up_out, feed[:, :up_cols], feed_place)
            for t in range(4):
                put(
                    down_out,
                    feed[:, up_cols + t * down_cols : up_cols + (t + 1) * down_cols],
                    feed_place,
                    t * part,
                )
            put(qkv_out, att[:, :qkv_cols], att_place)
            put(out_out, att[:, qkv_cols:], att_place)


def assemble(places, pieces, shapes):
    return pl.pallas_call(
        assemble_kernel,
        in_specs=[whole(pltpu.SMEM)] + [whole(pl.ANY)] * 4,
        out_specs=[whole()] * 4,
        out_shape=[jax.ShapeDtypeStruct(shape, F32) for shape in shapes],
        scratch_shapes=[pltpu.VMEM(piece.shape, BF) for piece in pieces]
        + [pltpu.SemaphoreType.DMA((4,))],
        compiler_params=pltpu.CompilerParams(vmem_limit_bytes=40 * VMEM_MIB),
        name="assemble",
    )(places, *pieces)


OUTER = 4
BLOCK = 128


def slot_order(z0, z1):
    return [2 * (1 - z1) + (1 - z0), 2 * z1 + (1 - z0), 2 * (1 - z1) + z0, 2 * z1 + z0]


def slot_group(slot, z0, z1):
    far = jnp.where(slot % 2 == 0, 1 - z1, z1)
    return 2 * far + jnp.where(slot < 2, 1 - z0, z0)


def slot_product(group, left, left_at, right, right_at, cols, tall, emit):
    rights = right[:, right_at : right_at + cols]
    if tall:
        for y in range(2):
            start = pl.multiple_of(left_at + group * 8 * BLOCK + y * 4 * BLOCK, BLOCK)
            result = product_left(left[:, pl.ds(start, 4 * BLOCK)], rights).astype(BF)
            half = BLOCK // 2
            for c in range(2):
                for t in range(4):
                    row = c * 2 * BLOCK + t * half
                    emit(y, c * half, t * cols, result[row : row + half])
    else:
        start = pl.multiple_of(left_at + group * 2 * BLOCK, BLOCK)
        result = product_left(left[:, pl.ds(start, 2 * BLOCK)], rights).astype(BF)
        for y in range(2):
            emit(y, 0, 0, result[y * BLOCK : (y + 1) * BLOCK])


class Sender:
    def __init__(self, send, recv, partners):
        self.send, self.recv, self.partners = send, recv, partners
        self.copies = []

    def start(self, source, target, partner):
        index = len(self.copies)
        copy = pltpu.make_async_remote_copy(
            src_ref=source,
            dst_ref=target,
            send_sem=self.send.at[index],
            recv_sem=self.recv.at[index],
            device_id=self.partners[partner],
            device_id_type=MESH,
        )
        copy.start()
        self.copies.append(copy)
        return copy

    def finish(self):
        for copy in self.copies:
            copy.wait_send()


def reduce_kernel(
    small_ref, f1_keep, f1_came, la1, la1_x, pg1, pg1_x, rt1, rt1_x, lf0, lf0_y, rt0,
    rt0_y, la0, la0_x, pm0, pm0_send,
    f0_out, a0_out, f1_out, a1_out, small_out,
    left_a1, right_a1, left_f0, right_f0, left_a0, right_a0, pm0_x,
    part_f1, part_a1, part_f0, part_a0, z0_f1, y_f1, y_a1, x_f0, y_a0,
    z0_a1, z0_f0, z0_a0, z1_f1, z1_a1, z1_f0, z1_a0,
    fin_f1, fin_a1, fin_f0, fin_a0, far_f1, far_a1, far_f0, far_a0, turned, last_f0, chosen,
    sums, sums_in, local, send, recv,
):
    me = lax.axis_index("blk")
    x_at = lax.axis_index("grp")
    c_at, y_at, z0, z1 = [lax.rem(me // (1 << bit), 2) for bit in range(4)]
    partners = {"x": {"grp": 1 - x_at}}
    for bit, name in enumerate(("c", "y", "z0", "z1")):
        partners[name] = {"blk": me ^ (1 << bit)}
    barrier = pltpu.get_barrier_semaphore()
    for partner in partners.values():
        pl.semaphore_signal(barrier, 1, device_id=partner, device_id_type=MESH)
    pl.semaphore_wait(barrier, len(partners))
    sender = Sender(send, recv, partners)
    rows = la1.shape[0]
    locals_ = []

    def load(source, target):
        copy = pltpu.make_async_copy(source, target, local.at[len(locals_)])
        copy.start()
        locals_.append(copy)
        return copy

    stores = []

    def store(source, target):
        stores.append(load(source, target))

    def ready(copies):
        for copy in copies:
            copy.wait_recv()

    def quarter(ref, start, cols, core):
        return ref.at[:, pl.ds(pl.multiple_of(start + core * cols, BLOCK), cols)]

    def own_right(ref, start, cols, target, to, index):
        here = slice(index * rows, (index + 1) * rows)
        there = slice((2 + index) * rows, (3 + index) * rows)
        return [
            load(quarter(ref, start, cols, c_at), target.at[here, to : to + cols]),
            sender.start(
                quarter(ref, start, cols, 1 - c_at), target.at[there, to : to + cols], "c"
            ),
        ]

    def own_left(ref, target, index):
        return [
            load(ref, target.at[index * rows : (index + 1) * rows]),
            sender.start(ref, target.at[(2 + index) * rows : (3 + index) * rows], "c"),
        ]

    qkv_cols, out_cols = right_a1.shape[1] * 3 // 4, right_a1.shape[1] // 4
    up_cols, down_cols = right_f0.shape[1] * 4 // 5, right_f0.shape[1] // 5
    width = left_a1.shape[1] // 2
    pm0_copy = sender.start(pm0_send, pm0_x, "x")
    f1_loads = [load(f1_keep, part_f1), load(f1_came, z0_f1)]
    a1_ready = (
        own_left(la1, left_a1, 0)
        + own_left(la1_x, left_a1, 1)
        + own_right(pg1, 0, qkv_cols, right_a1, 0, 0)
        + own_right(pg1_x, 0, qkv_cols, right_a1, 0, 1)
        + own_right(rt1, 0, out_cols, right_a1, qkv_cols, 0)
        + own_right(rt1_x, 0, out_cols, right_a1, qkv_cols, 1)
    )

    def ask_f0():
        return (
            own_left(lf0, left_f0, 0)
            + own_left(lf0_y, left_f0, 1)
            + own_right(rt0, 0, up_cols, right_f0, 0, 0)
            + own_right(rt0, 2 * up_cols, down_cols, right_f0, up_cols, 0)
            + own_right(rt0_y, 0, up_cols, right_f0, 0, 1)
            + own_right(rt0_y, 2 * up_cols, down_cols, right_f0, up_cols, 1)
        )

    def ask_a0():
        pm0_copy.wait_recv()
        return (
            own_left(la0, left_a0, 0)
            + own_left(la0_x, left_a0, 1)
            + own_right(pm0, 0, qkv_cols, right_a0, 0, 0)
            + own_right(pm0, 2 * qkv_cols, out_cols, right_a0, qkv_cols, 0)
            + own_right(pm0_x, 0, qkv_cols, right_a0, 0, 1)
            + own_right(pm0_x, 2 * qkv_cols, out_cols, right_a0, qkv_cols, 1)
        )

    small_load = load(small_ref, sums.at[0])

    class Finish:
        def finish(self):
            half = BLOCK // 2
            other = self.own(3).at[pl.ds(pl.multiple_of((1 - c_at) * half, half), half)]
            self.c_copy = sender.start(other, self.fin.at[1], "c")
            self.fin[0] = self.own(3)[pl.ds(pl.multiple_of(c_at * half, half), half)]
            self.far_copies = [sender.start(self.fin.at[0], self.far.at[0], "x")]

        def fourth(self):
            self.c_copy.wait_recv()
            self.far_copies.append(sender.start(self.fin.at[1], self.far.at[1], "x"))
            if not self.turns:
                store(self.fin, self.out.at[0:2])

        def fifth(self, core):
            self.far_copies[core].wait_recv()
            aligned = x_at == y_at
            chosen[core] = jnp.where(aligned, self.fin[core], self.far[core])
            store(chosen.at[core], self.out.at[core])
            turned[core] = jnp.where(aligned, self.far[core], self.fin[core])
            self.far_copies[core] = sender.start(turned.at[core], last_f0.at[core], "y")

        def last(self):
            for copy in self.far_copies:
                copy.wait_recv()
            store(last_f0 if self.turns else self.far, self.out.at[2:4])

    class Group(Finish):
        def __init__(self, part, over, over_z0, over_z1, fin, far, out, axis):
            self.part, self.over, self.over_z0, self.over_z1 = part, over, over_z0, over_z1
            self.fin, self.far, self.out, self.axis = fin, far, out, axis
            self.at = {"x": x_at, "y": y_at}[axis]
            self.turns = axis == "x"
            self.copies, self.z0_copies = [], []

        def own(self, slot):
            return self.part.at[slot, self.at]

        def total(self, slot):
            return self.own(slot)[...].astype(F32) + self.over[slot].astype(F32)

        def made(self, slot):
            self.copies.append(
                sender.start(self.part.at[slot, 1 - self.at], self.over.at[slot], self.axis)
            )

        def step(self, slot):
            self.copies[slot].wait_recv()
            (lambda: self.first(0), lambda: self.first(1), self.second, self.third)[slot]()

        def first(self, slot):
            self.own(slot)[...] = self.total(slot).astype(BF)
            self.z0_copies.append(sender.start(self.own(slot), self.over_z0.at[slot], "z0"))

        def second(self):
            value = self.total(2)
            self.z0_copies[0].wait_recv()
            self.own(2)[...] = (value + self.over_z0[0].astype(F32)).astype(BF)
            self.z1_copy = sender.start(self.own(2), self.over_z1, "z1")

        def third(self):
            value = self.total(3)
            self.z0_copies[1].wait_recv()
            value = value + self.over_z0[1].astype(F32)
            self.z1_copy.wait_recv()
            self.own(3)[...] = (value + self.over_z1[...].astype(F32)).astype(BF)
            self.finish()

    class Early(Finish):
        def __init__(self, part, came, over, over_z1, fin, far, out, keep=None):
            self.part, self.came, self.over, self.over_z1 = part, came, over, over_z1
            self.keep = part if keep is None else keep
            self.fin, self.far, self.out, self.turns = fin, far, out, False
            self.copies, self.z0_copies = [], []

        def own(self, slot):
            return self.keep.at[slot - 2, y_at]

        def total(self, slot, at):
            return self.keep[slot, at].astype(F32) + self.came[slot, at].astype(F32)

        def made(self, slot):
            if slot < 2:
                self.z0_copies.append(
                    sender.start(self.part.at[slot], self.came.at[slot], "z0")
                )

        def send(self, slot):
            if self.z0_copies:
                self.z0_copies[slot].wait_recv()
            self.keep[slot, 1 - y_at] = self.total(slot, 1 - y_at).astype(BF)
            self.copies.append(
                sender.start(self.keep.at[slot, 1 - y_at], self.over.at[slot], "y")
            )

        def step(self, slot):
            self.copies[slot].wait_recv()
            value = self.total(slot, y_at) + self.over[slot].astype(F32)
            if slot == 1:
                self.z1_copy.wait_recv()
                value = value + self.over_z1[...].astype(F32)
            self.keep[slot, y_at] = value.astype(BF)
            if slot == 0:
                self.z1_copy = sender.start(self.keep.at[0, y_at], self.over_z1, "z1")
            else:
                self.finish()

    f1 = Early(part_f1, z0_f1, y_f1, z1_f1, fin_f1, far_f1, f1_out)
    a1 = Early(
        part_a1, z0_a1, y_a1, z1_a1, fin_a1, far_a1, a1_out, part_a1.at[2:4]
    )
    f0 = Group(part_f0, x_f0, z0_f0, z1_f0, fin_f0, far_f0, f0_out, "x")
    a0 = Group(part_a0, y_a0, z0_a0, z1_a0, fin_a0, far_a0, a0_out, "y")

    def products(group, left, right, terms, slots=range(OUTER)):
        for slot in slots:
            at = slot_group(slot, z0, z1)
            base = 0
            for left_at, right_at, cols, tall in terms:

                def emit(y, row, col, values, slot=slot, base=base):
                    height, wide = values.shape
                    group.part[
                        slot, y, row : row + height, base + col : base + col + wide
                    ] = values

                slot_product(at, left, left_at, right, right_at, cols, tall, emit)
                base += cols * (4 if tall else 1)
            group.made(slot)

    att_terms = [(0, 0, qkv_cols, False), (width, qkv_cols, out_cols, False)]
    feed_terms = [(0, 0, up_cols, False), (width, up_cols, down_cols, True)]
    small_copies = []

    def small_step(name=None):
        index = len(small_copies)
        if index:
            small_copies[-1].wait_recv()
            sums[index] = sums[index - 1] + sums_in[index - 1]
        else:
            small_load.wait()
        if name is not None:
            small_copies.append(sender.start(sums.at[index], sums_in.at[index], name))
        else:
            store(sums.at[index], small_out)

    small_step("x")
    for copy in f1_loads:
        copy.wait()
    f1.send(0)
    f1.send(1)
    ready(a1_ready)
    f0_ready = ask_f0()
    products(a1, left_a1, right_a1, att_terms)
    f1.step(0)
    small_step("c")
    ready(f0_ready)
    a0_ready = ask_a0()
    a1.send(0)
    products(f0, left_f0, right_f0, feed_terms)
    small_step("y")
    ready(a0_ready)
    products(a0, left_a0, right_a0, att_terms)
    a1.send(1)
    f0.step(0)
    a1.step(0)
    f1.step(1)
    small_step("z0")
    f1.fourth()
    a0.step(0)
    a1.step(1)
    f0.step(1)
    small_step("z1")
    f0.step(2)
    a0.step(1)
    a1.fourth()
    a1.last()
    f1.last()
    a0.step(2)
    small_step()
    f0.step(3)
    f0.fourth()
    f0.fifth(0)
    a0.step(3)
    a0.fourth()
    f0.fifth(1)
    a0.last()
    f0.last()
    assert len(sender.copies) == send.shape[0]
    assert len(locals_) == local.shape[0]
    ready(stores)
    sender.finish()


def reduce_all(small, f1, a1, f0, a0):
    rows = f0[0].shape[0]
    feed, att = f1[0].shape[-1], f1[0].shape[-1] // 2
    left_feed, left_att = f0[0].shape[1], a0[0].shape[1]
    half = BLOCK // 2

    def low(*shape):
        return pltpu.VMEM(shape, BF)

    wides = (feed, att, feed, att)
    outs = [jax.ShapeDtypeStruct((4, half, wide), BF) for wide in wides]
    return pl.pallas_call(
        reduce_kernel,
        in_specs=[whole(pl.ANY)] * 17,
        out_specs=[whole(pl.ANY)] * 5,
        out_shape=outs + [jax.ShapeDtypeStruct(small.shape, F32)],
        scratch_shapes=[
            low(4 * rows, left_att),
            low(4 * rows, att),
            low(4 * rows, left_feed),
            low(4 * rows, feed * 5 // 8),
            low(4 * rows, left_att),
            low(4 * rows, att),
            low(*a0[3].shape),
            low(2, 2, BLOCK, feed),
            low(OUTER, 2, BLOCK, att),
            low(OUTER, 2, BLOCK, feed),
            low(OUTER, 2, BLOCK, att),
            low(2, 2, BLOCK, feed),
            low(2, BLOCK, feed),
            low(2, BLOCK, att),
            low(OUTER, BLOCK, feed),
            low(OUTER, BLOCK, att),
            low(2, 2, BLOCK, att),
            low(2, BLOCK, feed),
            low(2, BLOCK, att),
        ]
        + [low(BLOCK, wide) for wide in wides]
        + [low(2, half, wide) for wide in wides] * 2
        + [low(2, half, feed)] * 3
        + [
            pltpu.VMEM((6, *small.shape), F32),
            pltpu.VMEM((5, *small.shape), F32),
            pltpu.SemaphoreType.DMA((31,)),
            pltpu.SemaphoreType.DMA((60,)),
            pltpu.SemaphoreType.DMA((60,)),
        ],
        compiler_params=pltpu.CompilerParams(
            vmem_limit_bytes=60 * VMEM_MIB, collective_id=3, has_side_effects=True
        ),
        cost_estimate=pl.CostEstimate(
            flops=8 * rows * (left_feed + 2 * left_att) * feed,
            bytes_accessed=2**25,
            transcendentals=0,
        ),
        name="reduce_all",
    )(small, *f1, *a1, *f0, *a0)


PEERS = HEADS
FOLD = FRAME // 2
EXTRA = 16
GROUPS = 4
BACK_GROUPS = 8
MESH = pl.DeviceIdType.MESH


def fold_pair(values):
    lane = lax.broadcasted_iota(jnp.int32, (FOLD, LANES), 1)
    top, bottom = values[:FOLD], values[FOLD:]
    one = jnp.where(lane < HD, top, pltpu.roll(bottom, HD, 1))
    two = jnp.where(lane < HD, pltpu.roll(top, HD, 1), bottom)
    return one, two


def unfold_pair(one, two):
    lane = lax.broadcasted_iota(jnp.int32, (FOLD, LANES), 1)
    top = jnp.where(lane < HD, one, pltpu.roll(two, HD, 1))
    bottom = jnp.where(lane < HD, pltpu.roll(one, HD, 1), two)
    return top, bottom


def unfold_head(folded):
    lane = lax.broadcasted_iota(jnp.int32, (FOLD, LANES), 1)
    folded = folded.astype(F32)
    top = jnp.where(lane < HD, folded, 0.0)
    bottom = jnp.where(lane < HD, pltpu.roll(folded, HD, 1), 0.0)
    return top.astype(BF), bottom.astype(BF)


def fold_head(values):
    lane = lax.broadcasted_iota(jnp.int32, (FOLD, LANES), 1)
    return jnp.where(lane < HD, values[:FOLD], pltpu.roll(values[FOLD:], HD, 1))


def exchange(me, k, source, target, sems):
    return pltpu.make_async_remote_copy(
        src_ref=source,
        dst_ref=target,
        send_sem=sems.at[0, k],
        recv_sem=sems.at[1, k],
        device_id={"blk": me ^ k},
        device_id_type=MESH,
    )


def call_peers(me, partner):
    barrier = pltpu.get_barrier_semaphore()
    for k in range(1, PEERS):
        pl.semaphore_signal(barrier, 1, device_id={"blk": me ^ k}, device_id_type=MESH)
    pl.semaphore_signal(barrier, 1, device_id=partner, device_id_type=MESH)
    return lambda: pl.semaphore_wait(barrier, PEERS)


def all_to_all(me, source, target, sems, own_sem):
    copies = [exchange(me, k, source.at[me ^ k], target.at[me], sems) for k in range(PEERS - 1, 0, -1)]
    for copy in copies:
        copy.start()
    own = pltpu.make_async_copy(source.at[me], target.at[me], own_sem)
    own.start()
    return copies + [own]


def head_forward(me, qkv_ref, tag_ref, att_ref, r):
    width = att_ref.shape[1]
    for head in range(HEADS):
        r.pack[head, 3 * FOLD :] = tag_ref[...]
    for pair in range(width // LANES):
        for part in range(3):
            block = qkv_ref[:, part * width + pair * LANES : part * width + (pair + 1) * LANES]
            one, two = fold_pair(block.astype(F32))
            r.pack[2 * pair, part * FOLD : (part + 1) * FOLD] = one.astype(BF)
            r.pack[2 * pair + 1, part * FOLD : (part + 1) * FOLD] = two.astype(BF)
    for copy in all_to_all(me, r.pack, r.got, r.out_sems, r.own_sems.at[0]):
        copy.wait()
    for s in range(PEERS):
        for part, target in enumerate((r.queries_sc, r.keys_sc, r.values_sc)):
            top, bottom = unfold_head(r.got[s, part * FOLD : (part + 1) * FOLD])
            target[s * FRAME : s * FRAME + FOLD] = top
            target[s * FRAME + FOLD : (s + 1) * FRAME] = bottom
        r.marks_sc[s : s + 1] = r.got[s, 3 * FOLD : 3 * FOLD + 1].astype(F32)
        r.marks_sc[PEERS + s : PEERS + s + 1] = r.got[s, 3 * FOLD + 1 : 3 * FOLD + 2].astype(F32)
    keys, values = r.keys_sc[...], r.values_sc[...]
    tags = jnp.concatenate([r.marks_sc[s : s + 1] for s in range(PEERS)], axis=1)
    sends = []
    own = None
    per = PEERS // GROUPS
    for j in range(GROUPS - 1, -1, -1):
        block = (me // per) ^ j
        at = pl.ds(pl.multiple_of(block * per * FRAME, per * FRAME), per * FRAME)
        scores = product_right(r.queries_sc[at], keys) * SCALE
        scenes = jnp.concatenate(
            [
                jnp.broadcast_to(
                    r.marks_sc[pl.ds(PEERS + block * per + i, 1)][:, :1], (FRAME, 1)
                )
                for i in range(per)
            ],
            axis=0,
        )
        scores = jnp.where(tags == scenes, scores, NEG)
        top = jnp.max(scores, axis=-1, keepdims=True)
        shares = jnp.exp(scores - top)
        total = jnp.sum(shares, axis=-1, keepdims=True)
        result = product(shares.astype(BF), values) / total
        r.outs_sc[at] = result
        r.lse_sc[:, at] = as_row(top + jnp.log(total))
        for i in range(per):
            r.answers[block * per + i] = fold_head(result[i * FRAME : (i + 1) * FRAME]).astype(BF)
        for k in range(j * per, (j + 1) * per):
            if k:
                copy = exchange(me, k, r.answers.at[me ^ k], r.back.at[me], r.back_sems)
            else:
                copy = pltpu.make_async_copy(r.answers.at[me], r.back.at[me], r.own_sems.at[1])
            copy.start()
            sends.append(copy)
    for copy in sends:
        copy.wait()
    for pair in range(width // LANES):
        top, bottom = unfold_pair(r.back[2 * pair].astype(F32), r.back[2 * pair + 1].astype(F32))
        att_ref[:FOLD, pair * LANES : (pair + 1) * LANES] = top.astype(BF)
        att_ref[FOLD:, pair * LANES : (pair + 1) * LANES] = bottom.astype(BF)


def head_backward(me, grad_ref, dqkv_ref, r, meanwhile):
    width = grad_ref.shape[1]
    for pair in range(width // LANES):
        one, two = fold_pair(grad_ref[:, pair * LANES : (pair + 1) * LANES].astype(F32))
        r.pack[2 * pair] = one.astype(BF)
        r.pack[2 * pair + 1] = two.astype(BF)
    for copy in all_to_all(me, r.pack, r.got, r.out_sems, r.own_sems.at[0]):
        copy.wait()
    deltas = []
    for s in range(PEERS):
        at = slice(s * FRAME, (s + 1) * FRAME)
        top, bottom = unfold_head(r.got[s])
        r.grads_sc[s * FRAME : s * FRAME + FOLD] = top
        r.grads_sc[s * FRAME + FOLD : (s + 1) * FRAME] = bottom
        weighted = r.grads_sc[at].astype(F32) * r.outs_sc[at]
        deltas.append(jnp.sum(jnp.transpose(weighted), axis=0, keepdims=True))
    delta = jnp.concatenate(deltas, axis=1)
    queries, outs, lse = r.queries_sc[...], r.grads_sc[...], r.lse_sc[...]
    scenes = jnp.concatenate(
        [r.marks_sc[PEERS + s : PEERS + s + 1] for s in range(PEERS)], axis=1
    )
    query_grad = None
    sends = []
    per = PEERS // BACK_GROUPS
    for j in range(BACK_GROUPS - 1, -1, -1):
        block = (me // per) ^ j
        at = pl.ds(pl.multiple_of(block * per * FRAME, per * FRAME), per * FRAME)
        keys, values = r.keys_sc[at], r.values_sc[at]
        tags = jnp.concatenate(
            [as_column(r.marks_sc[pl.ds(block * per + i, 1)]) for i in range(per)], axis=0
        )
        scores = product_right(keys, queries) * SCALE
        shares = jnp.where(tags == scenes, jnp.exp(scores - lse), 0.0)
        share_grad = product_right(values, outs)
        score_grad = (shares * (share_grad - delta)).astype(BF)
        value_grad = product(shares.astype(BF), outs)
        key_grad = product(score_grad, queries) * SCALE
        turned = jnp.transpose(keys.astype(F32)).astype(BF)[:HD]
        piece = product(turned, score_grad)
        query_grad = piece if query_grad is None else query_grad + piece
        for i in range(per):
            part = slice(i * FRAME, (i + 1) * FRAME)
            r.pairs[block * per + i, :FOLD] = fold_head(key_grad[part]).astype(BF)
            r.pairs[block * per + i, FOLD:] = fold_head(value_grad[part]).astype(BF)
        for k in range(j * per, (j + 1) * per):
            if k:
                copy = exchange(me, k, r.pairs.at[me ^ k], r.pairs_in.at[me], r.pair_sems)
            else:
                copy = pltpu.make_async_copy(r.pairs.at[me], r.pairs_in.at[me], r.own_sems.at[1])
            copy.start()
            sends.append(copy)
    padded = jnp.concatenate([query_grad * SCALE, jnp.zeros_like(query_grad)], axis=0)
    for s in range(PEERS):
        block = jnp.transpose(padded[:, s * FRAME : (s + 1) * FRAME])
        r.asked[s] = fold_head(block).astype(BF)
    sends += all_to_all(me, r.asked, r.asked_in, r.back_sems, r.own_sems.at[2])
    meanwhile()
    for copy in sends:
        copy.wait()
    for pair in range(width // LANES):
        for part in range(3):
            if part == 0:
                one, two = r.asked_in[2 * pair], r.asked_in[2 * pair + 1]
            else:
                rows = slice((part - 1) * FOLD, part * FOLD)
                one, two = r.pairs_in[2 * pair, rows], r.pairs_in[2 * pair + 1, rows]
            top, bottom = unfold_pair(one.astype(F32), two.astype(F32))
            cols = slice(part * width + pair * LANES, part * width + (pair + 1) * LANES)
            dqkv_ref[:FOLD, cols] = top.astype(BF)
            dqkv_ref[FOLD:, cols] = bottom.astype(BF)


def begin_kernel(r):
    me, x_at = lax.axis_index("blk"), lax.axis_index("grp")
    partner = {"grp": 1 - x_at}
    peers_here = call_peers(me, partner)
    width, units = r.tok.shape[1], r.up_w.shape[2]
    mover = Mover(r.moves)
    loads = [
        mover.start(getattr(r, key), getattr(r, key + "_sc"))
        for key in ("tok", "vectors", "head_rows", "up_bias", "usable")
    ]
    loads.append(mover.start(r.marks, r.marks_in_sc))
    copies = weight_copies(
        column_pieces(r.qkv_w.at[0], 3)
        + [r.out_w.at[0]]
        + interleaved(column_pieces(r.up_w.at[0], 4), row_pieces(r.down_w.at[0], 4)),
        column_pieces(r.w_qkv, 3)
        + [r.w_out]
        + interleaved(column_pieces(r.w_up, 4), row_pieces(r.w_down, 4)),
        r.sems,
    )
    for copy in loads:
        copy.wait()
    residual = r.tok_sc[...].astype(F32)
    normed0, att0 = r.leftatt0_sc.at[:, :width], r.leftatt0_sc.at[:, width:]
    project(
        0, residual, r.vectors_sc, r.head_rows_sc, r.w_qkv, copies[:3], normed0, r.pre0_sc,
        r.qkv0_sc,
    )
    mover.flush(r.pre0_sc, r.pre0)
    mover.flush(r.qkv0_sc, r.qkv0)
    frame_attend(r.usable_sc[...], r.qkv0_sc, att0)
    next_copies = weight_copies(
        column_pieces(r.qkv_w.at[1], 3), column_pieces(r.w_qkv, 3), r.next_sems
    )
    mover.flush(r.leftatt0_sc, r.leftatt0)
    peers_here()
    across = pltpu.make_async_remote_copy(
        src_ref=r.leftatt0_sc,
        dst_ref=r.leftatt0_x,
        send_sem=r.x_sems.at[0],
        recv_sem=r.x_sems.at[1],
        device_id=partner,
        device_id_type=MESH,
    )
    across.start()
    lifted0, active0 = r.left0_sc.at[:, :width], r.left0_sc.at[:, width:]
    result = feed_forward(
        0, att0[...], residual, r.vectors_sc, r.up_bias_sc, r.w_out, r.w_up, r.w_down, copies[3:],
        r.mixed0_sc, r.middle0_sc, lifted0, r.slope0_sc, active0, r.feed0_sc,
    )
    r.res1_sc[...] = result
    for key in ("left0", "mixed0", "middle0", "slope0", "feed0", "res1"):
        mover.flush(getattr(r, key + "_sc"), getattr(r, key))
    normed1, att1 = r.leftatt1_sc.at[:, :width], r.leftatt1_sc.at[:, width:]
    project(
        1, result, r.vectors_sc, r.head_rows_sc, r.w_qkv, next_copies, normed1, r.pre1_sc, r.qkv1_sc
    )
    mover.flush(r.pre1_sc, r.pre1)
    head_forward(me, r.qkv1_sc, r.marks_in_sc, att1, r)
    for key in ("queries", "keys", "values", "outs", "lse", "marks_all", "leftatt1"):
        source = r.marks_sc if key == "marks_all" else getattr(r, key + "_sc")
        mover.flush(source, getattr(r, key))
    across.wait()
    mover.finish()


def begin(
    tokens, usable, marks, vectors, up_bias, head_rows, qkv_weight, out_weight, up_weight,
    down_weight,
):
    rows, width = tokens.shape
    hidden = up_weight.shape[2]
    every = PEERS * FRAME
    loaded = {
        "tok": tokens, "vectors": vectors, "head_rows": head_rows, "up_bias": up_bias,
        "usable": usable, "marks": marks,
    }
    stored = {
        "left0": ((rows, hidden + width), BF),
        "leftatt0": ((rows, 2 * width), BF),
        "pre0": ((rows, 2 * width), F32),
        "qkv0": ((rows, 3 * width), BF),
        "mixed0": ((rows, width), F32),
        "middle0": ((rows, width), F32),
        "slope0": ((rows, hidden), F32),
        "feed0": ((rows, width), F32),
        "res1": ((rows, width), F32),
        "leftatt1": ((rows, 2 * width), BF),
        "pre1": ((rows, 2 * width), F32),
        "queries": ((every, LANES), BF),
        "keys": ((every, LANES), BF),
        "values": ((every, LANES), BF),
        "outs": ((every, LANES), F32),
        "lse": ((1, every), F32),
        "marks_all": ((2 * PEERS, LANES), F32),
    }
    scratch = {key + "_sc": pltpu.VMEM(value.shape, value.dtype) for key, value in loaded.items()}
    scratch["marks_in_sc"] = scratch.pop("marks_sc")
    stored_scratch = {key + "_sc": pltpu.VMEM(*value) for key, value in stored.items()}
    stored_scratch["marks_sc"] = stored_scratch.pop("marks_all_sc")
    return named_call(
        begin_kernel,
        {
            **loaded, "qkv_w": qkv_weight, "out_w": out_weight, "up_w": up_weight,
            "down_w": down_weight,
        },
        {
            **{key: (*value, True) for key, value in stored.items()},
            "leftatt0_x": ((rows, 2 * width), BF, True),
        },
        {
            **scratch,
            **stored_scratch,
            "qkv1_sc": low(rows, 3 * width),
            "w_qkv": low(width, 3 * width),
            "w_out": low(width, width),
            "w_up": low(width, hidden),
            "w_down": low(hidden, width),
            "pack": low(PEERS, 3 * FOLD + EXTRA, LANES),
            "got": low(PEERS, 3 * FOLD + EXTRA, LANES),
            "answers": low(PEERS, FOLD, LANES),
            "back": low(PEERS, FOLD, LANES),
            "sems": pltpu.SemaphoreType.DMA((12,)),
            "next_sems": pltpu.SemaphoreType.DMA((3,)),
            "moves": pltpu.SemaphoreType.DMA((6 + len(stored),)),
            "own_sems": pltpu.SemaphoreType.DMA((2,)),
            "out_sems": pltpu.SemaphoreType.DMA((2, PEERS)),
            "back_sems": pltpu.SemaphoreType.DMA((2, PEERS)),
            "x_sems": pltpu.SemaphoreType.DMA((2,)),
        },
        60,
        pl.CostEstimate(
            flops=2 * rows * width * (7 * width + 2 * hidden) + 4 * every * every * LANES,
            bytes_accessed=2 * width * (7 * width + 2 * hidden),
            transcendentals=2 * rows * hidden + every * every,
        ),
        "begin",
        collective_id=1,
    )


def middle_kernel(r):
    me, x_at = lax.axis_index("blk"), lax.axis_index("grp")
    c_at, _, z0, z1 = [lax.rem(me // (1 << bit), 2) for bit in range(4)]
    partners = {"x": {"grp": 1 - x_at}, "c": {"blk": me ^ 1}}
    peers_here = call_peers(me, partners["x"])
    sender = Sender(r.ring_sems.at[0], r.ring_sems.at[1], partners)
    rows, width = r.res.shape
    units = r.up_w.shape[2]
    mover = Mover(r.moves)
    early = ("vectors", "leftatt1", "res", "up_bias", "cot")
    later = ("queries", "keys", "values", "outs", "lse")
    loads = [mover.start(getattr(r, key), getattr(r, key + "_sc")) for key in early]
    copies = weight_copies(
        [r.out_w.at[1]]
        + interleaved(column_pieces(r.up_w.at[1], 4), row_pieces(r.down_w.at[1], 4)),
        [r.w_out] + interleaved(column_pieces(r.w_up, 4), row_pieces(r.w_down, 4)),
        r.sems,
    )
    late_loads = [mover.start(getattr(r, key), getattr(r, key + "_sc")) for key in later]
    late_loads.append(mover.start(r.marks_all, r.marks_sc))
    for copy in loads:
        copy.wait()
    own = slice(0, rows)
    lifted, active = r.left_sc.at[own, :width], r.left_sc.at[own, width:]
    result = feed_forward(
        1, r.leftatt1_sc[:, width:], r.res_sc[...], r.vectors_sc, r.up_bias_sc, r.w_out, r.w_up,
        r.w_down, copies, r.mixed_sc, r.middle_sc, lifted, r.slope_sc, active, r.feed_sc,
    )
    peers_here()
    left_x = sender.start(r.left_sc.at[own], r.left_sc.at[rows : 2 * rows], "x")
    left_c = sender.start(r.left_sc.at[own], r.left_sc.at[2 * rows : 3 * rows], "c")
    r.output_sc[...] = result.astype(BF)
    mover.flush(r.output_sc, r.output)
    grad = feed_backward(
        1, r.cot_sc[...].astype(F32), r.feed_sc[...], r.middle_sc[...], r.mixed_sc[...],
        r.slope_sc, r.vectors_sc, r.w_up, r.w_down, None, r.fg_sc, r.hg_sc, r.mg_sc, r.bias_out,
        r.rows_out, 0,
    )
    half, part = units // 2, width // 2

    def columns(ref, start, count):
        return ref.at[:, pl.ds(pl.multiple_of(start, LANES), count)]

    rights = [
        sender.start(columns(r.hg_sc, (1 - x_at) * half, half), r.far_sc.at[:, :half], "x"),
        sender.start(columns(r.fg_sc, (1 - x_at) * part, part), r.far_sc.at[:, half:], "x"),
    ]
    mixed_x = sender.start(columns(r.mg_sc, (1 - x_at) * part, part), r.mixed1_x, "x")
    q_up, q_down = half // 2, part // 2
    ready = [left_c]

    def place(up, down, up_at, down_at, index):
        here = slice(index * rows, (index + 1) * rows)
        there = slice((2 + index) * rows, (3 + index) * rows)
        for ref, start, count, to in ((up, up_at, q_up, 0), (down, down_at, q_down, q_up)):
            ready.append(
                mover.start(
                    columns(ref, start + c_at * count, count), r.right_sc.at[here, to : to + count]
                )
            )
            ready.append(
                sender.start(
                    columns(ref, start + (1 - c_at) * count, count),
                    r.right_sc.at[there, to : to + count],
                    "c",
                )
            )

    place(r.hg_sc, r.fg_sc, x_at * half, x_at * part, 0)
    mover.flush(columns(r.mg_sc, x_at * part, part), r.mixed1)
    r.middle_grad_sc[...] = grad
    mover.flush(r.middle_grad_sc, r.middle_grad)
    r.att_grad_sc[...] = product_right(r.mg_sc[...], r.w_out[...]).astype(BF)
    for copy in late_loads:
        copy.wait()

    def meanwhile():
        left_x.wait_recv()
        ready.append(
            sender.start(
                r.left_sc.at[rows : 2 * rows], r.left_sc.at[3 * rows : 4 * rows], "c"
            )
        )

    head_backward(me, r.att_grad_sc, r.dqkv_sc, r, meanwhile)
    mover.flush(r.dqkv_sc, r.dqkv)
    for copy in rights:
        copy.wait_recv()
    place(r.far_sc, r.far_sc, 0, half, 1)
    for copy in ready:
        copy.wait_recv()
    for slot in range(OUTER):
        target = (r.away_sc if slot < 2 else r.stay_sc).at[slot % 2]

        def emit(base, y, row, col, values, target=target):
            height, wide = values.shape
            target[y, row : row + height, base + col : base + col + wide] = values

        group = slot_group(slot, z0, z1)
        slot_product(
            group, r.left_sc, 0, r.right_sc, 0, q_up, False, functools.partial(emit, 0)
        )
        slot_product(
            group, r.left_sc, width, r.right_sc, q_up, q_down, True, functools.partial(emit, q_up)
        )
        if slot == 1:
            mover.flush(r.away_sc, r.away)
    mover.flush(r.stay_sc, r.stay)
    mixed_x.wait_recv()
    assert len(sender.copies) == r.ring_sems.shape[1]
    sender.finish()
    mover.finish()


def middle(first, cotangent, vectors, up_bias, out_weight, up_weight, down_weight):
    rows, width = cotangent.shape
    hidden = up_weight.shape[2]
    every = PEERS * FRAME
    loaded = {
        "vectors": vectors, "leftatt1": first.leftatt1, "res": first.res1, "up_bias": up_bias,
        "cot": cotangent, "queries": first.queries, "keys": first.keys, "values": first.values,
        "outs": first.outs, "lse": first.lse,
    }
    columns = hidden // 2
    stored = {
        "output": ((rows, width), BF),
        "middle_grad": ((rows, width), F32),
        "dqkv": ((rows, 3 * width), BF),
        "stay": ((2, 2, BLOCK, columns), BF),
        "away": ((2, 2, BLOCK, columns), BF),
    }
    return named_call(
        middle_kernel,
        {
            **loaded, "marks_all": first.marks_all, "out_w": out_weight, "up_w": up_weight,
            "down_w": down_weight,
        },
        {
            **{key: (*value, True) for key, value in stored.items()},
            "mixed1": ((rows, width // 2), BF, True),
            "mixed1_x": ((rows, width // 2), BF, True),
            "bias_out": ((1, hidden), F32, False),
            "rows_out": ((8, width), F32, False),
        },
        {
            **{key + "_sc": pltpu.VMEM(value.shape, value.dtype) for key, value in loaded.items()},
            **{key + "_sc": pltpu.VMEM(*value) for key, value in stored.items()},
            "marks_sc": full(2 * PEERS, LANES),
            "w_out": low(width, width),
            "w_up": low(width, hidden),
            "w_down": low(hidden, width),
            "left_sc": low(4 * rows, hidden + width),
            "right_sc": low(4 * rows, (hidden + width) // 4),
            "far_sc": low(rows, (hidden + width) // 2),
            "mixed_sc": full(rows, width),
            "middle_sc": full(rows, width),
            "slope_sc": full(rows, hidden),
            "feed_sc": full(rows, width),
            "fg_sc": low(rows, width),
            "hg_sc": low(rows, hidden),
            "mg_sc": low(rows, width),
            "att_grad_sc": low(rows, width),
            "grads_sc": low(every, LANES),
            "pack": low(PEERS, FOLD, LANES),
            "got": low(PEERS, FOLD, LANES),
            "pairs": low(PEERS, 2 * FOLD, LANES),
            "pairs_in": low(PEERS, 2 * FOLD, LANES),
            "asked": low(PEERS, FOLD, LANES),
            "asked_in": low(PEERS, FOLD, LANES),
            "sems": pltpu.SemaphoreType.DMA((9,)),
            "moves": pltpu.SemaphoreType.DMA((21,)),
            "own_sems": pltpu.SemaphoreType.DMA((3,)),
            "out_sems": pltpu.SemaphoreType.DMA((2, PEERS)),
            "back_sems": pltpu.SemaphoreType.DMA((2, PEERS)),
            "pair_sems": pltpu.SemaphoreType.DMA((2, PEERS)),
            "ring_sems": pltpu.SemaphoreType.DMA((2, 10)),
        },
        60,
        pl.CostEstimate(
            flops=4 * rows * width * (width + 2 * hidden) + 10 * every * every * LANES,
            bytes_accessed=2 * width * (width + 2 * hidden),
            transcendentals=2 * rows * hidden + every * every,
        ),
        "middle",
        collective_id=2,
    )


def per_device(
    tokens,
    qkv_weight,
    out_weight,
    up_weight,
    down_weight,
    vectors,
    up_bias,
    head_norm,
    token_valid,
    frame_scene,
    cotangent,
):
    count = lax.axis_size("blk")
    outer = count // 4
    me = lax.axis_index("blk")
    x_at = lax.axis_index("grp")
    c_at = lax.rem(me, 2)
    y_at = lax.rem(me // 2, 2)
    c_pairs = [(i, i ^ 1) for i in range(count)]
    y_pairs = [(i, i ^ 2) for i in range(count)]
    z_groups = [[4 * o + k for o in range(outer)] for k in range(4)]
    over_y = count == HEADS
    halves_at = jnp.stack([x_at, y_at if over_y else x_at]).astype(jnp.int32)
    places = jnp.stack(
        [c_at, y_at, x_at, lax.rem(me // 4, 2), lax.rem(me // 8, 2), halves_at[1]]
    ).astype(jnp.int32)


    def swap_x(value):
        return lax.ppermute(value, "grp", [(0, 1), (1, 0)])

    def swap_c(value):
        return lax.ppermute(value, "blk", c_pairs)

    def swap_y(value):
        return lax.ppermute(value, "blk", y_pairs)

    def part(value, index, parts, axis):
        size = value.shape[axis] // parts
        return lax.dynamic_slice_in_dim(value, index * size, size, axis)

    def tied(value, *others):
        return lax.optimization_barrier((value, *others))

    def ready_sum(keep, arrived):
        return (keep.astype(F32) + arrived.astype(F32)).astype(BF)

    def scattered(own):
        return lax.psum_scatter(
            own, "blk", scatter_dimension=0, tiled=True, axis_index_groups=z_groups
        )

    def finished(total):
        pair = jnp.stack([part(total, c_at, 2, 0), swap_c(part(total, 1 - c_at, 2, 0))])
        return jnp.concatenate([pair, swap_x(pair)], axis=0)

    def total_of(value):
        value = value + swap_x(value)
        step = 1
        while step < count:
            pairs = [(i, i ^ step) for i in range(count)]
            value = value + lax.ppermute(value, "blk", pairs)
            step *= 2
        return value

    row_count, width = tokens.shape[1:]
    position = lax.broadcasted_iota(jnp.int32, (row_count,), 0)
    usable = (token_valid[0, 0] == 1) | (position < SPECIAL)
    usable_row = usable.astype(F32).reshape(1, row_count)
    scene = frame_scene[0, 0].astype(F32)
    tag_rows = jnp.where(usable, scene, -1.0)
    head_rows = jnp.tile(head_norm.reshape(2, 3, HD), (1, 1, WIDE // HD))
    head_rows = jnp.concatenate([head_rows, jnp.zeros((2, 5, WIDE), F32)], axis=1)

    hidden = up_weight.shape[2]
    if count == HEADS:
        marks = jnp.concatenate(
            [
                tag_rows.reshape(1, row_count),
                jnp.full((1, row_count), scene),
                jnp.zeros((EXTRA - 2, row_count), F32),
            ],
            axis=0,
        ).astype(BF)
        first = begin(
            tokens[0], usable_row, marks, vectors, up_bias, head_rows, qkv_weight, out_weight,
            up_weight, down_weight,
        )
        second = middle(
            first, cotangent[0], vectors, up_bias, out_weight, up_weight, down_weight
        )
        away = lax.ppermute(second.away, "blk", [(i, i ^ 4) for i in range(count)])
        left0_far, leftatt1_x = swap_y(first.left0), swap_x(first.leftatt1)
        pre0, qkv0, mixed0, middle0, slope0, feed0, res1, pre1 = (
            first.pre0, first.qkv0, first.mixed0, first.middle0, first.slope0, first.feed0,
            first.res1, first.pre1,
        )
        output, middle_grad1, dqkv1, bias1, rows1 = (
            second.output, second.middle_grad, second.dqkv, second.bias_out, second.rows_out
        )
    else:
        left0, leftatt0, pre0, qkv0, mixed0, middle0, slope0, feed0, res1, normed1, pre1, qkv1 = (
            front(
                tokens[0], usable_row, vectors, up_bias, head_rows, qkv_weight, out_weight,
                up_weight, down_weight,
            )
        )
        att1, kept = gathered_forward(qkv1, tag_rows, scene)
        left1, leftatt1, output, right1, right1_send, att_grad1, middle_grad1, bias1, rows1 = turn(
            halves_at, att1, normed1, res1, cotangent[0], vectors, up_bias, out_weight, up_weight,
            down_weight,
        )
        dqkv1 = gathered_backward(att_grad1, kept, tag_rows, scene)
    swap_far = swap_y if over_y else swap_x
    third = back_one(
        halves_at, dqkv1, pre1, res1, middle_grad1, feed0, middle0, mixed0, slope0, vectors,
        head_rows, qkv_weight, up_weight, down_weight,
    )
    pg1_x, right0_far = swap_x(third.pg_send), swap_far(third.right_send)
    fourth = back_two(
        halves_at, third.mixed_grad, third.middle_grad, qkv0, pre0, tokens[0], usable_row, vectors,
        head_rows, third.rows_out, rows1, third.bias_out, bias1, third.head_out, out_weight,
        qkv_weight,
    )
    small = fourth.small

    def feed_grads(name, lefts, rights):
        return weight_grads(
            name,
            outer,
            width,
            places,
            [
                (lefts, 0, width, rights, 0, hidden // 2, False),
                (lefts, width, hidden, rights, hidden // 2, width // 2, True),
            ],
        )

    def att_grads(name, lefts, projected, rights, at):
        return weight_grads(
            name,
            outer,
            width,
            places,
            [
                (lefts, 0, width, projected, 0, 3 * width // 2, False),
                (lefts, width, width, rights, at, width // 2, False),
            ],
        )

    def four(own, far):
        return (own, far, swap_c(own), swap_c(far))

    def reduce_apart():
        pg0_all = four(fourth.pg_keep, swap_x(fourth.pg_send))
        right1_all = four(right1, swap_x(right1_send))
        results = []
        for keep, send in (
            feed_grads(
                "feed_grads0", four(left0, swap_x(left0)), four(third.right_keep, right0_far)
            ),
            att_grads(
                "att_grads0", four(leftatt0, swap_x(leftatt0)), pg0_all, pg0_all, 3 * width // 2
            ),
            feed_grads("feed_grads1", four(left1, swap_x(left1)), right1_all),
            att_grads(
                "att_grads1", four(leftatt1, swap_x(leftatt1)), four(third.pg_keep, pg1_x),
                right1_all, (hidden + width) // 2,
            ),
        ):
            results.append(finished(scattered(ready_sum(keep, swap_y(send)))))
        return results

    if count == HEADS:
        *pieces, small = reduce_all(
            small,
            (second.stay, away),
            (
                first.leftatt1, leftatt1_x, third.pg_keep, pg1_x, second.mixed1, second.mixed1_x,
            ),
            (first.left0, left0_far, third.right_keep, right0_far),
            (first.leftatt0, first.leftatt0_x, fourth.pg_keep, fourth.pg_send),
        )
    else:
        small = total_of(small)
        pieces = reduce_apart()
    weight_shapes = [
        (2, width // count, 3 * width),
        (2, width // count, width),
        (2, width // count, up_weight.shape[2]),
        (2, up_weight.shape[2] // count, width),
    ]
    qkv_grad, out_grad, up_grad, down_grad = assemble(
        places, pieces, weight_shapes
    )

    vector_rows = 2 * vectors.shape[1]
    bias_rows = 2 * hidden // width
    vector_grad = small[:vector_rows].reshape(2, -1, width)
    bias_grad = small[vector_rows : vector_rows + bias_rows].reshape(2, hidden)
    head_grad = small[vector_rows + bias_rows, : 6 * HD].reshape(2, 3 * HD)
    return (
        output[None],
        fourth.input_grad[None],
        qkv_grad,
        out_grad,
        up_grad,
        down_grad,
        part(vector_grad, me, count, 2),
        part(bias_grad, me, count, 1),
        head_grad,
    )


def gathered_forward(qkv, tag_rows, scene):
    rows, width = qkv.shape[0], qkv.shape[1] // 3
    marks = jnp.zeros((KEEP, 2 * width), BF)
    marks = marks.at[0, :rows].set(tag_rows.astype(BF))
    marks = marks.at[1, :rows].set(jnp.full((rows,), scene).astype(BF))
    pairs = lax.all_gather(
        jnp.concatenate([qkv[:, width:], marks], axis=0), "blk", axis=0, tiled=False
    )
    tags = pairs[:, FRAME, :FRAME].astype(F32).reshape(1, -1)
    scenes = pairs[:, FRAME + 1, :FRAME].astype(F32).reshape(1, -1)
    queries = qkv[:, :width]
    attended, lse = global_attend(queries, pairs, tags, jnp.full((8, LANES), scene))
    every_query = lax.all_gather(
        with_rows(queries, lse.reshape(HEADS, rows)), "blk", axis=0, tiled=False
    )
    return attended.astype(BF), (qkv, pairs, tags, scenes, attended, lse, every_query)


def gathered_backward(attended_grad, kept, tag_rows, scene):
    qkv, pairs, tags, scenes, attended, lse, every_query = kept
    rows, width = attended_grad.shape
    delta = jnp.sum(
        (attended_grad.astype(F32) * attended).reshape(rows, HEADS, HD), axis=-1
    ).T
    every_grad = lax.all_gather(with_rows(attended_grad, delta), "blk", axis=0, tiled=False)
    query_grad = global_query_grad(
        qkv[:, :width],
        pairs,
        tags,
        jnp.full((8, LANES), scene),
        attended_grad,
        lse,
        delta.reshape(PAIRS, 2, rows),
    )
    key_grad, value_grad = global_key_grad(
        qkv[:, width : 2 * width],
        qkv[:, 2 * width :],
        tag_rows.reshape(1, rows),
        scenes,
        every_query,
        every_grad,
        rows_of(every_query, width),
        rows_of(every_grad, width),
    )
    return jnp.concatenate([query_grad, key_grad, value_grad], axis=1).astype(BF)


def solution(mesh):
    return jax.shard_map(
        per_device,
        mesh=mesh,
        in_specs=(
            P("grp", "blk", None),
            P(),
            P(),
            P(),
            P(),
            P(),
            P(),
            P(),
            P("grp", "blk", None),
            P("grp", "blk"),
            P("grp", "blk", None),
        ),
        out_specs=(
            P("grp", "blk", None),
            P("grp", "blk", None),
            P(None, "blk", None),
            P(None, "blk", None),
            P(None, "blk", None),
            P(None, "blk", None),
            P(None, None, "blk"),
            P(None, "blk"),
            P(),
        ),
        check_vma=False,
    )
```

```python
import functools
import types

import jax
import jax.numpy as jnp
from jax import lax
from jax.experimental import pallas as pl
from jax.experimental.pallas import tpu as pltpu
from jax.sharding import PartitionSpec as P

HEADS = 16
HD = 64
SPECIAL = 5
PAIRS = HEADS // 2
LANES = 2 * HD
FRAME = 128
KEEP = 16
EPS = 1e-06
NEG = -1e30
SCALE = HD**-0.5
BF = jnp.bfloat16
F32 = jnp.float32


def product(left_side, right_side):
    return jnp.dot(left_side, right_side, preferred_element_type=F32)


def product_left(left_side, right_side):
    return lax.dot_general(
        left_side, right_side, (((0,), (0,)), ((), ())), preferred_element_type=F32
    )


def product_right(left_side, right_side):
    return lax.dot_general(
        left_side, right_side, (((1,), (1,)), ((), ())), preferred_element_type=F32
    )


def lane_masks(dtype):
    lane = lax.broadcasted_iota(jnp.int32, (1, LANES), 1)
    first = (lane < HD).astype(dtype)
    return (first, 1 - first)


def as_column(row):
    size = row.shape[1]
    return jnp.transpose(jnp.broadcast_to(row, (LANES, size)))[:, :1]


def as_row(column):
    size = column.shape[0]
    return jnp.transpose(jnp.broadcast_to(column, (size, LANES)))[:1, :]


def flat(ref):
    block = ref[...]
    return block.reshape(block.shape[0] * block.shape[1], block.shape[2])


def attend_kernel(blocks, q_ref, k_ref, v_ref, tag_ref, scene_ref, o_ref, lse_ref, m_sc, l_sc, a_sc):
    step = pl.program_id(1)
    keys, values = flat(k_ref), flat(v_ref)
    allowed = tag_ref[...] == scene_ref[:1, :1]
    queries = q_ref[...]
    pieces = []
    for index, mask in enumerate(lane_masks(BF)):
        scores = product_right(queries * mask, keys) * SCALE
        scores = jnp.where(allowed, scores, NEG)
        top = jnp.max(scores, axis=-1, keepdims=True)

        if blocks > 1:

            @pl.when(step == 0)
            def _():
                m_sc[index] = jnp.full_like(m_sc[index], NEG)
                l_sc[index] = jnp.zeros_like(l_sc[index])
                a_sc[index] = jnp.zeros_like(a_sc[index])

            old = m_sc[index][:, :1]
            top = jnp.maximum(top, old)
            keep = jnp.exp(old - top)
        shares = jnp.where(allowed, jnp.exp(scores - top), 0.0)
        total = jnp.sum(shares, axis=-1, keepdims=True)
        weighted = product(shares.astype(BF), values)
        if blocks > 1:
            total = total + keep * l_sc[index][:, :1]
            weighted = weighted + keep * a_sc[index]
            m_sc[index] = jnp.broadcast_to(top, m_sc[index].shape)
            l_sc[index] = jnp.broadcast_to(total, l_sc[index].shape)
            a_sc[index] = weighted
        pieces.append(weighted / total)
        lse_ref[0, index : index + 1, :] = as_row(top + jnp.log(total))
    first, second = lane_masks(F32)
    o_ref[...] = jnp.where(first > 0, pieces[0], pieces[1])


def key_block(count):
    for size in (16, 8, 4, 2, 1):
        if count % size == 0:
            return size


def global_attend(queries, pairs, tags, scene):
    frames = pairs.shape[0]
    group = key_block(frames)
    blocks = frames // group
    return pl.pallas_call(
        functools.partial(attend_kernel, blocks),
        grid=(PAIRS, blocks),
        in_specs=[
            pl.BlockSpec((FRAME, LANES), lambda p, k: (0, p)),
            pl.BlockSpec((group, FRAME, LANES), lambda p, k: (k, 0, p)),
            pl.BlockSpec((group, FRAME, LANES), lambda p, k: (k, 0, PAIRS + p)),
            pl.BlockSpec((1, group * FRAME), lambda p, k: (0, k)),
            pl.BlockSpec((8, LANES), lambda p, k: (0, 0)),
        ],
        out_specs=[
            pl.BlockSpec((FRAME, LANES), lambda p, k: (0, p)),
            pl.BlockSpec((1, 2, FRAME), lambda p, k: (p, 0, 0)),
        ],
        out_shape=[
            jax.ShapeDtypeStruct((FRAME, PAIRS * LANES), F32),
            jax.ShapeDtypeStruct((PAIRS, 2, FRAME), F32),
        ],
        scratch_shapes=[pltpu.VMEM((2, FRAME, LANES), F32)] * 3,
        compiler_params=pltpu.CompilerParams(vmem_limit_bytes=48 * 2**20),
        cost_estimate=pl.CostEstimate(
            flops=4 * FRAME * frames * FRAME * LANES * HEADS,
            bytes_accessed=frames * FRAME * 4096,
            transcendentals=FRAME * frames * FRAME * HEADS,
        ),
        name="global_attend",
    )(queries, pairs, pairs, tags, scene)


def query_grad_kernel(
    q_ref, k_ref, v_ref, tag_ref, scene_ref, do_ref, lse_ref, delta_ref, dq_ref
):
    step = pl.program_id(1)
    keys, values = flat(k_ref), flat(v_ref)
    allowed = tag_ref[...] == scene_ref[:1, :1]
    queries, outs = q_ref[...], do_ref[...]
    pieces = []
    for index, mask in enumerate(lane_masks(BF)):
        scores = product_right(queries * mask, keys) * SCALE
        top = as_column(lse_ref[0, index : index + 1, :])
        delta = as_column(delta_ref[0, index : index + 1, :])
        shares = jnp.where(allowed, jnp.exp(scores - top), 0.0)
        share_grad = product_right(outs * mask, values)
        score_grad = (shares * (share_grad - delta)).astype(BF)
        pieces.append(product(score_grad, keys) * SCALE)
    first, second = lane_masks(F32)
    piece = jnp.where(first > 0, pieces[0], pieces[1])

    @pl.when(step == 0)
    def _():
        dq_ref[...] = piece

    @pl.when(step > 0)
    def _():
        dq_ref[...] += piece


def global_query_grad(queries, pairs, tags, scene, outs, lse, delta):
    frames = pairs.shape[0]
    group = key_block(frames)
    blocks = frames // group
    return pl.pallas_call(
        query_grad_kernel,
        grid=(PAIRS, blocks),
        in_specs=[
            pl.BlockSpec((FRAME, LANES), lambda p, k: (0, p)),
            pl.BlockSpec((group, FRAME, LANES), lambda p, k: (k, 0, p)),
            pl.BlockSpec((group, FRAME, LANES), lambda p, k: (k, 0, PAIRS + p)),
            pl.BlockSpec((1, group * FRAME), lambda p, k: (0, k)),
            pl.BlockSpec((8, LANES), lambda p, k: (0, 0)),
            pl.BlockSpec((FRAME, LANES), lambda p, k: (0, p)),
            pl.BlockSpec((1, 2, FRAME), lambda p, k: (p, 0, 0)),
            pl.BlockSpec((1, 2, FRAME), lambda p, k: (p, 0, 0)),
        ],
        out_specs=pl.BlockSpec((FRAME, LANES), lambda p, k: (0, p)),
        out_shape=jax.ShapeDtypeStruct((FRAME, PAIRS * LANES), F32),
        compiler_params=pltpu.CompilerParams(vmem_limit_bytes=48 * 2**20),
        cost_estimate=pl.CostEstimate(
            flops=6 * FRAME * frames * FRAME * LANES * HEADS,
            bytes_accessed=frames * FRAME * 4096,
            transcendentals=FRAME * frames * FRAME * HEADS,
        ),
        name="global_query_grad",
    )(queries, pairs, pairs, tags, scene, outs, lse, delta)


def key_grad_kernel(
    k_ref, v_ref, tag_ref, scene_ref, q_ref, do_ref, lse_ref, delta_ref, dk_ref, dv_ref
):
    step = pl.program_id(1)
    keys, values = k_ref[...], v_ref[...]
    queries, outs = flat(q_ref), flat(do_ref)
    allowed = as_column(tag_ref[...]) == scene_ref[...]
    key_pieces, value_pieces = [], []
    for index, mask in enumerate(lane_masks(BF)):
        scores = product_right(keys * mask, queries) * SCALE
        top = lse_ref[0, index : index + 1, :]
        delta = delta_ref[0, index : index + 1, :]
        shares = jnp.where(allowed, jnp.exp(scores - top), 0.0)
        share_grad = product_right(values * mask, outs)
        score_grad = (shares * (share_grad - delta)).astype(BF)
        key_pieces.append(product(score_grad, queries) * SCALE)
        value_pieces.append(product(shares.astype(BF), outs))
    first, second = lane_masks(F32)
    key_piece = jnp.where(first > 0, key_pieces[0], key_pieces[1])
    value_piece = jnp.where(first > 0, value_pieces[0], value_pieces[1])

    @pl.when(step == 0)
    def _():
        dk_ref[...] = key_piece
        dv_ref[...] = value_piece

    @pl.when(step > 0)
    def _():
        dk_ref[...] += key_piece
        dv_ref[...] += value_piece


def global_key_grad(keys, values, tags, scenes, queries, outs, lse, delta):
    frames = queries.shape[0]
    group = key_block(frames)
    blocks = frames // group
    return pl.pallas_call(
        key_grad_kernel,
        grid=(PAIRS, blocks),
        in_specs=[
            pl.BlockSpec((FRAME, LANES), lambda p, k: (0, p)),
            pl.BlockSpec((FRAME, LANES), lambda p, k: (0, p)),
            pl.BlockSpec((1, FRAME), lambda p, k: (0, 0)),
            pl.BlockSpec((1, group * FRAME), lambda p, k: (0, k)),
            pl.BlockSpec((group, FRAME, LANES), lambda p, k: (k, 0, p)),
            pl.BlockSpec((group, FRAME, LANES), lambda p, k: (k, 0, p)),
            pl.BlockSpec((1, 2, group * FRAME), lambda p, k: (p, 0, k)),
            pl.BlockSpec((1, 2, group * FRAME), lambda p, k: (p, 0, k)),
        ],
        out_specs=[pl.BlockSpec((FRAME, LANES), lambda p, k: (0, p))] * 2,
        out_shape=[jax.ShapeDtypeStruct((FRAME, PAIRS * LANES), F32)] * 2,
        compiler_params=pltpu.CompilerParams(vmem_limit_bytes=48 * 2**20),
        cost_estimate=pl.CostEstimate(
            flops=8 * FRAME * frames * FRAME * LANES * HEADS,
            bytes_accessed=frames * FRAME * 4096,
            transcendentals=FRAME * frames * FRAME * HEADS,
        ),
        name="global_key_grad",
    )(keys, values, tags, scenes, queries, outs, lse, delta)


def split_three(values):
    high = values.astype(BF)
    rest = values - high.astype(F32)
    middle = rest.astype(BF)
    return jnp.stack([high, middle, (rest - middle.astype(F32)).astype(BF)])


def with_rows(body, statistic):
    width = body.shape[1]
    extra = split_three(statistic).reshape(-1, width)
    pad = jnp.zeros((KEEP - extra.shape[0], width), BF)
    return jnp.concatenate([body, extra, pad], axis=0)


def rows_of(gathered, width):
    frames = gathered.shape[0]
    used = 3 * HEADS * FRAME // width
    terms = gathered[:, FRAME : FRAME + used].reshape(frames, 3, HEADS, FRAME).astype(F32)
    total = terms[:, 0] + terms[:, 1] + terms[:, 2]
    return total.transpose(1, 0, 2).reshape(PAIRS, 2, frames * FRAME)


VMEM_MIB = 2**20
WIDE = 256
ROOT_HALF = 0.7071067811865476
ROOT_TWO_PI = 0.3989422804014327


def whole(space=pltpu.VMEM):
    return pl.BlockSpec(memory_space=space)


def terms_of(values):
    high = values.astype(BF)
    rest = values - high.astype(F32)
    middle = rest.astype(BF)
    return (high, middle, (rest - middle.astype(F32)).astype(BF))


def head_averager():
    row = lax.broadcasted_iota(jnp.int32, (WIDE, WIDE), 0) // HD
    col = lax.broadcasted_iota(jnp.int32, (WIDE, WIDE), 1) // HD
    return jnp.where(row == col, 1.0 / HD, 0.0).astype(BF)


def head_mean(values, averager):
    high, middle, least = terms_of(values)
    return product(high, averager) + product(middle, averager) + product(least, averager)


def standard(values):
    centered = values - jnp.mean(values, axis=-1, keepdims=True)
    scale = lax.rsqrt(jnp.mean(centered * centered, axis=-1, keepdims=True) + EPS)
    return centered * scale, scale


def standard_heads(values, averager):
    centered = values - head_mean(values, averager)
    scale = lax.rsqrt(head_mean(centered * centered, averager) + EPS)
    return centered * scale, scale


def norm_pull(values, gain, grad):
    unit, scale = standard(values)
    scaled = grad * gain
    spread = jnp.mean(scaled * unit, axis=-1, keepdims=True)
    result = scale * (scaled - jnp.mean(scaled, axis=-1, keepdims=True) - unit * spread)
    return (
        result,
        jnp.sum(grad * unit, axis=0, keepdims=True),
        jnp.sum(grad, axis=0, keepdims=True),
    )


def weight_copies(sources, targets, sems):
    copies = [
        pltpu.make_async_copy(source, target, sems.at[index])
        for index, (source, target) in enumerate(zip(sources, targets))
    ]
    for copy in copies:
        copy.start()
    return copies


def column_pieces(ref, parts):
    size = ref.shape[-1] // parts
    return [ref.at[:, i * size : (i + 1) * size] for i in range(parts)]


def row_pieces(ref, parts):
    size = ref.shape[0] // parts
    return [ref.at[i * size : (i + 1) * size] for i in range(parts)]


def project(layer, residual, vec_ref, head_ref, w_ref, copies, normed_ref, pre_ref, qkv_ref):
    width = residual.shape[1]
    unit, _ = standard(residual)
    normed = (unit * vec_ref[layer, 0:1] + vec_ref[layer, 1:2]).astype(BF)
    normed_ref[...] = normed
    averager = head_averager()
    for part in range(3):
        copies[part].wait()
        bias = vec_ref[layer, 2 + part : 3 + part]
        for j in range(width // WIDE):
            at = slice(part * width + j * WIDE, part * width + (j + 1) * WIDE)
            value = product(normed, w_ref[:, at]) + bias[:, j * WIDE : (j + 1) * WIDE]
            if part < 2:
                pre_ref[:, at] = value
                unit, _ = standard_heads(value, averager)
                value = unit * head_ref[layer, 2 * part : 2 * part + 1]
                if part == 0:
                    value = value + head_ref[layer, 1:2]
            qkv_ref[:, at] = value.astype(BF)


def frame_attend(usable, qkv_ref, att_ref):
    width = att_ref.shape[1]
    first, _ = lane_masks(F32)
    for pair in range(width // LANES):
        q, k, v = [
            qkv_ref[:, part * width + pair * LANES : part * width + (pair + 1) * LANES]
            for part in range(3)
        ]
        pieces = []
        for mask in lane_masks(BF):
            shares = frame_shares(q * mask, k, usable)
            pieces.append(product(shares.astype(BF), v))
        at = slice(pair * LANES, (pair + 1) * LANES)
        att_ref[:, at] = jnp.where(first > 0, pieces[0], pieces[1]).astype(att_ref.dtype)


def frame_shares(queries, keys, usable):
    scores = jnp.where(usable > 0, product_right(queries, keys) * SCALE, NEG)
    shares = jnp.exp(scores - jnp.max(scores, axis=-1, keepdims=True))
    return shares / jnp.sum(shares, axis=-1, keepdims=True)


def feed_forward(
    layer, att, residual, vec_ref, bias_ref, w_out, w_up, w_down, copies, mixed_ref, middle_ref,
    lifted_ref, slope_ref, active_ref, feed_ref,
):
    chunks = w_up.shape[1] // 512
    copies[0].wait()
    mixed = product(att, w_out[...]) + vec_ref[layer, 5:6]
    mixed_ref[...] = mixed
    middle = residual + vec_ref[layer, 6:7] * mixed
    middle_ref[...] = middle
    unit, _ = standard(middle)
    lifted = (unit * vec_ref[layer, 7:8] + vec_ref[layer, 8:9]).astype(BF)
    lifted_ref[...] = lifted
    feed = None
    for j in range(chunks):
        at = slice(j * 512, (j + 1) * 512)
        if j % 2 == 0:
            copies[1 + j].wait()
            copies[2 + j].wait()
        hidden = product(lifted, w_up[:, at]) + bias_ref[layer : layer + 1, at]
        bell = 0.5 * (1.0 + lax.erf(hidden * ROOT_HALF))
        slope_ref[:, at] = bell + hidden * jnp.exp(-0.5 * hidden * hidden) * ROOT_TWO_PI
        active = (hidden * bell).astype(BF)
        active_ref[:, at] = active
        piece = product(active, w_down[at])
        feed = piece if feed is None else feed + piece
    feed = feed + vec_ref[layer, 9:10]
    feed_ref[...] = feed
    return middle + vec_ref[layer, 10:11] * feed


def split_columns(value_refs, x_at, keep_ref, send_ref):
    start = 0
    for value_ref in value_refs:
        half = value_ref.shape[1] // 2
        to = slice(start, start + half)
        keep_ref[:, to] = value_ref[:, pl.ds(pl.multiple_of(x_at * half, LANES), half)]
        send_ref[:, to] = value_ref[:, pl.ds(pl.multiple_of((1 - x_at) * half, LANES), half)]
        start += half


def feed_backward(
    layer, grad, feed, middle, mixed, slope_ref, vec_ref, w_up, w_down, copies, feed_grad_ref,
    hidden_grad_ref, mixed_grad_ref, bias_out, rows_ref, row0,
):
    chunks = w_up.shape[1] // 512
    feed_grad = (vec_ref[layer, 10:11] * grad).astype(BF)
    feed_grad_ref[...] = feed_grad
    rows_ref[row0 + 4 : row0 + 5] = jnp.sum(feed_grad.astype(F32), axis=0, keepdims=True)
    rows_ref[row0 + 5 : row0 + 6] = jnp.sum(grad * feed, axis=0, keepdims=True)
    lifted_grad = None
    for j in range(chunks):
        at = slice(j * 512, (j + 1) * 512)
        if copies is not None and j % 2 == 0:
            copies[j].wait()
            copies[j + 1].wait()
        hidden_grad = (slope_ref[:, at] * product_right(feed_grad, w_down[at])).astype(BF)
        hidden_grad_ref[:, at] = hidden_grad
        bias_out[:, at] = jnp.sum(hidden_grad.astype(F32), axis=0, keepdims=True)
        piece = product_right(hidden_grad, w_up[:, at])
        lifted_grad = piece if lifted_grad is None else lifted_grad + piece
    part, gain_grad, shift_grad = norm_pull(middle, vec_ref[layer, 7:8], lifted_grad)
    middle_grad = grad + part
    mixed_grad = (vec_ref[layer, 6:7] * middle_grad).astype(BF)
    mixed_grad_ref[...] = mixed_grad
    rows_ref[row0 : row0 + 1] = jnp.sum(mixed_grad.astype(F32), axis=0, keepdims=True)
    rows_ref[row0 + 1 : row0 + 2] = jnp.sum(middle_grad * mixed, axis=0, keepdims=True)
    rows_ref[row0 + 2 : row0 + 3] = gain_grad
    rows_ref[row0 + 3 : row0 + 4] = shift_grad
    return middle_grad


def project_backward(
    layer, residual, dqkv_ref, pre_ref, vec_ref, head_ref, w_ref, copies, pg_ref, rows_ref, head_out
):
    width = residual.shape[1]
    averager = head_averager()
    sums = [None, None, None]
    for part in range(3):
        for j in range(width // WIDE):
            at = slice(part * width + j * WIDE, part * width + (j + 1) * WIDE)
            value = dqkv_ref[:, at].astype(F32)
            if part < 2:
                unit, scale = standard_heads(pre_ref[:, at], averager)
                news = [(2 * part, jnp.sum(value * unit, axis=0, keepdims=True))]
                if part == 0:
                    news.append((1, jnp.sum(value, axis=0, keepdims=True)))
                for index, new in news:
                    sums[index] = new if sums[index] is None else sums[index] + new
                scaled = value * head_ref[layer, 2 * part : 2 * part + 1]
                value = scale * (
                    scaled
                    - head_mean(scaled, averager)
                    - unit * head_mean(scaled * unit, averager)
                )
            low = value.astype(BF)
            pg_ref[:, at] = low
            rows_ref[2 + part : 3 + part, j * WIDE : (j + 1) * WIDE] = jnp.sum(
                low.astype(F32), axis=0, keepdims=True
            )
    head_out[...] = jnp.concatenate(sums + [jnp.zeros((5, WIDE), F32)], axis=0)
    normed_grad = None
    for part in range(3):
        copies[part].wait()
        at = slice(part * width, (part + 1) * width)
        piece = product_right(pg_ref[:, at], w_ref[:, at])
        normed_grad = piece if normed_grad is None else normed_grad + piece
    part, gain_grad, shift_grad = norm_pull(residual, vec_ref[layer, 0:1], normed_grad)
    rows_ref[0:1] = gain_grad
    rows_ref[1:2] = shift_grad
    return part


def named_call(kernel, inputs, outputs, scratch, vmem_mib, cost, name, collective_id=None):
    names = [*inputs, *outputs, *scratch]

    def body(*refs):
        kernel(types.SimpleNamespace(**dict(zip(names, refs))))

    more = {}
    if collective_id is not None:
        more = {"collective_id": collective_id, "has_side_effects": True}
    results = pl.pallas_call(
        body,
        in_specs=[
            whole(pltpu.SMEM) if key.startswith("smem") else whole(pl.ANY) for key in inputs
        ],
        out_specs=[whole(pl.ANY if value[2] else pltpu.VMEM) for value in outputs.values()],
        out_shape=[jax.ShapeDtypeStruct(value[0], value[1]) for value in outputs.values()],
        scratch_shapes=list(scratch.values()),
        compiler_params=pltpu.CompilerParams(vmem_limit_bytes=vmem_mib * VMEM_MIB, **more),
        cost_estimate=cost,
        name=name,
    )(*inputs.values())
    return types.SimpleNamespace(**dict(zip(outputs, results)))


def low(*shape):
    return pltpu.VMEM(shape, BF)


def full(*shape):
    return pltpu.VMEM(shape, F32)


class Mover:
    def __init__(self, sems):
        self.sems, self.count, self.open = sems, 0, []

    def start(self, source, target):
        copy = pltpu.make_async_copy(source, target, self.sems.at[self.count])
        copy.start()
        self.count += 1
        return copy

    def flush(self, source, target):
        self.open.append(self.start(source, target))

    def finish(self):
        assert self.count == self.sems.shape[0]
        for copy in self.open:
            copy.wait()


def interleaved(one, two):
    return [piece for pair in zip(one, two) for piece in pair]


def front_kernel(
    tok_ref, usable_ref, vec_ref, bias_ref, head_ref, qkv_w, out_w, up_w, down_w,
    left_pack, att_pack, pre0, qkv0, mixed0, middle0, slope0, feed0, res1, normed1, pre1, qkv1,
    w_qkv, w_out, w_up, w_down, w_next, sems,
):
    width, units = tok_ref.shape[1], up_w.shape[2]
    lifted0 = left_pack.at[:, :width]
    active0 = left_pack.at[:, width : width + units]
    normed0, att0 = att_pack.at[:, :width], att_pack.at[:, width:]
    copies = weight_copies(
        column_pieces(qkv_w.at[0], 3)
        + [out_w.at[0]]
        + interleaved(column_pieces(up_w.at[0], 4), row_pieces(down_w.at[0], 4))
        + column_pieces(qkv_w.at[1], 3),
        column_pieces(w_qkv, 3)
        + [w_out]
        + interleaved(column_pieces(w_up, 4), row_pieces(w_down, 4))
        + column_pieces(w_next, 3),
        sems,
    )
    residual = tok_ref[...].astype(F32)
    project(0, residual, vec_ref, head_ref, w_qkv, copies[:3], normed0, pre0, qkv0)
    frame_attend(usable_ref[...], qkv0, att0)
    result = feed_forward(
        0, att0[...], residual, vec_ref, bias_ref, w_out, w_up, w_down, copies[3:12], mixed0,
        middle0, lifted0, slope0, active0, feed0,
    )
    res1[...] = result
    project(1, result, vec_ref, head_ref, w_next, copies[12:], normed1, pre1, qkv1)


def front(tokens, usable, vectors, up_bias, head_rows, qkv_weight, out_weight, up_weight, down_weight):
    rows, width = tokens.shape
    hidden = up_weight.shape[2]
    shapes = [
        ((rows, hidden + width), BF),
        ((rows, 2 * width), BF),
        ((rows, 2 * width), F32),
        ((rows, 3 * width), BF),
        ((rows, width), F32),
        ((rows, width), F32),
        ((rows, hidden), F32),
        ((rows, width), F32),
        ((rows, width), F32),
        ((rows, width), BF),
        ((rows, 2 * width), F32),
        ((rows, 3 * width), BF),
    ]
    return pl.pallas_call(
        front_kernel,
        in_specs=[whole()] * 5 + [whole(pl.ANY)] * 4,
        out_specs=[whole()] * len(shapes),
        out_shape=[jax.ShapeDtypeStruct(*shape) for shape in shapes],
        scratch_shapes=[
            pltpu.VMEM((width, 3 * width), BF),
            pltpu.VMEM((width, width), BF),
            pltpu.VMEM((width, hidden), BF),
            pltpu.VMEM((hidden, width), BF),
            pltpu.VMEM((width, 3 * width), BF),
            pltpu.SemaphoreType.DMA((15,)),
        ],
        compiler_params=pltpu.CompilerParams(vmem_limit_bytes=58 * VMEM_MIB),
        cost_estimate=pl.CostEstimate(
            flops=2 * rows * width * (7 * width + 2 * hidden),
            bytes_accessed=2 * width * (7 * width + 2 * hidden),
            transcendentals=2 * rows * hidden,
        ),
        name="front",
    )(tokens, usable, vectors, up_bias, head_rows, qkv_weight, out_weight, up_weight, down_weight)


def turn_kernel(
    x_ref, att_ref, normed_ref, res_ref, cot_ref, vec_ref, bias_ref, out_w, up_w, down_w,
    left_pack, att_pack, output, right_keep, right_send, att_grad, middle_grad, bias_out, rows_out,
    w_out, w_up, w_down, mixed_sc, middle_sc, slope_sc, feed_sc, fg_sc, hg_sc, mg_sc, sems,
):
    width, units = att_ref.shape[1], up_w.shape[2]
    lifted = left_pack.at[:, :width]
    active = left_pack.at[:, width : width + units]
    att_pack[:, :width] = normed_ref[...]
    att_pack[:, width:] = att_ref[...]
    copies = weight_copies(
        [out_w.at[1]] + interleaved(column_pieces(up_w.at[1], 4), row_pieces(down_w.at[1], 4)),
        [w_out] + interleaved(column_pieces(w_up, 4), row_pieces(w_down, 4)),
        sems,
    )
    result = feed_forward(
        1, att_ref[...], res_ref[...], vec_ref, bias_ref, w_out, w_up, w_down, copies, mixed_sc,
        middle_sc, lifted, slope_sc, active, feed_sc,
    )
    output[...] = result.astype(BF)
    grad = feed_backward(
        1, cot_ref[...].astype(F32), feed_sc[...], middle_sc[...], mixed_sc[...], slope_sc, vec_ref,
        w_up, w_down, None, fg_sc, hg_sc, mg_sc, bias_out, rows_out, 0,
    )
    middle_grad[...] = grad
    att_grad[...] = product_right(mg_sc[...], w_out[...]).astype(BF)
    split_columns([hg_sc, fg_sc, mg_sc], x_ref[0], right_keep, right_send)


def turn(x_at, att, normed, res, cotangent, vectors, up_bias, out_weight, up_weight, down_weight):
    rows, width = res.shape
    hidden = up_weight.shape[2]
    shapes = [
        ((rows, hidden + width), BF),
        ((rows, 2 * width), BF),
        ((rows, width), BF),
        ((rows, hidden // 2 + width), BF),
        ((rows, hidden // 2 + width), BF),
        ((rows, width), BF),
        ((rows, width), F32),
        ((1, hidden), F32),
        ((8, width), F32),
    ]
    return pl.pallas_call(
        turn_kernel,
        in_specs=[whole(pltpu.SMEM)] + [whole()] * 6 + [whole(pl.ANY)] * 3,
        out_specs=[whole()] * len(shapes),
        out_shape=[jax.ShapeDtypeStruct(*shape) for shape in shapes],
        scratch_shapes=[
            pltpu.VMEM((width, width), BF),
            pltpu.VMEM((width, hidden), BF),
            pltpu.VMEM((hidden, width), BF),
            pltpu.VMEM((rows, width), F32),
            pltpu.VMEM((rows, width), F32),
            pltpu.VMEM((rows, hidden), F32),
            pltpu.VMEM((rows, width), F32),
            pltpu.VMEM((rows, width), BF),
            pltpu.VMEM((rows, hidden), BF),
            pltpu.VMEM((rows, width), BF),
            pltpu.SemaphoreType.DMA((9,)),
        ],
        compiler_params=pltpu.CompilerParams(vmem_limit_bytes=58 * VMEM_MIB),
        cost_estimate=pl.CostEstimate(
            flops=4 * rows * width * (width + 2 * hidden),
            bytes_accessed=2 * width * (width + 2 * hidden),
            transcendentals=2 * rows * hidden,
        ),
        name="turn",
    )(x_at, att, normed, res, cotangent, vectors, up_bias, out_weight, up_weight, down_weight)


def back_one_kernel(r):
    mover = Mover(r.moves)
    early = [
        mover.start(*pair)
        for pair in (
            (r.vectors, r.vectors_sc), (r.head_rows, r.head_rows_sc), (r.dqkv, r.dqkv_sc),
            (r.pre, r.pre_sc), (r.res, r.res_sc), (r.grad, r.grad_sc),
        )
    ]
    copies = weight_copies(column_pieces(r.qkv_w.at[1], 3), column_pieces(r.w_qkv, 3), r.sems)
    later = [
        mover.start(*pair)
        for pair in (
            (r.feed, r.feed_sc), (r.middle, r.middle_sc), (r.mixed, r.mixed_sc),
            (r.slope, r.slope_sc),
        )
    ]
    copies = copies + weight_copies(
        interleaved(column_pieces(r.up_w.at[0], 4), row_pieces(r.down_w.at[0], 4)),
        interleaved(column_pieces(r.w_up, 4), row_pieces(r.w_down, 4)),
        r.more_sems,
    )
    for copy in early:
        copy.wait()
    part = project_backward(
        1, r.res_sc[...], r.dqkv_sc, r.pre_sc, r.vectors_sc, r.head_rows_sc, r.w_qkv, copies[:3],
        r.pg_sc, r.rows_out, r.head_out,
    )
    split_columns([r.pg_sc], r.smem_at[0], r.pg_keep_sc, r.pg_send_sc)
    mover.flush(r.pg_send_sc, r.pg_send)
    mover.flush(r.pg_keep_sc, r.pg_keep)
    for copy in later:
        copy.wait()
    r.middle_grad_sc[...] = feed_backward(
        0, r.grad_sc[...] + part, r.feed_sc[...], r.middle_sc[...], r.mixed_sc[...], r.slope_sc,
        r.vectors_sc, r.w_up, r.w_down, copies[3:], r.fg_sc, r.hg_sc, r.mixed_grad_sc, r.bias_out,
        r.rows_out, 8,
    )
    mover.flush(r.middle_grad_sc, r.middle_grad)
    mover.flush(r.mixed_grad_sc, r.mixed_grad)
    split_columns([r.hg_sc, r.fg_sc], r.smem_at[1], r.right_keep_sc, r.right_send_sc)
    mover.flush(r.right_send_sc, r.right_send)
    mover.flush(r.right_keep_sc, r.right_keep)
    mover.finish()


def back_one(
    places, dqkv, pre, res, grad, feed, middle, mixed, slope, vectors, head_rows, qkv_weight,
    up_weight, down_weight,
):
    rows, width = res.shape
    hidden = up_weight.shape[2]
    loaded = dict(
        vectors=vectors, head_rows=head_rows, dqkv=dqkv, pre=pre, res=res,
        grad=grad, feed=feed, middle=middle, mixed=mixed, slope=slope,
    )
    stored = dict(
        pg_keep=((rows, 3 * width // 2), BF),
        pg_send=((rows, 3 * width // 2), BF),
        right_keep=((rows, (hidden + width) // 2), BF),
        right_send=((rows, (hidden + width) // 2), BF),
        mixed_grad=((rows, width), BF),
        middle_grad=((rows, width), F32),
    )
    return named_call(
        back_one_kernel,
        dict(smem_at=places, **loaded, qkv_w=qkv_weight, up_w=up_weight, down_w=down_weight),
        dict(
            **{key: (*value, True) for key, value in stored.items()},
            bias_out=((1, hidden), F32, False),
            rows_out=((16, width), F32, False),
            head_out=((8, WIDE), F32, False),
        ),
        dict(
            **{key + "_sc": pltpu.VMEM(value.shape, value.dtype) for key, value in loaded.items()},
            **{key + "_sc": pltpu.VMEM(*value) for key, value in stored.items()},
            w_qkv=low(width, 3 * width),
            w_up=low(width, hidden),
            w_down=low(hidden, width),
            pg_sc=low(rows, 3 * width),
            fg_sc=low(rows, width),
            hg_sc=low(rows, hidden),
            sems=pltpu.SemaphoreType.DMA((3,)),
            more_sems=pltpu.SemaphoreType.DMA((8,)),
            moves=pltpu.SemaphoreType.DMA((16,)),
        ),
        60,
        pl.CostEstimate(
            flops=2 * rows * width * (3 * width + 2 * hidden),
            bytes_accessed=2 * width * (3 * width + 2 * hidden),
            transcendentals=0,
        ),
        "back_one",
    )


def frame_backward(att_grad, usable, qkv_ref, dqkv_ref):
    width = att_grad.shape[1]
    first, _ = lane_masks(F32)
    for pair in range(width // LANES):
        q, k, v = [
            qkv_ref[:, part * width + pair * LANES : part * width + (pair + 1) * LANES]
            for part in range(3)
        ]
        out = att_grad[:, pair * LANES : (pair + 1) * LANES]
        pieces = []
        for mask in lane_masks(BF):
            shares = frame_shares(q * mask, k, usable)
            share_grad = product_right(out * mask, v)
            delta = jnp.sum(shares * share_grad, axis=-1, keepdims=True)
            score_grad = (shares * (share_grad - delta)).astype(BF)
            pieces.append(
                (
                    product(score_grad, k) * SCALE,
                    product_left(score_grad, q) * SCALE,
                    product_left(shares.astype(BF), out),
                )
            )
        for part in range(3):
            dqkv_ref[:, part * width + pair * LANES : part * width + (pair + 1) * LANES] = jnp.where(
                first > 0, pieces[0][part], pieces[1][part]
            )


def back_two_kernel(r):
    width = r.tok.shape[1]
    mover = Mover(r.moves)
    early = [
        mover.start(*pair)
        for pair in (
            (r.mixed_grad, r.mixed_grad_sc), (r.usable, r.usable_sc), (r.qkv, r.qkv_sc)
        )
    ]
    copies = weight_copies(
        [r.out_w.at[0]] + column_pieces(r.qkv_w.at[0], 3), [r.w_out] + column_pieces(r.w_qkv, 3),
        r.sems,
    )
    later = [
        mover.start(*pair)
        for pair in (
            (r.vectors, r.vectors_sc), (r.head_rows, r.head_rows_sc), (r.pre, r.pre_sc),
            (r.tok, r.tok_sc), (r.grad, r.grad_sc), (r.rows10, r.rows10_sc), (r.rows1, r.rows1_sc),
            (r.bias0, r.bias0_sc), (r.bias1, r.bias1_sc), (r.heads1, r.heads1_sc),
        )
    ]
    for copy in early:
        copy.wait()
    copies[0].wait()
    att_grad = product_right(r.mixed_grad_sc[...], r.w_out[...]).astype(BF)
    frame_backward(att_grad, r.usable_sc[...], r.qkv_sc, r.dqkv_sc)
    for copy in later:
        copy.wait()
    part = project_backward(
        0, r.tok_sc[...].astype(F32), r.dqkv_sc, r.pre_sc, r.vectors_sc, r.head_rows_sc, r.w_qkv,
        copies[1:], r.pg_sc, r.rows_sc, r.heads_sc,
    )
    split_columns([r.pg_sc, r.mixed_grad_sc], r.smem_at[0], r.pg_keep_sc, r.pg_send_sc)
    mover.flush(r.pg_send_sc, r.pg_send)
    mover.flush(r.pg_keep_sc, r.pg_keep)
    r.input_grad_sc[...] = (r.grad_sc[...] + part).astype(BF)
    mover.flush(r.input_grad_sc, r.input_grad)
    small = r.small_sc
    small[0:5] = r.rows_sc[0:5]
    small[5:11] = r.rows10_sc[8:14]
    small[11:16] = r.rows10_sc[0:5]
    small[16:22] = r.rows1_sc[0:6]
    at = 22
    for bias in (r.bias0_sc, r.bias1_sc):
        for j in range(bias.shape[1] // width):
            small[at : at + 1] = bias[:, j * width : (j + 1) * width]
            at += 1
    place = lax.broadcasted_iota(jnp.int32, (1, width), 1) // HD
    row = jnp.zeros((1, width), F32)
    for index, heads in enumerate((r.heads_sc, r.heads1_sc)):
        total = heads[...]
        total = total + pltpu.roll(total, WIDE // 2, 1)
        total = total + pltpu.roll(total, HD, 1)
        for j in range(3):
            many = jnp.concatenate([total[j : j + 1]] * (width // WIDE), axis=1)
            row = jnp.where(place == 3 * index + j, many, row)
    small[at : at + 1] = row
    small[at + 1 :] = jnp.zeros((small.shape[0] - at - 1, width), F32)
    mover.flush(r.small_sc, r.small)
    mover.finish()


def back_two(
    places, mixed_grad, grad, qkv, pre, tokens, usable, vectors, head_rows, rows10, rows1, bias0,
    bias1, heads1, out_weight, qkv_weight,
):
    rows, width = tokens.shape
    loaded = dict(
        mixed_grad=mixed_grad, usable=usable, qkv=qkv, vectors=vectors,
        head_rows=head_rows, pre=pre, tok=tokens, grad=grad, rows10=rows10,
        rows1=rows1, bias0=bias0, bias1=bias1, heads1=heads1,
    )
    small_rows = 2 * vectors.shape[1] + 2 * bias0.shape[1] // width + 2
    stored = dict(
        pg_keep=((rows, 2 * width), BF),
        pg_send=((rows, 2 * width), BF),
        input_grad=((rows, width), BF),
        small=((small_rows, width), F32),
    )
    return named_call(
        back_two_kernel,
        dict(smem_at=places, **loaded, out_w=out_weight, qkv_w=qkv_weight),
        {key: (*value, True) for key, value in stored.items()},
        dict(
            **{key + "_sc": pltpu.VMEM(value.shape, value.dtype) for key, value in loaded.items()},
            **{key + "_sc": pltpu.VMEM(*value) for key, value in stored.items()},
            w_out=low(width, width),
            w_qkv=low(width, 3 * width),
            dqkv_sc=full(rows, 3 * width),
            pg_sc=low(rows, 3 * width),
            rows_sc=full(8, width),
            heads_sc=full(8, WIDE),
            sems=pltpu.SemaphoreType.DMA((4,)),
            moves=pltpu.SemaphoreType.DMA((17,)),
        ),
        60,
        pl.CostEstimate(
            flops=2 * rows * width * 4 * width,
            bytes_accessed=2 * width * 4 * width,
            transcendentals=HEADS * rows * rows,
        ),
        "back_two",
    )


def weight_grad_kernel(outer, tall, starts, at_ref, *refs):
    count = len(tall)
    lefts, rights = refs[: 4 * count], refs[4 * count : 8 * count]
    keep, send = refs[8 * count : 8 * count + 2]
    left_sc = refs[8 * count + 2 : 9 * count + 2]
    right_sc = refs[9 * count + 2 : 10 * count + 2]
    sems = refs[10 * count + 2]
    c_at, y_at = at_ref[0], at_ref[1]
    rows = lefts[0].shape[0]
    group = keep.shape[0] // outer
    copies = []
    for w in range(count):
        cols, left_cols = right_sc[w].shape[1], left_sc[w].shape[1]
        left_start, right_start = starts[w]
        for s in range(4):
            at = pl.ds(pl.multiple_of(right_start + c_at * cols, LANES), cols)
            copies.append(
                pltpu.make_async_copy(
                    rights[4 * w + s].at[:, at],
                    right_sc[w].at[s * rows : (s + 1) * rows],
                    sems.at[len(copies)],
                )
            )
            copies.append(
                pltpu.make_async_copy(
                    lefts[4 * w + s].at[:, left_start : left_start + left_cols],
                    left_sc[w].at[s * rows : (s + 1) * rows],
                    sems.at[len(copies)],
                )
            )
    for copy in copies:
        copy.start()
    start = 0
    for w in range(count):
        for copy in copies[8 * w : 8 * w + 8]:
            copy.wait()
        cols = right_sc[w].shape[1]
        right = right_sc[w][...]
        for block in range(left_sc[w].shape[1] // 512):
            result = product_left(left_sc[w][:, block * 512 : (block + 1) * 512], right).astype(BF)
            targets = {0: [], 1: []}
            if tall[w]:
                size, part = 4 * group, group // 2
                for piece in range(512 // part):
                    row = block * 512 + piece * part
                    o, y = row // (2 * size), (row // size) % 2
                    core, t = (row % size) // (size // 2), (row % (size // 2)) // part
                    targets[y].append(
                        (piece * part, part, o * group + core * part, start + t * cols)
                    )
            else:
                for piece in range(512 // group):
                    row = block * 512 + piece * group
                    o, y = row // (2 * group), (row // group) % 2
                    targets[y].append((piece * group, group, o * group, start))
            for y in range(2):
                if not targets[y]:
                    continue

                def store(ref, y=y):
                    for source, size, row, col in targets[y]:
                        ref[row : row + size, col : col + cols] = result[source : source + size]

                @pl.when(y_at == y)
                def _():
                    store(keep)

                @pl.when(y_at != y)
                def _():
                    store(send)

        start += cols * (4 if tall[w] else 1)


def weight_grads(name, outer, width, places, products):
    rows = products[0][0][0].shape[0]
    group = width // (2 * outer)
    lefts, left_starts, left_cols, rights, right_starts, halves, tall = zip(*products)
    columns = [half // 2 for half in halves]
    total = sum(c * (4 if t else 1) for c, t in zip(columns, tall))
    shape = jax.ShapeDtypeStruct((outer * group, total), BF)
    count = len(products)
    return pl.pallas_call(
        functools.partial(
            weight_grad_kernel, outer, tall, tuple(zip(left_starts, right_starts))
        ),
        in_specs=[whole(pltpu.SMEM)] + [whole(pl.ANY)] * (8 * count),
        out_specs=[whole()] * 2,
        out_shape=[shape] * 2,
        scratch_shapes=[pltpu.VMEM((4 * rows, c), BF) for c in left_cols]
        + [pltpu.VMEM((4 * rows, c), BF) for c in columns]
        + [pltpu.SemaphoreType.DMA((8 * count,))],
        compiler_params=pltpu.CompilerParams(vmem_limit_bytes=48 * VMEM_MIB),
        cost_estimate=pl.CostEstimate(
            flops=16 * rows * outer * group * total,
            bytes_accessed=8 * outer * group * total,
            transcendentals=0,
        ),
        name=name,
    )(places, *[a for l in lefts for a in l], *[a for r in rights for a in r])


def assemble_kernel(at_ref, *refs):
    more = len(refs) - 13
    sources, outs = refs[: 4 + more // 5], refs[4 + more // 5 : 8 + more // 5]
    rest = refs[8 + more // 5 :]
    smalls, pieces, sems = rest[: 3 * more // 5], rest[3 * more // 5 : -1], rest[-1]
    copies = [
        pltpu.make_async_copy(source, piece, sems.at[index])
        for index, (source, piece) in enumerate(zip(sources, pieces))
    ]
    for copy in copies:
        copy.start()
    for copy in copies:
        copy.wait()
    qkv_out, out_out, up_out, down_out = outs
    c_at, x_at = at_ref[0], at_ref[2]
    if smalls:
        share_small(at_ref[6], pieces[4], *smalls)
    half_at = (at_ref[5], x_at)
    part = qkv_out.shape[1]
    for layer in range(2):
        for source in range(4):
            feed, att = pieces[2 * layer].at[source], pieces[2 * layer + 1].at[source]
            c = c_at if source % 2 == 0 else 1 - c_at
            feed_place, att_place = [
                2 * (half if source < 2 else 1 - half) + c for half in (half_at[layer], x_at)
            ]

            def put(ref, values, place, row=0, layer=layer):
                cols = values.shape[1]
                at = pl.ds(pl.multiple_of(place * cols, LANES), cols)
                ref[layer, row : row + values.shape[0], at] = values.astype(F32)

            up_cols = up_out.shape[2] // 4
            down_cols = down_out.shape[2] // 4
            qkv_cols = qkv_out.shape[2] // 4
            put(up_out, feed[:, :up_cols], feed_place)
            for t in range(4):
                put(
                    down_out,
                    feed[:, up_cols + t * down_cols : up_cols + (t + 1) * down_cols],
                    feed_place,
                    t * part,
                )
            put(qkv_out, att[:, :qkv_cols], att_place)
            put(out_out, att[:, qkv_cols:], att_place)


def share_small(me, small, vector_out, bias_out, head_out):
    vector_rows = vector_out.shape[1]
    lanes = pl.ds(pl.multiple_of((me // 2) * LANES, LANES), LANES)
    pair = small[: 2 * vector_rows, lanes]
    pair = jnp.where(lax.rem(me, 2) == 0, pair, pltpu.roll(pair, HD, 1))
    columns = bias_out.shape[1]
    per_row = small.shape[1] // columns
    rows = PEERS // per_row
    for layer in range(2):
        vector_out[layer] = pair[layer * vector_rows : (layer + 1) * vector_rows, :HD]
        row = pl.ds(2 * vector_rows + layer * rows + me // per_row, 1)
        at = pl.ds(pl.multiple_of(lax.rem(me, per_row) * columns, LANES), columns)
        bias_out[layer : layer + 1] = small[row, at]
        last = 2 * vector_rows + 2 * rows
        head_out[layer : layer + 1] = small[
            last : last + 1, layer * 3 * HD : (layer + 1) * 3 * HD
        ]


def assemble(places, pieces, shapes):
    return pl.pallas_call(
        assemble_kernel,
        in_specs=[whole(pltpu.SMEM)] + [whole(pl.ANY)] * len(pieces),
        out_specs=[whole()] * len(shapes),
        out_shape=[jax.ShapeDtypeStruct(shape, F32) for shape in shapes],
        scratch_shapes=[pltpu.VMEM(piece.shape, piece.dtype) for piece in pieces]
        + [pltpu.SemaphoreType.DMA((len(pieces),))],
        compiler_params=pltpu.CompilerParams(vmem_limit_bytes=60 * VMEM_MIB),
        name="assemble",
    )(places, *pieces)


OUTER = 4
BLOCK = 128


def slot_order(z0, z1):
    return [2 * (1 - z1) + (1 - z0), 2 * z1 + (1 - z0), 2 * (1 - z1) + z0, 2 * z1 + z0]


def slot_group(slot, z0, z1):
    far = jnp.where(slot % 2 == 0, 1 - z1, z1)
    return 2 * far + jnp.where(slot < 2, 1 - z0, z0)


def slot_product(group, left, left_at, right, right_at, cols, tall, emit):
    rights = right[:, right_at : right_at + cols]
    if tall:
        for y in range(2):
            start = pl.multiple_of(left_at + group * 8 * BLOCK + y * 4 * BLOCK, BLOCK)
            result = product_left(left[:, pl.ds(start, 4 * BLOCK)], rights).astype(BF)
            half = BLOCK // 2
            for c in range(2):
                for t in range(4):
                    row = c * 2 * BLOCK + t * half
                    emit(y, c * half, t * cols, result[row : row + half])
    else:
        start = pl.multiple_of(left_at + group * 2 * BLOCK, BLOCK)
        result = product_left(left[:, pl.ds(start, 2 * BLOCK)], rights).astype(BF)
        for y in range(2):
            emit(y, 0, 0, result[y * BLOCK : (y + 1) * BLOCK])


class Sender:
    def __init__(self, send, recv, partners):
        self.send, self.recv, self.partners = send, recv, partners
        self.copies = []

    def start(self, source, target, partner):
        index = len(self.copies)
        copy = pltpu.make_async_remote_copy(
            src_ref=source,
            dst_ref=target,
            send_sem=self.send.at[index],
            recv_sem=self.recv.at[index],
            device_id=self.partners[partner],
            device_id_type=MESH,
        )
        copy.start()
        self.copies.append(copy)
        return copy

    def finish(self):
        for copy in self.copies:
            copy.wait_send()


def reduce_kernel(
    small_ref, f1_keep, f1_came, la1, la1_x, pg1, pg1_x, rt1, rt1_x, lf0, lf0_y, rt0,
    rt0_y, la0, la0_x, pm0, pm0_send,
    f0_out, a0_out, f1_out, a1_out, small_out,
    left_a1, right_a1, left_f0, right_f0, left_a0, right_a0, pm0_x,
    part_f1, part_a1, part_f0, part_a0, z0_f1, y_f1, y_a1, x_f0, y_a0,
    z0_a1, z0_f0, z0_a0, z1_f1, z1_a1, z1_f0, z1_a0,
    fin_f1, fin_a1, fin_f0, fin_a0, far_f1, far_a1, far_f0, far_a0, turned, last_f0, chosen,
    sums, sums_in, local, send, recv,
):
    me = lax.axis_index("blk")
    x_at = lax.axis_index("grp")
    c_at, y_at, z0, z1 = [lax.rem(me // (1 << bit), 2) for bit in range(4)]
    partners = {"x": {"grp": 1 - x_at}}
    for bit, name in enumerate(("c", "y", "z0", "z1")):
        partners[name] = {"blk": me ^ (1 << bit)}
    barrier = pltpu.get_barrier_semaphore()
    for partner in partners.values():
        pl.semaphore_signal(barrier, 1, device_id=partner, device_id_type=MESH)
    pl.semaphore_wait(barrier, len(partners))
    sender = Sender(send, recv, partners)
    rows = la1.shape[0]
    locals_ = []

    def load(source, target):
        copy = pltpu.make_async_copy(source, target, local.at[len(locals_)])
        copy.start()
        locals_.append(copy)
        return copy

    stores = []

    def store(source, target):
        stores.append(load(source, target))

    def ready(copies):
        for copy in copies:
            copy.wait_recv()

    def quarter(ref, start, cols, core):
        return ref.at[:, pl.ds(pl.multiple_of(start + core * cols, BLOCK), cols)]

    def own_right(ref, start, cols, target, to, index):
        here = slice(index * rows, (index + 1) * rows)
        there = slice((2 + index) * rows, (3 + index) * rows)
        return [
            load(quarter(ref, start, cols, c_at), target.at[here, to : to + cols]),
            sender.start(
                quarter(ref, start, cols, 1 - c_at), target.at[there, to : to + cols], "c"
            ),
        ]

    def own_left(ref, target, index):
        return [
            load(ref, target.at[index * rows : (index + 1) * rows]),
            sender.start(ref, target.at[(2 + index) * rows : (3 + index) * rows], "c"),
        ]

    qkv_cols, out_cols = right_a1.shape[1] * 3 // 4, right_a1.shape[1] // 4
    up_cols, down_cols = right_f0.shape[1] * 4 // 5, right_f0.shape[1] // 5
    width = left_a1.shape[1] // 2
    pm0_copy = sender.start(pm0_send, pm0_x, "x")
    f1_loads = [load(f1_keep, part_f1), load(f1_came, z0_f1)]
    a1_ready = (
        own_left(la1, left_a1, 0)
        + own_left(la1_x, left_a1, 1)
        + own_right(pg1, 0, qkv_cols, right_a1, 0, 0)
        + own_right(pg1_x, 0, qkv_cols, right_a1, 0, 1)
        + own_right(rt1, 0, out_cols, right_a1, qkv_cols, 0)
        + own_right(rt1_x, 0, out_cols, right_a1, qkv_cols, 1)
    )

    def ask_f0():
        return (
            own_left(lf0, left_f0, 0)
            + own_left(lf0_y, left_f0, 1)
            + own_right(rt0, 0, up_cols, right_f0, 0, 0)
            + own_right(rt0, 2 * up_cols, down_cols, right_f0, up_cols, 0)
            + own_right(rt0_y, 0, up_cols, right_f0, 0, 1)
            + own_right(rt0_y, 2 * up_cols, down_cols, right_f0, up_cols, 1)
        )

    def ask_a0():
        pm0_copy.wait_recv()
        return (
            own_left(la0, left_a0, 0)
            + own_left(la0_x, left_a0, 1)
            + own_right(pm0, 0, qkv_cols, right_a0, 0, 0)
            + own_right(pm0, 2 * qkv_cols, out_cols, right_a0, qkv_cols, 0)
            + own_right(pm0_x, 0, qkv_cols, right_a0, 0, 1)
            + own_right(pm0_x, 2 * qkv_cols, out_cols, right_a0, qkv_cols, 1)
        )

    small_load = load(small_ref, sums.at[0])

    class Finish:
        def finish(self):
            half = BLOCK // 2
            other = self.own(3).at[pl.ds(pl.multiple_of((1 - c_at) * half, half), half)]
            self.c_copy = sender.start(other, self.fin.at[1], "c")
            self.fin[0] = self.own(3)[pl.ds(pl.multiple_of(c_at * half, half), half)]
            self.far_copies = [sender.start(self.fin.at[0], self.far.at[0], "x")]

        def fourth(self):
            self.c_copy.wait_recv()
            self.far_copies.append(sender.start(self.fin.at[1], self.far.at[1], "x"))
            if not self.turns:
                store(self.fin, self.out.at[0:2])

        def fifth(self, core):
            self.far_copies[core].wait_recv()
            aligned = x_at == y_at
            chosen[core] = jnp.where(aligned, self.fin[core], self.far[core])
            store(chosen.at[core], self.out.at[core])
            turned[core] = jnp.where(aligned, self.far[core], self.fin[core])
            self.far_copies[core] = sender.start(turned.at[core], last_f0.at[core], "y")

        def last(self):
            for copy in self.far_copies:
                copy.wait_recv()
            store(last_f0 if self.turns else self.far, self.out.at[2:4])

    class Group(Finish):
        def __init__(self, part, over, over_z0, over_z1, fin, far, out, axis):
            self.part, self.over, self.over_z0, self.over_z1 = part, over, over_z0, over_z1
            self.fin, self.far, self.out, self.axis = fin, far, out, axis
            self.at = {"x": x_at, "y": y_at}[axis]
            self.turns = axis == "x"
            self.copies, self.z0_copies = [], []

        def own(self, slot):
            return self.part.at[slot, self.at]

        def total(self, slot):
            return self.own(slot)[...].astype(F32) + self.over[slot].astype(F32)

        def made(self, slot):
            self.copies.append(
                sender.start(self.part.at[slot, 1 - self.at], self.over.at[slot], self.axis)
            )

        def step(self, slot):
            self.copies[slot].wait_recv()
            (lambda: self.first(0), lambda: self.first(1), self.second, self.third)[slot]()

        def first(self, slot):
            self.own(slot)[...] = self.total(slot).astype(BF)
            self.z0_copies.append(sender.start(self.own(slot), self.over_z0.at[slot], "z0"))

        def second(self):
            value = self.total(2)
            self.z0_copies[0].wait_recv()
            self.own(2)[...] = (value + self.over_z0[0].astype(F32)).astype(BF)
            self.z1_copy = sender.start(self.own(2), self.over_z1, "z1")

        def third(self):
            value = self.total(3)
            self.z0_copies[1].wait_recv()
            value = value + self.over_z0[1].astype(F32)
            self.z1_copy.wait_recv()
            self.own(3)[...] = (value + self.over_z1[...].astype(F32)).astype(BF)
            self.finish()

    class Early(Finish):
        def __init__(self, part, came, over, over_z1, fin, far, out, keep=None):
            self.part, self.came, self.over, self.over_z1 = part, came, over, over_z1
            self.keep = part if keep is None else keep
            self.fin, self.far, self.out, self.turns = fin, far, out, False
            self.copies, self.z0_copies = [], []

        def own(self, slot):
            return self.keep.at[slot - 2, y_at]

        def total(self, slot, at):
            return self.keep[slot, at].astype(F32) + self.came[slot, at].astype(F32)

        def made(self, slot):
            if slot < 2:
                self.z0_copies.append(
                    sender.start(self.part.at[slot], self.came.at[slot], "z0")
                )

        def send(self, slot):
            if self.z0_copies:
                self.z0_copies[slot].wait_recv()
            self.keep[slot, 1 - y_at] = self.total(slot, 1 - y_at).astype(BF)
            self.copies.append(
                sender.start(self.keep.at[slot, 1 - y_at], self.over.at[slot], "y")
            )

        def step(self, slot):
            self.copies[slot].wait_recv()
            value = self.total(slot, y_at) + self.over[slot].astype(F32)
            if slot == 1:
                self.z1_copy.wait_recv()
                value = value + self.over_z1[...].astype(F32)
            self.keep[slot, y_at] = value.astype(BF)
            if slot == 0:
                self.z1_copy = sender.start(self.keep.at[0, y_at], self.over_z1, "z1")
            else:
                self.finish()

    f1 = Early(part_f1, z0_f1, y_f1, z1_f1, fin_f1, far_f1, f1_out)
    a1 = Early(
        part_a1, z0_a1, y_a1, z1_a1, fin_a1, far_a1, a1_out, part_a1.at[2:4]
    )
    f0 = Group(part_f0, x_f0, z0_f0, z1_f0, fin_f0, far_f0, f0_out, "x")
    a0 = Group(part_a0, y_a0, z0_a0, z1_a0, fin_a0, far_a0, a0_out, "y")

    def products(group, left, right, terms, slots=range(OUTER)):
        for slot in slots:
            at = slot_group(slot, z0, z1)
            base = 0
            for left_at, right_at, cols, tall in terms:

                def emit(y, row, col, values, slot=slot, base=base):
                    height, wide = values.shape
                    group.part[
                        slot, y, row : row + height, base + col : base + col + wide
                    ] = values

                slot_product(at, left, left_at, right, right_at, cols, tall, emit)
                base += cols * (4 if tall else 1)
            group.made(slot)

    att_terms = [(0, 0, qkv_cols, False), (width, qkv_cols, out_cols, False)]
    feed_terms = [(0, 0, up_cols, False), (width, up_cols, down_cols, True)]
    small_copies = []

    def small_step(name=None):
        index = len(small_copies)
        if index:
            small_copies[-1].wait_recv()
            sums[index] = sums[index - 1] + sums_in[index - 1]
        else:
            small_load.wait()
        if name is not None:
            small_copies.append(sender.start(sums.at[index], sums_in.at[index], name))
        else:
            store(sums.at[index], small_out)

    small_step("x")
    for copy in f1_loads:
        copy.wait()
    f1.send(0)
    f1.send(1)
    ready(a1_ready)
    f0_ready = ask_f0()
    products(a1, left_a1, right_a1, att_terms)
    f1.step(0)
    small_step("c")
    ready(f0_ready)
    a0_ready = ask_a0()
    a1.send(0)
    products(f0, left_f0, right_f0, feed_terms)
    small_step("y")
    ready(a0_ready)
    products(a0, left_a0, right_a0, att_terms)
    a1.send(1)
    f0.step(0)
    a1.step(0)
    f1.step(1)
    small_step("z0")
    f1.fourth()
    a0.step(0)
    a1.step(1)
    f0.step(1)
    small_step("z1")
    f0.step(2)
    a0.step(1)
    a1.fourth()
    a1.last()
    f1.last()
    a0.step(2)
    small_step()
    f0.step(3)
    f0.fourth()
    f0.fifth(0)
    a0.step(3)
    a0.fourth()
    f0.fifth(1)
    a0.last()
    f0.last()
    assert len(sender.copies) == send.shape[0]
    assert len(locals_) == local.shape[0]
    ready(stores)
    sender.finish()


def reduce_all(small, f1, a1, f0, a0):
    rows = f0[0].shape[0]
    feed, att = f1[0].shape[-1], f1[0].shape[-1] // 2
    left_feed, left_att = f0[0].shape[1], a0[0].shape[1]
    half = BLOCK // 2

    def low(*shape):
        return pltpu.VMEM(shape, BF)

    wides = (feed, att, feed, att)
    outs = [jax.ShapeDtypeStruct((4, half, wide), BF) for wide in wides]
    return pl.pallas_call(
        reduce_kernel,
        in_specs=[whole(pl.ANY)] * 17,
        out_specs=[whole(pl.ANY)] * 5,
        out_shape=outs + [jax.ShapeDtypeStruct(small.shape, F32)],
        scratch_shapes=[
            low(4 * rows, left_att),
            low(4 * rows, att),
            low(4 * rows, left_feed),
            low(4 * rows, feed * 5 // 8),
            low(4 * rows, left_att),
            low(4 * rows, att),
            low(*a0[3].shape),
            low(2, 2, BLOCK, feed),
            low(OUTER, 2, BLOCK, att),
            low(OUTER, 2, BLOCK, feed),
            low(OUTER, 2, BLOCK, att),
            low(2, 2, BLOCK, feed),
            low(2, BLOCK, feed),
            low(2, BLOCK, att),
            low(OUTER, BLOCK, feed),
            low(OUTER, BLOCK, att),
            low(2, 2, BLOCK, att),
            low(2, BLOCK, feed),
            low(2, BLOCK, att),
        ]
        + [low(BLOCK, wide) for wide in wides]
        + [low(2, half, wide) for wide in wides] * 2
        + [low(2, half, feed)] * 3
        + [
            pltpu.VMEM((6, *small.shape), F32),
            pltpu.VMEM((5, *small.shape), F32),
            pltpu.SemaphoreType.DMA((31,)),
            pltpu.SemaphoreType.DMA((60,)),
            pltpu.SemaphoreType.DMA((60,)),
        ],
        compiler_params=pltpu.CompilerParams(
            vmem_limit_bytes=60 * VMEM_MIB, collective_id=3, has_side_effects=True
        ),
        cost_estimate=pl.CostEstimate(
            flops=8 * rows * (left_feed + 2 * left_att) * feed,
            bytes_accessed=2**25,
            transcendentals=0,
        ),
        name="reduce_all",
    )(small, *f1, *a1, *f0, *a0)


PEERS = HEADS
FOLD = FRAME // 2
EXTRA = 16
GROUPS = 4
BACK_GROUPS = 8
MESH = pl.DeviceIdType.MESH


def fold_pair(values):
    lane = lax.broadcasted_iota(jnp.int32, (FOLD, LANES), 1)
    top, bottom = values[:FOLD], values[FOLD:]
    one = jnp.where(lane < HD, top, pltpu.roll(bottom, HD, 1))
    two = jnp.where(lane < HD, pltpu.roll(top, HD, 1), bottom)
    return one, two


def unfold_pair(one, two):
    lane = lax.broadcasted_iota(jnp.int32, (FOLD, LANES), 1)
    top = jnp.where(lane < HD, one, pltpu.roll(two, HD, 1))
    bottom = jnp.where(lane < HD, pltpu.roll(one, HD, 1), two)
    return top, bottom


def unfold_head(folded):
    lane = lax.broadcasted_iota(jnp.int32, (FOLD, LANES), 1)
    folded = folded.astype(F32)
    top = jnp.where(lane < HD, folded, 0.0)
    bottom = jnp.where(lane < HD, pltpu.roll(folded, HD, 1), 0.0)
    return top.astype(BF), bottom.astype(BF)


def fold_head(values):
    lane = lax.broadcasted_iota(jnp.int32, (FOLD, LANES), 1)
    return jnp.where(lane < HD, values[:FOLD], pltpu.roll(values[FOLD:], HD, 1))


def exchange(me, k, source, target, sems):
    return pltpu.make_async_remote_copy(
        src_ref=source,
        dst_ref=target,
        send_sem=sems.at[0, k],
        recv_sem=sems.at[1, k],
        device_id={"blk": me ^ k},
        device_id_type=MESH,
    )


def call_peers(me, partner):
    barrier = pltpu.get_barrier_semaphore()
    for k in range(1, PEERS):
        pl.semaphore_signal(barrier, 1, device_id={"blk": me ^ k}, device_id_type=MESH)
    pl.semaphore_signal(barrier, 1, device_id=partner, device_id_type=MESH)
    return lambda: pl.semaphore_wait(barrier, PEERS)


def all_to_all(me, source, target, sems, own_sem):
    copies = [exchange(me, k, source.at[me ^ k], target.at[me], sems) for k in range(PEERS - 1, 0, -1)]
    for copy in copies:
        copy.start()
    own = pltpu.make_async_copy(source.at[me], target.at[me], own_sem)
    own.start()
    return copies + [own]


def head_forward(me, qkv_ref, tag_ref, att_ref, r):
    width = att_ref.shape[1]
    for head in range(HEADS):
        r.pack[head, 3 * FOLD :] = tag_ref[...]
    for pair in range(width // LANES):
        for part in range(3):
            block = qkv_ref[:, part * width + pair * LANES : part * width + (pair + 1) * LANES]
            one, two = fold_pair(block.astype(F32))
            r.pack[2 * pair, part * FOLD : (part + 1) * FOLD] = one.astype(BF)
            r.pack[2 * pair + 1, part * FOLD : (part + 1) * FOLD] = two.astype(BF)
    for copy in all_to_all(me, r.pack, r.got, r.out_sems, r.own_sems.at[0]):
        copy.wait()
    for s in range(PEERS):
        for part, target in enumerate((r.queries_sc, r.keys_sc, r.values_sc)):
            top, bottom = unfold_head(r.got[s, part * FOLD : (part + 1) * FOLD])
            target[s * FRAME : s * FRAME + FOLD] = top
            target[s * FRAME + FOLD : (s + 1) * FRAME] = bottom
        r.marks_sc[s : s + 1] = r.got[s, 3 * FOLD : 3 * FOLD + 1].astype(F32)
        r.marks_sc[PEERS + s : PEERS + s + 1] = r.got[s, 3 * FOLD + 1 : 3 * FOLD + 2].astype(F32)
    keys, values = r.keys_sc[...], r.values_sc[...]
    tags = jnp.concatenate([r.marks_sc[s : s + 1] for s in range(PEERS)], axis=1)
    sends = []
    own = None
    per = PEERS // GROUPS
    for j in range(GROUPS - 1, -1, -1):
        block = (me // per) ^ j
        at = pl.ds(pl.multiple_of(block * per * FRAME, per * FRAME), per * FRAME)
        scores = product_right(r.queries_sc[at], keys) * SCALE
        scenes = jnp.concatenate(
            [
                jnp.broadcast_to(
                    r.marks_sc[pl.ds(PEERS + block * per + i, 1)][:, :1], (FRAME, 1)
                )
                for i in range(per)
            ],
            axis=0,
        )
        scores = jnp.where(tags == scenes, scores, NEG)
        top = jnp.max(scores, axis=-1, keepdims=True)
        shares = jnp.exp(scores - top)
        total = jnp.sum(shares, axis=-1, keepdims=True)
        result = product(shares.astype(BF), values) / total
        r.outs_sc[at] = result
        r.lse_sc[:, at] = as_row(top + jnp.log(total))
        for i in range(per):
            r.answers[block * per + i] = fold_head(result[i * FRAME : (i + 1) * FRAME]).astype(BF)
        for k in range(j * per, (j + 1) * per):
            if k:
                copy = exchange(me, k, r.answers.at[me ^ k], r.back.at[me], r.back_sems)
            else:
                copy = pltpu.make_async_copy(r.answers.at[me], r.back.at[me], r.own_sems.at[1])
            copy.start()
            sends.append(copy)
    for copy in sends:
        copy.wait()
    for pair in range(width // LANES):
        top, bottom = unfold_pair(r.back[2 * pair].astype(F32), r.back[2 * pair + 1].astype(F32))
        att_ref[:FOLD, pair * LANES : (pair + 1) * LANES] = top.astype(BF)
        att_ref[FOLD:, pair * LANES : (pair + 1) * LANES] = bottom.astype(BF)


def head_backward(me, grad_ref, dqkv_ref, r, meanwhile):
    width = grad_ref.shape[1]
    for pair in range(width // LANES):
        one, two = fold_pair(grad_ref[:, pair * LANES : (pair + 1) * LANES].astype(F32))
        r.pack[2 * pair] = one.astype(BF)
        r.pack[2 * pair + 1] = two.astype(BF)
    for copy in all_to_all(me, r.pack, r.got, r.out_sems, r.own_sems.at[0]):
        copy.wait()
    deltas = []
    for s in range(PEERS):
        at = slice(s * FRAME, (s + 1) * FRAME)
        top, bottom = unfold_head(r.got[s])
        r.grads_sc[s * FRAME : s * FRAME + FOLD] = top
        r.grads_sc[s * FRAME + FOLD : (s + 1) * FRAME] = bottom
        weighted = r.grads_sc[at].astype(F32) * r.outs_sc[at]
        deltas.append(jnp.sum(jnp.transpose(weighted), axis=0, keepdims=True))
    delta = jnp.concatenate(deltas, axis=1)
    queries, outs, lse = r.queries_sc[...], r.grads_sc[...], r.lse_sc[...]
    scenes = jnp.concatenate(
        [r.marks_sc[PEERS + s : PEERS + s + 1] for s in range(PEERS)], axis=1
    )
    query_grad = None
    sends = []
    per = PEERS // BACK_GROUPS
    for j in range(BACK_GROUPS - 1, -1, -1):
        block = (me // per) ^ j
        at = pl.ds(pl.multiple_of(block * per * FRAME, per * FRAME), per * FRAME)
        keys, values = r.keys_sc[at], r.values_sc[at]
        tags = jnp.concatenate(
            [as_column(r.marks_sc[pl.ds(block * per + i, 1)]) for i in range(per)], axis=0
        )
        scores = product_right(keys, queries) * SCALE
        shares = jnp.where(tags == scenes, jnp.exp(scores - lse), 0.0)
        share_grad = product_right(values, outs)
        score_grad = (shares * (share_grad - delta)).astype(BF)
        value_grad = product(shares.astype(BF), outs)
        key_grad = product(score_grad, queries) * SCALE
        turned = jnp.transpose(keys.astype(F32)).astype(BF)[:HD]
        piece = product(turned, score_grad)
        query_grad = piece if query_grad is None else query_grad + piece
        for i in range(per):
            part = slice(i * FRAME, (i + 1) * FRAME)
            r.pairs[block * per + i, :FOLD] = fold_head(key_grad[part]).astype(BF)
            r.pairs[block * per + i, FOLD:] = fold_head(value_grad[part]).astype(BF)
        for k in range(j * per, (j + 1) * per):
            if k:
                copy = exchange(me, k, r.pairs.at[me ^ k], r.pairs_in.at[me], r.pair_sems)
            else:
                copy = pltpu.make_async_copy(r.pairs.at[me], r.pairs_in.at[me], r.own_sems.at[1])
            copy.start()
            sends.append(copy)
    padded = jnp.concatenate([query_grad * SCALE, jnp.zeros_like(query_grad)], axis=0)
    for s in range(PEERS):
        block = jnp.transpose(padded[:, s * FRAME : (s + 1) * FRAME])
        r.asked[s] = fold_head(block).astype(BF)
    sends += all_to_all(me, r.asked, r.asked_in, r.back_sems, r.own_sems.at[2])
    meanwhile()
    for copy in sends:
        copy.wait()
    for pair in range(width // LANES):
        for part in range(3):
            if part == 0:
                one, two = r.asked_in[2 * pair], r.asked_in[2 * pair + 1]
            else:
                rows = slice((part - 1) * FOLD, part * FOLD)
                one, two = r.pairs_in[2 * pair, rows], r.pairs_in[2 * pair + 1, rows]
            top, bottom = unfold_pair(one.astype(F32), two.astype(F32))
            cols = slice(part * width + pair * LANES, part * width + (pair + 1) * LANES)
            dqkv_ref[:FOLD, cols] = top.astype(BF)
            dqkv_ref[FOLD:, cols] = bottom.astype(BF)


def tile_heads(source, target):
    lane = lax.broadcasted_iota(jnp.int32, (1, WIDE), 1)
    for layer in range(2):
        every = jnp.concatenate(
            [source[layer : layer + 1], jnp.zeros((1, WIDE - 3 * HD), F32)], axis=1
        )
        for index in range(3):
            one = jnp.where((lane >= index * HD) & (lane < (index + 1) * HD), every, 0.0)
            two = one + pltpu.roll(one, HD, 1)
            target[layer, index : index + 1] = two + pltpu.roll(two, 2 * HD, 1)
        target[layer, 3:] = jnp.zeros((5, WIDE), F32)


def begin_kernel(r):
    me, x_at = lax.axis_index("blk"), lax.axis_index("grp")
    partner = {"grp": 1 - x_at}
    peers_here = call_peers(me, partner)
    width, units = r.tok.shape[1], r.up_w.shape[2]
    mover = Mover(r.moves)
    loads = [
        mover.start(*pair)
        for pair in (
            (r.tok, r.tok_sc), (r.vectors, r.vectors_sc), (r.head_norm, r.head_norm_sc),
            (r.up_bias, r.up_bias_sc), (r.valid, r.valid_sc),
        )
    ]
    copies = weight_copies(
        column_pieces(r.qkv_w.at[0], 3)
        + [r.out_w.at[0]]
        + interleaved(column_pieces(r.up_w.at[0], 4), row_pieces(r.down_w.at[0], 4)),
        column_pieces(r.w_qkv, 3)
        + [r.w_out]
        + interleaved(column_pieces(r.w_up, 4), row_pieces(r.w_down, 4)),
        r.sems,
    )
    for copy in loads:
        copy.wait()
    tile_heads(r.head_norm_sc, r.head_rows_sc)
    position = lax.broadcasted_iota(jnp.int32, (1, FRAME), 1)
    valid = jnp.where((r.valid_sc[...] == 1) | (position < SPECIAL), 1.0, 0.0)
    r.usable_sc[...] = valid
    scene = r.smem_scene[0].astype(F32)
    row = lax.broadcasted_iota(jnp.int32, (EXTRA, FRAME), 0)
    tags = jnp.where(valid > 0, scene, -1.0)
    r.marks_in_sc[...] = jnp.where(row == 0, tags, jnp.where(row == 1, scene, 0.0)).astype(BF)
    mover.flush(r.head_rows_sc, r.head_rows)
    mover.flush(r.usable_sc, r.usable)
    residual = r.tok_sc[...].astype(F32)
    normed0, att0 = r.leftatt0_sc.at[:, :width], r.leftatt0_sc.at[:, width:]
    project(
        0, residual, r.vectors_sc, r.head_rows_sc, r.w_qkv, copies[:3], normed0, r.pre0_sc,
        r.qkv0_sc,
    )
    mover.flush(r.pre0_sc, r.pre0)
    mover.flush(r.qkv0_sc, r.qkv0)
    frame_attend(r.usable_sc[...], r.qkv0_sc, att0)
    next_copies = weight_copies(
        column_pieces(r.qkv_w.at[1], 3), column_pieces(r.w_qkv, 3), r.next_sems
    )
    mover.flush(r.leftatt0_sc, r.leftatt0)
    peers_here()
    across = pltpu.make_async_remote_copy(
        src_ref=r.leftatt0_sc,
        dst_ref=r.leftatt0_x,
        send_sem=r.x_sems.at[0],
        recv_sem=r.x_sems.at[1],
        device_id=partner,
        device_id_type=MESH,
    )
    across.start()
    lifted0, active0 = r.left0_sc.at[:, :width], r.left0_sc.at[:, width:]
    result = feed_forward(
        0, att0[...], residual, r.vectors_sc, r.up_bias_sc, r.w_out, r.w_up, r.w_down, copies[3:],
        r.mixed0_sc, r.middle0_sc, lifted0, r.slope0_sc, active0, r.feed0_sc,
    )
    r.res1_sc[...] = result
    for pair in (
        (r.left0_sc, r.left0), (r.mixed0_sc, r.mixed0), (r.middle0_sc, r.middle0),
        (r.slope0_sc, r.slope0), (r.feed0_sc, r.feed0), (r.res1_sc, r.res1),
    ):
        mover.flush(*pair)
    normed1, att1 = r.leftatt1_sc.at[:, :width], r.leftatt1_sc.at[:, width:]
    project(
        1, result, r.vectors_sc, r.head_rows_sc, r.w_qkv, next_copies, normed1, r.pre1_sc, r.qkv1_sc
    )
    mover.flush(r.pre1_sc, r.pre1)
    head_forward(me, r.qkv1_sc, r.marks_in_sc, att1, r)
    for pair in (
        (r.queries_sc, r.queries), (r.keys_sc, r.keys), (r.values_sc, r.values), (r.outs_sc, r.outs),
        (r.lse_sc, r.lse), (r.marks_sc, r.marks), (r.leftatt1_sc, r.leftatt1),
    ):
        mover.flush(*pair)
    across.wait()
    mover.finish()


def begin(
    tokens, valid, scene, vectors, up_bias, head_norm, qkv_weight, out_weight, up_weight, down_weight
):
    rows, width = tokens.shape
    hidden = up_weight.shape[2]
    every = PEERS * FRAME
    loaded = dict(
        tok=tokens, vectors=vectors, head_norm=head_norm, up_bias=up_bias,
        valid=valid,
    )
    stored = dict(
        left0=((rows, hidden + width), BF),
        leftatt0=((rows, 2 * width), BF),
        pre0=((rows, 2 * width), F32),
        qkv0=((rows, 3 * width), BF),
        mixed0=((rows, width), F32),
        middle0=((rows, width), F32),
        slope0=((rows, hidden), F32),
        feed0=((rows, width), F32),
        res1=((rows, width), F32),
        leftatt1=((rows, 2 * width), BF),
        pre1=((rows, 2 * width), F32),
        queries=((every, LANES), BF),
        keys=((every, LANES), BF),
        values=((every, LANES), BF),
        outs=((every, LANES), F32),
        lse=((1, every), F32),
        marks=((2 * PEERS, LANES), F32),
        head_rows=((2, 8, WIDE), F32),
        usable=((1, rows), F32),
    )
    return named_call(
        begin_kernel,
        dict(
            smem_scene=scene, **loaded, qkv_w=qkv_weight, out_w=out_weight,
            up_w=up_weight, down_w=down_weight,
        ),
        dict(
            **{key: (*value, True) for key, value in stored.items()},
            leftatt0_x=((rows, 2 * width), BF, True),
        ),
        dict(
            **{key + "_sc": pltpu.VMEM(value.shape, value.dtype) for key, value in loaded.items()},
            **{key + "_sc": pltpu.VMEM(*value) for key, value in stored.items()},
            marks_in_sc=low(EXTRA, FRAME),
            qkv1_sc=low(rows, 3 * width),
            w_qkv=low(width, 3 * width),
            w_out=low(width, width),
            w_up=low(width, hidden),
            w_down=low(hidden, width),
            pack=low(PEERS, 3 * FOLD + EXTRA, LANES),
            got=low(PEERS, 3 * FOLD + EXTRA, LANES),
            answers=low(PEERS, FOLD, LANES),
            back=low(PEERS, FOLD, LANES),
            sems=pltpu.SemaphoreType.DMA((12,)),
            next_sems=pltpu.SemaphoreType.DMA((3,)),
            moves=pltpu.SemaphoreType.DMA((5 + len(stored),)),
            own_sems=pltpu.SemaphoreType.DMA((2,)),
            out_sems=pltpu.SemaphoreType.DMA((2, PEERS)),
            back_sems=pltpu.SemaphoreType.DMA((2, PEERS)),
            x_sems=pltpu.SemaphoreType.DMA((2,)),
        ),
        60,
        pl.CostEstimate(
            flops=2 * rows * width * (7 * width + 2 * hidden) + 4 * every * every * LANES,
            bytes_accessed=2 * width * (7 * width + 2 * hidden),
            transcendentals=2 * rows * hidden + every * every,
        ),
        "begin",
        collective_id=1,
    )


def middle_kernel(r):
    me, x_at = lax.axis_index("blk"), lax.axis_index("grp")
    c_at, _, z0, z1 = [lax.rem(me // (1 << bit), 2) for bit in range(4)]
    partners = {"x": {"grp": 1 - x_at}, "c": {"blk": me ^ 1}}
    peers_here = call_peers(me, partners["x"])
    sender = Sender(r.ring_sems.at[0], r.ring_sems.at[1], partners)
    rows, width = r.res.shape
    units = r.up_w.shape[2]
    mover = Mover(r.moves)
    loads = [
        mover.start(*pair)
        for pair in (
            (r.vectors, r.vectors_sc), (r.leftatt1, r.leftatt1_sc), (r.res, r.res_sc),
            (r.up_bias, r.up_bias_sc), (r.cot, r.cot_sc),
        )
    ]
    copies = weight_copies(
        [r.out_w.at[1]]
        + interleaved(column_pieces(r.up_w.at[1], 4), row_pieces(r.down_w.at[1], 4)),
        [r.w_out] + interleaved(column_pieces(r.w_up, 4), row_pieces(r.w_down, 4)),
        r.sems,
    )
    late_loads = [
        mover.start(*pair)
        for pair in (
            (r.queries, r.queries_sc), (r.keys, r.keys_sc), (r.values, r.values_sc),
            (r.outs, r.outs_sc), (r.lse, r.lse_sc), (r.marks, r.marks_sc),
        )
    ]
    for copy in loads:
        copy.wait()
    own = slice(0, rows)
    lifted, active = r.left_sc.at[own, :width], r.left_sc.at[own, width:]
    result = feed_forward(
        1, r.leftatt1_sc[:, width:], r.res_sc[...], r.vectors_sc, r.up_bias_sc, r.w_out, r.w_up,
        r.w_down, copies, r.mixed_sc, r.middle_sc, lifted, r.slope_sc, active, r.feed_sc,
    )
    peers_here()
    left_x = sender.start(r.left_sc.at[own], r.left_sc.at[rows : 2 * rows], "x")
    left_c = sender.start(r.left_sc.at[own], r.left_sc.at[2 * rows : 3 * rows], "c")
    r.output_sc[...] = result.astype(BF)
    mover.flush(r.output_sc, r.output)
    grad = feed_backward(
        1, r.cot_sc[...].astype(F32), r.feed_sc[...], r.middle_sc[...], r.mixed_sc[...],
        r.slope_sc, r.vectors_sc, r.w_up, r.w_down, None, r.fg_sc, r.hg_sc, r.mg_sc, r.bias_out,
        r.rows_out, 0,
    )
    half, part = units // 2, width // 2

    def columns(ref, start, count):
        return ref.at[:, pl.ds(pl.multiple_of(start, LANES), count)]

    rights = [
        sender.start(columns(r.hg_sc, (1 - x_at) * half, half), r.far_sc.at[:, :half], "x"),
        sender.start(columns(r.fg_sc, (1 - x_at) * part, part), r.far_sc.at[:, half:], "x"),
    ]
    mixed_x = sender.start(columns(r.mg_sc, (1 - x_at) * part, part), r.mixed1_x, "x")
    q_up, q_down = half // 2, part // 2
    ready = [left_c]

    def place(up, down, up_at, down_at, index):
        here = slice(index * rows, (index + 1) * rows)
        there = slice((2 + index) * rows, (3 + index) * rows)
        for ref, start, count, to in ((up, up_at, q_up, 0), (down, down_at, q_down, q_up)):
            ready.append(
                mover.start(
                    columns(ref, start + c_at * count, count), r.right_sc.at[here, to : to + count]
                )
            )
            ready.append(
                sender.start(
                    columns(ref, start + (1 - c_at) * count, count),
                    r.right_sc.at[there, to : to + count],
                    "c",
                )
            )

    place(r.hg_sc, r.fg_sc, x_at * half, x_at * part, 0)
    mover.flush(columns(r.mg_sc, x_at * part, part), r.mixed1)
    r.middle_grad_sc[...] = grad
    mover.flush(r.middle_grad_sc, r.middle_grad)
    r.att_grad_sc[...] = product_right(r.mg_sc[...], r.w_out[...]).astype(BF)
    for copy in late_loads:
        copy.wait()

    def meanwhile():
        left_x.wait_recv()
        ready.append(
            sender.start(
                r.left_sc.at[rows : 2 * rows], r.left_sc.at[3 * rows : 4 * rows], "c"
            )
        )

    head_backward(me, r.att_grad_sc, r.dqkv_sc, r, meanwhile)
    mover.flush(r.dqkv_sc, r.dqkv)
    for copy in rights:
        copy.wait_recv()
    place(r.far_sc, r.far_sc, 0, half, 1)
    for copy in ready:
        copy.wait_recv()
    for slot in range(OUTER):
        target = (r.away_sc if slot < 2 else r.stay_sc).at[slot % 2]

        def emit(base, y, row, col, values, target=target):
            height, wide = values.shape
            target[y, row : row + height, base + col : base + col + wide] = values

        group = slot_group(slot, z0, z1)
        slot_product(
            group, r.left_sc, 0, r.right_sc, 0, q_up, False, functools.partial(emit, 0)
        )
        slot_product(
            group, r.left_sc, width, r.right_sc, q_up, q_down, True, functools.partial(emit, q_up)
        )
        if slot == 1:
            mover.flush(r.away_sc, r.away)
    mover.flush(r.stay_sc, r.stay)
    mixed_x.wait_recv()
    assert len(sender.copies) == r.ring_sems.shape[1]
    sender.finish()
    mover.finish()


def middle(first, cotangent, vectors, up_bias, out_weight, up_weight, down_weight):
    rows, width = cotangent.shape
    hidden = up_weight.shape[2]
    every = PEERS * FRAME
    loaded = dict(
        vectors=vectors, leftatt1=first.leftatt1, res=first.res1, up_bias=up_bias,
        cot=cotangent, queries=first.queries, keys=first.keys, values=first.values,
        outs=first.outs, lse=first.lse, marks=first.marks,
    )
    columns = hidden // 2
    stored = dict(
        output=((rows, width), BF),
        middle_grad=((rows, width), F32),
        dqkv=((rows, 3 * width), BF),
        stay=((2, 2, BLOCK, columns), BF),
        away=((2, 2, BLOCK, columns), BF),
    )
    return named_call(
        middle_kernel,
        dict(
            **loaded, out_w=out_weight, up_w=up_weight, down_w=down_weight,
        ),
        dict(
            **{key: (*value, True) for key, value in stored.items()},
            mixed1=((rows, width // 2), BF, True),
            mixed1_x=((rows, width // 2), BF, True),
            bias_out=((1, hidden), F32, False),
            rows_out=((8, width), F32, False),
        ),
        dict(
            **{key + "_sc": pltpu.VMEM(value.shape, value.dtype) for key, value in loaded.items()},
            **{key + "_sc": pltpu.VMEM(*value) for key, value in stored.items()},
            w_out=low(width, width),
            w_up=low(width, hidden),
            w_down=low(hidden, width),
            left_sc=low(4 * rows, hidden + width),
            right_sc=low(4 * rows, (hidden + width) // 4),
            far_sc=low(rows, (hidden + width) // 2),
            mixed_sc=full(rows, width),
            middle_sc=full(rows, width),
            slope_sc=full(rows, hidden),
            feed_sc=full(rows, width),
            fg_sc=low(rows, width),
            hg_sc=low(rows, hidden),
            mg_sc=low(rows, width),
            att_grad_sc=low(rows, width),
            grads_sc=low(every, LANES),
            pack=low(PEERS, FOLD, LANES),
            got=low(PEERS, FOLD, LANES),
            pairs=low(PEERS, 2 * FOLD, LANES),
            pairs_in=low(PEERS, 2 * FOLD, LANES),
            asked=low(PEERS, FOLD, LANES),
            asked_in=low(PEERS, FOLD, LANES),
            sems=pltpu.SemaphoreType.DMA((9,)),
            moves=pltpu.SemaphoreType.DMA((21,)),
            own_sems=pltpu.SemaphoreType.DMA((3,)),
            out_sems=pltpu.SemaphoreType.DMA((2, PEERS)),
            back_sems=pltpu.SemaphoreType.DMA((2, PEERS)),
            pair_sems=pltpu.SemaphoreType.DMA((2, PEERS)),
            ring_sems=pltpu.SemaphoreType.DMA((2, 10)),
        ),
        60,
        pl.CostEstimate(
            flops=4 * rows * width * (width + 2 * hidden) + 10 * every * every * LANES,
            bytes_accessed=2 * width * (width + 2 * hidden),
            transcendentals=2 * rows * hidden + every * every,
        ),
        "middle",
        collective_id=2,
    )


def per_device(
    tokens,
    qkv_weight,
    out_weight,
    up_weight,
    down_weight,
    vectors,
    up_bias,
    head_norm,
    token_valid,
    frame_scene,
    cotangent,
):
    count = lax.axis_size("blk")
    outer = count // 4
    me = lax.axis_index("blk")
    x_at = lax.axis_index("grp")
    c_at = lax.rem(me, 2)
    y_at = lax.rem(me // 2, 2)
    c_pairs = [(i, i ^ 1) for i in range(count)]
    y_pairs = [(i, i ^ 2) for i in range(count)]
    z_groups = [[4 * o + k for o in range(outer)] for k in range(4)]
    over_y = count == HEADS
    halves_at = jnp.stack([x_at, y_at if over_y else x_at]).astype(jnp.int32)
    places = jnp.stack(
        [c_at, y_at, x_at, lax.rem(me // 4, 2), lax.rem(me // 8, 2), halves_at[1], me]
    ).astype(jnp.int32)


    def swap_x(value):
        return lax.ppermute(value, "grp", [(0, 1), (1, 0)])

    def swap_c(value):
        return lax.ppermute(value, "blk", c_pairs)

    def swap_y(value):
        return lax.ppermute(value, "blk", y_pairs)

    def part(value, index, parts, axis):
        size = value.shape[axis] // parts
        return lax.dynamic_slice_in_dim(value, index * size, size, axis)

    def tied(value, *others):
        return lax.optimization_barrier((value, *others))

    def ready_sum(keep, arrived):
        return (keep.astype(F32) + arrived.astype(F32)).astype(BF)

    def scattered(own):
        return lax.psum_scatter(
            own, "blk", scatter_dimension=0, tiled=True, axis_index_groups=z_groups
        )

    def finished(total):
        pair = jnp.stack([part(total, c_at, 2, 0), swap_c(part(total, 1 - c_at, 2, 0))])
        return jnp.concatenate([pair, swap_x(pair)], axis=0)

    def total_of(value):
        value = value + swap_x(value)
        step = 1
        while step < count:
            pairs = [(i, i ^ step) for i in range(count)]
            value = value + lax.ppermute(value, "blk", pairs)
            step *= 2
        return value

    row_count, width = tokens.shape[1:]
    hidden = up_weight.shape[2]
    if count == HEADS:
        first = begin(
            tokens[0], token_valid[0], frame_scene[0], vectors, up_bias, head_norm, qkv_weight,
            out_weight, up_weight, down_weight,
        )
        head_rows, usable_row = first.head_rows, first.usable
        second = middle(
            first, cotangent[0], vectors, up_bias, out_weight, up_weight, down_weight
        )
        away = lax.ppermute(second.away, "blk", [(i, i ^ 4) for i in range(count)])
        left0_far, leftatt1_x = swap_y(first.left0), swap_x(first.leftatt1)
        pre0, qkv0, mixed0, middle0, slope0, feed0, res1, pre1 = (
            first.pre0, first.qkv0, first.mixed0, first.middle0, first.slope0, first.feed0,
            first.res1, first.pre1,
        )
        output, middle_grad1, dqkv1, bias1, rows1 = (
            second.output, second.middle_grad, second.dqkv, second.bias_out, second.rows_out
        )
    else:
        position = lax.broadcasted_iota(jnp.int32, (row_count,), 0)
        usable = (token_valid[0, 0] == 1) | (position < SPECIAL)
        usable_row = usable.astype(F32).reshape(1, row_count)
        scene = frame_scene[0, 0].astype(F32)
        tag_rows = jnp.where(usable, scene, -1.0)
        head_rows = jnp.tile(head_norm.reshape(2, 3, HD), (1, 1, WIDE // HD))
        head_rows = jnp.concatenate([head_rows, jnp.zeros((2, 5, WIDE), F32)], axis=1)
        left0, leftatt0, pre0, qkv0, mixed0, middle0, slope0, feed0, res1, normed1, pre1, qkv1 = (
            front(
                tokens[0], usable_row, vectors, up_bias, head_rows, qkv_weight, out_weight,
                up_weight, down_weight,
            )
        )
        att1, kept = gathered_forward(qkv1, tag_rows, scene)
        left1, leftatt1, output, right1, right1_send, att_grad1, middle_grad1, bias1, rows1 = turn(
            halves_at, att1, normed1, res1, cotangent[0], vectors, up_bias, out_weight, up_weight,
            down_weight,
        )
        dqkv1 = gathered_backward(att_grad1, kept, tag_rows, scene)
    swap_far = swap_y if over_y else swap_x
    third = back_one(
        halves_at, dqkv1, pre1, res1, middle_grad1, feed0, middle0, mixed0, slope0, vectors,
        head_rows, qkv_weight, up_weight, down_weight,
    )
    pg1_x, right0_far = swap_x(third.pg_send), swap_far(third.right_send)
    fourth = back_two(
        halves_at, third.mixed_grad, third.middle_grad, qkv0, pre0, tokens[0], usable_row, vectors,
        head_rows, third.rows_out, rows1, third.bias_out, bias1, third.head_out, out_weight,
        qkv_weight,
    )
    small = fourth.small

    def feed_grads(name, lefts, rights):
        return weight_grads(
            name,
            outer,
            width,
            places,
            [
                (lefts, 0, width, rights, 0, hidden // 2, False),
                (lefts, width, hidden, rights, hidden // 2, width // 2, True),
            ],
        )

    def att_grads(name, lefts, projected, rights, at):
        return weight_grads(
            name,
            outer,
            width,
            places,
            [
                (lefts, 0, width, projected, 0, 3 * width // 2, False),
                (lefts, width, width, rights, at, width // 2, False),
            ],
        )

    def four(own, far):
        return (own, far, swap_c(own), swap_c(far))

    def reduce_apart():
        pg0_all = four(fourth.pg_keep, swap_x(fourth.pg_send))
        right1_all = four(right1, swap_x(right1_send))
        results = []
        for keep, send in (
            feed_grads(
                "feed_grads0", four(left0, swap_x(left0)), four(third.right_keep, right0_far)
            ),
            att_grads(
                "att_grads0", four(leftatt0, swap_x(leftatt0)), pg0_all, pg0_all, 3 * width // 2
            ),
            feed_grads("feed_grads1", four(left1, swap_x(left1)), right1_all),
            att_grads(
                "att_grads1", four(leftatt1, swap_x(leftatt1)), four(third.pg_keep, pg1_x),
                right1_all, (hidden + width) // 2,
            ),
        ):
            results.append(finished(scattered(ready_sum(keep, swap_y(send)))))
        return results

    if count == HEADS:
        *pieces, small = reduce_all(
            small,
            (second.stay, away),
            (
                first.leftatt1, leftatt1_x, third.pg_keep, pg1_x, second.mixed1, second.mixed1_x,
            ),
            (first.left0, left0_far, third.right_keep, right0_far),
            (first.leftatt0, first.leftatt0_x, fourth.pg_keep, fourth.pg_send),
        )
    else:
        small = total_of(small)
        pieces = reduce_apart()
    weight_shapes = [
        (2, width // count, 3 * width),
        (2, width // count, width),
        (2, width // count, up_weight.shape[2]),
        (2, up_weight.shape[2] // count, width),
    ]
    vector_count = vectors.shape[1]
    if count == HEADS:
        small_shapes = [(2, vector_count, HD), (2, hidden // count), (2, 3 * HD)]
        qkv_grad, out_grad, up_grad, down_grad, vector_grad, bias_grad, head_grad = assemble(
            places, [*pieces, small], weight_shapes + small_shapes
        )
    else:
        qkv_grad, out_grad, up_grad, down_grad = assemble(places, pieces, weight_shapes)
        bias_rows = 2 * hidden // width
        vector_grad = part(small[: 2 * vector_count].reshape(2, -1, width), me, count, 2)
        bias_grad = small[2 * vector_count : 2 * vector_count + bias_rows].reshape(2, hidden)
        bias_grad = part(bias_grad, me, count, 1)
        head_grad = small[2 * vector_count + bias_rows, : 6 * HD].reshape(2, 3 * HD)
    return (
        output[None],
        fourth.input_grad[None],
        qkv_grad,
        out_grad,
        up_grad,
        down_grad,
        vector_grad,
        bias_grad,
        head_grad,
    )


def gathered_forward(qkv, tag_rows, scene):
    rows, width = qkv.shape[0], qkv.shape[1] // 3
    marks = jnp.zeros((KEEP, 2 * width), BF)
    marks = marks.at[0, :rows].set(tag_rows.astype(BF))
    marks = marks.at[1, :rows].set(jnp.full((rows,), scene).astype(BF))
    pairs = lax.all_gather(
        jnp.concatenate([qkv[:, width:], marks], axis=0), "blk", axis=0, tiled=False
    )
    tags = pairs[:, FRAME, :FRAME].astype(F32).reshape(1, -1)
    scenes = pairs[:, FRAME + 1, :FRAME].astype(F32).reshape(1, -1)
    queries = qkv[:, :width]
    attended, lse = global_attend(queries, pairs, tags, jnp.full((8, LANES), scene))
    every_query = lax.all_gather(
        with_rows(queries, lse.reshape(HEADS, rows)), "blk", axis=0, tiled=False
    )
    return attended.astype(BF), (qkv, pairs, tags, scenes, attended, lse, every_query)


def gathered_backward(attended_grad, kept, tag_rows, scene):
    qkv, pairs, tags, scenes, attended, lse, every_query = kept
    rows, width = attended_grad.shape
    delta = jnp.sum(
        (attended_grad.astype(F32) * attended).reshape(rows, HEADS, HD), axis=-1
    ).T
    every_grad = lax.all_gather(with_rows(attended_grad, delta), "blk", axis=0, tiled=False)
    query_grad = global_query_grad(
        qkv[:, :width],
        pairs,
        tags,
        jnp.full((8, LANES), scene),
        attended_grad,
        lse,
        delta.reshape(PAIRS, 2, rows),
    )
    key_grad, value_grad = global_key_grad(
        qkv[:, width : 2 * width],
        qkv[:, 2 * width :],
        tag_rows.reshape(1, rows),
        scenes,
        every_query,
        every_grad,
        rows_of(every_query, width),
        rows_of(every_grad, width),
    )
    return jnp.concatenate([query_grad, key_grad, value_grad], axis=1).astype(BF)


def solution(mesh):
    return jax.shard_map(
        per_device,
        mesh=mesh,
        in_specs=(
            P("grp", "blk", None),
            P(),
            P(),
            P(),
            P(),
            P(),
            P(),
            P(),
            P("grp", "blk", None),
            P("grp", "blk"),
            P("grp", "blk", None),
        ),
        out_specs=(
            P("grp", "blk", None),
            P("grp", "blk", None),
            P(None, "blk", None),
            P(None, "blk", None),
            P(None, "blk", None),
            P(None, "blk", None),
            P(None, None, "blk"),
            P(None, "blk"),
            P(),
        ),
        check_vma=False,
    )
```

```python
import functools
import types
from itertools import chain

import jax
import jax.numpy as jnp
from jax import lax
from jax.experimental import pallas as pl
from jax.experimental.pallas import tpu as pltpu
from jax.sharding import PartitionSpec as P

HEADS = 16
HD = 64
SPECIAL = 5
PAIRS = HEADS // 2
LANES = 2 * HD
FRAME = 128
KEEP = 16
EPS = 1e-06
NEG = -1e30
SCALE = HD**-0.5
BF = jnp.bfloat16
F32 = jnp.float32


def product(left_side, right_side):
    return jnp.dot(left_side, right_side, preferred_element_type=F32)


def product_left(left_side, right_side):
    return lax.dot_general(
        left_side, right_side, (((0,), (0,)), ((), ())), preferred_element_type=F32
    )


def product_right(left_side, right_side):
    return lax.dot_general(
        left_side, right_side, (((1,), (1,)), ((), ())), preferred_element_type=F32
    )


def lane_masks(dtype):
    lane = lax.broadcasted_iota(jnp.int32, (1, LANES), 1)
    first = (lane < HD).astype(dtype)
    return (first, 1 - first)


def as_column(row):
    size = row.shape[1]
    return jnp.transpose(jnp.broadcast_to(row, (LANES, size)))[:, :1]


def as_row(column):
    size = column.shape[0]
    return jnp.transpose(jnp.broadcast_to(column, (size, LANES)))[:1, :]


def flat(ref):
    block = ref[...]
    return block.reshape(block.shape[0] * block.shape[1], block.shape[2])


def attend_kernel(blocks, q_ref, k_ref, v_ref, tag_ref, scene_ref, o_ref, lse_ref, m_sc, l_sc, a_sc):
    step = pl.program_id(1)
    keys, values = flat(k_ref), flat(v_ref)
    allowed = tag_ref[...] == scene_ref[:1, :1]
    queries = q_ref[...]
    pieces = []
    for index, mask in enumerate(lane_masks(BF)):
        scores = product_right(queries * mask, keys) * SCALE
        scores = jnp.where(allowed, scores, NEG)
        top = jnp.max(scores, axis=-1, keepdims=True)

        if blocks > 1:

            @pl.when(step == 0)
            def _():
                m_sc[index] = jnp.full_like(m_sc[index], NEG)
                l_sc[index] = jnp.zeros_like(l_sc[index])
                a_sc[index] = jnp.zeros_like(a_sc[index])

            old = m_sc[index][:, :1]
            top = jnp.maximum(top, old)
            keep = jnp.exp(old - top)
        shares = jnp.where(allowed, jnp.exp(scores - top), 0.0)
        total = jnp.sum(shares, axis=-1, keepdims=True)
        weighted = product(shares.astype(BF), values)
        if blocks > 1:
            total = total + keep * l_sc[index][:, :1]
            weighted = weighted + keep * a_sc[index]
            m_sc[index] = jnp.broadcast_to(top, m_sc[index].shape)
            l_sc[index] = jnp.broadcast_to(total, l_sc[index].shape)
            a_sc[index] = weighted
        pieces.append(weighted / total)
        lse_ref[0, index : index + 1, :] = as_row(top + jnp.log(total))
    first, second = lane_masks(F32)
    o_ref[...] = jnp.where(first > 0, pieces[0], pieces[1])


def key_block(count):
    for size in (16, 8, 4, 2, 1):
        if count % size == 0:
            return size


def global_attend(queries, pairs, tags, scene):
    frames = pairs.shape[0]
    group = key_block(frames)
    blocks = frames // group
    return pl.pallas_call(
        functools.partial(attend_kernel, blocks),
        grid=(PAIRS, blocks),
        in_specs=[
            pl.BlockSpec((FRAME, LANES), lambda p, k: (0, p)),
            pl.BlockSpec((group, FRAME, LANES), lambda p, k: (k, 0, p)),
            pl.BlockSpec((group, FRAME, LANES), lambda p, k: (k, 0, PAIRS + p)),
            pl.BlockSpec((1, group * FRAME), lambda p, k: (0, k)),
            pl.BlockSpec((8, LANES), lambda p, k: (0, 0)),
        ],
        out_specs=[
            pl.BlockSpec((FRAME, LANES), lambda p, k: (0, p)),
            pl.BlockSpec((1, 2, FRAME), lambda p, k: (p, 0, 0)),
        ],
        out_shape=[
            jax.ShapeDtypeStruct((FRAME, PAIRS * LANES), F32),
            jax.ShapeDtypeStruct((PAIRS, 2, FRAME), F32),
        ],
        scratch_shapes=[pltpu.VMEM((2, FRAME, LANES), F32)] * 3,
        compiler_params=pltpu.CompilerParams(vmem_limit_bytes=48 * 2**20),
        cost_estimate=pl.CostEstimate(
            flops=4 * FRAME * frames * FRAME * LANES * HEADS,
            bytes_accessed=frames * FRAME * 4096,
            transcendentals=FRAME * frames * FRAME * HEADS,
        ),
        name="global_attend",
    )(queries, pairs, pairs, tags, scene)


def query_grad_kernel(
    q_ref, k_ref, v_ref, tag_ref, scene_ref, do_ref, lse_ref, delta_ref, dq_ref
):
    step = pl.program_id(1)
    keys, values = flat(k_ref), flat(v_ref)
    allowed = tag_ref[...] == scene_ref[:1, :1]
    queries, outs = q_ref[...], do_ref[...]
    pieces = []
    for index, mask in enumerate(lane_masks(BF)):
        scores = product_right(queries * mask, keys) * SCALE
        top = as_column(lse_ref[0, index : index + 1, :])
        delta = as_column(delta_ref[0, index : index + 1, :])
        shares = jnp.where(allowed, jnp.exp(scores - top), 0.0)
        share_grad = product_right(outs * mask, values)
        score_grad = (shares * (share_grad - delta)).astype(BF)
        pieces.append(product(score_grad, keys) * SCALE)
    first, second = lane_masks(F32)
    piece = jnp.where(first > 0, pieces[0], pieces[1])

    @pl.when(step == 0)
    def _():
        dq_ref[...] = piece

    @pl.when(step > 0)
    def _():
        dq_ref[...] += piece


def global_query_grad(queries, pairs, tags, scene, outs, lse, delta):
    frames = pairs.shape[0]
    group = key_block(frames)
    blocks = frames // group
    return pl.pallas_call(
        query_grad_kernel,
        grid=(PAIRS, blocks),
        in_specs=[
            pl.BlockSpec((FRAME, LANES), lambda p, k: (0, p)),
            pl.BlockSpec((group, FRAME, LANES), lambda p, k: (k, 0, p)),
            pl.BlockSpec((group, FRAME, LANES), lambda p, k: (k, 0, PAIRS + p)),
            pl.BlockSpec((1, group * FRAME), lambda p, k: (0, k)),
            pl.BlockSpec((8, LANES), lambda p, k: (0, 0)),
            pl.BlockSpec((FRAME, LANES), lambda p, k: (0, p)),
            pl.BlockSpec((1, 2, FRAME), lambda p, k: (p, 0, 0)),
            pl.BlockSpec((1, 2, FRAME), lambda p, k: (p, 0, 0)),
        ],
        out_specs=pl.BlockSpec((FRAME, LANES), lambda p, k: (0, p)),
        out_shape=jax.ShapeDtypeStruct((FRAME, PAIRS * LANES), F32),
        compiler_params=pltpu.CompilerParams(vmem_limit_bytes=48 * 2**20),
        cost_estimate=pl.CostEstimate(
            flops=6 * FRAME * frames * FRAME * LANES * HEADS,
            bytes_accessed=frames * FRAME * 4096,
            transcendentals=FRAME * frames * FRAME * HEADS,
        ),
        name="global_query_grad",
    )(queries, pairs, pairs, tags, scene, outs, lse, delta)


def key_grad_kernel(
    k_ref, v_ref, tag_ref, scene_ref, q_ref, do_ref, lse_ref, delta_ref, dk_ref, dv_ref
):
    step = pl.program_id(1)
    keys, values = k_ref[...], v_ref[...]
    queries, outs = flat(q_ref), flat(do_ref)
    allowed = as_column(tag_ref[...]) == scene_ref[...]
    key_pieces, value_pieces = [], []
    for index, mask in enumerate(lane_masks(BF)):
        scores = product_right(keys * mask, queries) * SCALE
        top = lse_ref[0, index : index + 1, :]
        delta = delta_ref[0, index : index + 1, :]
        shares = jnp.where(allowed, jnp.exp(scores - top), 0.0)
        share_grad = product_right(values * mask, outs)
        score_grad = (shares * (share_grad - delta)).astype(BF)
        key_pieces.append(product(score_grad, queries) * SCALE)
        value_pieces.append(product(shares.astype(BF), outs))
    first, second = lane_masks(F32)
    key_piece = jnp.where(first > 0, key_pieces[0], key_pieces[1])
    value_piece = jnp.where(first > 0, value_pieces[0], value_pieces[1])

    @pl.when(step == 0)
    def _():
        dk_ref[...] = key_piece
        dv_ref[...] = value_piece

    @pl.when(step > 0)
    def _():
        dk_ref[...] += key_piece
        dv_ref[...] += value_piece


def global_key_grad(keys, values, tags, scenes, queries, outs, lse, delta):
    frames = queries.shape[0]
    group = key_block(frames)
    blocks = frames // group
    return pl.pallas_call(
        key_grad_kernel,
        grid=(PAIRS, blocks),
        in_specs=[
            pl.BlockSpec((FRAME, LANES), lambda p, k: (0, p)),
            pl.BlockSpec((FRAME, LANES), lambda p, k: (0, p)),
            pl.BlockSpec((1, FRAME), lambda p, k: (0, 0)),
            pl.BlockSpec((1, group * FRAME), lambda p, k: (0, k)),
            pl.BlockSpec((group, FRAME, LANES), lambda p, k: (k, 0, p)),
            pl.BlockSpec((group, FRAME, LANES), lambda p, k: (k, 0, p)),
            pl.BlockSpec((1, 2, group * FRAME), lambda p, k: (p, 0, k)),
            pl.BlockSpec((1, 2, group * FRAME), lambda p, k: (p, 0, k)),
        ],
        out_specs=[pl.BlockSpec((FRAME, LANES), lambda p, k: (0, p))] * 2,
        out_shape=[jax.ShapeDtypeStruct((FRAME, PAIRS * LANES), F32)] * 2,
        compiler_params=pltpu.CompilerParams(vmem_limit_bytes=48 * 2**20),
        cost_estimate=pl.CostEstimate(
            flops=8 * FRAME * frames * FRAME * LANES * HEADS,
            bytes_accessed=frames * FRAME * 4096,
            transcendentals=FRAME * frames * FRAME * HEADS,
        ),
        name="global_key_grad",
    )(keys, values, tags, scenes, queries, outs, lse, delta)


def split_three(values):
    high = values.astype(BF)
    rest = values - high.astype(F32)
    middle = rest.astype(BF)
    return jnp.stack([high, middle, (rest - middle.astype(F32)).astype(BF)])


def with_rows(body, statistic):
    width = body.shape[1]
    extra = split_three(statistic).reshape(-1, width)
    pad = jnp.zeros((KEEP - extra.shape[0], width), BF)
    return jnp.concatenate([body, extra, pad], axis=0)


def rows_of(gathered, width):
    frames = gathered.shape[0]
    used = 3 * HEADS * FRAME // width
    terms = gathered[:, FRAME : FRAME + used].reshape(frames, 3, HEADS, FRAME).astype(F32)
    total = terms[:, 0] + terms[:, 1] + terms[:, 2]
    return total.transpose(1, 0, 2).reshape(PAIRS, 2, frames * FRAME)


VMEM_MIB = 2**20
WIDE = 256
ROOT_HALF = 0.7071067811865476
ROOT_TWO_PI = 0.3989422804014327


def whole(space=pltpu.VMEM):
    return pl.BlockSpec(memory_space=space)


def terms_of(values):
    high = values.astype(BF)
    rest = values - high.astype(F32)
    middle = rest.astype(BF)
    return (high, middle, (rest - middle.astype(F32)).astype(BF))


def head_averager():
    row = lax.broadcasted_iota(jnp.int32, (WIDE, WIDE), 0) // HD
    col = lax.broadcasted_iota(jnp.int32, (WIDE, WIDE), 1) // HD
    return jnp.where(row == col, 1.0 / HD, 0.0).astype(BF)


def head_mean(values, averager):
    high, middle, least = terms_of(values)
    return product(high, averager) + product(middle, averager) + product(least, averager)


def standard(values):
    centered = values - jnp.mean(values, axis=-1, keepdims=True)
    scale = lax.rsqrt(jnp.mean(centered * centered, axis=-1, keepdims=True) + EPS)
    return centered * scale, scale


def standard_heads(values, averager):
    centered = values - head_mean(values, averager)
    scale = lax.rsqrt(head_mean(centered * centered, averager) + EPS)
    return centered * scale, scale


def norm_pull(values, gain, grad):
    unit, scale = standard(values)
    scaled = grad * gain
    spread = jnp.mean(scaled * unit, axis=-1, keepdims=True)
    result = scale * (scaled - jnp.mean(scaled, axis=-1, keepdims=True) - unit * spread)
    return (
        result,
        jnp.sum(grad * unit, axis=0, keepdims=True),
        jnp.sum(grad, axis=0, keepdims=True),
    )


def weight_copies(sources, targets, sems):
    copies = [
        pltpu.make_async_copy(source, target, sems.at[index])
        for index, (source, target) in enumerate(zip(sources, targets))
    ]
    for copy in copies:
        copy.start()
    return copies


def column_pieces(ref, parts):
    size = ref.shape[-1] // parts
    return [ref.at[:, i * size : (i + 1) * size] for i in range(parts)]


def row_pieces(ref, parts):
    size = ref.shape[0] // parts
    return [ref.at[i * size : (i + 1) * size] for i in range(parts)]


def project(layer, residual, vec_ref, head_ref, w_ref, copies, normed_ref, pre_ref, qkv_ref):
    width = residual.shape[1]
    unit, _ = standard(residual)
    normed = (unit * vec_ref[layer, 0:1] + vec_ref[layer, 1:2]).astype(BF)
    normed_ref[...] = normed
    averager = head_averager()
    for part in range(3):
        copies[part].wait()
        bias = vec_ref[layer, 2 + part : 3 + part]
        for j in range(width // WIDE):
            at = slice(part * width + j * WIDE, part * width + (j + 1) * WIDE)
            value = product(normed, w_ref[:, at]) + bias[:, j * WIDE : (j + 1) * WIDE]
            if part < 2:
                pre_ref[:, at] = value
                unit, _ = standard_heads(value, averager)
                value = unit * head_ref[layer, 2 * part : 2 * part + 1]
                if part == 0:
                    value = value + head_ref[layer, 1:2]
            qkv_ref[:, at] = value.astype(BF)


def frame_attend(usable, qkv_ref, att_ref):
    width = att_ref.shape[1]
    first, _ = lane_masks(F32)
    for pair in range(width // LANES):
        q, k, v = [
            qkv_ref[:, part * width + pair * LANES : part * width + (pair + 1) * LANES]
            for part in range(3)
        ]
        pieces = []
        for mask in lane_masks(BF):
            shares = frame_shares(q * mask, k, usable)
            pieces.append(product(shares.astype(BF), v))
        at = slice(pair * LANES, (pair + 1) * LANES)
        att_ref[:, at] = jnp.where(first > 0, pieces[0], pieces[1]).astype(att_ref.dtype)


def frame_shares(queries, keys, usable):
    scores = jnp.where(usable > 0, product_right(queries, keys) * SCALE, NEG)
    shares = jnp.exp(scores - jnp.max(scores, axis=-1, keepdims=True))
    return shares / jnp.sum(shares, axis=-1, keepdims=True)


def feed_forward(
    layer, att, residual, vec_ref, bias_ref, w_out, w_up, w_down, copies, mixed_ref, middle_ref,
    lifted_ref, slope_ref, active_ref, feed_ref, done=None,
):
    chunks = w_up.shape[1] // 512
    copies[0].wait()
    mixed = product(att, w_out[...]) + vec_ref[layer, 5:6]
    mixed_ref[...] = mixed
    middle = residual + vec_ref[layer, 6:7] * mixed
    middle_ref[...] = middle
    unit, _ = standard(middle)
    lifted = (unit * vec_ref[layer, 7:8] + vec_ref[layer, 8:9]).astype(BF)
    lifted_ref[...] = lifted
    feed = None
    for j in range(chunks):
        at = slice(j * 512, (j + 1) * 512)
        if j % 2 == 0:
            copies[1 + j].wait()
            copies[2 + j].wait()
        hidden = product(lifted, w_up[:, at]) + bias_ref[layer : layer + 1, at]
        bell = 0.5 * (1.0 + lax.erf(hidden * ROOT_HALF))
        slope_ref[:, at] = bell + hidden * jnp.exp(-0.5 * hidden * hidden) * ROOT_TWO_PI
        active = (hidden * bell).astype(BF)
        if done is None:
            active_ref[:, at] = active
        else:
            done(j, active)
        piece = product(active, w_down[at])
        feed = piece if feed is None else feed + piece
    feed = feed + vec_ref[layer, 9:10]
    feed_ref[...] = feed
    return middle + vec_ref[layer, 10:11] * feed


def split_columns(value_refs, x_at, keep_ref, send_ref):
    start = 0
    for value_ref in value_refs:
        half = value_ref.shape[1] // 2
        to = slice(start, start + half)
        keep_ref[:, to] = value_ref[:, pl.ds(pl.multiple_of(x_at * half, LANES), half)]
        send_ref[:, to] = value_ref[:, pl.ds(pl.multiple_of((1 - x_at) * half, LANES), half)]
        start += half


def feed_backward(
    layer, grad, feed, middle, mixed, slope_ref, vec_ref, w_up, w_down, copies, feed_grad_ref,
    hidden_grad_ref, mixed_grad_ref, bias_out, rows_ref, row0,
):
    chunks = w_up.shape[1] // 512
    feed_grad = (vec_ref[layer, 10:11] * grad).astype(BF)
    feed_grad_ref[...] = feed_grad
    rows_ref[row0 + 4 : row0 + 5] = jnp.sum(feed_grad.astype(F32), axis=0, keepdims=True)
    rows_ref[row0 + 5 : row0 + 6] = jnp.sum(grad * feed, axis=0, keepdims=True)
    lifted_grad = None
    for j in range(chunks):
        at = slice(j * 512, (j + 1) * 512)
        if copies is not None and j % 2 == 0:
            copies[j].wait()
            copies[j + 1].wait()
        hidden_grad = (slope_ref[:, at] * product_right(feed_grad, w_down[at])).astype(BF)
        hidden_grad_ref[:, at] = hidden_grad
        bias_out[:, at] = jnp.sum(hidden_grad.astype(F32), axis=0, keepdims=True)
        piece = product_right(hidden_grad, w_up[:, at])
        lifted_grad = piece if lifted_grad is None else lifted_grad + piece
    part, gain_grad, shift_grad = norm_pull(middle, vec_ref[layer, 7:8], lifted_grad)
    middle_grad = grad + part
    mixed_grad = (vec_ref[layer, 6:7] * middle_grad).astype(BF)
    mixed_grad_ref[...] = mixed_grad
    rows_ref[row0 : row0 + 1] = jnp.sum(mixed_grad.astype(F32), axis=0, keepdims=True)
    rows_ref[row0 + 1 : row0 + 2] = jnp.sum(middle_grad * mixed, axis=0, keepdims=True)
    rows_ref[row0 + 2 : row0 + 3] = gain_grad
    rows_ref[row0 + 3 : row0 + 4] = shift_grad
    return middle_grad


def project_backward(*args):
    results = []
    for _ in project_steps(results, *args):
        pass
    return results[0]


def project_steps(
    results, layer, residual, dqkv_ref, pre_ref, vec_ref, head_ref, w_ref, copies, pg_ref, rows_ref,
    head_out,
):
    width = residual.shape[1]
    averager = head_averager()
    sums = [None, None, None]
    for part in range(3):
        for j in range(width // WIDE):
            at = slice(part * width + j * WIDE, part * width + (j + 1) * WIDE)
            value = dqkv_ref[:, at].astype(F32)
            if part < 2:
                unit, scale = standard_heads(pre_ref[:, at], averager)
                news = [(2 * part, jnp.sum(value * unit, axis=0, keepdims=True))]
                if part == 0:
                    news.append((1, jnp.sum(value, axis=0, keepdims=True)))
                for index, new in news:
                    sums[index] = new if sums[index] is None else sums[index] + new
                scaled = value * head_ref[layer, 2 * part : 2 * part + 1]
                value = scale * (
                    scaled
                    - head_mean(scaled, averager)
                    - unit * head_mean(scaled * unit, averager)
                )
            low = value.astype(BF)
            pg_ref[:, at] = low
            rows_ref[2 + part : 3 + part, j * WIDE : (j + 1) * WIDE] = jnp.sum(
                low.astype(F32), axis=0, keepdims=True
            )
            if (part * width // WIDE + j) % 3 == 2:
                yield
    head_out[...] = jnp.concatenate(sums + [jnp.zeros((5, WIDE), F32)], axis=0)
    normed_grad = None
    for part in range(3):
        copies[part].wait()
        at = slice(part * width, (part + 1) * width)
        piece = product_right(pg_ref[:, at], w_ref[:, at])
        normed_grad = piece if normed_grad is None else normed_grad + piece
        yield
    part, gain_grad, shift_grad = norm_pull(residual, vec_ref[layer, 0:1], normed_grad)
    rows_ref[0:1] = gain_grad
    rows_ref[1:2] = shift_grad
    results.append(part)


def named_call(kernel, inputs, outputs, scratch, vmem_mib, cost, name, collective_id=None):
    names = [*inputs, *outputs, *scratch]

    def body(*refs):
        kernel(types.SimpleNamespace(**dict(zip(names, refs))))

    more = {}
    if collective_id is not None:
        more = {"collective_id": collective_id, "has_side_effects": True}
    results = pl.pallas_call(
        body,
        in_specs=[
            whole(pltpu.SMEM) if key.startswith("smem") else whole(pl.ANY) for key in inputs
        ],
        out_specs=[whole(pl.ANY if value[2] else pltpu.VMEM) for value in outputs.values()],
        out_shape=[jax.ShapeDtypeStruct(value[0], value[1]) for value in outputs.values()],
        scratch_shapes=list(scratch.values()),
        compiler_params=pltpu.CompilerParams(vmem_limit_bytes=vmem_mib * VMEM_MIB, **more),
        cost_estimate=cost,
        name=name,
    )(*inputs.values())
    return types.SimpleNamespace(**dict(zip(outputs, results)))


def low(*shape):
    return pltpu.VMEM(shape, BF)


def full(*shape):
    return pltpu.VMEM(shape, F32)


class Mover:
    def __init__(self, sems):
        self.sems, self.count, self.open = sems, 0, []

    def start(self, source, target):
        copy = pltpu.make_async_copy(source, target, self.sems.at[self.count])
        copy.start()
        self.count += 1
        return copy

    def flush(self, source, target):
        self.open.append(self.start(source, target))

    def finish(self):
        assert self.count == self.sems.shape[0]
        for copy in self.open:
            copy.wait()


def interleaved(one, two):
    return [piece for pair in zip(one, two) for piece in pair]


def front_kernel(
    tok_ref, usable_ref, vec_ref, bias_ref, head_ref, qkv_w, out_w, up_w, down_w,
    left_pack, att_pack, pre0, qkv0, mixed0, middle0, slope0, feed0, res1, normed1, pre1, qkv1,
    w_qkv, w_out, w_up, w_down, w_next, sems,
):
    width, units = tok_ref.shape[1], up_w.shape[2]
    lifted0 = left_pack.at[:, :width]
    active0 = left_pack.at[:, width : width + units]
    normed0, att0 = att_pack.at[:, :width], att_pack.at[:, width:]
    copies = weight_copies(
        column_pieces(qkv_w.at[0], 3)
        + [out_w.at[0]]
        + interleaved(column_pieces(up_w.at[0], 4), row_pieces(down_w.at[0], 4))
        + column_pieces(qkv_w.at[1], 3),
        column_pieces(w_qkv, 3)
        + [w_out]
        + interleaved(column_pieces(w_up, 4), row_pieces(w_down, 4))
        + column_pieces(w_next, 3),
        sems,
    )
    residual = tok_ref[...].astype(F32)
    project(0, residual, vec_ref, head_ref, w_qkv, copies[:3], normed0, pre0, qkv0)
    frame_attend(usable_ref[...], qkv0, att0)
    result = feed_forward(
        0, att0[...], residual, vec_ref, bias_ref, w_out, w_up, w_down, copies[3:12], mixed0,
        middle0, lifted0, slope0, active0, feed0,
    )
    res1[...] = result
    project(1, result, vec_ref, head_ref, w_next, copies[12:], normed1, pre1, qkv1)


def front(tokens, usable, vectors, up_bias, head_rows, qkv_weight, out_weight, up_weight, down_weight):
    rows, width = tokens.shape
    hidden = up_weight.shape[2]
    shapes = [
        ((rows, hidden + width), BF),
        ((rows, 2 * width), BF),
        ((rows, 2 * width), F32),
        ((rows, 3 * width), BF),
        ((rows, width), F32),
        ((rows, width), F32),
        ((rows, hidden), F32),
        ((rows, width), F32),
        ((rows, width), F32),
        ((rows, width), BF),
        ((rows, 2 * width), F32),
        ((rows, 3 * width), BF),
    ]
    return pl.pallas_call(
        front_kernel,
        in_specs=[whole()] * 5 + [whole(pl.ANY)] * 4,
        out_specs=[whole()] * len(shapes),
        out_shape=[jax.ShapeDtypeStruct(*shape) for shape in shapes],
        scratch_shapes=[
            pltpu.VMEM((width, 3 * width), BF),
            pltpu.VMEM((width, width), BF),
            pltpu.VMEM((width, hidden), BF),
            pltpu.VMEM((hidden, width), BF),
            pltpu.VMEM((width, 3 * width), BF),
            pltpu.SemaphoreType.DMA((15,)),
        ],
        compiler_params=pltpu.CompilerParams(vmem_limit_bytes=58 * VMEM_MIB),
        cost_estimate=pl.CostEstimate(
            flops=2 * rows * width * (7 * width + 2 * hidden),
            bytes_accessed=2 * width * (7 * width + 2 * hidden),
            transcendentals=2 * rows * hidden,
        ),
        name="front",
    )(tokens, usable, vectors, up_bias, head_rows, qkv_weight, out_weight, up_weight, down_weight)


def turn_kernel(
    x_ref, att_ref, normed_ref, res_ref, cot_ref, vec_ref, bias_ref, out_w, up_w, down_w,
    left_pack, att_pack, output, right_keep, right_send, att_grad, middle_grad, bias_out, rows_out,
    w_out, w_up, w_down, mixed_sc, middle_sc, slope_sc, feed_sc, fg_sc, hg_sc, mg_sc, sems,
):
    width, units = att_ref.shape[1], up_w.shape[2]
    lifted = left_pack.at[:, :width]
    active = left_pack.at[:, width : width + units]
    att_pack[:, :width] = normed_ref[...]
    att_pack[:, width:] = att_ref[...]
    copies = weight_copies(
        [out_w.at[1]] + interleaved(column_pieces(up_w.at[1], 4), row_pieces(down_w.at[1], 4)),
        [w_out] + interleaved(column_pieces(w_up, 4), row_pieces(w_down, 4)),
        sems,
    )
    result = feed_forward(
        1, att_ref[...], res_ref[...], vec_ref, bias_ref, w_out, w_up, w_down, copies, mixed_sc,
        middle_sc, lifted, slope_sc, active, feed_sc,
    )
    output[...] = result.astype(BF)
    grad = feed_backward(
        1, cot_ref[...].astype(F32), feed_sc[...], middle_sc[...], mixed_sc[...], slope_sc, vec_ref,
        w_up, w_down, None, fg_sc, hg_sc, mg_sc, bias_out, rows_out, 0,
    )
    middle_grad[...] = grad
    att_grad[...] = product_right(mg_sc[...], w_out[...]).astype(BF)
    split_columns([hg_sc, fg_sc, mg_sc], x_ref[0], right_keep, right_send)


def turn(x_at, att, normed, res, cotangent, vectors, up_bias, out_weight, up_weight, down_weight):
    rows, width = res.shape
    hidden = up_weight.shape[2]
    shapes = [
        ((rows, hidden + width), BF),
        ((rows, 2 * width), BF),
        ((rows, width), BF),
        ((rows, hidden // 2 + width), BF),
        ((rows, hidden // 2 + width), BF),
        ((rows, width), BF),
        ((rows, width), F32),
        ((1, hidden), F32),
        ((8, width), F32),
    ]
    return pl.pallas_call(
        turn_kernel,
        in_specs=[whole(pltpu.SMEM)] + [whole()] * 6 + [whole(pl.ANY)] * 3,
        out_specs=[whole()] * len(shapes),
        out_shape=[jax.ShapeDtypeStruct(*shape) for shape in shapes],
        scratch_shapes=[
            pltpu.VMEM((width, width), BF),
            pltpu.VMEM((width, hidden), BF),
            pltpu.VMEM((hidden, width), BF),
            pltpu.VMEM((rows, width), F32),
            pltpu.VMEM((rows, width), F32),
            pltpu.VMEM((rows, hidden), F32),
            pltpu.VMEM((rows, width), F32),
            pltpu.VMEM((rows, width), BF),
            pltpu.VMEM((rows, hidden), BF),
            pltpu.VMEM((rows, width), BF),
            pltpu.SemaphoreType.DMA((9,)),
        ],
        compiler_params=pltpu.CompilerParams(vmem_limit_bytes=58 * VMEM_MIB),
        cost_estimate=pl.CostEstimate(
            flops=4 * rows * width * (width + 2 * hidden),
            bytes_accessed=2 * width * (width + 2 * hidden),
            transcendentals=2 * rows * hidden,
        ),
        name="turn",
    )(x_at, att, normed, res, cotangent, vectors, up_bias, out_weight, up_weight, down_weight)


def back_one_kernel(r):
    mover = Mover(r.moves)
    early = [
        mover.start(*pair)
        for pair in (
            (r.vectors, r.vectors_sc), (r.head_rows, r.head_rows_sc), (r.dqkv, r.dqkv_sc),
            (r.pre, r.pre_sc), (r.res, r.res_sc), (r.grad, r.grad_sc),
        )
    ]
    copies = weight_copies(column_pieces(r.qkv_w.at[1], 3), column_pieces(r.w_qkv, 3), r.sems)
    later = [
        mover.start(*pair)
        for pair in (
            (r.feed, r.feed_sc), (r.middle, r.middle_sc), (r.mixed, r.mixed_sc),
            (r.slope, r.slope_sc),
        )
    ]
    copies = copies + weight_copies(
        interleaved(column_pieces(r.up_w.at[0], 4), row_pieces(r.down_w.at[0], 4)),
        interleaved(column_pieces(r.w_up, 4), row_pieces(r.w_down, 4)),
        r.more_sems,
    )
    for copy in early:
        copy.wait()
    part = project_backward(
        1, r.res_sc[...], r.dqkv_sc, r.pre_sc, r.vectors_sc, r.head_rows_sc, r.w_qkv, copies[:3],
        r.pg_sc, r.rows_out, r.head_out,
    )
    split_columns([r.pg_sc], r.smem_at[0], r.pg_keep_sc, r.pg_send_sc)
    mover.flush(r.pg_send_sc, r.pg_send)
    mover.flush(r.pg_keep_sc, r.pg_keep)
    for copy in later:
        copy.wait()
    r.middle_grad_sc[...] = feed_backward(
        0, r.grad_sc[...] + part, r.feed_sc[...], r.middle_sc[...], r.mixed_sc[...], r.slope_sc,
        r.vectors_sc, r.w_up, r.w_down, copies[3:], r.fg_sc, r.hg_sc, r.mixed_grad_sc, r.bias_out,
        r.rows_out, 8,
    )
    mover.flush(r.middle_grad_sc, r.middle_grad)
    mover.flush(r.mixed_grad_sc, r.mixed_grad)
    split_columns([r.hg_sc, r.fg_sc], r.smem_at[1], r.right_keep_sc, r.right_send_sc)
    mover.flush(r.right_send_sc, r.right_send)
    mover.flush(r.right_keep_sc, r.right_keep)
    mover.finish()


def back_one(
    places, dqkv, pre, res, grad, feed, middle, mixed, slope, vectors, head_rows, qkv_weight,
    up_weight, down_weight,
):
    rows, width = res.shape
    hidden = up_weight.shape[2]
    loaded = dict(
        vectors=vectors, head_rows=head_rows, dqkv=dqkv, pre=pre, res=res,
        grad=grad, feed=feed, middle=middle, mixed=mixed, slope=slope,
    )
    stored = dict(
        pg_keep=((rows, 3 * width // 2), BF),
        pg_send=((rows, 3 * width // 2), BF),
        right_keep=((rows, (hidden + width) // 2), BF),
        right_send=((rows, (hidden + width) // 2), BF),
        mixed_grad=((rows, width), BF),
        middle_grad=((rows, width), F32),
    )
    return named_call(
        back_one_kernel,
        dict(smem_at=places, **loaded, qkv_w=qkv_weight, up_w=up_weight, down_w=down_weight),
        dict(
            **{key: (*value, True) for key, value in stored.items()},
            bias_out=((1, hidden), F32, False),
            rows_out=((16, width), F32, False),
            head_out=((8, WIDE), F32, False),
        ),
        dict(
            **{key + "_sc": pltpu.VMEM(value.shape, value.dtype) for key, value in loaded.items()},
            **{key + "_sc": pltpu.VMEM(*value) for key, value in stored.items()},
            w_qkv=low(width, 3 * width),
            w_up=low(width, hidden),
            w_down=low(hidden, width),
            pg_sc=low(rows, 3 * width),
            fg_sc=low(rows, width),
            hg_sc=low(rows, hidden),
            sems=pltpu.SemaphoreType.DMA((3,)),
            more_sems=pltpu.SemaphoreType.DMA((8,)),
            moves=pltpu.SemaphoreType.DMA((16,)),
        ),
        60,
        pl.CostEstimate(
            flops=2 * rows * width * (3 * width + 2 * hidden),
            bytes_accessed=2 * width * (3 * width + 2 * hidden),
            transcendentals=0,
        ),
        "back_one",
    )


def frame_steps(att_grad, usable, qkv_ref, dqkv_ref):
    width = att_grad.shape[1]
    first, _ = lane_masks(F32)
    for pair in range(width // LANES):
        q, k, v = [
            qkv_ref[:, part * width + pair * LANES : part * width + (pair + 1) * LANES]
            for part in range(3)
        ]
        out = att_grad[:, pair * LANES : (pair + 1) * LANES]
        pieces = []
        for mask in lane_masks(BF):
            shares = frame_shares(q * mask, k, usable)
            share_grad = product_right(out * mask, v)
            delta = jnp.sum(shares * share_grad, axis=-1, keepdims=True)
            score_grad = (shares * (share_grad - delta)).astype(BF)
            pieces.append(
                (
                    product(score_grad, k) * SCALE,
                    product_left(score_grad, q) * SCALE,
                    product_left(shares.astype(BF), out),
                )
            )
        for part in range(3):
            dqkv_ref[:, part * width + pair * LANES : part * width + (pair + 1) * LANES] = jnp.where(
                first > 0, pieces[0][part], pieces[1][part]
            )
        if pair % 2 == 1:
            yield


def frame_loads(r, mover):
    early = [
        mover.start(*pair)
        for pair in (
            (r.mixed_grad, r.mixed_grad_sc), (r.usable, r.usable_sc), (r.qkv, r.qkv_sc)
        )
    ]
    copies = weight_copies(
        [r.out_w.at[0]] + column_pieces(r.qkv_w.at[0], 3), [r.w_out] + column_pieces(r.w_qkv, 3),
        r.sems,
    )
    later = [
        mover.start(*pair)
        for pair in (
            (r.vectors, r.vectors_sc), (r.head_rows, r.head_rows_sc), (r.pre, r.pre_sc),
            (r.tok, r.tok_sc), (r.grad, r.grad_sc), (r.rows10, r.rows10_sc), (r.rows1, r.rows1_sc),
            (r.bias0, r.bias0_sc), (r.bias1, r.bias1_sc), (r.heads1, r.heads1_sc),
        )
    ]
    return early, later, copies


def frame_part(r, early, copies):
    for copy in early:
        copy.wait()
    copies[0].wait()
    att_grad = product_right(r.mixed_grad_sc[...], r.w_out[...]).astype(BF)
    yield
    yield from frame_steps(att_grad, r.usable_sc[...], r.qkv_sc, r.dqkv_sc)


def input_part(r, later, copies, x_at):
    width = r.tok_sc.shape[1]
    for copy in later:
        copy.wait()
    results = []
    yield from project_steps(
        results, 0, r.tok_sc[...].astype(F32), r.dqkv_sc, r.pre_sc, r.vectors_sc, r.head_rows_sc,
        r.w_qkv, copies[1:], r.pg_sc, r.rows_sc, r.heads_sc,
    )
    part = results[0]
    split_columns([r.pg_sc, r.mixed_grad_sc], x_at, r.pg_keep_sc, r.pg_send_sc)
    r.input_grad_sc[...] = (r.grad_sc[...] + part).astype(BF)
    small = r.small_sc
    small[0:5] = r.rows_sc[0:5]
    small[5:11] = r.rows10_sc[8:14]
    small[11:16] = r.rows10_sc[0:5]
    small[16:22] = r.rows1_sc[0:6]
    at = 22
    for bias in (r.bias0_sc, r.bias1_sc):
        for j in range(bias.shape[1] // width):
            small[at : at + 1] = bias[:, j * width : (j + 1) * width]
            at += 1
    place = lax.broadcasted_iota(jnp.int32, (1, width), 1) // HD
    row = jnp.zeros((1, width), F32)
    for index, heads in enumerate((r.heads_sc, r.heads1_sc)):
        total = heads[...]
        total = total + pltpu.roll(total, WIDE // 2, 1)
        total = total + pltpu.roll(total, HD, 1)
        for j in range(3):
            many = jnp.concatenate([total[j : j + 1]] * (width // WIDE), axis=1)
            row = jnp.where(place == 3 * index + j, many, row)
    small[at : at + 1] = row
    small[at + 1 :] = jnp.zeros((small.shape[0] - at - 1, width), F32)
    yield


def back_two_kernel(r):
    mover = Mover(r.moves)
    early, later, copies = frame_loads(r, mover)
    for _ in frame_part(r, early, copies):
        pass
    for _ in input_part(r, later, copies, r.smem_at[0]):
        pass
    mover.flush(r.pg_send_sc, r.pg_send)
    mover.flush(r.pg_keep_sc, r.pg_keep)
    mover.flush(r.input_grad_sc, r.input_grad)
    mover.flush(r.small_sc, r.small)
    mover.finish()


def back_two(
    places, mixed_grad, grad, qkv, pre, tok, usable, vectors, head_rows, rows10, rows1, bias0,
    bias1, heads1, out_w, qkv_w,
):
    rows, width = tok.shape
    loaded = dict(
        mixed_grad=mixed_grad, usable=usable, qkv=qkv, vectors=vectors, head_rows=head_rows,
        pre=pre, tok=tok, grad=grad, rows10=rows10, rows1=rows1, bias0=bias0, bias1=bias1,
        heads1=heads1,
    )
    small_rows = 2 * vectors.shape[1] + 2 * bias0.shape[1] // width + 2
    stored = dict(
        pg_keep=((rows, 2 * width), BF),
        pg_send=((rows, 2 * width), BF),
        input_grad=((rows, width), BF),
        small=((small_rows, width), F32),
    )
    return named_call(
        back_two_kernel,
        dict(smem_at=places, **loaded, out_w=out_w, qkv_w=qkv_w),
        {key: (*value, True) for key, value in stored.items()},
        dict(
            **{key + "_sc": pltpu.VMEM(value.shape, value.dtype) for key, value in loaded.items()},
            **{key + "_sc": pltpu.VMEM(*value) for key, value in stored.items()},
            w_out=low(width, width),
            w_qkv=low(width, 3 * width),
            dqkv_sc=full(rows, 3 * width),
            pg_sc=low(rows, 3 * width),
            rows_sc=full(8, width),
            heads_sc=full(8, WIDE),
            sems=pltpu.SemaphoreType.DMA((4,)),
            moves=pltpu.SemaphoreType.DMA((17,)),
        ),
        60,
        pl.CostEstimate(
            flops=2 * rows * width * 4 * width,
            bytes_accessed=2 * width * 4 * width,
            transcendentals=HEADS * rows * rows,
        ),
        "back_two",
    )


def weight_grad_kernel(outer, tall, starts, at_ref, *refs):
    count = len(tall)
    lefts, rights = refs[: 4 * count], refs[4 * count : 8 * count]
    keep, send = refs[8 * count : 8 * count + 2]
    left_sc = refs[8 * count + 2 : 9 * count + 2]
    right_sc = refs[9 * count + 2 : 10 * count + 2]
    sems = refs[10 * count + 2]
    c_at, y_at = at_ref[0], at_ref[1]
    rows = lefts[0].shape[0]
    group = keep.shape[0] // outer
    copies = []
    for w in range(count):
        cols, left_cols = right_sc[w].shape[1], left_sc[w].shape[1]
        left_start, right_start = starts[w]
        for s in range(4):
            at = pl.ds(pl.multiple_of(right_start + c_at * cols, LANES), cols)
            copies.append(
                pltpu.make_async_copy(
                    rights[4 * w + s].at[:, at],
                    right_sc[w].at[s * rows : (s + 1) * rows],
                    sems.at[len(copies)],
                )
            )
            copies.append(
                pltpu.make_async_copy(
                    lefts[4 * w + s].at[:, left_start : left_start + left_cols],
                    left_sc[w].at[s * rows : (s + 1) * rows],
                    sems.at[len(copies)],
                )
            )
    for copy in copies:
        copy.start()
    start = 0
    for w in range(count):
        for copy in copies[8 * w : 8 * w + 8]:
            copy.wait()
        cols = right_sc[w].shape[1]
        right = right_sc[w][...]
        for block in range(left_sc[w].shape[1] // 512):
            result = product_left(left_sc[w][:, block * 512 : (block + 1) * 512], right).astype(BF)
            targets = {0: [], 1: []}
            if tall[w]:
                size, part = 4 * group, group // 2
                for piece in range(512 // part):
                    row = block * 512 + piece * part
                    o, y = row // (2 * size), (row // size) % 2
                    core, t = (row % size) // (size // 2), (row % (size // 2)) // part
                    targets[y].append(
                        (piece * part, part, o * group + core * part, start + t * cols)
                    )
            else:
                for piece in range(512 // group):
                    row = block * 512 + piece * group
                    o, y = row // (2 * group), (row // group) % 2
                    targets[y].append((piece * group, group, o * group, start))
            for y in range(2):
                if not targets[y]:
                    continue

                def store(ref, y=y):
                    for source, size, row, col in targets[y]:
                        ref[row : row + size, col : col + cols] = result[source : source + size]

                @pl.when(y_at == y)
                def _():
                    store(keep)

                @pl.when(y_at != y)
                def _():
                    store(send)

        start += cols * (4 if tall[w] else 1)


def weight_grads(name, outer, width, places, products):
    rows = products[0][0][0].shape[0]
    group = width // (2 * outer)
    lefts, left_starts, left_cols, rights, right_starts, halves, tall = zip(*products)
    columns = [half // 2 for half in halves]
    total = sum(c * (4 if t else 1) for c, t in zip(columns, tall))
    shape = jax.ShapeDtypeStruct((outer * group, total), BF)
    count = len(products)
    return pl.pallas_call(
        functools.partial(
            weight_grad_kernel, outer, tall, tuple(zip(left_starts, right_starts))
        ),
        in_specs=[whole(pltpu.SMEM)] + [whole(pl.ANY)] * (8 * count),
        out_specs=[whole()] * 2,
        out_shape=[shape] * 2,
        scratch_shapes=[pltpu.VMEM((4 * rows, c), BF) for c in left_cols]
        + [pltpu.VMEM((4 * rows, c), BF) for c in columns]
        + [pltpu.SemaphoreType.DMA((8 * count,))],
        compiler_params=pltpu.CompilerParams(vmem_limit_bytes=48 * VMEM_MIB),
        cost_estimate=pl.CostEstimate(
            flops=16 * rows * outer * group * total,
            bytes_accessed=8 * outer * group * total,
            transcendentals=0,
        ),
        name=name,
    )(places, *[a for l in lefts for a in l], *[a for r in rights for a in r])


def assemble_kernel(at_ref, *refs):
    more = len(refs) - 13
    sources, outs = refs[: 4 + more // 5], refs[4 + more // 5 : 8 + more // 5]
    rest = refs[8 + more // 5 :]
    smalls, pieces, sems = rest[: 3 * more // 5], rest[3 * more // 5 : -1], rest[-1]
    copies = [
        pltpu.make_async_copy(source, piece, sems.at[index])
        for index, (source, piece) in enumerate(zip(sources, pieces))
    ]
    for copy in copies:
        copy.start()
    for copy in copies:
        copy.wait()
    qkv_out, out_out, up_out, down_out = outs
    c_at, x_at = at_ref[0], at_ref[2]
    spread = bool(smalls)
    if smalls:
        share_small(at_ref[6], pieces[4], *smalls)
    half_at = (at_ref[5], x_at)
    part = qkv_out.shape[1]
    for layer in range(2):
        for source in range(4):
            feed, att = pieces[2 * layer].at[source], pieces[2 * layer + 1].at[source]
            c = c_at if source % 2 == 0 else 1 - c_at
            feed_place, att_place = [
                2 * (half if source < 2 else 1 - half) + c for half in (half_at[layer], x_at)
            ]

            def put(ref, values, place, row=0, layer=layer):
                cols = values.shape[1]
                at = pl.ds(pl.multiple_of(place * cols, LANES), cols)
                ref[layer, row : row + values.shape[0], at] = values.astype(F32)

            up_cols = up_out.shape[2] // 4
            down_cols = down_out.shape[2] // 4
            qkv_cols = qkv_out.shape[2] // 4
            put(up_out, feed[:, :up_cols], feed_place)
            if spread and layer == 1:
                for t in range(2):
                    start = up_cols + t * 2 * down_cols
                    rows = pl.ds(pl.multiple_of((2 * (feed_place // 2) + t) * part, part), part)
                    cols = pl.ds(pl.multiple_of(c * 2 * down_cols, LANES), 2 * down_cols)
                    down_out[layer, rows, cols] = feed[:, start : start + 2 * down_cols].astype(F32)
                put(qkv_out, att[:, :qkv_cols], att_place)
                put(out_out, att[:, qkv_cols:], att_place)
                continue
            for t in range(4):
                put(
                    down_out,
                    feed[:, up_cols + t * down_cols : up_cols + (t + 1) * down_cols],
                    feed_place,
                    t * part,
                )
            put(qkv_out, att[:, :qkv_cols], att_place)
            put(out_out, att[:, qkv_cols:], att_place)


def share_small(me, small, vector_out, bias_out, head_out):
    vector_rows = vector_out.shape[1]
    lanes = pl.ds(pl.multiple_of((me // 2) * LANES, LANES), LANES)
    pair = small[: 2 * vector_rows, lanes]
    pair = jnp.where(lax.rem(me, 2) == 0, pair, pltpu.roll(pair, HD, 1))
    columns = bias_out.shape[1]
    per_row = small.shape[1] // columns
    rows = PEERS // per_row
    for layer in range(2):
        vector_out[layer] = pair[layer * vector_rows : (layer + 1) * vector_rows, :HD]
        row = pl.ds(2 * vector_rows + layer * rows + me // per_row, 1)
        at = pl.ds(pl.multiple_of(lax.rem(me, per_row) * columns, LANES), columns)
        bias_out[layer : layer + 1] = small[row, at]
        last = 2 * vector_rows + 2 * rows
        head_out[layer : layer + 1] = small[
            last : last + 1, layer * 3 * HD : (layer + 1) * 3 * HD
        ]


def assemble(places, pieces, shapes):
    return pl.pallas_call(
        assemble_kernel,
        in_specs=[whole(pltpu.SMEM)] + [whole(pl.ANY)] * len(pieces),
        out_specs=[whole()] * len(shapes),
        out_shape=[jax.ShapeDtypeStruct(shape, F32) for shape in shapes],
        scratch_shapes=[pltpu.VMEM(piece.shape, piece.dtype) for piece in pieces]
        + [pltpu.SemaphoreType.DMA((len(pieces),))],
        compiler_params=pltpu.CompilerParams(vmem_limit_bytes=60 * VMEM_MIB),
        name="assemble",
    )(places, *pieces)


OUTER = 4
BLOCK = 128


def slot_order(z0, z1):
    return [2 * (1 - z1) + (1 - z0), 2 * z1 + (1 - z0), 2 * (1 - z1) + z0, 2 * z1 + z0]


def slot_group(slot, z0, z1):
    far = jnp.where(slot % 2 == 0, 1 - z1, z1)
    return 2 * far + jnp.where(slot < 2, 1 - z0, z0)


def slot_product(group, left, left_at, right, right_at, cols, tall, emit):
    rights = right[:, right_at : right_at + cols]
    if tall:
        for y in range(2):
            start = pl.multiple_of(left_at + group * 8 * BLOCK + y * 4 * BLOCK, BLOCK)
            result = product_left(left[:, pl.ds(start, 4 * BLOCK)], rights).astype(BF)
            half = BLOCK // 2
            for c in range(2):
                for t in range(4):
                    row = c * 2 * BLOCK + t * half
                    emit(y, c * half, t * cols, result[row : row + half])
    else:
        start = pl.multiple_of(left_at + group * 2 * BLOCK, BLOCK)
        result = product_left(left[:, pl.ds(start, 2 * BLOCK)], rights).astype(BF)
        for y in range(2):
            emit(y, 0, 0, result[y * BLOCK : (y + 1) * BLOCK])


class Sender:
    def __init__(self, send, recv, partners):
        self.send, self.recv, self.partners = send, recv, partners
        self.copies = []

    def start(self, source, target, partner):
        index = len(self.copies)
        copy = pltpu.make_async_remote_copy(
            src_ref=source,
            dst_ref=target,
            send_sem=self.send.at[index],
            recv_sem=self.recv.at[index],
            device_id=self.partners[partner],
            device_id_type=MESH,
        )
        copy.start()
        self.copies.append(copy)
        return copy

    def finish(self):
        for copy in self.copies:
            copy.wait_send()


def finish_kernel(r):
    me = lax.axis_index("blk")
    x_at = lax.axis_index("grp")
    c_at, y_at, z0, z1 = [lax.rem(me // (1 << bit), 2) for bit in range(4)]
    partners = {"x": {"grp": 1 - x_at}}
    for bit, name in enumerate(("c", "y", "z0", "z1")):
        partners[name] = {"blk": me ^ (1 << bit)}
    barrier = pltpu.get_barrier_semaphore()
    for partner in partners.values():
        pl.semaphore_signal(barrier, 1, device_id=partner, device_id_type=MESH)
    mover = Mover(r.moves)
    early, later, weights = frame_loads(r, mover)
    pl.semaphore_wait(barrier, len(partners))
    sender = Sender(r.send, r.recv, partners)
    local = r.local
    rows = r.la1.shape[0]
    locals_ = []

    def load(source, target):
        copy = pltpu.make_async_copy(source, target, local.at[len(locals_)])
        copy.start()
        locals_.append(copy)
        return copy

    stores = []

    def store(source, target):
        stores.append(load(source, target))

    def ready(copies):
        for copy in copies:
            copy.wait_recv()

    def quarter(ref, start, cols, core):
        return ref.at[:, pl.ds(pl.multiple_of(start + core * cols, BLOCK), cols)]

    def own_right(ref, start, cols, target, to, index):
        here = slice(index * rows, (index + 1) * rows)
        there = slice((2 + index) * rows, (3 + index) * rows)
        return [
            load(quarter(ref, start, cols, c_at), target.at[here, to : to + cols]),
            sender.start(
                quarter(ref, start, cols, 1 - c_at), target.at[there, to : to + cols], "c"
            ),
        ]

    def own_left(ref, target, index):
        return [
            load(ref, target.at[index * rows : (index + 1) * rows]),
            sender.start(ref, target.at[(2 + index) * rows : (3 + index) * rows], "c"),
        ]

    right_a1, right_f0, right_a0 = r.right_a1, r.right_f0, r.right_a0
    left_a1, left_f0, left_a0 = r.left_a1, r.left_f0, r.left_a0
    qkv_cols, out_cols = right_a1.shape[1] * 3 // 4, right_a1.shape[1] // 4
    up_cols, down_cols = right_f0.shape[1] * 4 // 5, right_f0.shape[1] // 5
    width = left_a1.shape[1] // 2
    pg1_copy = sender.start(r.pg1_send, r.pg1_x, "x")
    rt0_copy = sender.start(r.rt0_send, r.rt0_x, "x")
    d1_loads = [load(r.stay_down, r.part_d1), load(r.came_down, r.y_d1)]
    u1_loads = [load(r.stay_up, r.part_u1), load(r.came_up, r.z0_u1)]
    a1_ready = (
        own_left(r.la1, left_a1, 0)
        + own_left(r.la1_x, left_a1, 1)
        + own_right(r.pg1, 0, qkv_cols, right_a1, 0, 0)
        + own_right(r.rt1, 0, out_cols, right_a1, qkv_cols, 0)
        + own_right(r.rt1_x, 0, out_cols, right_a1, qkv_cols, 1)
    )
    f0_ready = (
        own_left(r.lf0, left_f0, 0)
        + own_left(r.lf0_x, left_f0, 1)
        + own_right(r.rt0, 0, up_cols, right_f0, 0, 0)
        + own_right(r.rt0, 2 * up_cols, down_cols, right_f0, up_cols, 0)
    )
    a0_ready = own_left(r.la0, left_a0, 0) + own_left(r.la0_x, left_a0, 1)

    def rest_a1():
        pg1_copy.wait_recv()
        return own_right(r.pg1_x, 0, qkv_cols, right_a1, 0, 1)

    def rest_f0():
        rt0_copy.wait_recv()
        return own_right(r.rt0_x, 0, up_cols, right_f0, 0, 1) + own_right(
            r.rt0_x, 2 * up_cols, down_cols, right_f0, up_cols, 1
        )

    def rest_a0(copy):
        copies = own_right(r.pg_keep_sc, 0, qkv_cols, right_a0, 0, 0) + own_right(
            r.pg_keep_sc, 2 * qkv_cols, out_cols, right_a0, qkv_cols, 0
        )
        copy.wait_recv()
        return (
            copies
            + own_right(r.pm0_x, 0, qkv_cols, right_a0, 0, 1)
            + own_right(r.pm0_x, 2 * qkv_cols, out_cols, right_a0, qkv_cols, 1)
        )

    class Finish:
        def finish(self):
            half = BLOCK // 2
            other = self.own(3).at[pl.ds(pl.multiple_of((1 - c_at) * half, half), half)]
            self.c_copy = sender.start(other, self.fin.at[1], "c")
            self.fin[0] = self.own(3)[pl.ds(pl.multiple_of(c_at * half, half), half)]
            self.far_copies = [sender.start(self.fin.at[0], self.far.at[0], "x")]

        def fourth(self):
            self.c_copy.wait_recv()
            self.far_copies.append(sender.start(self.fin.at[1], self.far.at[1], "x"))
            store(self.fin, self.out.at[0:2, :, self.columns])

        def last(self):
            for copy in self.far_copies:
                copy.wait_recv()
            store(self.far, self.out.at[2:4, :, self.columns])

    class Group(Finish):
        def __init__(self, part, over, over_z0, over_z1, fin, far, out, columns, came=False):
            self.part, self.over, self.over_z0, self.over_z1 = part, over, over_z0, over_z1
            self.fin, self.far, self.out, self.columns = fin, far, out, columns
            self.came, self.copies, self.z0_copies = came, {}, {}

        def own(self, slot):
            return self.part.at[slot] if self.came else self.part.at[slot, y_at]

        def total(self, slot):
            return self.own(slot)[...].astype(F32) + self.over[slot].astype(F32)

        def made(self, slot):
            self.copies[slot] = sender.start(
                self.part.at[slot, 1 - y_at], self.over.at[slot], "y"
            )

        def step(self, slot):
            if not self.came:
                self.copies[slot].wait_recv()
            (lambda: self.first(0), lambda: self.first(1), self.second, self.third)[slot]()

        def first(self, slot):
            self.own(slot)[...] = self.total(slot).astype(BF)
            self.z0_copies[slot] = sender.start(self.own(slot), self.over_z0.at[slot], "z0")

        def second(self):
            value = self.total(2)
            self.z0_copies[0].wait_recv()
            self.own(2)[...] = (value + self.over_z0[0].astype(F32)).astype(BF)
            self.z1_copy = sender.start(self.own(2), self.over_z1, "z1")

        def third(self):
            value = self.total(3)
            self.z0_copies[1].wait_recv()
            value = value + self.over_z0[1].astype(F32)
            self.z1_copy.wait_recv()
            self.own(3)[...] = (value + self.over_z1[...].astype(F32)).astype(BF)
            self.finish()

    class Early(Finish):
        def __init__(self, part, came, over, over_z1, fin, far, out, columns, keep=None):
            self.part, self.came, self.over, self.over_z1 = part, came, over, over_z1
            self.keep = part if keep is None else keep
            self.fin, self.far, self.out, self.columns = fin, far, out, columns
            self.copies, self.z0_copies = {}, {}

        def own(self, slot):
            return self.keep.at[slot - 2, y_at]

        def total(self, slot, at):
            return self.keep[slot, at].astype(F32) + self.came[slot, at].astype(F32)

        def made(self, slot):
            if slot < 2:
                self.z0_copies[slot] = sender.start(
                    self.part.at[slot], self.came.at[slot], "z0"
                )

        def send(self, slot):
            if self.z0_copies:
                self.z0_copies[slot].wait_recv()
            self.keep[slot, 1 - y_at] = self.total(slot, 1 - y_at).astype(BF)
            self.copies[slot] = sender.start(
                self.keep.at[slot, 1 - y_at], self.over.at[slot], "y"
            )

        def step(self, slot):
            self.copies[slot].wait_recv()
            value = self.total(slot, y_at) + self.over[slot].astype(F32)
            if slot == 1:
                self.z1_copy.wait_recv()
                value = value + self.over_z1[...].astype(F32)
            self.keep[slot, y_at] = value.astype(BF)
            if slot == 0:
                self.z1_copy = sender.start(self.keep.at[0, y_at], self.over_z1, "z1")
            else:
                self.finish()

    every = slice(None)
    half_cols = r.part_u1.shape[3]
    u1 = Early(
        r.part_u1, r.z0_u1, r.y_u1, r.z1_u1, r.fin_u1, r.far_u1, r.f1_out, slice(0, half_cols)
    )
    d1 = Group(
        r.part_d1, r.y_d1, r.z0_d1, r.z1_d1, r.fin_d1, r.far_d1, r.f1_out,
        slice(half_cols, 2 * half_cols), True,
    )
    a1 = Early(
        r.part_a1, r.z0_a1, r.y_a1, r.z1_a1, r.fin_a1, r.far_a1, r.a1_out, every, r.part_a1.at[2:4]
    )
    f0 = Group(r.part_f0, r.y_f0, r.z0_f0, r.z1_f0, r.fin_f0, r.far_f0, r.f0_out, every)
    a0 = Group(r.part_a0, r.y_a0, r.z0_a0, r.z1_a0, r.fin_a0, r.far_a0, r.a0_out, every)

    def products(group, left, right, terms, slots=range(OUTER)):
        for slot in slots:
            at = slot_group(slot, z0, z1)
            base = 0
            for left_at, right_at, cols, tall in terms:

                def emit(y, row, col, values, slot=slot, base=base):
                    height, wide = values.shape
                    group.part[
                        slot, y, row : row + height, base + col : base + col + wide
                    ] = values

                slot_product(at, left, left_at, right, right_at, cols, tall, emit)
                base += cols * (4 if tall else 1)
            group.made(slot)

    att_terms = [(0, 0, qkv_cols, False), (width, qkv_cols, out_cols, False)]
    feed_terms = [(0, 0, up_cols, False), (width, up_cols, down_cols, True)]
    sums, sums_in, small_copies = r.sums, r.sums_in, []

    def small_step(name=None):
        index = len(small_copies)
        if index:
            small_copies[-1].wait_recv()
            sums[index] = sums[index - 1] + sums_in[index - 1]
        if name is not None:
            small_copies.append(sender.start(sums.at[index], sums_in.at[index], name))
        else:
            store(sums.at[index], r.small_out)

    backward = chain(frame_part(r, early, weights), input_part(r, later, weights, x_at))
    ready(d1_loads)
    d1.step(0)
    next(backward)
    d1.step(1)
    ready(u1_loads)
    u1.send(1)
    d1.step(2)
    a1_ready += rest_a1()
    next(backward)
    next(backward)
    next(backward)
    ready(a1_ready)
    products(a1, left_a1, right_a1, att_terms, (0,))
    u1.send(0)
    next(backward)
    f0_ready += rest_f0()
    ready(f0_ready)
    products(f0, left_f0, right_f0, feed_terms, (0,))
    next(backward)
    products(a1, left_a1, right_a1, att_terms, (1,))
    products(a1, left_a1, right_a1, att_terms, (2,))
    next(backward)
    products(f0, left_f0, right_f0, feed_terms, (1,))
    products(f0, left_f0, right_f0, feed_terms, (2,))
    d1.step(3)
    d1.fourth()
    f0.step(0)
    next(backward)
    a1.send(0)
    next(backward)
    next(backward)
    next(backward)
    u1.step(0)
    next(backward)
    next(backward)
    pm0_copy = sender.start(r.pg_send_sc, r.pm0_x, "x")
    store(r.input_grad_sc, r.input_grad)
    sums[0] = r.small_sc[...]
    small_step("x")
    products(a1, left_a1, right_a1, att_terms, (3,))
    a0_ready += rest_a0(pm0_copy)
    f0.step(1)
    f0.step(2)
    small_step("c")
    ready(a0_ready)
    products(a0, left_a0, right_a0, att_terms, (0,))
    a1.step(0)
    products(f0, left_f0, right_f0, feed_terms, (3,))
    small_step("y")
    products(a0, left_a0, right_a0, att_terms, (1,))
    a0.step(0)
    products(a0, left_a0, right_a0, att_terms, (2,))
    u1.step(1)
    small_step("z0")
    f0.step(3)
    f0.fourth()
    u1.fourth()
    a0.step(1)
    small_step("z1")
    a1.send(1)
    a0.step(2)
    products(a0, left_a0, right_a0, att_terms, (3,))
    a1.step(1)
    small_step()
    d1.last()
    a1.fourth()
    f0.last()
    u1.last()
    a0.step(3)
    a0.fourth()
    a1.last()
    a0.last()
    assert len(sender.copies) == r.send.shape[0]
    assert len(locals_) == local.shape[0]
    ready(stores)
    sender.finish()
    mover.finish()


def finish_all(frame, u1, d1, a1, f0, a0):
    rows, width = frame["tok"].shape
    wide, att = 2 * u1[0].shape[-1], u1[0].shape[-1]
    half = BLOCK // 2
    small_rows = 2 * frame["vectors"].shape[1] + 2 * frame["bias0"].shape[1] // width + 2
    loaded = dict(frame)
    out_weight, qkv_weight = loaded.pop("out_w"), loaded.pop("qkv_w")

    def piece(columns):
        return ((4, half, columns), BF, True)

    return named_call(
        finish_kernel,
        dict(
            **loaded, out_w=out_weight, qkv_w=qkv_weight, stay_up=u1[0], came_up=u1[1],
            stay_down=d1[0], came_down=d1[1], la1=a1[0], la1_x=a1[1], pg1=a1[2], pg1_send=a1[3],
            rt1=a1[4], rt1_x=a1[5], lf0=f0[0], lf0_x=f0[1], rt0=f0[2], rt0_send=f0[3], la0=a0[0],
            la0_x=a0[1],
        ),
        dict(
            f0_out=piece(wide), a0_out=piece(att), f1_out=piece(wide), a1_out=piece(att),
            small_out=((small_rows, width), F32, True), input_grad=((rows, width), BF, True),
        ),
        dict(
            **{key + "_sc": pltpu.VMEM(value.shape, value.dtype) for key, value in loaded.items()},
            pg_keep_sc=low(rows, 2 * width),
            pg_send_sc=low(rows, 2 * width),
            input_grad_sc=low(rows, width),
            small_sc=full(small_rows, width),
            w_out=low(width, width),
            w_qkv=low(width, 3 * width),
            dqkv_sc=full(rows, 3 * width),
            pg_sc=low(rows, 3 * width),
            rows_sc=full(8, width),
            heads_sc=full(8, WIDE),
            sems=pltpu.SemaphoreType.DMA((4,)),
            moves=pltpu.SemaphoreType.DMA((13,)),
            left_a1=low(4 * rows, 2 * width),
            right_a1=low(4 * rows, att),
            left_f0=low(4 * rows, f0[0].shape[1]),
            right_f0=low(4 * rows, wide * 5 // 8),
            left_a0=low(4 * rows, 2 * width),
            right_a0=low(4 * rows, att),
            pg1_x=low(rows, 3 * width // 2),
            rt0_x=low(*f0[2].shape),
            pm0_x=low(rows, 2 * width),
            part_u1=low(2, 2, BLOCK, att),
            part_d1=low(OUTER, BLOCK, att),
            part_a1=low(OUTER, 2, BLOCK, att),
            part_f0=low(OUTER, 2, BLOCK, wide),
            part_a0=low(OUTER, 2, BLOCK, att),
            y_u1=low(2, BLOCK, att),
            y_d1=low(OUTER, BLOCK, att),
            y_a1=low(2, BLOCK, att),
            y_f0=low(OUTER, BLOCK, wide),
            y_a0=low(OUTER, BLOCK, att),
            z0_u1=low(2, 2, BLOCK, att),
            z0_d1=low(2, BLOCK, att),
            z0_a1=low(2, 2, BLOCK, att),
            z0_f0=low(2, BLOCK, wide),
            z0_a0=low(2, BLOCK, att),
            z1_u1=low(BLOCK, att),
            z1_d1=low(BLOCK, att),
            z1_a1=low(BLOCK, att),
            z1_f0=low(BLOCK, wide),
            z1_a0=low(BLOCK, att),
            fin_u1=low(2, half, att),
            fin_d1=low(2, half, att),
            fin_a1=low(2, half, att),
            fin_f0=low(2, half, wide),
            fin_a0=low(2, half, att),
            far_u1=low(2, half, att),
            far_d1=low(2, half, att),
            far_a1=low(2, half, att),
            far_f0=low(2, half, wide),
            far_a0=low(2, half, att),
            sums=full(6, small_rows, width),
            sums_in=full(5, small_rows, width),
            local=pltpu.SemaphoreType.DMA((34,)),
            send=pltpu.SemaphoreType.DMA((66,)),
            recv=pltpu.SemaphoreType.DMA((66,)),
        ),
        60,
        pl.CostEstimate(
            flops=2 * rows * width * 4 * width + 2**33,
            bytes_accessed=2**26,
            transcendentals=HEADS * rows * rows,
        ),
        "finish_all",
        collective_id=3,
    )


PEERS = HEADS
FOLD = FRAME // 2
EXTRA = 16
GROUPS = 4
BACK_GROUPS = 8
MESH = pl.DeviceIdType.MESH


def fold_pair(values):
    lane = lax.broadcasted_iota(jnp.int32, (FOLD, LANES), 1)
    top, bottom = values[:FOLD], values[FOLD:]
    one = jnp.where(lane < HD, top, pltpu.roll(bottom, HD, 1))
    two = jnp.where(lane < HD, pltpu.roll(top, HD, 1), bottom)
    return one, two


def unfold_pair(one, two):
    lane = lax.broadcasted_iota(jnp.int32, (FOLD, LANES), 1)
    top = jnp.where(lane < HD, one, pltpu.roll(two, HD, 1))
    bottom = jnp.where(lane < HD, pltpu.roll(one, HD, 1), two)
    return top, bottom


def unfold_head(folded):
    lane = lax.broadcasted_iota(jnp.int32, (FOLD, LANES), 1)
    folded = folded.astype(F32)
    top = jnp.where(lane < HD, folded, 0.0)
    bottom = jnp.where(lane < HD, pltpu.roll(folded, HD, 1), 0.0)
    return top.astype(BF), bottom.astype(BF)


def fold_head(values):
    lane = lax.broadcasted_iota(jnp.int32, (FOLD, LANES), 1)
    return jnp.where(lane < HD, values[:FOLD], pltpu.roll(values[FOLD:], HD, 1))


def exchange(me, k, source, target, sems):
    return pltpu.make_async_remote_copy(
        src_ref=source,
        dst_ref=target,
        send_sem=sems.at[0, k],
        recv_sem=sems.at[1, k],
        device_id={"blk": me ^ k},
        device_id_type=MESH,
    )


def call_peers(me, partner):
    barrier = pltpu.get_barrier_semaphore()
    for k in range(1, PEERS):
        pl.semaphore_signal(barrier, 1, device_id={"blk": me ^ k}, device_id_type=MESH)
    pl.semaphore_signal(barrier, 1, device_id=partner, device_id_type=MESH)
    return lambda: pl.semaphore_wait(barrier, PEERS)


def all_to_all(me, source, target, sems, own_sem):
    copies = [exchange(me, k, source.at[me ^ k], target.at[me], sems) for k in range(PEERS - 1, 0, -1)]
    for copy in copies:
        copy.start()
    own = pltpu.make_async_copy(source.at[me], target.at[me], own_sem)
    own.start()
    return copies + [own]


def head_forward(me, qkv_ref, tag_ref, att_ref, r):
    width = att_ref.shape[1]
    for head in range(HEADS):
        r.pack[head, 3 * FOLD :] = tag_ref[...]
    for pair in range(width // LANES):
        for part in range(3):
            block = qkv_ref[:, part * width + pair * LANES : part * width + (pair + 1) * LANES]
            one, two = fold_pair(block.astype(F32) * (SCALE if part == 0 else 1.0))
            r.pack[2 * pair, part * FOLD : (part + 1) * FOLD] = one.astype(BF)
            r.pack[2 * pair + 1, part * FOLD : (part + 1) * FOLD] = two.astype(BF)
    for copy in all_to_all(me, r.pack, r.got, r.out_sems, r.own_sems.at[0]):
        copy.wait()
    for s in range(PEERS):
        for part, target in enumerate((r.queries_sc, r.keys_sc, r.values_sc)):
            top, bottom = unfold_head(r.got[s, part * FOLD : (part + 1) * FOLD])
            target[s * FRAME : s * FRAME + FOLD] = top
            target[s * FRAME + FOLD : (s + 1) * FRAME] = bottom
        r.marks_sc[s : s + 1] = r.got[s, 3 * FOLD : 3 * FOLD + 1].astype(F32)
        r.marks_sc[PEERS + s : PEERS + s + 1] = r.got[s, 3 * FOLD + 1 : 3 * FOLD + 2].astype(F32)
    keys, values = r.keys_sc[...], r.values_sc[...]
    tags = jnp.concatenate([r.marks_sc[s : s + 1] for s in range(PEERS)], axis=1)
    sends = []
    own = None
    per = PEERS // GROUPS
    for j in range(GROUPS - 1, -1, -1):
        block = (me // per) ^ j
        at = pl.ds(pl.multiple_of(block * per * FRAME, per * FRAME), per * FRAME)
        scores = product_right(r.queries_sc[at], keys)
        tops, totals, shares = [], [], []
        for i in range(per):
            scene = r.marks_sc[pl.ds(PEERS + block * per + i, 1)][:, :1]
            row = scores[i * FRAME : (i + 1) * FRAME] + jnp.where(tags == scene, 0.0, NEG)
            tops.append(jnp.max(row, axis=-1, keepdims=True))
            row = jnp.exp(row - tops[-1])
            totals.append(jnp.sum(row, axis=-1, keepdims=True))
            shares.append(row.astype(BF))
        top, total = jnp.concatenate(tops, axis=0), jnp.concatenate(totals, axis=0)
        result = product(jnp.concatenate(shares, axis=0), values) / total
        r.outs_sc[at] = result
        r.lse_sc[:, at] = as_row(top + jnp.log(total))
        for i in range(per):
            r.answers[block * per + i] = fold_head(result[i * FRAME : (i + 1) * FRAME]).astype(BF)
        for k in range(j * per, (j + 1) * per):
            if k:
                copy = exchange(me, k, r.answers.at[me ^ k], r.back.at[me], r.back_sems)
            else:
                copy = pltpu.make_async_copy(r.answers.at[me], r.back.at[me], r.own_sems.at[1])
            copy.start()
            sends.append(copy)
    for copy in sends:
        copy.wait()
    for pair in range(width // LANES):
        top, bottom = unfold_pair(r.back[2 * pair].astype(F32), r.back[2 * pair + 1].astype(F32))
        att_ref[:FOLD, pair * LANES : (pair + 1) * LANES] = top.astype(BF)
        att_ref[FOLD:, pair * LANES : (pair + 1) * LANES] = bottom.astype(BF)


def head_backward(me, grad_ref, dqkv_ref, r, meanwhile):
    width = grad_ref.shape[1]
    for pair in range(width // LANES):
        one, two = fold_pair(grad_ref[:, pair * LANES : (pair + 1) * LANES].astype(F32))
        r.pack[2 * pair] = one.astype(BF)
        r.pack[2 * pair + 1] = two.astype(BF)
    copies = all_to_all(me, r.pack, r.got, r.out_sems, r.own_sems.at[0])
    lane = lax.broadcasted_iota(jnp.int32, (1, LANES), 1)

    def lanes(terms, value):
        for index, term in enumerate(terms):
            value = jnp.where(lane == HD + index, term, value)
        return value

    for s in range(PEERS):
        at = slice(s * FRAME, (s + 1) * FRAME)
        tag = as_column(r.marks_sc[s : s + 1])
        scene = r.marks_sc[PEERS + s : PEERS + s + 1, :1]
        blocked = [jnp.where(tag == mark, NEG, 0.0) for mark in (0.0, 1.0, -1.0)]
        r.keys_sc[at] = lanes(blocked + [1.0] * 3, r.keys_sc[at].astype(F32)).astype(BF)
        other = [jnp.where(scene == mark, 0.0, 1.0) for mark in (0.0, 1.0)]
        less = [-term.astype(F32) for term in terms_of(as_column(r.lse_sc[:, at]))]
        r.queries_sc[at] = lanes(other + [1.0] + less, r.queries_sc[at].astype(F32)).astype(BF)
        r.values_sc[at] = lanes([1.0] * 3, r.values_sc[at].astype(F32)).astype(BF)
    for copy in copies:
        copy.wait()
    for s in range(PEERS):
        at = slice(s * FRAME, (s + 1) * FRAME)
        grads = jnp.concatenate(unfold_head(r.got[s]), axis=0).astype(F32)
        delta = jnp.sum(grads * r.outs_sc[at], axis=-1, keepdims=True)
        less = [-term.astype(F32) for term in terms_of(delta)]
        r.grads_sc[at] = lanes(less, grads).astype(BF)
    queries, outs = r.queries_sc[...], r.grads_sc[...]
    query_grad = None
    sends = []
    per = PEERS // BACK_GROUPS
    for j in range(BACK_GROUPS - 1, -1, -1):
        block = (me // per) ^ j
        at = pl.ds(pl.multiple_of(block * per * FRAME, per * FRAME), per * FRAME)
        keys, values = r.keys_sc[at], r.values_sc[at]
        shares = jnp.exp(product_right(keys, queries))
        score_grad = (shares * product_right(values, outs)).astype(BF)
        value_grad = product(shares.astype(BF), outs)
        key_grad = product(score_grad, queries)
        turned = jnp.transpose(keys.astype(F32)).astype(BF)[:HD]
        piece = product(turned, score_grad)
        query_grad = piece if query_grad is None else query_grad + piece
        for i in range(per):
            part = slice(i * FRAME, (i + 1) * FRAME)
            r.pairs[block * per + i, :FOLD] = fold_head(key_grad[part]).astype(BF)
            r.pairs[block * per + i, FOLD:] = fold_head(value_grad[part]).astype(BF)
        for k in range(j * per, (j + 1) * per):
            if k:
                copy = exchange(me, k, r.pairs.at[me ^ k], r.pairs_in.at[me], r.pair_sems)
            else:
                copy = pltpu.make_async_copy(r.pairs.at[me], r.pairs_in.at[me], r.own_sems.at[1])
            copy.start()
            sends.append(copy)
    padded = jnp.concatenate([query_grad * SCALE, jnp.zeros_like(query_grad)], axis=0)
    for s in range(PEERS):
        block = jnp.transpose(padded[:, s * FRAME : (s + 1) * FRAME])
        r.asked[s] = fold_head(block).astype(BF)
    sends += all_to_all(me, r.asked, r.asked_in, r.back_sems, r.own_sems.at[2])
    meanwhile()
    for copy in sends:
        copy.wait()
    for pair in range(width // LANES):
        for part in range(3):
            if part == 0:
                one, two = r.asked_in[2 * pair], r.asked_in[2 * pair + 1]
            else:
                rows = slice((part - 1) * FOLD, part * FOLD)
                one, two = r.pairs_in[2 * pair, rows], r.pairs_in[2 * pair + 1, rows]
            top, bottom = unfold_pair(one.astype(F32), two.astype(F32))
            cols = slice(part * width + pair * LANES, part * width + (pair + 1) * LANES)
            dqkv_ref[:FOLD, cols] = top.astype(BF)
            dqkv_ref[FOLD:, cols] = bottom.astype(BF)


def tile_heads(source, target):
    lane = lax.broadcasted_iota(jnp.int32, (1, WIDE), 1)
    for layer in range(2):
        every = jnp.concatenate(
            [source[layer : layer + 1], jnp.zeros((1, WIDE - 3 * HD), F32)], axis=1
        )
        for index in range(3):
            one = jnp.where((lane >= index * HD) & (lane < (index + 1) * HD), every, 0.0)
            two = one + pltpu.roll(one, HD, 1)
            target[layer, index : index + 1] = two + pltpu.roll(two, 2 * HD, 1)
        target[layer, 3:] = jnp.zeros((5, WIDE), F32)


def begin_kernel(r):
    me, x_at = lax.axis_index("blk"), lax.axis_index("grp")
    partner = {"grp": 1 - x_at}
    peers_here = call_peers(me, partner)
    width, units = r.tok.shape[1], r.up_w.shape[2]
    mover = Mover(r.moves)
    loads = [
        mover.start(*pair)
        for pair in (
            (r.tok, r.tok_sc), (r.vectors, r.vectors_sc), (r.head_norm, r.head_norm_sc),
            (r.up_bias, r.up_bias_sc), (r.valid, r.valid_sc),
        )
    ]
    copies = weight_copies(
        column_pieces(r.qkv_w.at[0], 3)
        + [r.out_w.at[0]]
        + interleaved(column_pieces(r.up_w.at[0], 4), row_pieces(r.down_w.at[0], 4)),
        column_pieces(r.w_qkv, 3)
        + [r.w_out]
        + interleaved(column_pieces(r.w_up, 4), row_pieces(r.w_down, 4)),
        r.sems,
    )
    for copy in loads:
        copy.wait()
    tile_heads(r.head_norm_sc, r.head_rows_sc)
    position = lax.broadcasted_iota(jnp.int32, (1, FRAME), 1)
    valid = jnp.where((r.valid_sc[...] == 1) | (position < SPECIAL), 1.0, 0.0)
    r.usable_sc[...] = valid
    scene = r.smem_scene[0].astype(F32)
    row = lax.broadcasted_iota(jnp.int32, (EXTRA, FRAME), 0)
    tags = jnp.where(valid > 0, scene, -1.0)
    r.marks_in_sc[...] = jnp.where(row == 0, tags, jnp.where(row == 1, scene, 0.0)).astype(BF)
    mover.flush(r.head_rows_sc, r.head_rows)
    mover.flush(r.usable_sc, r.usable)
    residual = r.tok_sc[...].astype(F32)
    normed0, att0 = r.leftatt0_sc.at[:, :width], r.leftatt0_sc.at[:, width:]
    project(
        0, residual, r.vectors_sc, r.head_rows_sc, r.w_qkv, copies[:3], normed0, r.pre0_sc,
        r.qkv0_sc,
    )
    mover.flush(r.pre0_sc, r.pre0)
    mover.flush(r.qkv0_sc, r.qkv0)
    frame_attend(r.usable_sc[...], r.qkv0_sc, att0)
    next_copies = weight_copies(
        column_pieces(r.qkv_w.at[1], 3), column_pieces(r.w_qkv, 3), r.next_sems
    )
    mover.flush(r.leftatt0_sc, r.leftatt0)
    peers_here()
    sender = Sender(r.x_sems.at[0], r.x_sems.at[1], dict(x=partner))
    across = [sender.start(r.leftatt0_sc, r.leftatt0_x, "x")]
    lifted0, active0 = r.left0_sc.at[:, :width], r.left0_sc.at[:, width:]
    result = feed_forward(
        0, att0[...], residual, r.vectors_sc, r.up_bias_sc, r.w_out, r.w_up, r.w_down, copies[3:],
        r.mixed0_sc, r.middle0_sc, lifted0, r.slope0_sc, active0, r.feed0_sc,
    )
    r.res1_sc[...] = result
    for pair in (
        (r.left0_sc, r.left0), (r.mixed0_sc, r.mixed0), (r.middle0_sc, r.middle0),
        (r.slope0_sc, r.slope0), (r.feed0_sc, r.feed0), (r.res1_sc, r.res1),
    ):
        mover.flush(*pair)
    across.append(sender.start(r.left0_sc, r.left0_x, "x"))
    normed1, att1 = r.leftatt1_sc.at[:, :width], r.leftatt1_sc.at[:, width:]
    project(
        1, result, r.vectors_sc, r.head_rows_sc, r.w_qkv, next_copies, normed1, r.pre1_sc, r.qkv1_sc
    )
    mover.flush(r.pre1_sc, r.pre1)
    head_forward(me, r.qkv1_sc, r.marks_in_sc, att1, r)
    for pair in (
        (r.queries_sc, r.queries), (r.keys_sc, r.keys), (r.values_sc, r.values), (r.outs_sc, r.outs),
        (r.lse_sc, r.lse), (r.marks_sc, r.marks), (r.leftatt1_sc, r.leftatt1),
    ):
        mover.flush(*pair)
    for copy in across:
        copy.wait()
    mover.finish()


def begin(
    tokens, valid, scene, vectors, up_bias, head_norm, qkv_weight, out_weight, up_weight, down_weight
):
    rows, width = tokens.shape
    hidden = up_weight.shape[2]
    every = PEERS * FRAME
    loaded = dict(
        tok=tokens, vectors=vectors, head_norm=head_norm, up_bias=up_bias,
        valid=valid,
    )
    stored = dict(
        left0=((rows, hidden + width), BF),
        leftatt0=((rows, 2 * width), BF),
        pre0=((rows, 2 * width), F32),
        qkv0=((rows, 3 * width), BF),
        mixed0=((rows, width), F32),
        middle0=((rows, width), F32),
        slope0=((rows, hidden), F32),
        feed0=((rows, width), F32),
        res1=((rows, width), F32),
        leftatt1=((rows, 2 * width), BF),
        pre1=((rows, 2 * width), F32),
        queries=((every, LANES), BF),
        keys=((every, LANES), BF),
        values=((every, LANES), BF),
        outs=((every, LANES), F32),
        lse=((1, every), F32),
        marks=((2 * PEERS, LANES), F32),
        head_rows=((2, 8, WIDE), F32),
        usable=((1, rows), F32),
    )
    return named_call(
        begin_kernel,
        dict(
            smem_scene=scene, **loaded, qkv_w=qkv_weight, out_w=out_weight,
            up_w=up_weight, down_w=down_weight,
        ),
        dict(
            **{key: (*value, True) for key, value in stored.items()},
            leftatt0_x=((rows, 2 * width), BF, True),
            left0_x=((rows, hidden + width), BF, True),
        ),
        dict(
            **{key + "_sc": pltpu.VMEM(value.shape, value.dtype) for key, value in loaded.items()},
            **{key + "_sc": pltpu.VMEM(*value) for key, value in stored.items()},
            marks_in_sc=low(EXTRA, FRAME),
            qkv1_sc=low(rows, 3 * width),
            w_qkv=low(width, 3 * width),
            w_out=low(width, width),
            w_up=low(width, hidden),
            w_down=low(hidden, width),
            pack=low(PEERS, 3 * FOLD + EXTRA, LANES),
            got=low(PEERS, 3 * FOLD + EXTRA, LANES),
            answers=low(PEERS, FOLD, LANES),
            back=low(PEERS, FOLD, LANES),
            sems=pltpu.SemaphoreType.DMA((12,)),
            next_sems=pltpu.SemaphoreType.DMA((3,)),
            moves=pltpu.SemaphoreType.DMA((5 + len(stored),)),
            own_sems=pltpu.SemaphoreType.DMA((2,)),
            out_sems=pltpu.SemaphoreType.DMA((2, PEERS)),
            back_sems=pltpu.SemaphoreType.DMA((2, PEERS)),
            x_sems=pltpu.SemaphoreType.DMA((2, 2)),
        ),
        60,
        pl.CostEstimate(
            flops=2 * rows * width * (7 * width + 2 * hidden) + 4 * every * every * LANES,
            bytes_accessed=2 * width * (7 * width + 2 * hidden),
            transcendentals=2 * rows * hidden + every * every,
        ),
        "begin",
        collective_id=1,
    )


def middle_kernel(r):
    me, x_at = lax.axis_index("blk"), lax.axis_index("grp")
    c_at, y_at, z0, z1 = [lax.rem(me // (1 << bit), 2) for bit in range(4)]
    partners = {"x": {"grp": 1 - x_at}, "c": {"blk": me ^ 1}}
    peers_here = call_peers(me, partners["x"])
    sender = Sender(r.ring_sems.at[0], r.ring_sems.at[1], partners)
    rows, width = r.res.shape
    units = r.up_w.shape[2]
    mover = Mover(r.moves)
    loads = [
        mover.start(*pair)
        for pair in (
            (r.vectors, r.vectors_sc), (r.leftatt1, r.leftatt1_sc), (r.res, r.res_sc),
            (r.up_bias, r.up_bias_sc), (r.cot, r.cot_sc),
        )
    ]
    copies = weight_copies(
        [r.out_w.at[1]]
        + interleaved(column_pieces(r.up_w.at[1], 4), row_pieces(r.down_w.at[1], 4)),
        [r.w_out] + interleaved(column_pieces(r.w_up, 4), row_pieces(r.w_down, 4)),
        r.sems,
    )
    late_loads = [
        mover.start(*pair)
        for pair in (
            (r.queries, r.queries_sc), (r.keys, r.keys_sc), (r.values, r.values_sc),
            (r.outs, r.outs_sc), (r.lse, r.lse_sc), (r.marks, r.marks_sc),
        )
    ]
    for copy in loads:
        copy.wait()
    own, mate = slice(0, rows), slice(rows, 2 * rows)
    quarter = units // 4
    lefts = []

    def done(j, active):
        for block in range(active.shape[1] // (2 * LANES)):
            for x in range(2):
                start = (2 * block + x) * LANES
                at = (j * active.shape[1] // 2) + block * LANES
                r.act_sc[x, :, at : at + LANES] = active[:, start : start + LANES]
        if j == 0:
            peers_here()
            lefts.append(
                sender.start(r.left_sc.at[own, :width], r.left_sc.at[mate, :width], "x")
            )
        filled = (j + 1) * active.shape[1] // 2
        if filled % quarter == 0:
            at = slice(filled - quarter, filled)
            to = slice(width + filled - quarter, width + filled)
            lefts.append(
                sender.start(r.act_sc.at[1 - x_at, :, at], r.left_sc.at[mate, to], "x")
            )

    result = feed_forward(
        1, r.leftatt1_sc[:, width:], r.res_sc[...], r.vectors_sc, r.up_bias_sc, r.w_out, r.w_up,
        r.w_down, copies, r.mixed_sc, r.middle_sc, r.left_sc.at[own, :width], r.slope_sc, None,
        r.feed_sc, done,
    )
    r.left_sc[own, width:] = r.act_sc[x_at]
    left_c = sender.start(r.left_sc.at[own], r.left_sc.at[2 * rows : 3 * rows], "c")
    r.output_sc[...] = result.astype(BF)
    mover.flush(r.output_sc, r.output)
    grad = feed_backward(
        1, r.cot_sc[...].astype(F32), r.feed_sc[...], r.middle_sc[...], r.mixed_sc[...],
        r.slope_sc, r.vectors_sc, r.w_up, r.w_down, None, r.fg_sc, r.hg_sc, r.mg_sc, r.bias_out,
        r.rows_out, 0,
    )
    half, part = units // 2, width // 2

    def columns(ref, start, count):
        return ref.at[:, pl.ds(pl.multiple_of(start, LANES), count)]

    rights = [
        sender.start(columns(r.hg_sc, (1 - x_at) * half, half), r.far_sc.at[:, :half], "x"),
        sender.start(r.fg_sc, r.far_sc.at[:, half:], "x"),
    ]
    mixed_x = sender.start(columns(r.mg_sc, (1 - x_at) * part, part), r.mixed1_x, "x")
    q_up, q_down = half // 2, part
    ready = [left_c]

    def place(up, down, up_at, down_at, index):
        here = slice(index * rows, (index + 1) * rows)
        there = slice((2 + index) * rows, (3 + index) * rows)
        for ref, start, count, to in ((up, up_at, q_up, 0), (down, down_at, q_down, q_up)):
            ready.append(
                mover.start(
                    columns(ref, start + c_at * count, count), r.right_sc.at[here, to : to + count]
                )
            )
            ready.append(
                sender.start(
                    columns(ref, start + (1 - c_at) * count, count),
                    r.right_sc.at[there, to : to + count],
                    "c",
                )
            )

    place(r.hg_sc, r.fg_sc, x_at * half, 0, 0)
    mover.flush(columns(r.mg_sc, x_at * part, part), r.mixed1)
    r.middle_grad_sc[...] = grad
    mover.flush(r.middle_grad_sc, r.middle_grad)
    r.att_grad_sc[...] = product_right(r.mg_sc[...], r.w_out[...]).astype(BF)
    for copy in late_loads:
        copy.wait()

    def meanwhile():
        for copy in lefts:
            copy.wait_recv()
        ready.append(
            sender.start(r.left_sc.at[mate], r.left_sc.at[3 * rows : 4 * rows], "c")
        )

    head_backward(me, r.att_grad_sc, r.dqkv_sc, r, meanwhile)
    mover.flush(r.dqkv_sc, r.dqkv)
    for copy in rights:
        copy.wait_recv()
    place(r.far_sc, r.far_sc, 0, half, 1)
    for copy in ready:
        copy.wait_recv()
    for slot in range(OUTER):
        target = (r.away_up_sc if slot < 2 else r.stay_up_sc).at[slot % 2]

        def emit(target, y, row, col, values):
            height, wide = values.shape
            target[y, row : row + height, col : col + wide] = values

        group = slot_group(slot, z0, z1)
        slot_product(
            group, r.left_sc, 0, r.right_sc, 0, q_up, False, functools.partial(emit, target)
        )
        for y in range(2):
            start = pl.multiple_of(width + (2 * group + y) * 2 * BLOCK, BLOCK)
            result = product_left(
                r.left_sc[:, pl.ds(start, 2 * BLOCK)], r.right_sc[:, q_up:]
            ).astype(BF)
            piece = BLOCK // 2
            for c in range(2):
                for t in range(2):
                    row = (2 * c + t) * piece
                    emit(r.down_sc.at[slot], y, c * piece, t * q_down, result[row : row + piece])
        if slot == 1:
            mover.flush(r.away_up_sc, r.away_up)
    mover.flush(r.down_sc.at[:, 1 - y_at], r.away_down)
    mover.flush(r.down_sc.at[:, y_at], r.stay_down)
    mover.flush(r.stay_up_sc, r.stay_up)
    mixed_x.wait_recv()
    assert len(sender.copies) == r.ring_sems.shape[1]
    sender.finish()
    mover.finish()


def middle(first, cotangent, vectors, up_bias, out_weight, up_weight, down_weight):
    rows, width = cotangent.shape
    hidden = up_weight.shape[2]
    every = PEERS * FRAME
    loaded = dict(
        vectors=vectors, leftatt1=first.leftatt1, res=first.res1, up_bias=up_bias,
        cot=cotangent, queries=first.queries, keys=first.keys, values=first.values,
        outs=first.outs, lse=first.lse, marks=first.marks,
    )
    columns = hidden // 4
    stored = dict(
        output=((rows, width), BF),
        middle_grad=((rows, width), F32),
        dqkv=((rows, 3 * width), BF),
        stay_up=((2, 2, BLOCK, columns), BF),
        away_up=((2, 2, BLOCK, columns), BF),
    )
    return named_call(
        middle_kernel,
        dict(
            **loaded, out_w=out_weight, up_w=up_weight, down_w=down_weight,
        ),
        dict(
            **{key: (*value, True) for key, value in stored.items()},
            stay_down=((OUTER, BLOCK, columns), BF, True),
            away_down=((OUTER, BLOCK, columns), BF, True),
            mixed1=((rows, width // 2), BF, True),
            mixed1_x=((rows, width // 2), BF, True),
            bias_out=((1, hidden), F32, False),
            rows_out=((8, width), F32, False),
        ),
        dict(
            **{key + "_sc": pltpu.VMEM(value.shape, value.dtype) for key, value in loaded.items()},
            **{key + "_sc": pltpu.VMEM(*value) for key, value in stored.items()},
            w_out=low(width, width),
            w_up=low(width, hidden),
            w_down=low(hidden, width),
            left_sc=low(4 * rows, hidden // 2 + width),
            act_sc=low(2, rows, hidden // 2),
            down_sc=low(OUTER, 2, BLOCK, columns),
            right_sc=low(4 * rows, hidden // 4 + width // 2),
            far_sc=low(rows, hidden // 2 + width),
            mixed_sc=full(rows, width),
            middle_sc=full(rows, width),
            slope_sc=full(rows, hidden),
            feed_sc=full(rows, width),
            fg_sc=low(rows, width),
            hg_sc=low(rows, hidden),
            mg_sc=low(rows, width),
            att_grad_sc=low(rows, width),
            grads_sc=low(every, LANES),
            pack=low(PEERS, FOLD, LANES),
            got=low(PEERS, FOLD, LANES),
            pairs=low(PEERS, 2 * FOLD, LANES),
            pairs_in=low(PEERS, 2 * FOLD, LANES),
            asked=low(PEERS, FOLD, LANES),
            asked_in=low(PEERS, FOLD, LANES),
            sems=pltpu.SemaphoreType.DMA((9,)),
            moves=pltpu.SemaphoreType.DMA((23,)),
            own_sems=pltpu.SemaphoreType.DMA((3,)),
            out_sems=pltpu.SemaphoreType.DMA((2, PEERS)),
            back_sems=pltpu.SemaphoreType.DMA((2, PEERS)),
            pair_sems=pltpu.SemaphoreType.DMA((2, PEERS)),
            ring_sems=pltpu.SemaphoreType.DMA((2, 12)),
        ),
        60,
        pl.CostEstimate(
            flops=4 * rows * width * (width + 2 * hidden) + 10 * every * every * LANES,
            bytes_accessed=2 * width * (width + 2 * hidden),
            transcendentals=2 * rows * hidden + every * every,
        ),
        "middle",
        collective_id=2,
    )


def per_device(
    tokens,
    qkv_weight,
    out_weight,
    up_weight,
    down_weight,
    vectors,
    up_bias,
    head_norm,
    token_valid,
    frame_scene,
    cotangent,
):
    count = lax.axis_size("blk")
    outer = count // 4
    me = lax.axis_index("blk")
    x_at = lax.axis_index("grp")
    c_at = lax.rem(me, 2)
    y_at = lax.rem(me // 2, 2)
    c_pairs = [(i, i ^ 1) for i in range(count)]
    y_pairs = [(i, i ^ 2) for i in range(count)]
    z_groups = [[4 * o + k for o in range(outer)] for k in range(4)]
    halves_at = jnp.stack([x_at, x_at]).astype(jnp.int32)
    places = jnp.stack(
        [c_at, y_at, x_at, lax.rem(me // 4, 2), lax.rem(me // 8, 2), halves_at[1], me]
    ).astype(jnp.int32)


    def swap_x(value):
        return lax.ppermute(value, "grp", [(0, 1), (1, 0)])

    def swap_c(value):
        return lax.ppermute(value, "blk", c_pairs)

    def swap_y(value):
        return lax.ppermute(value, "blk", y_pairs)

    def part(value, index, parts, axis):
        size = value.shape[axis] // parts
        return lax.dynamic_slice_in_dim(value, index * size, size, axis)

    def tied(value, *others):
        return lax.optimization_barrier((value, *others))

    def ready_sum(keep, arrived):
        return (keep.astype(F32) + arrived.astype(F32)).astype(BF)

    def scattered(own):
        return lax.psum_scatter(
            own, "blk", scatter_dimension=0, tiled=True, axis_index_groups=z_groups
        )

    def finished(total):
        pair = jnp.stack([part(total, c_at, 2, 0), swap_c(part(total, 1 - c_at, 2, 0))])
        return jnp.concatenate([pair, swap_x(pair)], axis=0)

    def total_of(value):
        value = value + swap_x(value)
        step = 1
        while step < count:
            pairs = [(i, i ^ step) for i in range(count)]
            value = value + lax.ppermute(value, "blk", pairs)
            step *= 2
        return value

    row_count, width = tokens.shape[1:]
    hidden = up_weight.shape[2]
    if count == HEADS:
        first = begin(
            tokens[0], token_valid[0], frame_scene[0], vectors, up_bias, head_norm, qkv_weight,
            out_weight, up_weight, down_weight,
        )
        head_rows, usable_row = first.head_rows, first.usable
        second = middle(
            first, cotangent[0], vectors, up_bias, out_weight, up_weight, down_weight
        )
        came_up = lax.ppermute(second.away_up, "blk", [(i, i ^ 4) for i in range(count)])
        came_down, leftatt1_x = swap_y(second.away_down), swap_x(first.leftatt1)
        pre0, qkv0, mixed0, middle0, slope0, feed0, res1, pre1 = (
            first.pre0, first.qkv0, first.mixed0, first.middle0, first.slope0, first.feed0,
            first.res1, first.pre1,
        )
        output, middle_grad1, dqkv1, bias1, rows1 = (
            second.output, second.middle_grad, second.dqkv, second.bias_out, second.rows_out
        )
    else:
        position = lax.broadcasted_iota(jnp.int32, (row_count,), 0)
        usable = (token_valid[0, 0] == 1) | (position < SPECIAL)
        usable_row = usable.astype(F32).reshape(1, row_count)
        scene = frame_scene[0, 0].astype(F32)
        tag_rows = jnp.where(usable, scene, -1.0)
        head_rows = jnp.tile(head_norm.reshape(2, 3, HD), (1, 1, WIDE // HD))
        head_rows = jnp.concatenate([head_rows, jnp.zeros((2, 5, WIDE), F32)], axis=1)
        left0, leftatt0, pre0, qkv0, mixed0, middle0, slope0, feed0, res1, normed1, pre1, qkv1 = (
            front(
                tokens[0], usable_row, vectors, up_bias, head_rows, qkv_weight, out_weight,
                up_weight, down_weight,
            )
        )
        att1, kept = gathered_forward(qkv1, tag_rows, scene)
        left1, leftatt1, output, right1, right1_send, att_grad1, middle_grad1, bias1, rows1 = turn(
            halves_at, att1, normed1, res1, cotangent[0], vectors, up_bias, out_weight, up_weight,
            down_weight,
        )
        dqkv1 = gathered_backward(att_grad1, kept, tag_rows, scene)
    third = back_one(
        halves_at, dqkv1, pre1, res1, middle_grad1, feed0, middle0, mixed0, slope0, vectors,
        head_rows, qkv_weight, up_weight, down_weight,
    )
    frame = dict(
        mixed_grad=third.mixed_grad, grad=third.middle_grad, qkv=qkv0, pre=pre0, tok=tokens[0],
        usable=usable_row, vectors=vectors, head_rows=head_rows, rows10=third.rows_out, rows1=rows1,
        bias0=third.bias_out, bias1=bias1, heads1=third.head_out, out_w=out_weight, qkv_w=qkv_weight,
    )

    def feed_grads(name, lefts, rights):
        return weight_grads(
            name,
            outer,
            width,
            places,
            [
                (lefts, 0, width, rights, 0, hidden // 2, False),
                (lefts, width, hidden, rights, hidden // 2, width // 2, True),
            ],
        )

    def att_grads(name, lefts, projected, rights, at):
        return weight_grads(
            name,
            outer,
            width,
            places,
            [
                (lefts, 0, width, projected, 0, 3 * width // 2, False),
                (lefts, width, width, rights, at, width // 2, False),
            ],
        )

    def four(own, far):
        return (own, far, swap_c(own), swap_c(far))

    def reduce_apart(fourth):
        pg1_x, right0_far = swap_x(third.pg_send), swap_x(third.right_send)
        pg0_all = four(fourth.pg_keep, swap_x(fourth.pg_send))
        right1_all = four(right1, swap_x(right1_send))
        results = []
        for keep, send in (
            feed_grads(
                "feed_grads0", four(left0, swap_x(left0)), four(third.right_keep, right0_far)
            ),
            att_grads(
                "att_grads0", four(leftatt0, swap_x(leftatt0)), pg0_all, pg0_all, 3 * width // 2
            ),
            feed_grads("feed_grads1", four(left1, swap_x(left1)), right1_all),
            att_grads(
                "att_grads1", four(leftatt1, swap_x(leftatt1)), four(third.pg_keep, pg1_x),
                right1_all, (hidden + width) // 2,
            ),
        ):
            results.append(finished(scattered(ready_sum(keep, swap_y(send)))))
        return results

    if count == HEADS:
        fourth = finish_all(
            frame,
            (second.stay_up, came_up),
            (second.stay_down, came_down),
            (
                first.leftatt1, leftatt1_x, third.pg_keep, third.pg_send, second.mixed1,
                second.mixed1_x,
            ),
            (first.left0, first.left0_x, third.right_keep, third.right_send),
            (first.leftatt0, first.leftatt0_x),
        )
        pieces = [fourth.f0_out, fourth.a0_out, fourth.f1_out, fourth.a1_out]
        small = fourth.small_out
    else:
        fourth = back_two(halves_at, **frame)
        small = total_of(fourth.small)
        pieces = reduce_apart(fourth)
    weight_shapes = [
        (2, width // count, 3 * width),
        (2, width // count, width),
        (2, width // count, up_weight.shape[2]),
        (2, up_weight.shape[2] // count, width),
    ]
    vector_count = vectors.shape[1]
    if count == HEADS:
        small_shapes = [(2, vector_count, HD), (2, hidden // count), (2, 3 * HD)]
        qkv_grad, out_grad, up_grad, down_grad, vector_grad, bias_grad, head_grad = assemble(
            places, [*pieces, small], weight_shapes + small_shapes
        )
    else:
        qkv_grad, out_grad, up_grad, down_grad = assemble(places, pieces, weight_shapes)
        bias_rows = 2 * hidden // width
        vector_grad = part(small[: 2 * vector_count].reshape(2, -1, width), me, count, 2)
        bias_grad = small[2 * vector_count : 2 * vector_count + bias_rows].reshape(2, hidden)
        bias_grad = part(bias_grad, me, count, 1)
        head_grad = small[2 * vector_count + bias_rows, : 6 * HD].reshape(2, 3 * HD)
    return (
        output[None],
        fourth.input_grad[None],
        qkv_grad,
        out_grad,
        up_grad,
        down_grad,
        vector_grad,
        bias_grad,
        head_grad,
    )


def gathered_forward(qkv, tag_rows, scene):
    rows, width = qkv.shape[0], qkv.shape[1] // 3
    marks = jnp.zeros((KEEP, 2 * width), BF)
    marks = marks.at[0, :rows].set(tag_rows.astype(BF))
    marks = marks.at[1, :rows].set(jnp.full((rows,), scene).astype(BF))
    pairs = lax.all_gather(
        jnp.concatenate([qkv[:, width:], marks], axis=0), "blk", axis=0, tiled=False
    )
    tags = pairs[:, FRAME, :FRAME].astype(F32).reshape(1, -1)
    scenes = pairs[:, FRAME + 1, :FRAME].astype(F32).reshape(1, -1)
    queries = qkv[:, :width]
    attended, lse = global_attend(queries, pairs, tags, jnp.full((8, LANES), scene))
    every_query = lax.all_gather(
        with_rows(queries, lse.reshape(HEADS, rows)), "blk", axis=0, tiled=False
    )
    return attended.astype(BF), (qkv, pairs, tags, scenes, attended, lse, every_query)


def gathered_backward(attended_grad, kept, tag_rows, scene):
    qkv, pairs, tags, scenes, attended, lse, every_query = kept
    rows, width = attended_grad.shape
    delta = jnp.sum(
        (attended_grad.astype(F32) * attended).reshape(rows, HEADS, HD), axis=-1
    ).T
    every_grad = lax.all_gather(with_rows(attended_grad, delta), "blk", axis=0, tiled=False)
    query_grad = global_query_grad(
        qkv[:, :width],
        pairs,
        tags,
        jnp.full((8, LANES), scene),
        attended_grad,
        lse,
        delta.reshape(PAIRS, 2, rows),
    )
    key_grad, value_grad = global_key_grad(
        qkv[:, width : 2 * width],
        qkv[:, 2 * width :],
        tag_rows.reshape(1, rows),
        scenes,
        every_query,
        every_grad,
        rows_of(every_query, width),
        rows_of(every_grad, width),
    )
    return jnp.concatenate([query_grad, key_grad, value_grad], axis=1).astype(BF)


def solution(mesh):
    return jax.shard_map(
        per_device,
        mesh=mesh,
        in_specs=(
            P("grp", "blk", None),
            P(),
            P(),
            P(),
            P(),
            P(),
            P(),
            P(),
            P("grp", "blk", None),
            P("grp", "blk"),
            P("grp", "blk", None),
        ),
        out_specs=(
            P("grp", "blk", None),
            P("grp", "blk", None),
            P(None, "blk", None),
            P(None, "blk", None),
            P(None, "blk", None),
            P(None, "blk", None),
            P(None, None, "blk"),
            P(None, "blk"),
            P(),
        ),
        check_vma=False,
    )
```

```python
import functools
import types
from itertools import chain

import jax
import jax.numpy as jnp
from jax import lax
from jax.experimental import pallas as pl
from jax.experimental.pallas import tpu as pltpu
from jax.sharding import PartitionSpec as P

HEADS = 16
HD = 64
SPECIAL = 5
PAIRS = HEADS // 2
LANES = 2 * HD
FRAME = 128
KEEP = 16
EPS = 1e-06
NEG = -1e30
SCALE = HD**-0.5
BF = jnp.bfloat16
F32 = jnp.float32


def product(left_side, right_side):
    return jnp.dot(left_side, right_side, preferred_element_type=F32)


def product_left(left_side, right_side):
    return lax.dot_general(
        left_side, right_side, (((0,), (0,)), ((), ())), preferred_element_type=F32
    )


def product_right(left_side, right_side):
    return lax.dot_general(
        left_side, right_side, (((1,), (1,)), ((), ())), preferred_element_type=F32
    )


def lane_masks(dtype):
    lane = lax.broadcasted_iota(jnp.int32, (1, LANES), 1)
    first = (lane < HD).astype(dtype)
    return (first, 1 - first)


def as_column(row):
    size = row.shape[1]
    return jnp.transpose(jnp.broadcast_to(row, (LANES, size)))[:, :1]


def as_row(column):
    size = column.shape[0]
    return jnp.transpose(jnp.broadcast_to(column, (size, LANES)))[:1, :]


def flat(ref):
    block = ref[...]
    return block.reshape(block.shape[0] * block.shape[1], block.shape[2])


def attend_kernel(blocks, q_ref, k_ref, v_ref, tag_ref, scene_ref, o_ref, lse_ref, m_sc, l_sc, a_sc):
    step = pl.program_id(1)
    keys, values = flat(k_ref), flat(v_ref)
    allowed = tag_ref[...] == scene_ref[:1, :1]
    queries = q_ref[...]
    pieces = []
    for index, mask in enumerate(lane_masks(BF)):
        scores = product_right(queries * mask, keys) * SCALE
        scores = jnp.where(allowed, scores, NEG)
        top = jnp.max(scores, axis=-1, keepdims=True)

        if blocks > 1:

            @pl.when(step == 0)
            def _():
                m_sc[index] = jnp.full_like(m_sc[index], NEG)
                l_sc[index] = jnp.zeros_like(l_sc[index])
                a_sc[index] = jnp.zeros_like(a_sc[index])

            old = m_sc[index][:, :1]
            top = jnp.maximum(top, old)
            keep = jnp.exp(old - top)
        shares = jnp.where(allowed, jnp.exp(scores - top), 0.0)
        total = jnp.sum(shares, axis=-1, keepdims=True)
        weighted = product(shares.astype(BF), values)
        if blocks > 1:
            total = total + keep * l_sc[index][:, :1]
            weighted = weighted + keep * a_sc[index]
            m_sc[index] = jnp.broadcast_to(top, m_sc[index].shape)
            l_sc[index] = jnp.broadcast_to(total, l_sc[index].shape)
            a_sc[index] = weighted
        pieces.append(weighted / total)
        lse_ref[0, index : index + 1, :] = as_row(top + jnp.log(total))
    first, second = lane_masks(F32)
    o_ref[...] = jnp.where(first > 0, pieces[0], pieces[1])


def key_block(count):
    for size in (16, 8, 4, 2, 1):
        if count % size == 0:
            return size


def global_attend(queries, pairs, tags, scene):
    frames = pairs.shape[0]
    group = key_block(frames)
    blocks = frames // group
    return pl.pallas_call(
        functools.partial(attend_kernel, blocks),
        grid=(PAIRS, blocks),
        in_specs=[
            pl.BlockSpec((FRAME, LANES), lambda p, k: (0, p)),
            pl.BlockSpec((group, FRAME, LANES), lambda p, k: (k, 0, p)),
            pl.BlockSpec((group, FRAME, LANES), lambda p, k: (k, 0, PAIRS + p)),
            pl.BlockSpec((1, group * FRAME), lambda p, k: (0, k)),
            pl.BlockSpec((8, LANES), lambda p, k: (0, 0)),
        ],
        out_specs=[
            pl.BlockSpec((FRAME, LANES), lambda p, k: (0, p)),
            pl.BlockSpec((1, 2, FRAME), lambda p, k: (p, 0, 0)),
        ],
        out_shape=[
            jax.ShapeDtypeStruct((FRAME, PAIRS * LANES), F32),
            jax.ShapeDtypeStruct((PAIRS, 2, FRAME), F32),
        ],
        scratch_shapes=[pltpu.VMEM((2, FRAME, LANES), F32)] * 3,
        compiler_params=pltpu.CompilerParams(vmem_limit_bytes=48 * 2**20),
        cost_estimate=pl.CostEstimate(
            flops=4 * FRAME * frames * FRAME * LANES * HEADS,
            bytes_accessed=frames * FRAME * 4096,
            transcendentals=FRAME * frames * FRAME * HEADS,
        ),
        name="global_attend",
    )(queries, pairs, pairs, tags, scene)


def query_grad_kernel(
    q_ref, k_ref, v_ref, tag_ref, scene_ref, do_ref, lse_ref, delta_ref, dq_ref
):
    step = pl.program_id(1)
    keys, values = flat(k_ref), flat(v_ref)
    allowed = tag_ref[...] == scene_ref[:1, :1]
    queries, outs = q_ref[...], do_ref[...]
    pieces = []
    for index, mask in enumerate(lane_masks(BF)):
        scores = product_right(queries * mask, keys) * SCALE
        top = as_column(lse_ref[0, index : index + 1, :])
        delta = as_column(delta_ref[0, index : index + 1, :])
        shares = jnp.where(allowed, jnp.exp(scores - top), 0.0)
        share_grad = product_right(outs * mask, values)
        score_grad = (shares * (share_grad - delta)).astype(BF)
        pieces.append(product(score_grad, keys) * SCALE)
    first, second = lane_masks(F32)
    piece = jnp.where(first > 0, pieces[0], pieces[1])

    @pl.when(step == 0)
    def _():
        dq_ref[...] = piece

    @pl.when(step > 0)
    def _():
        dq_ref[...] += piece


def global_query_grad(queries, pairs, tags, scene, outs, lse, delta):
    frames = pairs.shape[0]
    group = key_block(frames)
    blocks = frames // group
    return pl.pallas_call(
        query_grad_kernel,
        grid=(PAIRS, blocks),
        in_specs=[
            pl.BlockSpec((FRAME, LANES), lambda p, k: (0, p)),
            pl.BlockSpec((group, FRAME, LANES), lambda p, k: (k, 0, p)),
            pl.BlockSpec((group, FRAME, LANES), lambda p, k: (k, 0, PAIRS + p)),
            pl.BlockSpec((1, group * FRAME), lambda p, k: (0, k)),
            pl.BlockSpec((8, LANES), lambda p, k: (0, 0)),
            pl.BlockSpec((FRAME, LANES), lambda p, k: (0, p)),
            pl.BlockSpec((1, 2, FRAME), lambda p, k: (p, 0, 0)),
            pl.BlockSpec((1, 2, FRAME), lambda p, k: (p, 0, 0)),
        ],
        out_specs=pl.BlockSpec((FRAME, LANES), lambda p, k: (0, p)),
        out_shape=jax.ShapeDtypeStruct((FRAME, PAIRS * LANES), F32),
        compiler_params=pltpu.CompilerParams(vmem_limit_bytes=48 * 2**20),
        cost_estimate=pl.CostEstimate(
            flops=6 * FRAME * frames * FRAME * LANES * HEADS,
            bytes_accessed=frames * FRAME * 4096,
            transcendentals=FRAME * frames * FRAME * HEADS,
        ),
        name="global_query_grad",
    )(queries, pairs, pairs, tags, scene, outs, lse, delta)


def key_grad_kernel(
    k_ref, v_ref, tag_ref, scene_ref, q_ref, do_ref, lse_ref, delta_ref, dk_ref, dv_ref
):
    step = pl.program_id(1)
    keys, values = k_ref[...], v_ref[...]
    queries, outs = flat(q_ref), flat(do_ref)
    allowed = as_column(tag_ref[...]) == scene_ref[...]
    key_pieces, value_pieces = [], []
    for index, mask in enumerate(lane_masks(BF)):
        scores = product_right(keys * mask, queries) * SCALE
        top = lse_ref[0, index : index + 1, :]
        delta = delta_ref[0, index : index + 1, :]
        shares = jnp.where(allowed, jnp.exp(scores - top), 0.0)
        share_grad = product_right(values * mask, outs)
        score_grad = (shares * (share_grad - delta)).astype(BF)
        key_pieces.append(product(score_grad, queries) * SCALE)
        value_pieces.append(product(shares.astype(BF), outs))
    first, second = lane_masks(F32)
    key_piece = jnp.where(first > 0, key_pieces[0], key_pieces[1])
    value_piece = jnp.where(first > 0, value_pieces[0], value_pieces[1])

    @pl.when(step == 0)
    def _():
        dk_ref[...] = key_piece
        dv_ref[...] = value_piece

    @pl.when(step > 0)
    def _():
        dk_ref[...] += key_piece
        dv_ref[...] += value_piece


def global_key_grad(keys, values, tags, scenes, queries, outs, lse, delta):
    frames = queries.shape[0]
    group = key_block(frames)
    blocks = frames // group
    return pl.pallas_call(
        key_grad_kernel,
        grid=(PAIRS, blocks),
        in_specs=[
            pl.BlockSpec((FRAME, LANES), lambda p, k: (0, p)),
            pl.BlockSpec((FRAME, LANES), lambda p, k: (0, p)),
            pl.BlockSpec((1, FRAME), lambda p, k: (0, 0)),
            pl.BlockSpec((1, group * FRAME), lambda p, k: (0, k)),
            pl.BlockSpec((group, FRAME, LANES), lambda p, k: (k, 0, p)),
            pl.BlockSpec((group, FRAME, LANES), lambda p, k: (k, 0, p)),
            pl.BlockSpec((1, 2, group * FRAME), lambda p, k: (p, 0, k)),
            pl.BlockSpec((1, 2, group * FRAME), lambda p, k: (p, 0, k)),
        ],
        out_specs=[pl.BlockSpec((FRAME, LANES), lambda p, k: (0, p))] * 2,
        out_shape=[jax.ShapeDtypeStruct((FRAME, PAIRS * LANES), F32)] * 2,
        compiler_params=pltpu.CompilerParams(vmem_limit_bytes=48 * 2**20),
        cost_estimate=pl.CostEstimate(
            flops=8 * FRAME * frames * FRAME * LANES * HEADS,
            bytes_accessed=frames * FRAME * 4096,
            transcendentals=FRAME * frames * FRAME * HEADS,
        ),
        name="global_key_grad",
    )(keys, values, tags, scenes, queries, outs, lse, delta)


def split_three(values):
    high = values.astype(BF)
    rest = values - high.astype(F32)
    middle = rest.astype(BF)
    return jnp.stack([high, middle, (rest - middle.astype(F32)).astype(BF)])


def with_rows(body, statistic):
    width = body.shape[1]
    extra = split_three(statistic).reshape(-1, width)
    pad = jnp.zeros((KEEP - extra.shape[0], width), BF)
    return jnp.concatenate([body, extra, pad], axis=0)


def rows_of(gathered, width):
    frames = gathered.shape[0]
    used = 3 * HEADS * FRAME // width
    terms = gathered[:, FRAME : FRAME + used].reshape(frames, 3, HEADS, FRAME).astype(F32)
    total = terms[:, 0] + terms[:, 1] + terms[:, 2]
    return total.transpose(1, 0, 2).reshape(PAIRS, 2, frames * FRAME)


VMEM_MIB = 2**20
WIDE = 256
ROOT_HALF = 0.7071067811865476
ROOT_TWO_PI = 0.3989422804014327


def whole(space=pltpu.VMEM):
    return pl.BlockSpec(memory_space=space)


def terms_of(values):
    high = values.astype(BF)
    rest = values - high.astype(F32)
    middle = rest.astype(BF)
    return (high, middle, (rest - middle.astype(F32)).astype(BF))


def head_averager():
    row = lax.broadcasted_iota(jnp.int32, (WIDE, WIDE), 0) // HD
    col = lax.broadcasted_iota(jnp.int32, (WIDE, WIDE), 1) // HD
    return jnp.where(row == col, 1.0 / HD, 0.0).astype(BF)


def head_mean(values, averager):
    high = values.astype(BF)
    rest = (values - high.astype(F32)).astype(BF)
    return product(high, averager) + product(rest, averager)


def standard(values):
    centered = values - jnp.mean(values, axis=-1, keepdims=True)
    scale = lax.rsqrt(jnp.mean(centered * centered, axis=-1, keepdims=True) + EPS)
    return centered * scale, scale


def standard_heads(values, averager):
    centered = values - head_mean(values, averager)
    scale = lax.rsqrt(head_mean(centered * centered, averager) + EPS)
    return centered * scale, scale


def norm_pull(values, gain, grad):
    unit, scale = standard(values)
    scaled = grad * gain
    spread = jnp.mean(scaled * unit, axis=-1, keepdims=True)
    result = scale * (scaled - jnp.mean(scaled, axis=-1, keepdims=True) - unit * spread)
    return (
        result,
        jnp.sum(grad * unit, axis=0, keepdims=True),
        jnp.sum(grad, axis=0, keepdims=True),
    )


def weight_copies(sources, targets, sems):
    copies = [
        pltpu.make_async_copy(source, target, sems.at[index])
        for index, (source, target) in enumerate(zip(sources, targets))
    ]
    for copy in copies:
        copy.start()
    return copies


def column_pieces(ref, parts):
    size = ref.shape[-1] // parts
    return [ref.at[:, i * size : (i + 1) * size] for i in range(parts)]


def row_pieces(ref, parts):
    size = ref.shape[0] // parts
    return [ref.at[i * size : (i + 1) * size] for i in range(parts)]


def project(layer, residual, vec_ref, head_ref, w_ref, copies, normed_ref, pre_ref, qkv_ref):
    width = residual.shape[1]
    unit, _ = standard(residual)
    normed = (unit * vec_ref[0, layer : layer + 1] + vec_ref[1, layer : layer + 1]).astype(BF)
    normed_ref[...] = normed
    averager = head_averager()
    for part in range(3):
        copies[part].wait()
        bias = vec_ref[2 + part, layer : layer + 1]
        for j in range(width // WIDE):
            at = slice(part * width + j * WIDE, part * width + (j + 1) * WIDE)
            value = product(normed, w_ref[:, at]) + bias[:, j * WIDE : (j + 1) * WIDE]
            if part < 2:
                pre_ref[:, at] = value
                unit, _ = standard_heads(value, averager)
                value = unit * head_ref[layer, 2 * part : 2 * part + 1]
                if part == 0:
                    value = value + head_ref[layer, 1:2]
            qkv_ref[:, at] = value.astype(BF)


def frame_attend(usable, qkv_ref, att_ref):
    width = att_ref.shape[1]
    first, _ = lane_masks(F32)
    for pair in range(width // LANES):
        q, k, v = [
            qkv_ref[:, part * width + pair * LANES : part * width + (pair + 1) * LANES]
            for part in range(3)
        ]
        pieces = []
        for mask in lane_masks(BF):
            shares = frame_shares(q * mask, k, usable)
            pieces.append(product(shares.astype(BF), v))
        at = slice(pair * LANES, (pair + 1) * LANES)
        att_ref[:, at] = jnp.where(first > 0, pieces[0], pieces[1]).astype(att_ref.dtype)


def frame_shares(queries, keys, usable):
    scores = jnp.where(usable > 0, product_right(queries, keys) * SCALE, NEG)
    shares = jnp.exp(scores - jnp.max(scores, axis=-1, keepdims=True))
    return shares / jnp.sum(shares, axis=-1, keepdims=True)


def feed_forward(
    layer, att, residual, vec_ref, bias_ref, w_out, w_up, w_down, copies, mixed_ref, middle_ref,
    lifted_ref, slope_ref, active_ref, feed_ref, done=None,
):
    chunks = w_up.shape[1] // 512
    copies[0].wait()
    mixed = product(att, w_out[...]) + vec_ref[5, layer : layer + 1]
    mixed_ref[...] = mixed
    middle = residual + vec_ref[6, layer : layer + 1] * mixed
    middle_ref[...] = middle
    unit, _ = standard(middle)
    lifted = (unit * vec_ref[7, layer : layer + 1] + vec_ref[8, layer : layer + 1]).astype(BF)
    lifted_ref[...] = lifted
    feed = None
    for j in range(chunks):
        at = slice(j * 512, (j + 1) * 512)
        if j % 2 == 0:
            copies[1 + j].wait()
            copies[2 + j].wait()
        hidden = product(lifted, w_up[:, at]) + bias_ref[layer : layer + 1, at]
        bell = 0.5 * (1.0 + lax.erf(hidden * ROOT_HALF))
        slope_ref[:, at] = bell + hidden * jnp.exp(-0.5 * hidden * hidden) * ROOT_TWO_PI
        active = (hidden * bell).astype(BF)
        if done is None:
            active_ref[:, at] = active
        else:
            done(j, active)
        piece = product(active, w_down[at])
        feed = piece if feed is None else feed + piece
    feed = feed + vec_ref[9, layer : layer + 1]
    feed_ref[...] = feed
    return middle + vec_ref[10, layer : layer + 1] * feed


def split_columns(value_refs, x_at, keep_ref, send_ref):
    start = 0
    for value_ref in value_refs:
        half = value_ref.shape[1] // 2
        to = slice(start, start + half)
        keep_ref[:, to] = value_ref[:, pl.ds(pl.multiple_of(x_at * half, LANES), half)]
        send_ref[:, to] = value_ref[:, pl.ds(pl.multiple_of((1 - x_at) * half, LANES), half)]
        start += half


def feed_backward(
    layer, grad, feed, middle, mixed, slope_ref, vec_ref, w_up, w_down, copies, feed_grad_ref,
    hidden_grad_ref, mixed_grad_ref, bias_out, rows_ref, row0,
):
    chunks = w_up.shape[1] // 512
    feed_grad = (vec_ref[10, layer : layer + 1] * grad).astype(BF)
    feed_grad_ref[...] = feed_grad
    rows_ref[row0 + 4 : row0 + 5] = jnp.sum(feed_grad.astype(F32), axis=0, keepdims=True)
    rows_ref[row0 + 5 : row0 + 6] = jnp.sum(grad * feed, axis=0, keepdims=True)
    lifted_grad = None
    for j in range(chunks):
        at = slice(j * 512, (j + 1) * 512)
        if copies is not None and j % 2 == 0:
            copies[j].wait()
            copies[j + 1].wait()
        hidden_grad = (slope_ref[:, at] * product_right(feed_grad, w_down[at])).astype(BF)
        hidden_grad_ref[:, at] = hidden_grad
        bias_out[:, at] = jnp.sum(hidden_grad.astype(F32), axis=0, keepdims=True)
        piece = product_right(hidden_grad, w_up[:, at])
        lifted_grad = piece if lifted_grad is None else lifted_grad + piece
    part, gain_grad, shift_grad = norm_pull(middle, vec_ref[7, layer : layer + 1], lifted_grad)
    middle_grad = grad + part
    mixed_grad = (vec_ref[6, layer : layer + 1] * middle_grad).astype(BF)
    mixed_grad_ref[...] = mixed_grad
    rows_ref[row0 : row0 + 1] = jnp.sum(mixed_grad.astype(F32), axis=0, keepdims=True)
    rows_ref[row0 + 1 : row0 + 2] = jnp.sum(middle_grad * mixed, axis=0, keepdims=True)
    rows_ref[row0 + 2 : row0 + 3] = gain_grad
    rows_ref[row0 + 3 : row0 + 4] = shift_grad
    return middle_grad


def project_backward(*args):
    results = []
    for _ in project_steps(results, *args):
        pass
    return results[0]


def project_steps(
    results, layer, residual, dqkv_ref, pre_ref, vec_ref, head_ref, w_ref, copies, pg_ref, rows_ref,
    head_out,
):
    width = residual.shape[1]
    averager = head_averager()
    sums = [None, None, None]
    for part in range(3):
        for j in range(width // WIDE):
            at = slice(part * width + j * WIDE, part * width + (j + 1) * WIDE)
            value = dqkv_ref[:, at].astype(F32)
            if part < 2:
                unit, scale = standard_heads(pre_ref[:, at], averager)
                news = [(2 * part, jnp.sum(value * unit, axis=0, keepdims=True))]
                if part == 0:
                    news.append((1, jnp.sum(value, axis=0, keepdims=True)))
                for index, new in news:
                    sums[index] = new if sums[index] is None else sums[index] + new
                scaled = value * head_ref[layer, 2 * part : 2 * part + 1]
                value = scale * (
                    scaled
                    - head_mean(scaled, averager)
                    - unit * head_mean(scaled * unit, averager)
                )
            low = value.astype(BF)
            pg_ref[:, at] = low
            rows_ref[2 + part : 3 + part, j * WIDE : (j + 1) * WIDE] = jnp.sum(
                low.astype(F32), axis=0, keepdims=True
            )
            if (part * width // WIDE + j) % 3 == 2:
                yield
    head_out[...] = jnp.concatenate(sums + [jnp.zeros((5, WIDE), F32)], axis=0)
    normed_grad = None
    for part in range(3):
        copies[part].wait()
        at = slice(part * width, (part + 1) * width)
        piece = product_right(pg_ref[:, at], w_ref[:, at])
        normed_grad = piece if normed_grad is None else normed_grad + piece
        yield
    part, gain_grad, shift_grad = norm_pull(residual, vec_ref[0, layer : layer + 1], normed_grad)
    rows_ref[0:1] = gain_grad
    rows_ref[1:2] = shift_grad
    results.append(part)


def named_call(kernel, inputs, outputs, scratch, vmem_mib, cost, name, collective_id=None):
    names = [*inputs, *outputs, *scratch]

    def body(*refs):
        kernel(types.SimpleNamespace(**dict(zip(names, refs))))

    more = {}
    if collective_id is not None:
        more = {"collective_id": collective_id, "has_side_effects": True}
    results = pl.pallas_call(
        body,
        in_specs=[
            whole(pltpu.SMEM) if key.startswith("smem") else whole(pl.ANY) for key in inputs
        ],
        out_specs=[whole(pl.ANY if value[2] else pltpu.VMEM) for value in outputs.values()],
        out_shape=[jax.ShapeDtypeStruct(value[0], value[1]) for value in outputs.values()],
        scratch_shapes=list(scratch.values()),
        compiler_params=pltpu.CompilerParams(vmem_limit_bytes=vmem_mib * VMEM_MIB, **more),
        cost_estimate=cost,
        name=name,
    )(*inputs.values())
    return types.SimpleNamespace(**dict(zip(outputs, results)))


def low(*shape):
    return pltpu.VMEM(shape, BF)


def full(*shape):
    return pltpu.VMEM(shape, F32)


class Mover:
    def __init__(self, sems):
        self.sems, self.count, self.open = sems, 0, []

    def start(self, source, target):
        copy = pltpu.make_async_copy(source, target, self.sems.at[self.count])
        copy.start()
        self.count += 1
        return copy

    def flush(self, source, target):
        self.open.append(self.start(source, target))

    def finish(self):
        assert self.count == self.sems.shape[0]
        for copy in self.open:
            copy.wait()


def interleaved(one, two):
    return [piece for pair in zip(one, two) for piece in pair]


def front_kernel(
    tok_ref, usable_ref, vec_ref, bias_ref, head_ref, qkv_w, out_w, up_w, down_w,
    left_pack, att_pack, pre0, qkv0, mixed0, middle0, slope0, feed0, res1, normed1, pre1, qkv1,
    w_qkv, w_out, w_up, w_down, w_next, sems,
):
    width, units = tok_ref.shape[1], up_w.shape[2]
    lifted0 = left_pack.at[:, :width]
    active0 = left_pack.at[:, width : width + units]
    normed0, att0 = att_pack.at[:, :width], att_pack.at[:, width:]
    copies = weight_copies(
        column_pieces(qkv_w.at[0], 3)
        + [out_w.at[0]]
        + interleaved(column_pieces(up_w.at[0], 4), row_pieces(down_w.at[0], 4))
        + column_pieces(qkv_w.at[1], 3),
        column_pieces(w_qkv, 3)
        + [w_out]
        + interleaved(column_pieces(w_up, 4), row_pieces(w_down, 4))
        + column_pieces(w_next, 3),
        sems,
    )
    residual = tok_ref[...].astype(F32)
    project(0, residual, vec_ref, head_ref, w_qkv, copies[:3], normed0, pre0, qkv0)
    frame_attend(usable_ref[...], qkv0, att0)
    result = feed_forward(
        0, att0[...], residual, vec_ref, bias_ref, w_out, w_up, w_down, copies[3:12], mixed0,
        middle0, lifted0, slope0, active0, feed0,
    )
    res1[...] = result
    project(1, result, vec_ref, head_ref, w_next, copies[12:], normed1, pre1, qkv1)


def front(tokens, usable, vectors, up_bias, head_rows, qkv_weight, out_weight, up_weight, down_weight):
    rows, width = tokens.shape
    hidden = up_weight.shape[2]
    shapes = [
        ((rows, hidden + width), BF),
        ((rows, 2 * width), BF),
        ((rows, 2 * width), F32),
        ((rows, 3 * width), BF),
        ((rows, width), F32),
        ((rows, width), F32),
        ((rows, hidden), F32),
        ((rows, width), F32),
        ((rows, width), F32),
        ((rows, width), BF),
        ((rows, 2 * width), F32),
        ((rows, 3 * width), BF),
    ]
    return pl.pallas_call(
        front_kernel,
        in_specs=[whole()] * 5 + [whole(pl.ANY)] * 4,
        out_specs=[whole()] * len(shapes),
        out_shape=[jax.ShapeDtypeStruct(*shape) for shape in shapes],
        scratch_shapes=[
            pltpu.VMEM((width, 3 * width), BF),
            pltpu.VMEM((width, width), BF),
            pltpu.VMEM((width, hidden), BF),
            pltpu.VMEM((hidden, width), BF),
            pltpu.VMEM((width, 3 * width), BF),
            pltpu.SemaphoreType.DMA((15,)),
        ],
        compiler_params=pltpu.CompilerParams(vmem_limit_bytes=58 * VMEM_MIB),
        cost_estimate=pl.CostEstimate(
            flops=2 * rows * width * (7 * width + 2 * hidden),
            bytes_accessed=2 * width * (7 * width + 2 * hidden),
            transcendentals=2 * rows * hidden,
        ),
        name="front",
    )(tokens, usable, vectors, up_bias, head_rows, qkv_weight, out_weight, up_weight, down_weight)


def turn_kernel(
    x_ref, att_ref, normed_ref, res_ref, cot_ref, vec_ref, bias_ref, out_w, up_w, down_w,
    left_pack, att_pack, output, right_keep, right_send, att_grad, middle_grad, bias_out, rows_out,
    w_out, w_up, w_down, mixed_sc, middle_sc, slope_sc, feed_sc, fg_sc, hg_sc, mg_sc, sems,
):
    width, units = att_ref.shape[1], up_w.shape[2]
    lifted = left_pack.at[:, :width]
    active = left_pack.at[:, width : width + units]
    att_pack[:, :width] = normed_ref[...]
    att_pack[:, width:] = att_ref[...]
    copies = weight_copies(
        [out_w.at[1]] + interleaved(column_pieces(up_w.at[1], 4), row_pieces(down_w.at[1], 4)),
        [w_out] + interleaved(column_pieces(w_up, 4), row_pieces(w_down, 4)),
        sems,
    )
    result = feed_forward(
        1, att_ref[...], res_ref[...], vec_ref, bias_ref, w_out, w_up, w_down, copies, mixed_sc,
        middle_sc, lifted, slope_sc, active, feed_sc,
    )
    output[...] = result.astype(BF)
    grad = feed_backward(
        1, cot_ref[...].astype(F32), feed_sc[...], middle_sc[...], mixed_sc[...], slope_sc, vec_ref,
        w_up, w_down, None, fg_sc, hg_sc, mg_sc, bias_out, rows_out, 0,
    )
    middle_grad[...] = grad
    att_grad[...] = product_right(mg_sc[...], w_out[...]).astype(BF)
    split_columns([hg_sc, fg_sc, mg_sc], x_ref[0], right_keep, right_send)


def turn(x_at, att, normed, res, cotangent, vectors, up_bias, out_weight, up_weight, down_weight):
    rows, width = res.shape
    hidden = up_weight.shape[2]
    shapes = [
        ((rows, hidden + width), BF),
        ((rows, 2 * width), BF),
        ((rows, width), BF),
        ((rows, hidden // 2 + width), BF),
        ((rows, hidden // 2 + width), BF),
        ((rows, width), BF),
        ((rows, width), F32),
        ((1, hidden), F32),
        ((8, width), F32),
    ]
    return pl.pallas_call(
        turn_kernel,
        in_specs=[whole(pltpu.SMEM)] + [whole()] * 6 + [whole(pl.ANY)] * 3,
        out_specs=[whole()] * len(shapes),
        out_shape=[jax.ShapeDtypeStruct(*shape) for shape in shapes],
        scratch_shapes=[
            pltpu.VMEM((width, width), BF),
            pltpu.VMEM((width, hidden), BF),
            pltpu.VMEM((hidden, width), BF),
            pltpu.VMEM((rows, width), F32),
            pltpu.VMEM((rows, width), F32),
            pltpu.VMEM((rows, hidden), F32),
            pltpu.VMEM((rows, width), F32),
            pltpu.VMEM((rows, width), BF),
            pltpu.VMEM((rows, hidden), BF),
            pltpu.VMEM((rows, width), BF),
            pltpu.SemaphoreType.DMA((9,)),
        ],
        compiler_params=pltpu.CompilerParams(vmem_limit_bytes=58 * VMEM_MIB),
        cost_estimate=pl.CostEstimate(
            flops=4 * rows * width * (width + 2 * hidden),
            bytes_accessed=2 * width * (width + 2 * hidden),
            transcendentals=2 * rows * hidden,
        ),
        name="turn",
    )(x_at, att, normed, res, cotangent, vectors, up_bias, out_weight, up_weight, down_weight)


def back_one_kernel(r):
    mover = Mover(r.moves)
    early = [
        mover.start(*pair)
        for pair in (
            (r.vectors, r.vectors_sc), (r.head_rows, r.head_rows_sc), (r.dqkv, r.dqkv_sc),
            (r.pre, r.pre_sc), (r.res, r.res_sc), (r.grad, r.grad_sc),
        )
    ]
    copies = weight_copies(column_pieces(r.qkv_w.at[1], 3), column_pieces(r.w_qkv, 3), r.sems)
    later = [
        mover.start(*pair)
        for pair in (
            (r.feed, r.feed_sc), (r.middle, r.middle_sc), (r.mixed, r.mixed_sc),
            (r.slope, r.slope_sc),
        )
    ]
    copies = copies + weight_copies(
        interleaved(column_pieces(r.up_w.at[0], 4), row_pieces(r.down_w.at[0], 4)),
        interleaved(column_pieces(r.w_up, 4), row_pieces(r.w_down, 4)),
        r.more_sems,
    )
    for copy in early:
        copy.wait()
    part = project_backward(
        1, r.res_sc[...], r.dqkv_sc, r.pre_sc, r.vectors_sc, r.head_rows_sc, r.w_qkv, copies[:3],
        r.pg_sc, r.rows_out, r.head_out,
    )
    x_at = lax.axis_index("grp")
    split_columns([r.pg_sc], x_at, r.pg_keep_sc, r.pg_send_sc)
    mover.flush(r.pg_send_sc, r.pg_send)
    mover.flush(r.pg_keep_sc, r.pg_keep)
    for copy in later:
        copy.wait()
    r.middle_grad_sc[...] = feed_backward(
        0, r.grad_sc[...] + part, r.feed_sc[...], r.middle_sc[...], r.mixed_sc[...], r.slope_sc,
        r.vectors_sc, r.w_up, r.w_down, copies[3:], r.fg_sc, r.hg_sc, r.mixed_grad_sc, r.bias_out,
        r.rows_out, 8,
    )
    mover.flush(r.middle_grad_sc, r.middle_grad)
    mover.flush(r.mixed_grad_sc, r.mixed_grad)
    split_columns([r.hg_sc, r.fg_sc], x_at, r.right_keep_sc, r.right_send_sc)
    mover.flush(r.right_send_sc, r.right_send)
    mover.flush(r.right_keep_sc, r.right_keep)
    mover.finish()


def back_one(
    dqkv, pre, res, grad, feed, middle, mixed, slope, vectors, head_rows, qkv_weight,
    up_weight, down_weight,
):
    rows, width = res.shape
    hidden = up_weight.shape[2]
    loaded = dict(
        vectors=vectors, head_rows=head_rows, dqkv=dqkv, pre=pre, res=res,
        grad=grad, feed=feed, middle=middle, mixed=mixed, slope=slope,
    )
    stored = dict(
        pg_keep=((rows, 3 * width // 2), BF),
        pg_send=((rows, 3 * width // 2), BF),
        right_keep=((rows, (hidden + width) // 2), BF),
        right_send=((rows, (hidden + width) // 2), BF),
        mixed_grad=((rows, width), BF),
        middle_grad=((rows, width), F32),
    )
    return named_call(
        back_one_kernel,
        dict(**loaded, qkv_w=qkv_weight, up_w=up_weight, down_w=down_weight),
        dict(
            **{key: (*value, True) for key, value in stored.items()},
            bias_out=((1, hidden), F32, False),
            rows_out=((16, width), F32, False),
            head_out=((8, WIDE), F32, False),
        ),
        dict(
            **{key + "_sc": pltpu.VMEM(value.shape, value.dtype) for key, value in loaded.items()},
            **{key + "_sc": pltpu.VMEM(*value) for key, value in stored.items()},
            w_qkv=low(width, 3 * width),
            w_up=low(width, hidden),
            w_down=low(hidden, width),
            pg_sc=low(rows, 3 * width),
            fg_sc=low(rows, width),
            hg_sc=low(rows, hidden),
            sems=pltpu.SemaphoreType.DMA((3,)),
            more_sems=pltpu.SemaphoreType.DMA((8,)),
            moves=pltpu.SemaphoreType.DMA((16,)),
        ),
        60,
        pl.CostEstimate(
            flops=2 * rows * width * (3 * width + 2 * hidden),
            bytes_accessed=2 * width * (3 * width + 2 * hidden),
            transcendentals=0,
        ),
        "back_one",
    )


def frame_steps(att_grad, usable, qkv_ref, dqkv_ref):
    width = att_grad.shape[1]
    first, _ = lane_masks(F32)
    for pair in range(width // LANES):
        q, k, v = [
            qkv_ref[:, part * width + pair * LANES : part * width + (pair + 1) * LANES]
            for part in range(3)
        ]
        out = att_grad[:, pair * LANES : (pair + 1) * LANES]
        pieces = []
        for mask in lane_masks(BF):
            shares = frame_shares(q * mask, k, usable)
            share_grad = product_right(out * mask, v)
            delta = jnp.sum(shares * share_grad, axis=-1, keepdims=True)
            score_grad = (shares * (share_grad - delta)).astype(BF)
            pieces.append(
                (
                    product(score_grad, k) * SCALE,
                    product_left(score_grad, q) * SCALE,
                    product_left(shares.astype(BF), out),
                )
            )
        for part in range(3):
            dqkv_ref[:, part * width + pair * LANES : part * width + (pair + 1) * LANES] = jnp.where(
                first > 0, pieces[0][part], pieces[1][part]
            )
        if pair % 2 == 1:
            yield


def frame_loads(r, mover):
    early = [
        mover.start(*pair)
        for pair in (
            (r.mixed_grad, r.mixed_grad_sc), (r.usable, r.usable_sc), (r.qkv, r.qkv_sc)
        )
    ]
    copies = weight_copies(
        [r.out_w.at[0]] + column_pieces(r.qkv_w.at[0], 3), [r.w_out] + column_pieces(r.w_qkv, 3),
        r.sems,
    )
    later = [
        mover.start(*pair)
        for pair in (
            (r.vectors, r.vectors_sc), (r.head_rows, r.head_rows_sc), (r.pre, r.pre_sc),
            (r.tok, r.tok_sc), (r.grad, r.grad_sc), (r.rows10, r.rows10_sc), (r.rows1, r.rows1_sc),
            (r.bias0, r.bias0_sc), (r.bias1, r.bias1_sc), (r.heads1, r.heads1_sc),
        )
    ]
    return early, later, copies


def frame_part(r, early, copies):
    for copy in early:
        copy.wait()
    copies[0].wait()
    att_grad = product_right(r.mixed_grad_sc[...], r.w_out[...]).astype(BF)
    yield
    yield from frame_steps(att_grad, r.usable_sc[...], r.qkv_sc, r.dqkv_sc)


def input_part(r, later, copies, x_at):
    width = r.tok_sc.shape[1]
    for copy in later:
        copy.wait()
    results = []
    yield from project_steps(
        results, 0, r.tok_sc[...].astype(F32), r.dqkv_sc, r.pre_sc, r.vectors_sc, r.head_rows_sc,
        r.w_qkv, copies[1:], r.pg_sc, r.rows_sc, r.heads_sc,
    )
    part = results[0]
    split_columns([r.pg_sc, r.mixed_grad_sc], x_at, r.pg_keep_sc, r.pg_send_sc)
    r.input_grad_sc[...] = (r.grad_sc[...] + part).astype(BF)
    small = r.small_sc
    small[0:5] = r.rows_sc[0:5]
    small[5:11] = r.rows10_sc[8:14]
    small[11:16] = r.rows10_sc[0:5]
    small[16:22] = r.rows1_sc[0:6]
    at = 22
    for bias in (r.bias0_sc, r.bias1_sc):
        for j in range(bias.shape[1] // width):
            small[at : at + 1] = bias[:, j * width : (j + 1) * width]
            at += 1
    place = lax.broadcasted_iota(jnp.int32, (1, width), 1) // HD
    row = jnp.zeros((1, width), F32)
    for index, heads in enumerate((r.heads_sc, r.heads1_sc)):
        total = heads[...]
        total = total + pltpu.roll(total, WIDE // 2, 1)
        total = total + pltpu.roll(total, HD, 1)
        for j in range(3):
            many = jnp.concatenate([total[j : j + 1]] * (width // WIDE), axis=1)
            row = jnp.where(place == 3 * index + j, many, row)
    small[at : at + 1] = row
    small[at + 1 :] = jnp.zeros((small.shape[0] - at - 1, width), F32)
    yield


def back_two_kernel(r):
    mover = Mover(r.moves)
    early, later, copies = frame_loads(r, mover)
    for _ in frame_part(r, early, copies):
        pass
    for _ in input_part(r, later, copies, r.smem_at[0]):
        pass
    mover.flush(r.pg_send_sc, r.pg_send)
    mover.flush(r.pg_keep_sc, r.pg_keep)
    mover.flush(r.input_grad_sc, r.input_grad)
    mover.flush(r.small_sc, r.small)
    mover.finish()


def back_two(
    places, mixed_grad, grad, qkv, pre, tok, usable, vectors, head_rows, rows10, rows1, bias0,
    bias1, heads1, out_w, qkv_w,
):
    rows, width = tok.shape
    loaded = dict(
        mixed_grad=mixed_grad, usable=usable, qkv=qkv, vectors=vectors, head_rows=head_rows,
        pre=pre, tok=tok, grad=grad, rows10=rows10, rows1=rows1, bias0=bias0, bias1=bias1,
        heads1=heads1,
    )
    small_rows = 2 * vectors.shape[0] + 2 * bias0.shape[1] // width + 2
    stored = dict(
        pg_keep=((rows, 2 * width), BF),
        pg_send=((rows, 2 * width), BF),
        input_grad=((rows, width), BF),
        small=((small_rows, width), F32),
    )
    return named_call(
        back_two_kernel,
        dict(smem_at=places, **loaded, out_w=out_w, qkv_w=qkv_w),
        {key: (*value, True) for key, value in stored.items()},
        dict(
            **{key + "_sc": pltpu.VMEM(value.shape, value.dtype) for key, value in loaded.items()},
            **{key + "_sc": pltpu.VMEM(*value) for key, value in stored.items()},
            w_out=low(width, width),
            w_qkv=low(width, 3 * width),
            dqkv_sc=full(rows, 3 * width),
            pg_sc=low(rows, 3 * width),
            rows_sc=full(8, width),
            heads_sc=full(8, WIDE),
            sems=pltpu.SemaphoreType.DMA((4,)),
            moves=pltpu.SemaphoreType.DMA((17,)),
        ),
        60,
        pl.CostEstimate(
            flops=2 * rows * width * 4 * width,
            bytes_accessed=2 * width * 4 * width,
            transcendentals=HEADS * rows * rows,
        ),
        "back_two",
    )


def weight_grad_kernel(outer, tall, starts, at_ref, *refs):
    count = len(tall)
    lefts, rights = refs[: 4 * count], refs[4 * count : 8 * count]
    keep, send = refs[8 * count : 8 * count + 2]
    left_sc = refs[8 * count + 2 : 9 * count + 2]
    right_sc = refs[9 * count + 2 : 10 * count + 2]
    sems = refs[10 * count + 2]
    c_at, y_at = at_ref[0], at_ref[1]
    rows = lefts[0].shape[0]
    group = keep.shape[0] // outer
    copies = []
    for w in range(count):
        cols, left_cols = right_sc[w].shape[1], left_sc[w].shape[1]
        left_start, right_start = starts[w]
        for s in range(4):
            at = pl.ds(pl.multiple_of(right_start + c_at * cols, LANES), cols)
            copies.append(
                pltpu.make_async_copy(
                    rights[4 * w + s].at[:, at],
                    right_sc[w].at[s * rows : (s + 1) * rows],
                    sems.at[len(copies)],
                )
            )
            copies.append(
                pltpu.make_async_copy(
                    lefts[4 * w + s].at[:, left_start : left_start + left_cols],
                    left_sc[w].at[s * rows : (s + 1) * rows],
                    sems.at[len(copies)],
                )
            )
    for copy in copies:
        copy.start()
    start = 0
    for w in range(count):
        for copy in copies[8 * w : 8 * w + 8]:
            copy.wait()
        cols = right_sc[w].shape[1]
        right = right_sc[w][...]
        for block in range(left_sc[w].shape[1] // 512):
            result = product_left(left_sc[w][:, block * 512 : (block + 1) * 512], right).astype(BF)
            targets = {0: [], 1: []}
            if tall[w]:
                size, part = 4 * group, group // 2
                for piece in range(512 // part):
                    row = block * 512 + piece * part
                    o, y = row // (2 * size), (row // size) % 2
                    core, t = (row % size) // (size // 2), (row % (size // 2)) // part
                    targets[y].append(
                        (piece * part, part, o * group + core * part, start + t * cols)
                    )
            else:
                for piece in range(512 // group):
                    row = block * 512 + piece * group
                    o, y = row // (2 * group), (row // group) % 2
                    targets[y].append((piece * group, group, o * group, start))
            for y in range(2):
                if not targets[y]:
                    continue

                def store(ref, y=y):
                    for source, size, row, col in targets[y]:
                        ref[row : row + size, col : col + cols] = result[source : source + size]

                @pl.when(y_at == y)
                def _():
                    store(keep)

                @pl.when(y_at != y)
                def _():
                    store(send)

        start += cols * (4 if tall[w] else 1)


def weight_grads(name, outer, width, places, products):
    rows = products[0][0][0].shape[0]
    group = width // (2 * outer)
    lefts, left_starts, left_cols, rights, right_starts, halves, tall = zip(*products)
    columns = [half // 2 for half in halves]
    total = sum(c * (4 if t else 1) for c, t in zip(columns, tall))
    shape = jax.ShapeDtypeStruct((outer * group, total), BF)
    count = len(products)
    return pl.pallas_call(
        functools.partial(
            weight_grad_kernel, outer, tall, tuple(zip(left_starts, right_starts))
        ),
        in_specs=[whole(pltpu.SMEM)] + [whole(pl.ANY)] * (8 * count),
        out_specs=[whole()] * 2,
        out_shape=[shape] * 2,
        scratch_shapes=[pltpu.VMEM((4 * rows, c), BF) for c in left_cols]
        + [pltpu.VMEM((4 * rows, c), BF) for c in columns]
        + [pltpu.SemaphoreType.DMA((8 * count,))],
        compiler_params=pltpu.CompilerParams(vmem_limit_bytes=48 * VMEM_MIB),
        cost_estimate=pl.CostEstimate(
            flops=16 * rows * outer * group * total,
            bytes_accessed=8 * outer * group * total,
            transcendentals=0,
        ),
        name=name,
    )(places, *[a for l in lefts for a in l], *[a for r in rights for a in r])


def assemble_kernel(count, *refs):
    inputs, results, passing = count
    sources, refs = refs[:inputs], refs[inputs:]
    passed, refs = refs[:passing], refs[passing:]
    finals, refs = refs[:results], refs[results:]
    passed_out, refs = refs[:passing], refs[passing:]
    pieces, refs = refs[:inputs], refs[inputs:]
    outs, smalls = refs[:4], refs[4:results]
    held = refs[results : results + passing]
    sems, out_sems = refs[results + passing :]
    copies = [
        pltpu.make_async_copy(source, piece, sems.at[index])
        for index, (source, piece) in enumerate(
            zip((*sources, *passed), (*pieces, *held))
        )
    ]
    for copy in copies:
        copy.start()
    leaving = []

    def leave(source, target):
        copy = pltpu.make_async_copy(source, target, out_sems.at[len(leaving)])
        copy.start()
        leaving.append(copy)

    qkv_out, out_out, up_out, down_out = outs
    me, x_at = lax.axis_index("blk"), lax.axis_index("grp")
    c_at = lax.rem(me, 2)
    spread = bool(smalls)
    if smalls:
        copies[4].wait()
        share_small(me, pieces[4], *smalls)
        for source, target in zip(smalls, finals[4:]):
            leave(source, target)
    part = qkv_out.shape[1]
    for layer in range(2):
        copies[2 * layer].wait()
        copies[2 * layer + 1].wait()
        for source in range(4):
            feed, att = pieces[2 * layer].at[source], pieces[2 * layer + 1].at[source]
            c = c_at if source % 2 == 0 else 1 - c_at
            feed_place = att_place = 2 * (x_at if source < 2 else 1 - x_at) + c

            def put(ref, values, place, row=0, layer=layer):
                cols = values.shape[1]
                at = pl.ds(pl.multiple_of(place * cols, LANES), cols)
                ref[layer, row : row + values.shape[0], at] = values.astype(F32)

            up_cols = up_out.shape[2] // 4
            down_cols = down_out.shape[2] // 4
            qkv_cols = qkv_out.shape[2] // 4
            put(up_out, feed[:, :up_cols], feed_place)
            if spread and layer == 1:
                for t in range(2):
                    start = up_cols + t * 2 * down_cols
                    rows = pl.ds(pl.multiple_of((2 * (feed_place // 2) + t) * part, part), part)
                    cols = pl.ds(pl.multiple_of(c * 2 * down_cols, LANES), 2 * down_cols)
                    down_out[layer, rows, cols] = feed[:, start : start + 2 * down_cols].astype(F32)
                put(qkv_out, att[:, :qkv_cols], att_place)
                put(out_out, att[:, qkv_cols:], att_place)
                continue
            for t in range(4):
                put(
                    down_out,
                    feed[:, up_cols + t * down_cols : up_cols + (t + 1) * down_cols],
                    feed_place,
                    t * part,
                )
            put(qkv_out, att[:, :qkv_cols], att_place)
            put(out_out, att[:, qkv_cols:], att_place)
        for source, target in zip(outs, finals):
            leave(source.at[layer], target.at[layer])
    for index, (source, target) in enumerate(zip(held, passed_out)):
        copies[inputs + index].wait()
        leave(source, target)
    for copy in leaving:
        copy.wait()


def share_small(me, small, vector_out, bias_out, head_out):
    vector_rows = vector_out.shape[0]
    lanes = pl.ds(pl.multiple_of((me // 2) * LANES, LANES), LANES)
    pair = small[: 2 * vector_rows, lanes]
    pair = jnp.where(lax.rem(me, 2) == 0, pair, pltpu.roll(pair, HD, 1))
    columns = bias_out.shape[1]
    per_row = small.shape[1] // columns
    rows = PEERS // per_row
    for layer in range(2):
        for index in range(vector_rows):
            row = layer * vector_rows + index
            vector_out[index, layer : layer + 1] = pair[row : row + 1, :HD]
        row = pl.ds(2 * vector_rows + layer * rows + me // per_row, 1)
        at = pl.ds(pl.multiple_of(lax.rem(me, per_row) * columns, LANES), columns)
        bias_out[layer : layer + 1] = small[row, at]
        last = 2 * vector_rows + 2 * rows
        head_out[layer : layer + 1] = small[
            last : last + 1, layer * 3 * HD : (layer + 1) * 3 * HD
        ]


def assemble(pieces, shapes, passed):
    results = [jax.ShapeDtypeStruct(shape, F32) for shape in shapes]
    results += [jax.ShapeDtypeStruct(array.shape, array.dtype) for array in passed]
    return pl.pallas_call(
        functools.partial(assemble_kernel, (len(pieces), len(shapes), len(passed))),
        in_specs=[whole(pl.ANY)] * (len(pieces) + len(passed)),
        out_specs=[whole(pl.ANY)] * len(results),
        out_shape=results,
        scratch_shapes=[pltpu.VMEM(piece.shape, piece.dtype) for piece in pieces]
        + [pltpu.VMEM(shape, F32) for shape in shapes]
        + [pltpu.VMEM(array.shape, array.dtype) for array in passed]
        + [
            pltpu.SemaphoreType.DMA((len(pieces) + len(passed),)),
            pltpu.SemaphoreType.DMA((len(results) + 4,)),
        ],
        compiler_params=pltpu.CompilerParams(vmem_limit_bytes=60 * VMEM_MIB),
        name="assemble",
    )(*pieces, *passed)


OUTER = 4
BLOCK = 128


def slot_order(z0, z1):
    return [2 * (1 - z1) + (1 - z0), 2 * z1 + (1 - z0), 2 * (1 - z1) + z0, 2 * z1 + z0]


def slot_group(slot, z0, z1):
    far = jnp.where(slot % 2 == 0, 1 - z1, z1)
    return 2 * far + jnp.where(slot < 2, 1 - z0, z0)


def slot_product(group, left, left_at, right, right_at, cols, tall, emit):
    rights = right[:, right_at : right_at + cols]
    if tall:
        for y in range(2):
            start = pl.multiple_of(left_at + group * 8 * BLOCK + y * 4 * BLOCK, BLOCK)
            result = product_left(left[:, pl.ds(start, 4 * BLOCK)], rights).astype(BF)
            half = BLOCK // 2
            for c in range(2):
                for t in range(4):
                    row = c * 2 * BLOCK + t * half
                    emit(y, c * half, t * cols, result[row : row + half])
    else:
        start = pl.multiple_of(left_at + group * 2 * BLOCK, BLOCK)
        result = product_left(left[:, pl.ds(start, 2 * BLOCK)], rights).astype(BF)
        for y in range(2):
            emit(y, 0, 0, result[y * BLOCK : (y + 1) * BLOCK])


class Sender:
    def __init__(self, send, recv, partners):
        self.send, self.recv, self.partners = send, recv, partners
        self.copies = []

    def start(self, source, target, partner):
        index = len(self.copies)
        copy = pltpu.make_async_remote_copy(
            src_ref=source,
            dst_ref=target,
            send_sem=self.send.at[index],
            recv_sem=self.recv.at[index],
            device_id=self.partners[partner],
            device_id_type=MESH,
        )
        copy.start()
        self.copies.append(copy)
        return copy

    def finish(self):
        for copy in self.copies:
            copy.wait_send()


def finish_kernel(r):
    me = lax.axis_index("blk")
    x_at = lax.axis_index("grp")
    c_at, y_at, z0, z1 = [lax.rem(me // (1 << bit), 2) for bit in range(4)]
    partners = {"x": {"grp": 1 - x_at}}
    for bit, name in enumerate(("c", "y", "z0", "z1")):
        partners[name] = {"blk": me ^ (1 << bit)}
    barrier = pltpu.get_barrier_semaphore()
    for partner in partners.values():
        pl.semaphore_signal(barrier, 1, device_id=partner, device_id_type=MESH)
    mover = Mover(r.moves)
    early, later, weights = frame_loads(r, mover)
    pl.semaphore_wait(barrier, len(partners))
    sender = Sender(r.send, r.recv, partners)
    local = r.local
    rows = r.la1.shape[0]
    locals_ = []

    def load(source, target):
        copy = pltpu.make_async_copy(source, target, local.at[len(locals_)])
        copy.start()
        locals_.append(copy)
        return copy

    stores = []

    def store(source, target):
        stores.append(load(source, target))

    def ready(copies):
        for copy in copies:
            copy.wait_recv()

    def quarter(ref, start, cols, core):
        return ref.at[:, pl.ds(pl.multiple_of(start + core * cols, BLOCK), cols)]

    def own_right(ref, start, cols, target, to, index):
        here = slice(index * rows, (index + 1) * rows)
        there = slice((2 + index) * rows, (3 + index) * rows)
        return [
            load(quarter(ref, start, cols, c_at), target.at[here, to : to + cols]),
            sender.start(
                quarter(ref, start, cols, 1 - c_at), target.at[there, to : to + cols], "c"
            ),
        ]

    def own_left(ref, target, index):
        return [
            load(ref, target.at[index * rows : (index + 1) * rows]),
            sender.start(ref, target.at[(2 + index) * rows : (3 + index) * rows], "c"),
        ]

    right_a1, right_f0, right_a0 = r.right_a1, r.right_f0, r.right_a0
    left_a1, left_f0, left_a0 = r.left_a1, r.left_f0, r.left_a0
    qkv_cols, out_cols = right_a1.shape[1] * 3 // 4, right_a1.shape[1] // 4
    up_cols, down_cols = right_f0.shape[1] * 4 // 5, right_f0.shape[1] // 5
    width = left_a1.shape[1] // 2
    pg1_copy = sender.start(r.pg1_send, r.pg1_x, "x")
    rt0_copy = sender.start(r.rt0_send, r.rt0_x, "x")
    d1_loads = [load(r.stay_down, r.part_d1), load(r.came_down, r.y_d1)]
    u1_loads = [load(r.stay_up, r.part_u1), load(r.came_up, r.z0_u1)]
    a1_ready = (
        own_left(r.la1, left_a1, 0)
        + own_left(r.la1_x, left_a1, 1)
        + own_right(r.pg1, 0, qkv_cols, right_a1, 0, 0)
        + own_right(r.rt1, 0, out_cols, right_a1, qkv_cols, 0)
        + own_right(r.rt1_x, 0, out_cols, right_a1, qkv_cols, 1)
    )
    f0_ready = (
        own_left(r.lf0, left_f0, 0)
        + own_left(r.lf0_x, left_f0, 1)
        + own_right(r.rt0, 0, up_cols, right_f0, 0, 0)
        + own_right(r.rt0, 2 * up_cols, down_cols, right_f0, up_cols, 0)
    )
    a0_ready = own_left(r.la0, left_a0, 0) + own_left(r.la0_x, left_a0, 1)

    def rest_a1():
        pg1_copy.wait_recv()
        return own_right(r.pg1_x, 0, qkv_cols, right_a1, 0, 1)

    def rest_f0():
        rt0_copy.wait_recv()
        return own_right(r.rt0_x, 0, up_cols, right_f0, 0, 1) + own_right(
            r.rt0_x, 2 * up_cols, down_cols, right_f0, up_cols, 1
        )

    def rest_a0(copy):
        copies = own_right(r.pg_keep_sc, 0, qkv_cols, right_a0, 0, 0) + own_right(
            r.pg_keep_sc, 2 * qkv_cols, out_cols, right_a0, qkv_cols, 0
        )
        copy.wait_recv()
        return (
            copies
            + own_right(r.pm0_x, 0, qkv_cols, right_a0, 0, 1)
            + own_right(r.pm0_x, 2 * qkv_cols, out_cols, right_a0, qkv_cols, 1)
        )

    class Finish:
        def finish(self):
            half = BLOCK // 2
            other = self.own(3).at[pl.ds(pl.multiple_of((1 - c_at) * half, half), half)]
            self.c_copy = sender.start(other, self.fin.at[1], "c")
            self.fin[0] = self.own(3)[pl.ds(pl.multiple_of(c_at * half, half), half)]
            self.far_copies = [sender.start(self.fin.at[0], self.far.at[0], "x")]

        def fourth(self):
            self.c_copy.wait_recv()
            self.far_copies.append(sender.start(self.fin.at[1], self.far.at[1], "x"))
            store(self.fin, self.out.at[0:2, :, self.columns])

        def last(self):
            for copy in self.far_copies:
                copy.wait_recv()
            store(self.far, self.out.at[2:4, :, self.columns])

    class Group(Finish):
        def __init__(self, part, over, over_z0, over_z1, fin, far, out, columns, came=False):
            self.part, self.over, self.over_z0, self.over_z1 = part, over, over_z0, over_z1
            self.fin, self.far, self.out, self.columns = fin, far, out, columns
            self.came, self.copies, self.z0_copies = came, {}, {}

        def own(self, slot):
            return self.part.at[slot] if self.came else self.part.at[slot, y_at]

        def total(self, slot):
            return self.own(slot)[...].astype(F32) + self.over[slot].astype(F32)

        def made(self, slot):
            self.copies[slot] = sender.start(
                self.part.at[slot, 1 - y_at], self.over.at[slot], "y"
            )

        def step(self, slot):
            if not self.came:
                self.copies[slot].wait_recv()
            (lambda: self.first(0), lambda: self.first(1), self.second, self.third)[slot]()

        def first(self, slot):
            self.own(slot)[...] = self.total(slot).astype(BF)
            self.z0_copies[slot] = sender.start(self.own(slot), self.over_z0.at[slot], "z0")

        def second(self):
            value = self.total(2)
            self.z0_copies[0].wait_recv()
            self.own(2)[...] = (value + self.over_z0[0].astype(F32)).astype(BF)
            self.z1_copy = sender.start(self.own(2), self.over_z1, "z1")

        def third(self):
            value = self.total(3)
            self.z0_copies[1].wait_recv()
            value = value + self.over_z0[1].astype(F32)
            self.z1_copy.wait_recv()
            self.own(3)[...] = (value + self.over_z1[...].astype(F32)).astype(BF)
            self.finish()

    class Early(Finish):
        def __init__(self, part, came, over, over_z1, fin, far, out, columns, keep=None):
            self.part, self.came, self.over, self.over_z1 = part, came, over, over_z1
            self.keep = part if keep is None else keep
            self.fin, self.far, self.out, self.columns = fin, far, out, columns
            self.copies, self.z0_copies = {}, {}

        def own(self, slot):
            return self.keep.at[slot - 2, y_at]

        def total(self, slot, at):
            return self.keep[slot, at].astype(F32) + self.came[slot, at].astype(F32)

        def made(self, slot):
            if slot < 2:
                self.z0_copies[slot] = sender.start(
                    self.part.at[slot], self.came.at[slot], "z0"
                )

        def send(self, slot):
            if self.z0_copies:
                self.z0_copies[slot].wait_recv()
            self.keep[slot, 1 - y_at] = self.total(slot, 1 - y_at).astype(BF)
            self.copies[slot] = sender.start(
                self.keep.at[slot, 1 - y_at], self.over.at[slot], "y"
            )

        def step(self, slot):
            self.copies[slot].wait_recv()
            value = self.total(slot, y_at) + self.over[slot].astype(F32)
            if slot == 1:
                self.z1_copy.wait_recv()
                value = value + self.over_z1[...].astype(F32)
            self.keep[slot, y_at] = value.astype(BF)
            if slot == 0:
                self.z1_copy = sender.start(self.keep.at[0, y_at], self.over_z1, "z1")
            else:
                self.finish()

    every = slice(None)
    half_cols = r.part_u1.shape[3]
    u1 = Early(
        r.part_u1, r.z0_u1, r.y_u1, r.z1_u1, r.fin_u1, r.far_u1, r.f1_out, slice(0, half_cols)
    )
    d1 = Group(
        r.part_d1, r.y_d1, r.z0_d1, r.z1_d1, r.fin_d1, r.far_d1, r.f1_out,
        slice(half_cols, 2 * half_cols), True,
    )
    a1 = Early(
        r.part_a1, r.z0_a1, r.y_a1, r.z1_a1, r.fin_a1, r.far_a1, r.a1_out, every, r.part_a1.at[2:4]
    )
    f0 = Group(r.part_f0, r.y_f0, r.z0_f0, r.z1_f0, r.fin_f0, r.far_f0, r.f0_out, every)
    a0 = Group(r.part_a0, r.y_a0, r.z0_a0, r.z1_a0, r.fin_a0, r.far_a0, r.a0_out, every)

    def products(group, left, right, terms, slots=range(OUTER)):
        for slot in slots:
            at = slot_group(slot, z0, z1)
            base = 0
            for left_at, right_at, cols, tall in terms:

                def emit(y, row, col, values, slot=slot, base=base):
                    height, wide = values.shape
                    group.part[
                        slot, y, row : row + height, base + col : base + col + wide
                    ] = values

                slot_product(at, left, left_at, right, right_at, cols, tall, emit)
                base += cols * (4 if tall else 1)
            group.made(slot)

    att_terms = [(0, 0, qkv_cols, False), (width, qkv_cols, out_cols, False)]
    feed_terms = [(0, 0, up_cols, False), (width, up_cols, down_cols, True)]
    sums, sums_in, small_copies = r.sums, r.sums_in, []

    def small_step(name=None):
        index = len(small_copies)
        if index:
            small_copies[-1].wait_recv()
            sums[index] = sums[index - 1] + sums_in[index - 1]
        if name is not None:
            small_copies.append(sender.start(sums.at[index], sums_in.at[index], name))
        else:
            store(sums.at[index], r.small_out)

    backward = chain(frame_part(r, early, weights), input_part(r, later, weights, x_at))
    ready(d1_loads)
    d1.step(0)
    next(backward)
    d1.step(1)
    ready(u1_loads)
    u1.send(1)
    d1.step(2)
    a1_ready += rest_a1()
    next(backward)
    next(backward)
    next(backward)
    ready(a1_ready)
    products(a1, left_a1, right_a1, att_terms, (0,))
    u1.send(0)
    next(backward)
    f0_ready += rest_f0()
    ready(f0_ready)
    products(f0, left_f0, right_f0, feed_terms, (0,))
    next(backward)
    products(a1, left_a1, right_a1, att_terms, (1,))
    products(a1, left_a1, right_a1, att_terms, (2,))
    next(backward)
    products(f0, left_f0, right_f0, feed_terms, (1,))
    products(f0, left_f0, right_f0, feed_terms, (2,))
    d1.step(3)
    d1.fourth()
    f0.step(0)
    next(backward)
    a1.send(0)
    next(backward)
    next(backward)
    next(backward)
    u1.step(0)
    next(backward)
    next(backward)
    pm0_copy = sender.start(r.pg_send_sc, r.pm0_x, "x")
    store(r.input_grad_sc, r.input_grad)
    sums[0] = r.small_sc[...]
    small_step("x")
    products(a1, left_a1, right_a1, att_terms, (3,))
    a0_ready += rest_a0(pm0_copy)
    f0.step(1)
    f0.step(2)
    small_step("c")
    ready(a0_ready)
    products(a0, left_a0, right_a0, att_terms, (0,))
    a1.step(0)
    products(f0, left_f0, right_f0, feed_terms, (3,))
    small_step("y")
    products(a0, left_a0, right_a0, att_terms, (1,))
    a0.step(0)
    products(a0, left_a0, right_a0, att_terms, (2,))
    u1.step(1)
    small_step("z0")
    f0.step(3)
    f0.fourth()
    u1.fourth()
    a0.step(1)
    small_step("z1")
    a1.send(1)
    a0.step(2)
    products(a0, left_a0, right_a0, att_terms, (3,))
    a1.step(1)
    small_step()
    d1.last()
    a1.fourth()
    f0.last()
    u1.last()
    a0.step(3)
    a0.fourth()
    a1.last()
    a0.last()
    assert len(sender.copies) == r.send.shape[0]
    assert len(locals_) == local.shape[0]
    ready(stores)
    sender.finish()
    mover.finish()


def finish_all(frame, u1, d1, a1, f0, a0):
    rows, width = frame["tok"].shape
    wide, att = 2 * u1[0].shape[-1], u1[0].shape[-1]
    half = BLOCK // 2
    small_rows = 2 * frame["vectors"].shape[0] + 2 * frame["bias0"].shape[1] // width + 2
    loaded = dict(frame)
    out_weight, qkv_weight = loaded.pop("out_w"), loaded.pop("qkv_w")

    def piece(columns):
        return ((4, half, columns), BF, True)

    return named_call(
        finish_kernel,
        dict(
            **loaded, out_w=out_weight, qkv_w=qkv_weight, stay_up=u1[0], came_up=u1[1],
            stay_down=d1[0], came_down=d1[1], la1=a1[0], la1_x=a1[1], pg1=a1[2], pg1_send=a1[3],
            rt1=a1[4], rt1_x=a1[5], lf0=f0[0], lf0_x=f0[1], rt0=f0[2], rt0_send=f0[3], la0=a0[0],
            la0_x=a0[1],
        ),
        dict(
            f0_out=piece(wide), a0_out=piece(att), f1_out=piece(wide), a1_out=piece(att),
            small_out=((small_rows, width), F32, True), input_grad=((rows, width), BF, True),
        ),
        dict(
            **{key + "_sc": pltpu.VMEM(value.shape, value.dtype) for key, value in loaded.items()},
            pg_keep_sc=low(rows, 2 * width),
            pg_send_sc=low(rows, 2 * width),
            input_grad_sc=low(rows, width),
            small_sc=full(small_rows, width),
            w_out=low(width, width),
            w_qkv=low(width, 3 * width),
            dqkv_sc=full(rows, 3 * width),
            pg_sc=low(rows, 3 * width),
            rows_sc=full(8, width),
            heads_sc=full(8, WIDE),
            sems=pltpu.SemaphoreType.DMA((4,)),
            moves=pltpu.SemaphoreType.DMA((13,)),
            left_a1=low(4 * rows, 2 * width),
            right_a1=low(4 * rows, att),
            left_f0=low(4 * rows, f0[0].shape[1]),
            right_f0=low(4 * rows, wide * 5 // 8),
            left_a0=low(4 * rows, 2 * width),
            right_a0=low(4 * rows, att),
            pg1_x=low(rows, 3 * width // 2),
            rt0_x=low(*f0[2].shape),
            pm0_x=low(rows, 2 * width),
            part_u1=low(2, 2, BLOCK, att),
            part_d1=low(OUTER, BLOCK, att),
            part_a1=low(OUTER, 2, BLOCK, att),
            part_f0=low(OUTER, 2, BLOCK, wide),
            part_a0=low(OUTER, 2, BLOCK, att),
            y_u1=low(2, BLOCK, att),
            y_d1=low(OUTER, BLOCK, att),
            y_a1=low(2, BLOCK, att),
            y_f0=low(OUTER, BLOCK, wide),
            y_a0=low(OUTER, BLOCK, att),
            z0_u1=low(2, 2, BLOCK, att),
            z0_d1=low(2, BLOCK, att),
            z0_a1=low(2, 2, BLOCK, att),
            z0_f0=low(2, BLOCK, wide),
            z0_a0=low(2, BLOCK, att),
            z1_u1=low(BLOCK, att),
            z1_d1=low(BLOCK, att),
            z1_a1=low(BLOCK, att),
            z1_f0=low(BLOCK, wide),
            z1_a0=low(BLOCK, att),
            fin_u1=low(2, half, att),
            fin_d1=low(2, half, att),
            fin_a1=low(2, half, att),
            fin_f0=low(2, half, wide),
            fin_a0=low(2, half, att),
            far_u1=low(2, half, att),
            far_d1=low(2, half, att),
            far_a1=low(2, half, att),
            far_f0=low(2, half, wide),
            far_a0=low(2, half, att),
            sums=full(6, small_rows, width),
            sums_in=full(5, small_rows, width),
            local=pltpu.SemaphoreType.DMA((34,)),
            send=pltpu.SemaphoreType.DMA((66,)),
            recv=pltpu.SemaphoreType.DMA((66,)),
        ),
        60,
        pl.CostEstimate(
            flops=2 * rows * width * 4 * width + 2**33,
            bytes_accessed=2**26,
            transcendentals=HEADS * rows * rows,
        ),
        "finish_all",
        collective_id=3,
    )


PEERS = HEADS
FOLD = FRAME // 2
EXTRA = 16
GROUPS = 4
BACK_GROUPS = 8
MESH = pl.DeviceIdType.MESH


def fold_pair(values):
    lane = lax.broadcasted_iota(jnp.int32, (FOLD, LANES), 1)
    top, bottom = values[:FOLD], values[FOLD:]
    one = jnp.where(lane < HD, top, pltpu.roll(bottom, HD, 1))
    two = jnp.where(lane < HD, pltpu.roll(top, HD, 1), bottom)
    return one, two


def unfold_pair(one, two):
    lane = lax.broadcasted_iota(jnp.int32, (FOLD, LANES), 1)
    top = jnp.where(lane < HD, one, pltpu.roll(two, HD, 1))
    bottom = jnp.where(lane < HD, pltpu.roll(one, HD, 1), two)
    return top, bottom


def unfold_head(folded):
    lane = lax.broadcasted_iota(jnp.int32, (FOLD, LANES), 1)
    folded = folded.astype(F32)
    top = jnp.where(lane < HD, folded, 0.0)
    bottom = jnp.where(lane < HD, pltpu.roll(folded, HD, 1), 0.0)
    return top.astype(BF), bottom.astype(BF)


def fold_head(values):
    lane = lax.broadcasted_iota(jnp.int32, (FOLD, LANES), 1)
    return jnp.where(lane < HD, values[:FOLD], pltpu.roll(values[FOLD:], HD, 1))


def exchange(me, k, source, target, sems):
    return pltpu.make_async_remote_copy(
        src_ref=source,
        dst_ref=target,
        send_sem=sems.at[0, k],
        recv_sem=sems.at[1, k],
        device_id={"blk": me ^ k},
        device_id_type=MESH,
    )


def call_peers(me, partner):
    barrier = pltpu.get_barrier_semaphore()
    for k in range(1, PEERS):
        pl.semaphore_signal(barrier, 1, device_id={"blk": me ^ k}, device_id_type=MESH)
    pl.semaphore_signal(barrier, 1, device_id=partner, device_id_type=MESH)
    return lambda: pl.semaphore_wait(barrier, PEERS)


def all_to_all(me, source, target, sems, own_sem):
    copies = [exchange(me, k, source.at[me ^ k], target.at[me], sems) for k in range(PEERS - 1, 0, -1)]
    for copy in copies:
        copy.start()
    own = pltpu.make_async_copy(source.at[me], target.at[me], own_sem)
    own.start()
    return copies + [own]


def head_forward(me, qkv_ref, mark_copies, att_ref, r):
    width = att_ref.shape[1]
    for pair in range(width // LANES):
        for part in range(3):
            block = qkv_ref[:, part * width + pair * LANES : part * width + (pair + 1) * LANES]
            one, two = fold_pair(block.astype(F32) * (SCALE if part == 0 else 1.0))
            r.pack[2 * pair, part * FOLD : (part + 1) * FOLD] = one.astype(BF)
            r.pack[2 * pair + 1, part * FOLD : (part + 1) * FOLD] = two.astype(BF)
    for copy in all_to_all(me, r.pack, r.got, r.out_sems, r.own_sems.at[0]) + mark_copies:
        copy.wait()
    for s in range(PEERS):
        for part, target in enumerate((r.queries_sc, r.keys_sc, r.values_sc)):
            top, bottom = unfold_head(r.got[s, part * FOLD : (part + 1) * FOLD])
            target[s * FRAME : s * FRAME + FOLD] = top
            target[s * FRAME + FOLD : (s + 1) * FRAME] = bottom
        for index in range(2):
            at = index * PEERS + s
            r.marks_sc[at : at + 1] = r.marks_got[s, index : index + 1].astype(F32)
    keys, values = r.keys_sc[...], r.values_sc[...]
    tags = jnp.concatenate([r.marks_sc[s : s + 1] for s in range(PEERS)], axis=1)
    sends = []
    own = None
    per = PEERS // GROUPS
    for j in range(GROUPS - 1, -1, -1):
        block = (me // per) ^ j
        at = pl.ds(pl.multiple_of(block * per * FRAME, per * FRAME), per * FRAME)
        scores = product_right(r.queries_sc[at], keys)
        tops, totals, shares = [], [], []
        for i in range(per):
            scene = r.marks_sc[pl.ds(PEERS + block * per + i, 1)][:, :1]
            row = scores[i * FRAME : (i + 1) * FRAME] + jnp.where(tags == scene, 0.0, NEG)
            tops.append(jnp.max(row, axis=-1, keepdims=True))
            row = jnp.exp(row - tops[-1])
            totals.append(jnp.sum(row, axis=-1, keepdims=True))
            shares.append(row.astype(BF))
        top, total = jnp.concatenate(tops, axis=0), jnp.concatenate(totals, axis=0)
        result = product(jnp.concatenate(shares, axis=0), values) / total
        r.outs_sc[at] = result
        r.lse_sc[:, at] = as_row(top + jnp.log(total))
        for i in range(per):
            r.answers[block * per + i] = fold_head(result[i * FRAME : (i + 1) * FRAME]).astype(BF)
        for k in range(j * per, (j + 1) * per):
            if k:
                copy = exchange(me, k, r.answers.at[me ^ k], r.back.at[me], r.back_sems)
            else:
                copy = pltpu.make_async_copy(r.answers.at[me], r.back.at[me], r.own_sems.at[1])
            copy.start()
            sends.append(copy)
    for copy in sends:
        copy.wait()
    for pair in range(width // LANES):
        top, bottom = unfold_pair(r.back[2 * pair].astype(F32), r.back[2 * pair + 1].astype(F32))
        att_ref[:FOLD, pair * LANES : (pair + 1) * LANES] = top.astype(BF)
        att_ref[FOLD:, pair * LANES : (pair + 1) * LANES] = bottom.astype(BF)


def head_backward(me, grad_ref, dqkv_ref, r, meanwhile):
    width = grad_ref.shape[1]
    for pair in range(width // LANES):
        one, two = fold_pair(grad_ref[:, pair * LANES : (pair + 1) * LANES].astype(F32))
        r.pack[2 * pair] = one.astype(BF)
        r.pack[2 * pair + 1] = two.astype(BF)
    copies = all_to_all(me, r.pack, r.got, r.out_sems, r.own_sems.at[0])
    lane = lax.broadcasted_iota(jnp.int32, (1, LANES), 1)

    def lanes(terms, value):
        for index, term in enumerate(terms):
            value = jnp.where(lane == HD + index, term, value)
        return value

    for s in range(PEERS):
        at = slice(s * FRAME, (s + 1) * FRAME)
        tag = as_column(r.marks_sc[s : s + 1])
        scene = r.marks_sc[PEERS + s : PEERS + s + 1, :1]
        blocked = [jnp.where(tag == mark, NEG, 0.0) for mark in (0.0, 1.0, -1.0)]
        r.keys_sc[at] = lanes(blocked + [1.0] * 3, r.keys_sc[at].astype(F32)).astype(BF)
        other = [jnp.where(scene == mark, 0.0, 1.0) for mark in (0.0, 1.0)]
        less = [-term.astype(F32) for term in terms_of(as_column(r.lse_sc[:, at]))]
        r.queries_sc[at] = lanes(other + [1.0] + less, r.queries_sc[at].astype(F32)).astype(BF)
        r.values_sc[at] = lanes([1.0] * 3, r.values_sc[at].astype(F32)).astype(BF)
    for copy in copies:
        copy.wait()
    for s in range(PEERS):
        at = slice(s * FRAME, (s + 1) * FRAME)
        grads = jnp.concatenate(unfold_head(r.got[s]), axis=0).astype(F32)
        delta = jnp.sum(grads * r.outs_sc[at], axis=-1, keepdims=True)
        less = [-term.astype(F32) for term in terms_of(delta)]
        r.grads_sc[at] = lanes(less, grads).astype(BF)
    queries, outs = r.queries_sc[...], r.grads_sc[...]
    query_grad = None
    sends = []
    per = PEERS // BACK_GROUPS
    for j in range(BACK_GROUPS - 1, -1, -1):
        block = (me // per) ^ j
        at = pl.ds(pl.multiple_of(block * per * FRAME, per * FRAME), per * FRAME)
        keys, values = r.keys_sc[at], r.values_sc[at]
        shares = jnp.exp(product_right(keys, queries))
        score_grad = (shares * product_right(values, outs)).astype(BF)
        value_grad = product(shares.astype(BF), outs)
        key_grad = product(score_grad, queries)
        turned = jnp.transpose(keys.astype(F32)).astype(BF)[:HD]
        piece = product(turned, score_grad)
        query_grad = piece if query_grad is None else query_grad + piece
        for i in range(per):
            part = slice(i * FRAME, (i + 1) * FRAME)
            r.pairs[block * per + i, :FOLD] = fold_head(key_grad[part]).astype(BF)
            r.pairs[block * per + i, FOLD:] = fold_head(value_grad[part]).astype(BF)
        for k in range(j * per, (j + 1) * per):
            if k:
                copy = exchange(me, k, r.pairs.at[me ^ k], r.pairs_in.at[me], r.pair_sems)
            else:
                copy = pltpu.make_async_copy(r.pairs.at[me], r.pairs_in.at[me], r.own_sems.at[1])
            copy.start()
            sends.append(copy)
    padded = jnp.concatenate([query_grad * SCALE, jnp.zeros_like(query_grad)], axis=0)
    for s in range(PEERS):
        block = jnp.transpose(padded[:, s * FRAME : (s + 1) * FRAME])
        r.asked[s] = fold_head(block).astype(BF)
    sends += all_to_all(me, r.asked, r.asked_in, r.back_sems, r.own_sems.at[2])
    meanwhile()
    for copy in sends:
        copy.wait()
    for pair in range(width // LANES):
        for part in range(3):
            if part == 0:
                one, two = r.asked_in[2 * pair], r.asked_in[2 * pair + 1]
            else:
                rows = slice((part - 1) * FOLD, part * FOLD)
                one, two = r.pairs_in[2 * pair, rows], r.pairs_in[2 * pair + 1, rows]
            top, bottom = unfold_pair(one.astype(F32), two.astype(F32))
            cols = slice(part * width + pair * LANES, part * width + (pair + 1) * LANES)
            dqkv_ref[:FOLD, cols] = top.astype(BF)
            dqkv_ref[FOLD:, cols] = bottom.astype(BF)


def tile_heads(source, target):
    lane = lax.broadcasted_iota(jnp.int32, (1, WIDE), 1)
    for layer in range(2):
        every = jnp.concatenate(
            [source[layer : layer + 1], jnp.zeros((1, WIDE - 3 * HD), F32)], axis=1
        )
        for index in range(3):
            one = jnp.where((lane >= index * HD) & (lane < (index + 1) * HD), every, 0.0)
            two = one + pltpu.roll(one, HD, 1)
            target[layer, index : index + 1] = two + pltpu.roll(two, 2 * HD, 1)
        target[layer, 3:] = jnp.zeros((5, WIDE), F32)


def begin_kernel(r):
    me, x_at = lax.axis_index("blk"), lax.axis_index("grp")
    partner = {"grp": 1 - x_at}
    peers_here = call_peers(me, partner)
    width, units = r.tok.shape[1], r.up_w.shape[2]
    mover = Mover(r.moves)
    loads = [
        mover.start(*pair)
        for pair in (
            (r.tok, r.tok_sc), (r.vectors, r.vectors_sc), (r.head_norm, r.head_norm_sc),
            (r.up_bias, r.up_bias_sc), (r.valid, r.valid_sc),
        )
    ]
    copies = weight_copies(
        column_pieces(r.qkv_w.at[0], 3)
        + [r.out_w.at[0]]
        + interleaved(column_pieces(r.up_w.at[0], 4), row_pieces(r.down_w.at[0], 4)),
        column_pieces(r.w_qkv, 3)
        + [r.w_out]
        + interleaved(column_pieces(r.w_up, 4), row_pieces(r.w_down, 4)),
        r.sems,
    )
    for copy in loads:
        copy.wait()
    tile_heads(r.head_norm_sc, r.head_rows_sc)
    position = lax.broadcasted_iota(jnp.int32, (1, FRAME), 1)
    valid = jnp.where((r.valid_sc[...] == 1) | (position < SPECIAL), 1.0, 0.0)
    r.usable_sc[...] = valid
    scene = r.smem_scene[0].astype(F32)
    row = lax.broadcasted_iota(jnp.int32, (EXTRA, FRAME), 0)
    tags = jnp.where(valid > 0, scene, -1.0)
    r.marks_in_sc[...] = jnp.where(row == 0, tags, jnp.where(row == 1, scene, 0.0)).astype(BF)
    mover.flush(r.head_rows_sc, r.head_rows)
    mover.flush(r.usable_sc, r.usable)
    residual = r.tok_sc[...].astype(F32)
    normed0, att0 = r.leftatt0_sc.at[:, :width], r.leftatt0_sc.at[:, width:]
    project(
        0, residual, r.vectors_sc, r.head_rows_sc, r.w_qkv, copies[:3], normed0, r.pre0_sc,
        r.qkv0_sc,
    )
    mover.flush(r.pre0_sc, r.pre0)
    mover.flush(r.qkv0_sc, r.qkv0)
    frame_attend(r.usable_sc[...], r.qkv0_sc, att0)
    next_copies = weight_copies(
        column_pieces(r.qkv_w.at[1], 3), column_pieces(r.w_qkv, 3), r.next_sems
    )
    mover.flush(r.leftatt0_sc, r.leftatt0)
    peers_here()
    mark_copies = [
        exchange(me, k, r.marks_in_sc, r.marks_got.at[me], r.mark_sems) for k in range(1, PEERS)
    ]
    for copy in mark_copies:
        copy.start()
    r.marks_got[me] = r.marks_in_sc[...]
    sender = Sender(r.x_sems.at[0], r.x_sems.at[1], dict(x=partner))
    across = [sender.start(r.leftatt0_sc, r.leftatt0_x, "x")]
    lifted0, active0 = r.left0_sc.at[:, :width], r.left0_sc.at[:, width:]
    result = feed_forward(
        0, att0[...], residual, r.vectors_sc, r.up_bias_sc, r.w_out, r.w_up, r.w_down, copies[3:],
        r.mixed0_sc, r.middle0_sc, lifted0, r.slope0_sc, active0, r.feed0_sc,
    )
    r.res1_sc[...] = result
    for pair in (
        (r.left0_sc, r.left0), (r.mixed0_sc, r.mixed0), (r.middle0_sc, r.middle0),
        (r.slope0_sc, r.slope0), (r.feed0_sc, r.feed0), (r.res1_sc, r.res1),
    ):
        mover.flush(*pair)
    across.append(sender.start(r.left0_sc, r.left0_x, "x"))
    normed1, att1 = r.leftatt1_sc.at[:, :width], r.leftatt1_sc.at[:, width:]
    project(
        1, result, r.vectors_sc, r.head_rows_sc, r.w_qkv, next_copies, normed1, r.pre1_sc, r.qkv1_sc
    )
    mover.flush(r.pre1_sc, r.pre1)
    head_forward(me, r.qkv1_sc, mark_copies, att1, r)
    for pair in (
        (r.queries_sc, r.queries), (r.keys_sc, r.keys), (r.values_sc, r.values), (r.outs_sc, r.outs),
        (r.lse_sc, r.lse), (r.marks_sc, r.marks), (r.leftatt1_sc, r.leftatt1),
    ):
        mover.flush(*pair)
    for copy in across:
        copy.wait()
    mover.finish()


def begin(
    tokens, valid, scene, vectors, up_bias, head_norm, qkv_weight, out_weight, up_weight, down_weight
):
    rows, width = tokens.shape
    hidden = up_weight.shape[2]
    every = PEERS * FRAME
    loaded = dict(
        tok=tokens, vectors=vectors, head_norm=head_norm, up_bias=up_bias,
        valid=valid,
    )
    stored = dict(
        left0=((rows, hidden + width), BF),
        leftatt0=((rows, 2 * width), BF),
        pre0=((rows, 2 * width), F32),
        qkv0=((rows, 3 * width), BF),
        mixed0=((rows, width), F32),
        middle0=((rows, width), F32),
        slope0=((rows, hidden), F32),
        feed0=((rows, width), F32),
        res1=((rows, width), F32),
        leftatt1=((rows, 2 * width), BF),
        pre1=((rows, 2 * width), F32),
        queries=((every, LANES), BF),
        keys=((every, LANES), BF),
        values=((every, LANES), BF),
        outs=((every, LANES), F32),
        lse=((1, every), F32),
        marks=((2 * PEERS, LANES), F32),
        head_rows=((2, 8, WIDE), F32),
        usable=((1, rows), F32),
    )
    return named_call(
        begin_kernel,
        dict(
            smem_scene=scene, **loaded, qkv_w=qkv_weight, out_w=out_weight,
            up_w=up_weight, down_w=down_weight,
        ),
        dict(
            **{key: (*value, True) for key, value in stored.items()},
            leftatt0_x=((rows, 2 * width), BF, True),
            left0_x=((rows, hidden + width), BF, True),
        ),
        dict(
            **{key + "_sc": pltpu.VMEM(value.shape, value.dtype) for key, value in loaded.items()},
            **{key + "_sc": pltpu.VMEM(*value) for key, value in stored.items()},
            marks_in_sc=low(EXTRA, FRAME),
            qkv1_sc=low(rows, 3 * width),
            w_qkv=low(width, 3 * width),
            w_out=low(width, width),
            w_up=low(width, hidden),
            w_down=low(hidden, width),
            pack=low(PEERS, 3 * FOLD, LANES),
            got=low(PEERS, 3 * FOLD, LANES),
            marks_got=low(PEERS, EXTRA, LANES),
            mark_sems=pltpu.SemaphoreType.DMA((2, PEERS)),
            answers=low(PEERS, FOLD, LANES),
            back=low(PEERS, FOLD, LANES),
            sems=pltpu.SemaphoreType.DMA((12,)),
            next_sems=pltpu.SemaphoreType.DMA((3,)),
            moves=pltpu.SemaphoreType.DMA((5 + len(stored),)),
            own_sems=pltpu.SemaphoreType.DMA((2,)),
            out_sems=pltpu.SemaphoreType.DMA((2, PEERS)),
            back_sems=pltpu.SemaphoreType.DMA((2, PEERS)),
            x_sems=pltpu.SemaphoreType.DMA((2, 2)),
        ),
        60,
        pl.CostEstimate(
            flops=2 * rows * width * (7 * width + 2 * hidden) + 4 * every * every * LANES,
            bytes_accessed=2 * width * (7 * width + 2 * hidden),
            transcendentals=2 * rows * hidden + every * every,
        ),
        "begin",
        collective_id=1,
    )


def middle_kernel(r):
    me, x_at = lax.axis_index("blk"), lax.axis_index("grp")
    c_at, y_at, z0, z1 = [lax.rem(me // (1 << bit), 2) for bit in range(4)]
    partners = {"x": {"grp": 1 - x_at}, "c": {"blk": me ^ 1}}
    peers_here = call_peers(me, partners["x"])
    sender = Sender(r.ring_sems.at[0], r.ring_sems.at[1], partners)
    rows, width = r.res.shape
    units = r.up_w.shape[2]
    mover = Mover(r.moves)
    loads = [
        mover.start(*pair)
        for pair in (
            (r.vectors, r.vectors_sc), (r.leftatt1, r.leftatt1_sc), (r.res, r.res_sc),
            (r.up_bias, r.up_bias_sc), (r.cot, r.cot_sc),
        )
    ]
    copies = weight_copies(
        [r.out_w.at[1]]
        + interleaved(column_pieces(r.up_w.at[1], 4), row_pieces(r.down_w.at[1], 4)),
        [r.w_out] + interleaved(column_pieces(r.w_up, 4), row_pieces(r.w_down, 4)),
        r.sems,
    )
    late_loads = [
        mover.start(*pair)
        for pair in (
            (r.queries, r.queries_sc), (r.keys, r.keys_sc), (r.values, r.values_sc),
            (r.outs, r.outs_sc), (r.lse, r.lse_sc), (r.marks, r.marks_sc),
        )
    ]
    for copy in loads:
        copy.wait()
    own, mate = slice(0, rows), slice(rows, 2 * rows)
    quarter = units // 4
    lefts = []

    def done(j, active):
        for block in range(active.shape[1] // (2 * LANES)):
            for x in range(2):
                start = (2 * block + x) * LANES
                at = (j * active.shape[1] // 2) + block * LANES
                r.act_sc[x, :, at : at + LANES] = active[:, start : start + LANES]
        if j == 0:
            peers_here()
            lefts.append(
                sender.start(r.left_sc.at[own, :width], r.left_sc.at[mate, :width], "x")
            )
        filled = (j + 1) * active.shape[1] // 2
        if filled % quarter == 0:
            at = slice(filled - quarter, filled)
            to = slice(width + filled - quarter, width + filled)
            lefts.append(
                sender.start(r.act_sc.at[1 - x_at, :, at], r.left_sc.at[mate, to], "x")
            )

    result = feed_forward(
        1, r.leftatt1_sc[:, width:], r.res_sc[...], r.vectors_sc, r.up_bias_sc, r.w_out, r.w_up,
        r.w_down, copies, r.mixed_sc, r.middle_sc, r.left_sc.at[own, :width], r.slope_sc, None,
        r.feed_sc, done,
    )
    r.left_sc[own, width:] = r.act_sc[x_at]
    left_c = sender.start(r.left_sc.at[own], r.left_sc.at[2 * rows : 3 * rows], "c")
    r.output_sc[...] = result.astype(BF)
    mover.flush(r.output_sc, r.output)
    grad = feed_backward(
        1, r.cot_sc[...].astype(F32), r.feed_sc[...], r.middle_sc[...], r.mixed_sc[...],
        r.slope_sc, r.vectors_sc, r.w_up, r.w_down, None, r.fg_sc, r.hg_sc, r.mg_sc, r.bias_out,
        r.rows_out, 0,
    )
    half, part = units // 2, width // 2

    def columns(ref, start, count):
        return ref.at[:, pl.ds(pl.multiple_of(start, LANES), count)]

    rights = [
        sender.start(columns(r.hg_sc, (1 - x_at) * half, half), r.far_sc.at[:, :half], "x"),
        sender.start(r.fg_sc, r.far_sc.at[:, half:], "x"),
    ]
    mixed_x = sender.start(columns(r.mg_sc, (1 - x_at) * part, part), r.mixed1_x, "x")
    q_up, q_down = half // 2, part
    ready = [left_c]

    def place(up, down, up_at, down_at, index):
        here = slice(index * rows, (index + 1) * rows)
        there = slice((2 + index) * rows, (3 + index) * rows)
        for ref, start, count, to in ((up, up_at, q_up, 0), (down, down_at, q_down, q_up)):
            ready.append(
                mover.start(
                    columns(ref, start + c_at * count, count), r.right_sc.at[here, to : to + count]
                )
            )
            ready.append(
                sender.start(
                    columns(ref, start + (1 - c_at) * count, count),
                    r.right_sc.at[there, to : to + count],
                    "c",
                )
            )

    place(r.hg_sc, r.fg_sc, x_at * half, 0, 0)
    mover.flush(columns(r.mg_sc, x_at * part, part), r.mixed1)
    r.middle_grad_sc[...] = grad
    mover.flush(r.middle_grad_sc, r.middle_grad)
    r.att_grad_sc[...] = product_right(r.mg_sc[...], r.w_out[...]).astype(BF)
    for copy in late_loads:
        copy.wait()

    def meanwhile():
        for copy in lefts:
            copy.wait_recv()
        ready.append(
            sender.start(r.left_sc.at[mate], r.left_sc.at[3 * rows : 4 * rows], "c")
        )

    head_backward(me, r.att_grad_sc, r.dqkv_sc, r, meanwhile)
    mover.flush(r.dqkv_sc, r.dqkv)
    for copy in rights:
        copy.wait_recv()
    place(r.far_sc, r.far_sc, 0, half, 1)
    for copy in ready:
        copy.wait_recv()
    for slot in range(OUTER):
        target = (r.away_up_sc if slot < 2 else r.stay_up_sc).at[slot % 2]

        def emit(target, y, row, col, values):
            height, wide = values.shape
            target[y, row : row + height, col : col + wide] = values

        group = slot_group(slot, z0, z1)
        slot_product(
            group, r.left_sc, 0, r.right_sc, 0, q_up, False, functools.partial(emit, target)
        )
        for y in range(2):
            start = pl.multiple_of(width + (2 * group + y) * 2 * BLOCK, BLOCK)
            result = product_left(
                r.left_sc[:, pl.ds(start, 2 * BLOCK)], r.right_sc[:, q_up:]
            ).astype(BF)
            piece = BLOCK // 2
            for c in range(2):
                for t in range(2):
                    row = (2 * c + t) * piece
                    emit(r.down_sc.at[slot], y, c * piece, t * q_down, result[row : row + piece])
        if slot == 1:
            mover.flush(r.away_up_sc, r.away_up)
    mover.flush(r.down_sc.at[:, 1 - y_at], r.away_down)
    mover.flush(r.down_sc.at[:, y_at], r.stay_down)
    mover.flush(r.stay_up_sc, r.stay_up)
    mixed_x.wait_recv()
    assert len(sender.copies) == r.ring_sems.shape[1]
    sender.finish()
    mover.finish()


def middle(first, cotangent, vectors, up_bias, out_weight, up_weight, down_weight):
    rows, width = cotangent.shape
    hidden = up_weight.shape[2]
    every = PEERS * FRAME
    loaded = dict(
        vectors=vectors, leftatt1=first.leftatt1, res=first.res1, up_bias=up_bias,
        cot=cotangent, queries=first.queries, keys=first.keys, values=first.values,
        outs=first.outs, lse=first.lse, marks=first.marks,
    )
    columns = hidden // 4
    stored = dict(
        output=((rows, width), BF),
        middle_grad=((rows, width), F32),
        dqkv=((rows, 3 * width), BF),
        stay_up=((2, 2, BLOCK, columns), BF),
        away_up=((2, 2, BLOCK, columns), BF),
    )
    return named_call(
        middle_kernel,
        dict(
            **loaded, out_w=out_weight, up_w=up_weight, down_w=down_weight,
        ),
        dict(
            **{key: (*value, True) for key, value in stored.items()},
            stay_down=((OUTER, BLOCK, columns), BF, True),
            away_down=((OUTER, BLOCK, columns), BF, True),
            mixed1=((rows, width // 2), BF, True),
            mixed1_x=((rows, width // 2), BF, True),
            bias_out=((1, hidden), F32, False),
            rows_out=((8, width), F32, False),
        ),
        dict(
            **{key + "_sc": pltpu.VMEM(value.shape, value.dtype) for key, value in loaded.items()},
            **{key + "_sc": pltpu.VMEM(*value) for key, value in stored.items()},
            w_out=low(width, width),
            w_up=low(width, hidden),
            w_down=low(hidden, width),
            left_sc=low(4 * rows, hidden // 2 + width),
            act_sc=low(2, rows, hidden // 2),
            down_sc=low(OUTER, 2, BLOCK, columns),
            right_sc=low(4 * rows, hidden // 4 + width // 2),
            far_sc=low(rows, hidden // 2 + width),
            mixed_sc=full(rows, width),
            middle_sc=full(rows, width),
            slope_sc=full(rows, hidden),
            feed_sc=full(rows, width),
            fg_sc=low(rows, width),
            hg_sc=low(rows, hidden),
            mg_sc=low(rows, width),
            att_grad_sc=low(rows, width),
            grads_sc=low(every, LANES),
            pack=low(PEERS, FOLD, LANES),
            got=low(PEERS, FOLD, LANES),
            pairs=low(PEERS, 2 * FOLD, LANES),
            pairs_in=low(PEERS, 2 * FOLD, LANES),
            asked=low(PEERS, FOLD, LANES),
            asked_in=low(PEERS, FOLD, LANES),
            sems=pltpu.SemaphoreType.DMA((9,)),
            moves=pltpu.SemaphoreType.DMA((23,)),
            own_sems=pltpu.SemaphoreType.DMA((3,)),
            out_sems=pltpu.SemaphoreType.DMA((2, PEERS)),
            back_sems=pltpu.SemaphoreType.DMA((2, PEERS)),
            pair_sems=pltpu.SemaphoreType.DMA((2, PEERS)),
            ring_sems=pltpu.SemaphoreType.DMA((2, 12)),
        ),
        60,
        pl.CostEstimate(
            flops=4 * rows * width * (width + 2 * hidden) + 10 * every * every * LANES,
            bytes_accessed=2 * width * (width + 2 * hidden),
            transcendentals=2 * rows * hidden + every * every,
        ),
        "middle",
        collective_id=2,
    )


def per_device(
    tokens,
    qkv_weight,
    out_weight,
    up_weight,
    down_weight,
    vectors,
    up_bias,
    head_norm,
    token_valid,
    frame_scene,
    cotangent,
):
    count = lax.axis_size("blk")
    outer = count // 4
    me = lax.axis_index("blk")
    x_at = lax.axis_index("grp")
    c_at = lax.rem(me, 2)
    y_at = lax.rem(me // 2, 2)
    c_pairs = [(i, i ^ 1) for i in range(count)]
    y_pairs = [(i, i ^ 2) for i in range(count)]
    z_groups = [[4 * o + k for o in range(outer)] for k in range(4)]
    halves_at = jnp.stack([x_at, x_at]).astype(jnp.int32)
    places = jnp.stack(
        [c_at, y_at, x_at, lax.rem(me // 4, 2), lax.rem(me // 8, 2), halves_at[1], me]
    ).astype(jnp.int32)


    def swap_x(value):
        return lax.ppermute(value, "grp", [(0, 1), (1, 0)])

    def swap_c(value):
        return lax.ppermute(value, "blk", c_pairs)

    def swap_y(value):
        return lax.ppermute(value, "blk", y_pairs)

    def part(value, index, parts, axis):
        size = value.shape[axis] // parts
        return lax.dynamic_slice_in_dim(value, index * size, size, axis)

    def tied(value, *others):
        return lax.optimization_barrier((value, *others))

    def ready_sum(keep, arrived):
        return (keep.astype(F32) + arrived.astype(F32)).astype(BF)

    def scattered(own):
        return lax.psum_scatter(
            own, "blk", scatter_dimension=0, tiled=True, axis_index_groups=z_groups
        )

    def finished(total):
        pair = jnp.stack([part(total, c_at, 2, 0), swap_c(part(total, 1 - c_at, 2, 0))])
        return jnp.concatenate([pair, swap_x(pair)], axis=0)

    def total_of(value):
        value = value + swap_x(value)
        step = 1
        while step < count:
            pairs = [(i, i ^ step) for i in range(count)]
            value = value + lax.ppermute(value, "blk", pairs)
            step *= 2
        return value

    row_count, width = tokens.shape[1:]
    vector_count = vectors.shape[1]
    vectors = vectors.transpose(1, 0, 2)
    hidden = up_weight.shape[2]
    if count == HEADS:
        first = begin(
            tokens[0], token_valid[0], frame_scene[0], vectors, up_bias, head_norm, qkv_weight,
            out_weight, up_weight, down_weight,
        )
        head_rows, usable_row = first.head_rows, first.usable
        second = middle(
            first, cotangent[0], vectors, up_bias, out_weight, up_weight, down_weight
        )
        came_up = lax.ppermute(second.away_up, "blk", [(i, i ^ 4) for i in range(count)])
        came_down, leftatt1_x = swap_y(second.away_down), swap_x(first.leftatt1)
        pre0, qkv0, mixed0, middle0, slope0, feed0, res1, pre1 = (
            first.pre0, first.qkv0, first.mixed0, first.middle0, first.slope0, first.feed0,
            first.res1, first.pre1,
        )
        output, middle_grad1, dqkv1, bias1, rows1 = (
            second.output, second.middle_grad, second.dqkv, second.bias_out, second.rows_out
        )
    else:
        position = lax.broadcasted_iota(jnp.int32, (row_count,), 0)
        usable = (token_valid[0, 0] == 1) | (position < SPECIAL)
        usable_row = usable.astype(F32).reshape(1, row_count)
        scene = frame_scene[0, 0].astype(F32)
        tag_rows = jnp.where(usable, scene, -1.0)
        head_rows = jnp.tile(head_norm.reshape(2, 3, HD), (1, 1, WIDE // HD))
        head_rows = jnp.concatenate([head_rows, jnp.zeros((2, 5, WIDE), F32)], axis=1)
        left0, leftatt0, pre0, qkv0, mixed0, middle0, slope0, feed0, res1, normed1, pre1, qkv1 = (
            front(
                tokens[0], usable_row, vectors, up_bias, head_rows, qkv_weight, out_weight,
                up_weight, down_weight,
            )
        )
        att1, kept = gathered_forward(qkv1, tag_rows, scene)
        left1, leftatt1, output, right1, right1_send, att_grad1, middle_grad1, bias1, rows1 = turn(
            halves_at, att1, normed1, res1, cotangent[0], vectors, up_bias, out_weight, up_weight,
            down_weight,
        )
        dqkv1 = gathered_backward(att_grad1, kept, tag_rows, scene)
    third = back_one(
        dqkv1, pre1, res1, middle_grad1, feed0, middle0, mixed0, slope0, vectors,
        head_rows, qkv_weight, up_weight, down_weight,
    )
    frame = dict(
        mixed_grad=third.mixed_grad, grad=third.middle_grad, qkv=qkv0, pre=pre0, tok=tokens[0],
        usable=usable_row, vectors=vectors, head_rows=head_rows, rows10=third.rows_out, rows1=rows1,
        bias0=third.bias_out, bias1=bias1, heads1=third.head_out, out_w=out_weight, qkv_w=qkv_weight,
    )

    def feed_grads(name, lefts, rights):
        return weight_grads(
            name,
            outer,
            width,
            places,
            [
                (lefts, 0, width, rights, 0, hidden // 2, False),
                (lefts, width, hidden, rights, hidden // 2, width // 2, True),
            ],
        )

    def att_grads(name, lefts, projected, rights, at):
        return weight_grads(
            name,
            outer,
            width,
            places,
            [
                (lefts, 0, width, projected, 0, 3 * width // 2, False),
                (lefts, width, width, rights, at, width // 2, False),
            ],
        )

    def four(own, far):
        return (own, far, swap_c(own), swap_c(far))

    def reduce_apart(fourth):
        pg1_x, right0_far = swap_x(third.pg_send), swap_x(third.right_send)
        pg0_all = four(fourth.pg_keep, swap_x(fourth.pg_send))
        right1_all = four(right1, swap_x(right1_send))
        results = []
        for keep, send in (
            feed_grads(
                "feed_grads0", four(left0, swap_x(left0)), four(third.right_keep, right0_far)
            ),
            att_grads(
                "att_grads0", four(leftatt0, swap_x(leftatt0)), pg0_all, pg0_all, 3 * width // 2
            ),
            feed_grads("feed_grads1", four(left1, swap_x(left1)), right1_all),
            att_grads(
                "att_grads1", four(leftatt1, swap_x(leftatt1)), four(third.pg_keep, pg1_x),
                right1_all, (hidden + width) // 2,
            ),
        ):
            results.append(finished(scattered(ready_sum(keep, swap_y(send)))))
        return results

    if count == HEADS:
        fourth = finish_all(
            frame,
            (second.stay_up, came_up),
            (second.stay_down, came_down),
            (
                first.leftatt1, leftatt1_x, third.pg_keep, third.pg_send, second.mixed1,
                second.mixed1_x,
            ),
            (first.left0, first.left0_x, third.right_keep, third.right_send),
            (first.leftatt0, first.leftatt0_x),
        )
        pieces = [fourth.f0_out, fourth.a0_out, fourth.f1_out, fourth.a1_out]
        small = fourth.small_out
    else:
        fourth = back_two(halves_at, **frame)
        small = total_of(fourth.small)
        pieces = reduce_apart(fourth)
    weight_shapes = [
        (2, width // count, 3 * width),
        (2, width // count, width),
        (2, width // count, up_weight.shape[2]),
        (2, up_weight.shape[2] // count, width),
    ]
    if count == HEADS:
        small_shapes = [(vector_count, 2, HD), (2, hidden // count), (2, 3 * HD)]
        (
            qkv_grad, out_grad, up_grad, down_grad, vector_grad, bias_grad, head_grad, output,
            input_grad,
        ) = assemble(
            [*pieces, small], weight_shapes + small_shapes, [output, fourth.input_grad]
        )
        vector_grad = vector_grad.transpose(1, 0, 2)
    else:
        qkv_grad, out_grad, up_grad, down_grad = assemble(pieces, weight_shapes, [])
        input_grad = fourth.input_grad
        bias_rows = 2 * hidden // width
        vector_grad = part(small[: 2 * vector_count].reshape(2, -1, width), me, count, 2)
        bias_grad = small[2 * vector_count : 2 * vector_count + bias_rows].reshape(2, hidden)
        bias_grad = part(bias_grad, me, count, 1)
        head_grad = small[2 * vector_count + bias_rows, : 6 * HD].reshape(2, 3 * HD)
    return (
        output[None],
        input_grad[None],
        qkv_grad,
        out_grad,
        up_grad,
        down_grad,
        vector_grad,
        bias_grad,
        head_grad,
    )


def gathered_forward(qkv, tag_rows, scene):
    rows, width = qkv.shape[0], qkv.shape[1] // 3
    marks = jnp.zeros((KEEP, 2 * width), BF)
    marks = marks.at[0, :rows].set(tag_rows.astype(BF))
    marks = marks.at[1, :rows].set(jnp.full((rows,), scene).astype(BF))
    pairs = lax.all_gather(
        jnp.concatenate([qkv[:, width:], marks], axis=0), "blk", axis=0, tiled=False
    )
    tags = pairs[:, FRAME, :FRAME].astype(F32).reshape(1, -1)
    scenes = pairs[:, FRAME + 1, :FRAME].astype(F32).reshape(1, -1)
    queries = qkv[:, :width]
    attended, lse = global_attend(queries, pairs, tags, jnp.full((8, LANES), scene))
    every_query = lax.all_gather(
        with_rows(queries, lse.reshape(HEADS, rows)), "blk", axis=0, tiled=False
    )
    return attended.astype(BF), (qkv, pairs, tags, scenes, attended, lse, every_query)


def gathered_backward(attended_grad, kept, tag_rows, scene):
    qkv, pairs, tags, scenes, attended, lse, every_query = kept
    rows, width = attended_grad.shape
    delta = jnp.sum(
        (attended_grad.astype(F32) * attended).reshape(rows, HEADS, HD), axis=-1
    ).T
    every_grad = lax.all_gather(with_rows(attended_grad, delta), "blk", axis=0, tiled=False)
    query_grad = global_query_grad(
        qkv[:, :width],
        pairs,
        tags,
        jnp.full((8, LANES), scene),
        attended_grad,
        lse,
        delta.reshape(PAIRS, 2, rows),
    )
    key_grad, value_grad = global_key_grad(
        qkv[:, width : 2 * width],
        qkv[:, 2 * width :],
        tag_rows.reshape(1, rows),
        scenes,
        every_query,
        every_grad,
        rows_of(every_query, width),
        rows_of(every_grad, width),
    )
    return jnp.concatenate([query_grad, key_grad, value_grad], axis=1).astype(BF)


def solution(mesh):
    return jax.shard_map(
        per_device,
        mesh=mesh,
        in_specs=(
            P("grp", "blk", None),
            P(),
            P(),
            P(),
            P(),
            P(),
            P(),
            P(),
            P("grp", "blk", None),
            P("grp", "blk"),
            P("grp", "blk", None),
        ),
        out_specs=(
            P("grp", "blk", None),
            P("grp", "blk", None),
            P(None, "blk", None),
            P(None, "blk", None),
            P(None, "blk", None),
            P(None, "blk", None),
            P(None, None, "blk"),
            P(None, "blk"),
            P(),
        ),
        check_vma=False,
    )
```

```python
import functools
import types
from itertools import chain

import jax
import jax.numpy as jnp
from jax import lax
from jax.experimental import pallas as pl
from jax.experimental.pallas import tpu as pltpu
from jax.sharding import PartitionSpec as P

HEADS = 16
HD = 64
SPECIAL = 5
PAIRS = HEADS // 2
LANES = 2 * HD
FRAME = 128
KEEP = 16
EPS = 1e-06
NEG = -1e30
SCALE = HD**-0.5
BF = jnp.bfloat16
F32 = jnp.float32


def product(left_side, right_side):
    return jnp.dot(left_side, right_side, preferred_element_type=F32)


def product_left(left_side, right_side):
    return lax.dot_general(
        left_side, right_side, (((0,), (0,)), ((), ())), preferred_element_type=F32
    )


def product_right(left_side, right_side):
    return lax.dot_general(
        left_side, right_side, (((1,), (1,)), ((), ())), preferred_element_type=F32
    )


def lane_masks(dtype):
    lane = lax.broadcasted_iota(jnp.int32, (1, LANES), 1)
    first = (lane < HD).astype(dtype)
    return (first, 1 - first)


def as_column(row):
    size = row.shape[1]
    return jnp.transpose(jnp.broadcast_to(row, (LANES, size)))[:, :1]


def as_row(column):
    size = column.shape[0]
    return jnp.transpose(jnp.broadcast_to(column, (size, LANES)))[:1, :]


def flat(ref):
    block = ref[...]
    return block.reshape(block.shape[0] * block.shape[1], block.shape[2])


def attend_kernel(blocks, q_ref, k_ref, v_ref, tag_ref, scene_ref, o_ref, lse_ref, m_sc, l_sc, a_sc):
    step = pl.program_id(1)
    keys, values = flat(k_ref), flat(v_ref)
    allowed = tag_ref[...] == scene_ref[:1, :1]
    queries = q_ref[...]
    pieces = []
    for index, mask in enumerate(lane_masks(BF)):
        scores = product_right(queries * mask, keys) * SCALE
        scores = jnp.where(allowed, scores, NEG)
        top = jnp.max(scores, axis=-1, keepdims=True)

        if blocks > 1:

            @pl.when(step == 0)
            def _():
                m_sc[index] = jnp.full_like(m_sc[index], NEG)
                l_sc[index] = jnp.zeros_like(l_sc[index])
                a_sc[index] = jnp.zeros_like(a_sc[index])

            old = m_sc[index][:, :1]
            top = jnp.maximum(top, old)
            keep = jnp.exp(old - top)
        shares = jnp.where(allowed, jnp.exp(scores - top), 0.0)
        total = jnp.sum(shares, axis=-1, keepdims=True)
        weighted = product(shares.astype(BF), values)
        if blocks > 1:
            total = total + keep * l_sc[index][:, :1]
            weighted = weighted + keep * a_sc[index]
            m_sc[index] = jnp.broadcast_to(top, m_sc[index].shape)
            l_sc[index] = jnp.broadcast_to(total, l_sc[index].shape)
            a_sc[index] = weighted
        pieces.append(weighted / total)
        lse_ref[0, index : index + 1, :] = as_row(top + jnp.log(total))
    first, second = lane_masks(F32)
    o_ref[...] = jnp.where(first > 0, pieces[0], pieces[1])


def key_block(count):
    for size in (16, 8, 4, 2, 1):
        if count % size == 0:
            return size


def global_attend(queries, pairs, tags, scene):
    frames = pairs.shape[0]
    group = key_block(frames)
    blocks = frames // group
    return pl.pallas_call(
        functools.partial(attend_kernel, blocks),
        grid=(PAIRS, blocks),
        in_specs=[
            pl.BlockSpec((FRAME, LANES), lambda p, k: (0, p)),
            pl.BlockSpec((group, FRAME, LANES), lambda p, k: (k, 0, p)),
            pl.BlockSpec((group, FRAME, LANES), lambda p, k: (k, 0, PAIRS + p)),
            pl.BlockSpec((1, group * FRAME), lambda p, k: (0, k)),
            pl.BlockSpec((8, LANES), lambda p, k: (0, 0)),
        ],
        out_specs=[
            pl.BlockSpec((FRAME, LANES), lambda p, k: (0, p)),
            pl.BlockSpec((1, 2, FRAME), lambda p, k: (p, 0, 0)),
        ],
        out_shape=[
            jax.ShapeDtypeStruct((FRAME, PAIRS * LANES), F32),
            jax.ShapeDtypeStruct((PAIRS, 2, FRAME), F32),
        ],
        scratch_shapes=[pltpu.VMEM((2, FRAME, LANES), F32)] * 3,
        compiler_params=pltpu.CompilerParams(vmem_limit_bytes=48 * 2**20),
        cost_estimate=pl.CostEstimate(
            flops=4 * FRAME * frames * FRAME * LANES * HEADS,
            bytes_accessed=frames * FRAME * 4096,
            transcendentals=FRAME * frames * FRAME * HEADS,
        ),
        name="global_attend",
    )(queries, pairs, pairs, tags, scene)


def query_grad_kernel(
    q_ref, k_ref, v_ref, tag_ref, scene_ref, do_ref, lse_ref, delta_ref, dq_ref
):
    step = pl.program_id(1)
    keys, values = flat(k_ref), flat(v_ref)
    allowed = tag_ref[...] == scene_ref[:1, :1]
    queries, outs = q_ref[...], do_ref[...]
    pieces = []
    for index, mask in enumerate(lane_masks(BF)):
        scores = product_right(queries * mask, keys) * SCALE
        top = as_column(lse_ref[0, index : index + 1, :])
        delta = as_column(delta_ref[0, index : index + 1, :])
        shares = jnp.where(allowed, jnp.exp(scores - top), 0.0)
        share_grad = product_right(outs * mask, values)
        score_grad = (shares * (share_grad - delta)).astype(BF)
        pieces.append(product(score_grad, keys) * SCALE)
    first, second = lane_masks(F32)
    piece = jnp.where(first > 0, pieces[0], pieces[1])

    @pl.when(step == 0)
    def _():
        dq_ref[...] = piece

    @pl.when(step > 0)
    def _():
        dq_ref[...] += piece


def global_query_grad(queries, pairs, tags, scene, outs, lse, delta):
    frames = pairs.shape[0]
    group = key_block(frames)
    blocks = frames // group
    return pl.pallas_call(
        query_grad_kernel,
        grid=(PAIRS, blocks),
        in_specs=[
            pl.BlockSpec((FRAME, LANES), lambda p, k: (0, p)),
            pl.BlockSpec((group, FRAME, LANES), lambda p, k: (k, 0, p)),
            pl.BlockSpec((group, FRAME, LANES), lambda p, k: (k, 0, PAIRS + p)),
            pl.BlockSpec((1, group * FRAME), lambda p, k: (0, k)),
            pl.BlockSpec((8, LANES), lambda p, k: (0, 0)),
            pl.BlockSpec((FRAME, LANES), lambda p, k: (0, p)),
            pl.BlockSpec((1, 2, FRAME), lambda p, k: (p, 0, 0)),
            pl.BlockSpec((1, 2, FRAME), lambda p, k: (p, 0, 0)),
        ],
        out_specs=pl.BlockSpec((FRAME, LANES), lambda p, k: (0, p)),
        out_shape=jax.ShapeDtypeStruct((FRAME, PAIRS * LANES), F32),
        compiler_params=pltpu.CompilerParams(vmem_limit_bytes=48 * 2**20),
        cost_estimate=pl.CostEstimate(
            flops=6 * FRAME * frames * FRAME * LANES * HEADS,
            bytes_accessed=frames * FRAME * 4096,
            transcendentals=FRAME * frames * FRAME * HEADS,
        ),
        name="global_query_grad",
    )(queries, pairs, pairs, tags, scene, outs, lse, delta)


def key_grad_kernel(
    k_ref, v_ref, tag_ref, scene_ref, q_ref, do_ref, lse_ref, delta_ref, dk_ref, dv_ref
):
    step = pl.program_id(1)
    keys, values = k_ref[...], v_ref[...]
    queries, outs = flat(q_ref), flat(do_ref)
    allowed = as_column(tag_ref[...]) == scene_ref[...]
    key_pieces, value_pieces = [], []
    for index, mask in enumerate(lane_masks(BF)):
        scores = product_right(keys * mask, queries) * SCALE
        top = lse_ref[0, index : index + 1, :]
        delta = delta_ref[0, index : index + 1, :]
        shares = jnp.where(allowed, jnp.exp(scores - top), 0.0)
        share_grad = product_right(values * mask, outs)
        score_grad = (shares * (share_grad - delta)).astype(BF)
        key_pieces.append(product(score_grad, queries) * SCALE)
        value_pieces.append(product(shares.astype(BF), outs))
    first, second = lane_masks(F32)
    key_piece = jnp.where(first > 0, key_pieces[0], key_pieces[1])
    value_piece = jnp.where(first > 0, value_pieces[0], value_pieces[1])

    @pl.when(step == 0)
    def _():
        dk_ref[...] = key_piece
        dv_ref[...] = value_piece

    @pl.when(step > 0)
    def _():
        dk_ref[...] += key_piece
        dv_ref[...] += value_piece


def global_key_grad(keys, values, tags, scenes, queries, outs, lse, delta):
    frames = queries.shape[0]
    group = key_block(frames)
    blocks = frames // group
    return pl.pallas_call(
        key_grad_kernel,
        grid=(PAIRS, blocks),
        in_specs=[
            pl.BlockSpec((FRAME, LANES), lambda p, k: (0, p)),
            pl.BlockSpec((FRAME, LANES), lambda p, k: (0, p)),
            pl.BlockSpec((1, FRAME), lambda p, k: (0, 0)),
            pl.BlockSpec((1, group * FRAME), lambda p, k: (0, k)),
            pl.BlockSpec((group, FRAME, LANES), lambda p, k: (k, 0, p)),
            pl.BlockSpec((group, FRAME, LANES), lambda p, k: (k, 0, p)),
            pl.BlockSpec((1, 2, group * FRAME), lambda p, k: (p, 0, k)),
            pl.BlockSpec((1, 2, group * FRAME), lambda p, k: (p, 0, k)),
        ],
        out_specs=[pl.BlockSpec((FRAME, LANES), lambda p, k: (0, p))] * 2,
        out_shape=[jax.ShapeDtypeStruct((FRAME, PAIRS * LANES), F32)] * 2,
        compiler_params=pltpu.CompilerParams(vmem_limit_bytes=48 * 2**20),
        cost_estimate=pl.CostEstimate(
            flops=8 * FRAME * frames * FRAME * LANES * HEADS,
            bytes_accessed=frames * FRAME * 4096,
            transcendentals=FRAME * frames * FRAME * HEADS,
        ),
        name="global_key_grad",
    )(keys, values, tags, scenes, queries, outs, lse, delta)


def split_three(values):
    high = values.astype(BF)
    rest = values - high.astype(F32)
    middle = rest.astype(BF)
    return jnp.stack([high, middle, (rest - middle.astype(F32)).astype(BF)])


def with_rows(body, statistic):
    width = body.shape[1]
    extra = split_three(statistic).reshape(-1, width)
    pad = jnp.zeros((KEEP - extra.shape[0], width), BF)
    return jnp.concatenate([body, extra, pad], axis=0)


def rows_of(gathered, width):
    frames = gathered.shape[0]
    used = 3 * HEADS * FRAME // width
    terms = gathered[:, FRAME : FRAME + used].reshape(frames, 3, HEADS, FRAME).astype(F32)
    total = terms[:, 0] + terms[:, 1] + terms[:, 2]
    return total.transpose(1, 0, 2).reshape(PAIRS, 2, frames * FRAME)


VMEM_MIB = 2**20
WIDE = 256
ROOT_HALF = 0.7071067811865476
ROOT_TWO_PI = 0.3989422804014327


def whole(space=pltpu.VMEM):
    return pl.BlockSpec(memory_space=space)


def terms_of(values):
    high = values.astype(BF)
    rest = values - high.astype(F32)
    middle = rest.astype(BF)
    return (high, middle, (rest - middle.astype(F32)).astype(BF))


def head_averager():
    row = lax.broadcasted_iota(jnp.int32, (WIDE, WIDE), 0) // HD
    col = lax.broadcasted_iota(jnp.int32, (WIDE, WIDE), 1) // HD
    return jnp.where(row == col, 1.0 / HD, 0.0).astype(BF)


def head_mean(values, averager):
    high = values.astype(BF)
    rest = (values - high.astype(F32)).astype(BF)
    return product(high, averager) + product(rest, averager)


def standard(values):
    centered = values - jnp.mean(values, axis=-1, keepdims=True)
    scale = lax.rsqrt(jnp.mean(centered * centered, axis=-1, keepdims=True) + EPS)
    return centered * scale, scale


def standard_heads(values, averager):
    centered = values - head_mean(values, averager)
    scale = lax.rsqrt(head_mean(centered * centered, averager) + EPS)
    return centered * scale, scale


def norm_pull(values, gain, grad):
    unit, scale = standard(values)
    scaled = grad * gain
    spread = jnp.mean(scaled * unit, axis=-1, keepdims=True)
    result = scale * (scaled - jnp.mean(scaled, axis=-1, keepdims=True) - unit * spread)
    return (
        result,
        jnp.sum(grad * unit, axis=0, keepdims=True),
        jnp.sum(grad, axis=0, keepdims=True),
    )


def weight_copies(sources, targets, sems):
    copies = [
        pltpu.make_async_copy(source, target, sems.at[index])
        for index, (source, target) in enumerate(zip(sources, targets))
    ]
    for copy in copies:
        copy.start()
    return copies


def column_pieces(ref, parts):
    size = ref.shape[-1] // parts
    return [ref.at[:, i * size : (i + 1) * size] for i in range(parts)]


def row_pieces(ref, parts):
    size = ref.shape[0] // parts
    return [ref.at[i * size : (i + 1) * size] for i in range(parts)]


def project(layer, residual, vec_ref, head_ref, w_ref, copies, normed_ref, pre_ref, qkv_ref):
    width = residual.shape[1]
    unit, _ = standard(residual)
    normed = (unit * vec_ref[0, layer : layer + 1] + vec_ref[1, layer : layer + 1]).astype(BF)
    normed_ref[...] = normed
    averager = head_averager()
    for part in range(3):
        copies[part].wait()
        bias = vec_ref[2 + part, layer : layer + 1]
        for j in range(width // WIDE):
            at = slice(part * width + j * WIDE, part * width + (j + 1) * WIDE)
            value = product(normed, w_ref[:, at]) + bias[:, j * WIDE : (j + 1) * WIDE]
            if part < 2:
                pre_ref[:, at] = value
                unit, _ = standard_heads(value, averager)
                value = unit * head_ref[layer, 2 * part : 2 * part + 1]
                if part == 0:
                    value = value + head_ref[layer, 1:2]
            qkv_ref[:, at] = value.astype(BF)


def frame_attend(usable, qkv_ref, att_ref):
    width = att_ref.shape[1]
    first, _ = lane_masks(F32)
    for pair in range(width // LANES):
        q, k, v = [
            qkv_ref[:, part * width + pair * LANES : part * width + (pair + 1) * LANES]
            for part in range(3)
        ]
        pieces = []
        for mask in lane_masks(BF):
            shares = frame_shares(q * mask, k, usable)
            pieces.append(product(shares.astype(BF), v))
        at = slice(pair * LANES, (pair + 1) * LANES)
        att_ref[:, at] = jnp.where(first > 0, pieces[0], pieces[1]).astype(att_ref.dtype)


def frame_shares(queries, keys, usable):
    scores = jnp.where(usable > 0, product_right(queries, keys) * SCALE, NEG)
    shares = jnp.exp(scores - jnp.max(scores, axis=-1, keepdims=True))
    return shares / jnp.sum(shares, axis=-1, keepdims=True)


def feed_forward(
    layer, att, residual, vec_ref, bias_ref, w_out, w_up, w_down, copies, mixed_ref, middle_ref,
    lifted_ref, slope_ref, active_ref, feed_ref, done=None,
):
    chunks = w_up.shape[1] // 512
    copies[0].wait()
    mixed = product(att, w_out[...]) + vec_ref[5, layer : layer + 1]
    mixed_ref[...] = mixed
    middle = residual + vec_ref[6, layer : layer + 1] * mixed
    middle_ref[...] = middle
    unit, _ = standard(middle)
    lifted = (unit * vec_ref[7, layer : layer + 1] + vec_ref[8, layer : layer + 1]).astype(BF)
    lifted_ref[...] = lifted
    feed = None
    for j in range(chunks):
        at = slice(j * 512, (j + 1) * 512)
        if j % 2 == 0:
            copies[1 + j].wait()
            copies[2 + j].wait()
        hidden = product(lifted, w_up[:, at]) + bias_ref[layer : layer + 1, at]
        bell = 0.5 * (1.0 + lax.erf(hidden * ROOT_HALF))
        slope_ref[:, at] = bell + hidden * jnp.exp(-0.5 * hidden * hidden) * ROOT_TWO_PI
        active = (hidden * bell).astype(BF)
        if done is None:
            active_ref[:, at] = active
        else:
            done(j, active)
        piece = product(active, w_down[at])
        feed = piece if feed is None else feed + piece
    feed = feed + vec_ref[9, layer : layer + 1]
    feed_ref[...] = feed
    return middle + vec_ref[10, layer : layer + 1] * feed


def split_columns(value_refs, x_at, keep_ref, send_ref):
    start = 0
    for value_ref in value_refs:
        half = value_ref.shape[1] // 2
        to = slice(start, start + half)
        keep_ref[:, to] = value_ref[:, pl.ds(pl.multiple_of(x_at * half, LANES), half)]
        send_ref[:, to] = value_ref[:, pl.ds(pl.multiple_of((1 - x_at) * half, LANES), half)]
        start += half


def feed_backward(
    layer, grad, feed, middle, mixed, slope_ref, vec_ref, w_up, w_down, copies, feed_grad_ref,
    hidden_grad_ref, mixed_grad_ref, bias_out, rows_ref, row0,
):
    chunks = w_up.shape[1] // 512
    feed_grad = (vec_ref[10, layer : layer + 1] * grad).astype(BF)
    feed_grad_ref[...] = feed_grad
    rows_ref[row0 + 4 : row0 + 5] = jnp.sum(feed_grad.astype(F32), axis=0, keepdims=True)
    rows_ref[row0 + 5 : row0 + 6] = jnp.sum(grad * feed, axis=0, keepdims=True)
    lifted_grad = None
    for j in range(chunks):
        at = slice(j * 512, (j + 1) * 512)
        if copies is not None and j % 2 == 0:
            copies[j].wait()
            copies[j + 1].wait()
        hidden_grad = (slope_ref[:, at] * product_right(feed_grad, w_down[at])).astype(BF)
        hidden_grad_ref[:, at] = hidden_grad
        bias_out[:, at] = jnp.sum(hidden_grad.astype(F32), axis=0, keepdims=True)
        piece = product_right(hidden_grad, w_up[:, at])
        lifted_grad = piece if lifted_grad is None else lifted_grad + piece
    part, gain_grad, shift_grad = norm_pull(middle, vec_ref[7, layer : layer + 1], lifted_grad)
    middle_grad = grad + part
    mixed_grad = (vec_ref[6, layer : layer + 1] * middle_grad).astype(BF)
    mixed_grad_ref[...] = mixed_grad
    rows_ref[row0 : row0 + 1] = jnp.sum(mixed_grad.astype(F32), axis=0, keepdims=True)
    rows_ref[row0 + 1 : row0 + 2] = jnp.sum(middle_grad * mixed, axis=0, keepdims=True)
    rows_ref[row0 + 2 : row0 + 3] = gain_grad
    rows_ref[row0 + 3 : row0 + 4] = shift_grad
    return middle_grad


def project_backward(*args):
    results = []
    for _ in project_steps(results, *args):
        pass
    return results[0]


def project_steps(
    results, layer, residual, dqkv_ref, pre_ref, vec_ref, head_ref, w_ref, copies, pg_ref, rows_ref,
    head_out,
):
    width = residual.shape[1]
    averager = head_averager()
    sums = [None, None, None]
    for part in range(3):
        for j in range(width // WIDE):
            at = slice(part * width + j * WIDE, part * width + (j + 1) * WIDE)
            value = dqkv_ref[:, at].astype(F32)
            if part < 2:
                unit, scale = standard_heads(pre_ref[:, at], averager)
                news = [(2 * part, jnp.sum(value * unit, axis=0, keepdims=True))]
                if part == 0:
                    news.append((1, jnp.sum(value, axis=0, keepdims=True)))
                for index, new in news:
                    sums[index] = new if sums[index] is None else sums[index] + new
                scaled = value * head_ref[layer, 2 * part : 2 * part + 1]
                value = scale * (
                    scaled
                    - head_mean(scaled, averager)
                    - unit * head_mean(scaled * unit, averager)
                )
            low = value.astype(BF)
            pg_ref[:, at] = low
            rows_ref[2 + part : 3 + part, j * WIDE : (j + 1) * WIDE] = jnp.sum(
                low.astype(F32), axis=0, keepdims=True
            )
            if (part * width // WIDE + j) % 3 == 2:
                yield
    head_out[...] = jnp.concatenate(sums + [jnp.zeros((5, WIDE), F32)], axis=0)
    normed_grad = None
    for part in range(3):
        copies[part].wait()
        at = slice(part * width, (part + 1) * width)
        piece = product_right(pg_ref[:, at], w_ref[:, at])
        normed_grad = piece if normed_grad is None else normed_grad + piece
        yield
    part, gain_grad, shift_grad = norm_pull(residual, vec_ref[0, layer : layer + 1], normed_grad)
    rows_ref[0:1] = gain_grad
    rows_ref[1:2] = shift_grad
    results.append(part)


def named_call(kernel, inputs, outputs, scratch, vmem_mib, cost, name, collective_id=None):
    names = [*inputs, *outputs, *scratch]

    def body(*refs):
        kernel(types.SimpleNamespace(**dict(zip(names, refs))))

    more = {}
    if collective_id is not None:
        more = {"collective_id": collective_id, "has_side_effects": True}
    results = pl.pallas_call(
        body,
        in_specs=[
            whole(pltpu.SMEM) if key.startswith("smem") else whole(pl.ANY) for key in inputs
        ],
        out_specs=[whole(pl.ANY if value[2] else pltpu.VMEM) for value in outputs.values()],
        out_shape=[jax.ShapeDtypeStruct(value[0], value[1]) for value in outputs.values()],
        scratch_shapes=list(scratch.values()),
        compiler_params=pltpu.CompilerParams(vmem_limit_bytes=vmem_mib * VMEM_MIB, **more),
        cost_estimate=cost,
        name=name,
    )(*inputs.values())
    return types.SimpleNamespace(**dict(zip(outputs, results)))


def low(*shape):
    return pltpu.VMEM(shape, BF)


def full(*shape):
    return pltpu.VMEM(shape, F32)


class Mover:
    def __init__(self, sems):
        self.sems, self.count, self.open = sems, 0, []

    def start(self, source, target):
        copy = pltpu.make_async_copy(source, target, self.sems.at[self.count])
        copy.start()
        self.count += 1
        return copy

    def flush(self, source, target):
        self.open.append(self.start(source, target))

    def finish(self):
        assert self.count == self.sems.shape[0]
        for copy in self.open:
            copy.wait()


def interleaved(one, two):
    return [piece for pair in zip(one, two) for piece in pair]


def front_kernel(
    tok_ref, usable_ref, vec_ref, bias_ref, head_ref, qkv_w, out_w, up_w, down_w,
    left_pack, att_pack, pre0, qkv0, mixed0, middle0, slope0, feed0, res1, normed1, pre1, qkv1,
    w_qkv, w_out, w_up, w_down, w_next, sems,
):
    width, units = tok_ref.shape[1], up_w.shape[2]
    lifted0 = left_pack.at[:, :width]
    active0 = left_pack.at[:, width : width + units]
    normed0, att0 = att_pack.at[:, :width], att_pack.at[:, width:]
    copies = weight_copies(
        column_pieces(qkv_w.at[0], 3)
        + [out_w.at[0]]
        + interleaved(column_pieces(up_w.at[0], 4), row_pieces(down_w.at[0], 4))
        + column_pieces(qkv_w.at[1], 3),
        column_pieces(w_qkv, 3)
        + [w_out]
        + interleaved(column_pieces(w_up, 4), row_pieces(w_down, 4))
        + column_pieces(w_next, 3),
        sems,
    )
    residual = tok_ref[...].astype(F32)
    project(0, residual, vec_ref, head_ref, w_qkv, copies[:3], normed0, pre0, qkv0)
    frame_attend(usable_ref[...], qkv0, att0)
    result = feed_forward(
        0, att0[...], residual, vec_ref, bias_ref, w_out, w_up, w_down, copies[3:12], mixed0,
        middle0, lifted0, slope0, active0, feed0,
    )
    res1[...] = result
    project(1, result, vec_ref, head_ref, w_next, copies[12:], normed1, pre1, qkv1)


def front(tokens, usable, vectors, up_bias, head_rows, qkv_weight, out_weight, up_weight, down_weight):
    rows, width = tokens.shape
    hidden = up_weight.shape[2]
    shapes = [
        ((rows, hidden + width), BF),
        ((rows, 2 * width), BF),
        ((rows, 2 * width), F32),
        ((rows, 3 * width), BF),
        ((rows, width), F32),
        ((rows, width), F32),
        ((rows, hidden), F32),
        ((rows, width), F32),
        ((rows, width), F32),
        ((rows, width), BF),
        ((rows, 2 * width), F32),
        ((rows, 3 * width), BF),
    ]
    return pl.pallas_call(
        front_kernel,
        in_specs=[whole()] * 5 + [whole(pl.ANY)] * 4,
        out_specs=[whole()] * len(shapes),
        out_shape=[jax.ShapeDtypeStruct(*shape) for shape in shapes],
        scratch_shapes=[
            pltpu.VMEM((width, 3 * width), BF),
            pltpu.VMEM((width, width), BF),
            pltpu.VMEM((width, hidden), BF),
            pltpu.VMEM((hidden, width), BF),
            pltpu.VMEM((width, 3 * width), BF),
            pltpu.SemaphoreType.DMA((15,)),
        ],
        compiler_params=pltpu.CompilerParams(vmem_limit_bytes=58 * VMEM_MIB),
        cost_estimate=pl.CostEstimate(
            flops=2 * rows * width * (7 * width + 2 * hidden),
            bytes_accessed=2 * width * (7 * width + 2 * hidden),
            transcendentals=2 * rows * hidden,
        ),
        name="front",
    )(tokens, usable, vectors, up_bias, head_rows, qkv_weight, out_weight, up_weight, down_weight)


def turn_kernel(
    x_ref, att_ref, normed_ref, res_ref, cot_ref, vec_ref, bias_ref, out_w, up_w, down_w,
    left_pack, att_pack, output, right_keep, right_send, att_grad, middle_grad, bias_out, rows_out,
    w_out, w_up, w_down, mixed_sc, middle_sc, slope_sc, feed_sc, fg_sc, hg_sc, mg_sc, sems,
):
    width, units = att_ref.shape[1], up_w.shape[2]
    lifted = left_pack.at[:, :width]
    active = left_pack.at[:, width : width + units]
    att_pack[:, :width] = normed_ref[...]
    att_pack[:, width:] = att_ref[...]
    copies = weight_copies(
        [out_w.at[1]] + interleaved(column_pieces(up_w.at[1], 4), row_pieces(down_w.at[1], 4)),
        [w_out] + interleaved(column_pieces(w_up, 4), row_pieces(w_down, 4)),
        sems,
    )
    result = feed_forward(
        1, att_ref[...], res_ref[...], vec_ref, bias_ref, w_out, w_up, w_down, copies, mixed_sc,
        middle_sc, lifted, slope_sc, active, feed_sc,
    )
    output[...] = result.astype(BF)
    grad = feed_backward(
        1, cot_ref[...].astype(F32), feed_sc[...], middle_sc[...], mixed_sc[...], slope_sc, vec_ref,
        w_up, w_down, None, fg_sc, hg_sc, mg_sc, bias_out, rows_out, 0,
    )
    middle_grad[...] = grad
    att_grad[...] = product_right(mg_sc[...], w_out[...]).astype(BF)
    split_columns([hg_sc, fg_sc, mg_sc], x_ref[0], right_keep, right_send)


def turn(x_at, att, normed, res, cotangent, vectors, up_bias, out_weight, up_weight, down_weight):
    rows, width = res.shape
    hidden = up_weight.shape[2]
    shapes = [
        ((rows, hidden + width), BF),
        ((rows, 2 * width), BF),
        ((rows, width), BF),
        ((rows, hidden // 2 + width), BF),
        ((rows, hidden // 2 + width), BF),
        ((rows, width), BF),
        ((rows, width), F32),
        ((1, hidden), F32),
        ((8, width), F32),
    ]
    return pl.pallas_call(
        turn_kernel,
        in_specs=[whole(pltpu.SMEM)] + [whole()] * 6 + [whole(pl.ANY)] * 3,
        out_specs=[whole()] * len(shapes),
        out_shape=[jax.ShapeDtypeStruct(*shape) for shape in shapes],
        scratch_shapes=[
            pltpu.VMEM((width, width), BF),
            pltpu.VMEM((width, hidden), BF),
            pltpu.VMEM((hidden, width), BF),
            pltpu.VMEM((rows, width), F32),
            pltpu.VMEM((rows, width), F32),
            pltpu.VMEM((rows, hidden), F32),
            pltpu.VMEM((rows, width), F32),
            pltpu.VMEM((rows, width), BF),
            pltpu.VMEM((rows, hidden), BF),
            pltpu.VMEM((rows, width), BF),
            pltpu.SemaphoreType.DMA((9,)),
        ],
        compiler_params=pltpu.CompilerParams(vmem_limit_bytes=58 * VMEM_MIB),
        cost_estimate=pl.CostEstimate(
            flops=4 * rows * width * (width + 2 * hidden),
            bytes_accessed=2 * width * (width + 2 * hidden),
            transcendentals=2 * rows * hidden,
        ),
        name="turn",
    )(x_at, att, normed, res, cotangent, vectors, up_bias, out_weight, up_weight, down_weight)


def back_one_kernel(r):
    mover = Mover(r.moves)
    early = [
        mover.start(*pair)
        for pair in (
            (r.vectors, r.vectors_sc), (r.head_rows, r.head_rows_sc), (r.dqkv, r.dqkv_sc),
            (r.pre, r.pre_sc), (r.res, r.res_sc), (r.grad, r.grad_sc),
        )
    ]
    copies = weight_copies(column_pieces(r.qkv_w.at[1], 3), column_pieces(r.w_qkv, 3), r.sems)
    later = [
        mover.start(*pair)
        for pair in (
            (r.feed, r.feed_sc), (r.middle, r.middle_sc), (r.mixed, r.mixed_sc),
            (r.slope, r.slope_sc),
        )
    ]
    copies = copies + weight_copies(
        interleaved(column_pieces(r.up_w.at[0], 4), row_pieces(r.down_w.at[0], 4)),
        interleaved(column_pieces(r.w_up, 4), row_pieces(r.w_down, 4)),
        r.more_sems,
    )
    for copy in early:
        copy.wait()
    part = project_backward(
        1, r.res_sc[...], r.dqkv_sc, r.pre_sc, r.vectors_sc, r.head_rows_sc, r.w_qkv, copies[:3],
        r.pg_sc, r.rows_out, r.head_out,
    )
    x_at = lax.axis_index("grp")
    split_columns([r.pg_sc], x_at, r.pg_keep_sc, r.pg_send_sc)
    mover.flush(r.pg_send_sc, r.pg_send)
    mover.flush(r.pg_keep_sc, r.pg_keep)
    for copy in later:
        copy.wait()
    r.middle_grad_sc[...] = feed_backward(
        0, r.grad_sc[...] + part, r.feed_sc[...], r.middle_sc[...], r.mixed_sc[...], r.slope_sc,
        r.vectors_sc, r.w_up, r.w_down, copies[3:], r.fg_sc, r.hg_sc, r.mixed_grad_sc, r.bias_out,
        r.rows_out, 8,
    )
    mover.flush(r.middle_grad_sc, r.middle_grad)
    mover.flush(r.mixed_grad_sc, r.mixed_grad)
    split_columns([r.hg_sc, r.fg_sc], x_at, r.right_keep_sc, r.right_send_sc)
    mover.flush(r.right_send_sc, r.right_send)
    mover.flush(r.right_keep_sc, r.right_keep)
    mover.finish()


def back_one(
    dqkv, pre, res, grad, feed, middle, mixed, slope, vectors, head_rows, qkv_weight,
    up_weight, down_weight,
):
    rows, width = res.shape
    hidden = up_weight.shape[2]
    loaded = dict(
        vectors=vectors, head_rows=head_rows, dqkv=dqkv, pre=pre, res=res,
        grad=grad, feed=feed, middle=middle, mixed=mixed, slope=slope,
    )
    stored = dict(
        pg_keep=((rows, 3 * width // 2), BF),
        pg_send=((rows, 3 * width // 2), BF),
        right_keep=((rows, (hidden + width) // 2), BF),
        right_send=((rows, (hidden + width) // 2), BF),
        mixed_grad=((rows, width), BF),
        middle_grad=((rows, width), F32),
    )
    return named_call(
        back_one_kernel,
        dict(**loaded, qkv_w=qkv_weight, up_w=up_weight, down_w=down_weight),
        dict(
            **{key: (*value, True) for key, value in stored.items()},
            bias_out=((1, hidden), F32, False),
            rows_out=((16, width), F32, False),
            head_out=((8, WIDE), F32, False),
        ),
        dict(
            **{key + "_sc": pltpu.VMEM(value.shape, value.dtype) for key, value in loaded.items()},
            **{key + "_sc": pltpu.VMEM(*value) for key, value in stored.items()},
            w_qkv=low(width, 3 * width),
            w_up=low(width, hidden),
            w_down=low(hidden, width),
            pg_sc=low(rows, 3 * width),
            fg_sc=low(rows, width),
            hg_sc=low(rows, hidden),
            sems=pltpu.SemaphoreType.DMA((3,)),
            more_sems=pltpu.SemaphoreType.DMA((8,)),
            moves=pltpu.SemaphoreType.DMA((16,)),
        ),
        60,
        pl.CostEstimate(
            flops=2 * rows * width * (3 * width + 2 * hidden),
            bytes_accessed=2 * width * (3 * width + 2 * hidden),
            transcendentals=0,
        ),
        "back_one",
    )


def frame_steps(att_grad, usable, qkv_ref, dqkv_ref):
    width = att_grad.shape[1]
    first, _ = lane_masks(F32)
    for pair in range(width // LANES):
        q, k, v = [
            qkv_ref[:, part * width + pair * LANES : part * width + (pair + 1) * LANES]
            for part in range(3)
        ]
        out = att_grad[:, pair * LANES : (pair + 1) * LANES]
        pieces = []
        for mask in lane_masks(BF):
            shares = frame_shares(q * mask, k, usable)
            share_grad = product_right(out * mask, v)
            delta = jnp.sum(shares * share_grad, axis=-1, keepdims=True)
            score_grad = (shares * (share_grad - delta)).astype(BF)
            pieces.append(
                (
                    product(score_grad, k) * SCALE,
                    product_left(score_grad, q) * SCALE,
                    product_left(shares.astype(BF), out),
                )
            )
        for part in range(3):
            dqkv_ref[:, part * width + pair * LANES : part * width + (pair + 1) * LANES] = jnp.where(
                first > 0, pieces[0][part], pieces[1][part]
            )
        if pair % 2 == 1:
            yield


def frame_loads(r, mover):
    early = [
        mover.start(*pair)
        for pair in (
            (r.mixed_grad, r.mixed_grad_sc), (r.usable, r.usable_sc), (r.qkv, r.qkv_sc)
        )
    ]
    copies = weight_copies(
        [r.out_w.at[0]] + column_pieces(r.qkv_w.at[0], 3), [r.w_out] + column_pieces(r.w_qkv, 3),
        r.sems,
    )
    later = [
        mover.start(*pair)
        for pair in (
            (r.vectors, r.vectors_sc), (r.head_rows, r.head_rows_sc), (r.pre, r.pre_sc),
            (r.tok, r.tok_sc), (r.grad, r.grad_sc), (r.rows10, r.rows10_sc), (r.rows1, r.rows1_sc),
            (r.bias0, r.bias0_sc), (r.bias1, r.bias1_sc), (r.heads1, r.heads1_sc),
        )
    ]
    return early, later, copies


def frame_part(r, early, copies):
    for copy in early:
        copy.wait()
    copies[0].wait()
    att_grad = product_right(r.mixed_grad_sc[...], r.w_out[...]).astype(BF)
    yield
    yield from frame_steps(att_grad, r.usable_sc[...], r.qkv_sc, r.dqkv_sc)


def input_part(r, later, copies, x_at):
    width = r.tok_sc.shape[1]
    for copy in later:
        copy.wait()
    results = []
    yield from project_steps(
        results, 0, r.tok_sc[...].astype(F32), r.dqkv_sc, r.pre_sc, r.vectors_sc, r.head_rows_sc,
        r.w_qkv, copies[1:], r.pg_sc, r.rows_sc, r.heads_sc,
    )
    part = results[0]
    split_columns([r.pg_sc, r.mixed_grad_sc], x_at, r.pg_keep_sc, r.pg_send_sc)
    r.input_grad_sc[...] = (r.grad_sc[...] + part).astype(BF)
    small = r.small_sc
    small[0:5] = r.rows_sc[0:5]
    small[5:11] = r.rows10_sc[8:14]
    small[11:16] = r.rows10_sc[0:5]
    small[16:22] = r.rows1_sc[0:6]
    at = 22
    for bias in (r.bias0_sc, r.bias1_sc):
        for j in range(bias.shape[1] // width):
            small[at : at + 1] = bias[:, j * width : (j + 1) * width]
            at += 1
    place = lax.broadcasted_iota(jnp.int32, (1, width), 1) // HD
    row = jnp.zeros((1, width), F32)
    for index, heads in enumerate((r.heads_sc, r.heads1_sc)):
        total = heads[...]
        total = total + pltpu.roll(total, WIDE // 2, 1)
        total = total + pltpu.roll(total, HD, 1)
        for j in range(3):
            many = jnp.concatenate([total[j : j + 1]] * (width // WIDE), axis=1)
            row = jnp.where(place == 3 * index + j, many, row)
    small[at : at + 1] = row
    small[at + 1 :] = jnp.zeros((small.shape[0] - at - 1, width), F32)
    yield


def back_two_kernel(r):
    mover = Mover(r.moves)
    early, later, copies = frame_loads(r, mover)
    for _ in frame_part(r, early, copies):
        pass
    for _ in input_part(r, later, copies, r.smem_at[0]):
        pass
    mover.flush(r.pg_send_sc, r.pg_send)
    mover.flush(r.pg_keep_sc, r.pg_keep)
    mover.flush(r.input_grad_sc, r.input_grad)
    mover.flush(r.small_sc, r.small)
    mover.finish()


def back_two(
    places, mixed_grad, grad, qkv, pre, tok, usable, vectors, head_rows, rows10, rows1, bias0,
    bias1, heads1, out_w, qkv_w,
):
    rows, width = tok.shape
    loaded = dict(
        mixed_grad=mixed_grad, usable=usable, qkv=qkv, vectors=vectors, head_rows=head_rows,
        pre=pre, tok=tok, grad=grad, rows10=rows10, rows1=rows1, bias0=bias0, bias1=bias1,
        heads1=heads1,
    )
    small_rows = 2 * vectors.shape[0] + 2 * bias0.shape[1] // width + 2
    stored = dict(
        pg_keep=((rows, 2 * width), BF),
        pg_send=((rows, 2 * width), BF),
        input_grad=((rows, width), BF),
        small=((small_rows, width), F32),
    )
    return named_call(
        back_two_kernel,
        dict(smem_at=places, **loaded, out_w=out_w, qkv_w=qkv_w),
        {key: (*value, True) for key, value in stored.items()},
        dict(
            **{key + "_sc": pltpu.VMEM(value.shape, value.dtype) for key, value in loaded.items()},
            **{key + "_sc": pltpu.VMEM(*value) for key, value in stored.items()},
            w_out=low(width, width),
            w_qkv=low(width, 3 * width),
            dqkv_sc=full(rows, 3 * width),
            pg_sc=low(rows, 3 * width),
            rows_sc=full(8, width),
            heads_sc=full(8, WIDE),
            sems=pltpu.SemaphoreType.DMA((4,)),
            moves=pltpu.SemaphoreType.DMA((17,)),
        ),
        60,
        pl.CostEstimate(
            flops=2 * rows * width * 4 * width,
            bytes_accessed=2 * width * 4 * width,
            transcendentals=HEADS * rows * rows,
        ),
        "back_two",
    )


def weight_grad_kernel(outer, tall, starts, at_ref, *refs):
    count = len(tall)
    lefts, rights = refs[: 4 * count], refs[4 * count : 8 * count]
    keep, send = refs[8 * count : 8 * count + 2]
    left_sc = refs[8 * count + 2 : 9 * count + 2]
    right_sc = refs[9 * count + 2 : 10 * count + 2]
    sems = refs[10 * count + 2]
    c_at, y_at = at_ref[0], at_ref[1]
    rows = lefts[0].shape[0]
    group = keep.shape[0] // outer
    copies = []
    for w in range(count):
        cols, left_cols = right_sc[w].shape[1], left_sc[w].shape[1]
        left_start, right_start = starts[w]
        for s in range(4):
            at = pl.ds(pl.multiple_of(right_start + c_at * cols, LANES), cols)
            copies.append(
                pltpu.make_async_copy(
                    rights[4 * w + s].at[:, at],
                    right_sc[w].at[s * rows : (s + 1) * rows],
                    sems.at[len(copies)],
                )
            )
            copies.append(
                pltpu.make_async_copy(
                    lefts[4 * w + s].at[:, left_start : left_start + left_cols],
                    left_sc[w].at[s * rows : (s + 1) * rows],
                    sems.at[len(copies)],
                )
            )
    for copy in copies:
        copy.start()
    start = 0
    for w in range(count):
        for copy in copies[8 * w : 8 * w + 8]:
            copy.wait()
        cols = right_sc[w].shape[1]
        right = right_sc[w][...]
        for block in range(left_sc[w].shape[1] // 512):
            result = product_left(left_sc[w][:, block * 512 : (block + 1) * 512], right).astype(BF)
            targets = {0: [], 1: []}
            if tall[w]:
                size, part = 4 * group, group // 2
                for piece in range(512 // part):
                    row = block * 512 + piece * part
                    o, y = row // (2 * size), (row // size) % 2
                    core, t = (row % size) // (size // 2), (row % (size // 2)) // part
                    targets[y].append(
                        (piece * part, part, o * group + core * part, start + t * cols)
                    )
            else:
                for piece in range(512 // group):
                    row = block * 512 + piece * group
                    o, y = row // (2 * group), (row // group) % 2
                    targets[y].append((piece * group, group, o * group, start))
            for y in range(2):
                if not targets[y]:
                    continue

                def store(ref, y=y):
                    for source, size, row, col in targets[y]:
                        ref[row : row + size, col : col + cols] = result[source : source + size]

                @pl.when(y_at == y)
                def _():
                    store(keep)

                @pl.when(y_at != y)
                def _():
                    store(send)

        start += cols * (4 if tall[w] else 1)


def weight_grads(name, outer, width, places, products):
    rows = products[0][0][0].shape[0]
    group = width // (2 * outer)
    lefts, left_starts, left_cols, rights, right_starts, halves, tall = zip(*products)
    columns = [half // 2 for half in halves]
    total = sum(c * (4 if t else 1) for c, t in zip(columns, tall))
    shape = jax.ShapeDtypeStruct((outer * group, total), BF)
    count = len(products)
    return pl.pallas_call(
        functools.partial(
            weight_grad_kernel, outer, tall, tuple(zip(left_starts, right_starts))
        ),
        in_specs=[whole(pltpu.SMEM)] + [whole(pl.ANY)] * (8 * count),
        out_specs=[whole()] * 2,
        out_shape=[shape] * 2,
        scratch_shapes=[pltpu.VMEM((4 * rows, c), BF) for c in left_cols]
        + [pltpu.VMEM((4 * rows, c), BF) for c in columns]
        + [pltpu.SemaphoreType.DMA((8 * count,))],
        compiler_params=pltpu.CompilerParams(vmem_limit_bytes=48 * VMEM_MIB),
        cost_estimate=pl.CostEstimate(
            flops=16 * rows * outer * group * total,
            bytes_accessed=8 * outer * group * total,
            transcendentals=0,
        ),
        name=name,
    )(places, *[a for l in lefts for a in l], *[a for r in rights for a in r])


def assemble_kernel(count, *refs):
    inputs, results, passing = count
    sources, refs = refs[:inputs], refs[inputs:]
    passed, refs = refs[:passing], refs[passing:]
    finals, refs = refs[:results], refs[results:]
    passed_out, refs = refs[:passing], refs[passing:]
    pieces, refs = refs[:inputs], refs[inputs:]
    outs, smalls = refs[:4], refs[4:results]
    held = refs[results : results + passing]
    sems, out_sems = refs[results + passing :]
    copies = [
        pltpu.make_async_copy(source, piece, sems.at[index])
        for index, (source, piece) in enumerate(
            zip((*sources, *passed), (*pieces, *held))
        )
    ]
    for copy in copies:
        copy.start()
    leaving = []

    def leave(source, target):
        copy = pltpu.make_async_copy(source, target, out_sems.at[len(leaving)])
        copy.start()
        leaving.append(copy)

    qkv_out, out_out, up_out, down_out = outs
    me, x_at = lax.axis_index("blk"), lax.axis_index("grp")
    c_at = lax.rem(me, 2)
    spread = bool(smalls)
    if smalls:
        copies[4].wait()
        share_small(me, pieces[4], *smalls)
        for source, target in zip(smalls, finals[4:]):
            leave(source, target)
    part = qkv_out.shape[1]
    for layer in range(2):
        copies[2 * layer].wait()
        copies[2 * layer + 1].wait()
        for source in range(4):
            feed, att = pieces[2 * layer].at[source], pieces[2 * layer + 1].at[source]
            c = c_at if source % 2 == 0 else 1 - c_at
            feed_place = att_place = 2 * (x_at if source < 2 else 1 - x_at) + c

            def put(ref, values, place, row=0, layer=layer):
                cols = values.shape[1]
                at = pl.ds(pl.multiple_of(place * cols, LANES), cols)
                ref[layer, row : row + values.shape[0], at] = values.astype(F32)

            up_cols = up_out.shape[2] // 4
            down_cols = down_out.shape[2] // 4
            qkv_cols = qkv_out.shape[2] // 4
            put(up_out, feed[:, :up_cols], feed_place)
            if spread and layer == 1:
                for t in range(2):
                    start = up_cols + t * 2 * down_cols
                    rows = pl.ds(pl.multiple_of((2 * (feed_place // 2) + t) * part, part), part)
                    cols = pl.ds(pl.multiple_of(c * 2 * down_cols, LANES), 2 * down_cols)
                    down_out[layer, rows, cols] = feed[:, start : start + 2 * down_cols].astype(F32)
                put(qkv_out, att[:, :qkv_cols], att_place)
                put(out_out, att[:, qkv_cols:], att_place)
                continue
            for t in range(4):
                put(
                    down_out,
                    feed[:, up_cols + t * down_cols : up_cols + (t + 1) * down_cols],
                    feed_place,
                    t * part,
                )
            put(qkv_out, att[:, :qkv_cols], att_place)
            put(out_out, att[:, qkv_cols:], att_place)
        for source, target in zip(outs, finals):
            leave(source.at[layer], target.at[layer])
    for index, (source, target) in enumerate(zip(held, passed_out)):
        copies[inputs + index].wait()
        leave(source, target)
    for copy in leaving:
        copy.wait()


def share_small(me, small, vector_out, bias_out, head_out):
    vector_rows = vector_out.shape[0]
    lanes = pl.ds(pl.multiple_of((me // 2) * LANES, LANES), LANES)
    pair = small[: 2 * vector_rows, lanes]
    pair = jnp.where(lax.rem(me, 2) == 0, pair, pltpu.roll(pair, HD, 1))
    columns = bias_out.shape[1]
    per_row = small.shape[1] // columns
    rows = PEERS // per_row
    for layer in range(2):
        for index in range(vector_rows):
            row = layer * vector_rows + index
            vector_out[index, layer : layer + 1] = pair[row : row + 1, :HD]
        row = pl.ds(2 * vector_rows + layer * rows + me // per_row, 1)
        at = pl.ds(pl.multiple_of(lax.rem(me, per_row) * columns, LANES), columns)
        bias_out[layer : layer + 1] = small[row, at]
        last = 2 * vector_rows + 2 * rows
        head_out[layer : layer + 1] = small[
            last : last + 1, layer * 3 * HD : (layer + 1) * 3 * HD
        ]


def assemble(pieces, shapes, passed):
    results = [jax.ShapeDtypeStruct(shape, F32) for shape in shapes]
    results += [jax.ShapeDtypeStruct(array.shape, array.dtype) for array in passed]
    return pl.pallas_call(
        functools.partial(assemble_kernel, (len(pieces), len(shapes), len(passed))),
        in_specs=[whole(pl.ANY)] * (len(pieces) + len(passed)),
        out_specs=[whole(pl.ANY)] * len(results),
        out_shape=results,
        scratch_shapes=[pltpu.VMEM(piece.shape, piece.dtype) for piece in pieces]
        + [pltpu.VMEM(shape, F32) for shape in shapes]
        + [pltpu.VMEM(array.shape, array.dtype) for array in passed]
        + [
            pltpu.SemaphoreType.DMA((len(pieces) + len(passed),)),
            pltpu.SemaphoreType.DMA((len(results) + 4,)),
        ],
        compiler_params=pltpu.CompilerParams(vmem_limit_bytes=60 * VMEM_MIB),
        name="assemble",
    )(*pieces, *passed)


OUTER = 4
BLOCK = 128


def slot_order(z0, z1):
    return [2 * (1 - z1) + (1 - z0), 2 * z1 + (1 - z0), 2 * (1 - z1) + z0, 2 * z1 + z0]


def slot_group(slot, z0, z1):
    far = jnp.where(slot % 2 == 0, 1 - z1, z1)
    return 2 * far + jnp.where(slot < 2, 1 - z0, z0)


def slot_product(group, left, left_at, right, right_at, cols, tall, emit):
    rights = right[:, right_at : right_at + cols]
    if tall:
        for y in range(2):
            start = pl.multiple_of(left_at + group * 8 * BLOCK + y * 4 * BLOCK, BLOCK)
            result = product_left(left[:, pl.ds(start, 4 * BLOCK)], rights).astype(BF)
            half = BLOCK // 2
            for c in range(2):
                for t in range(4):
                    row = c * 2 * BLOCK + t * half
                    emit(y, c * half, t * cols, result[row : row + half])
    else:
        start = pl.multiple_of(left_at + group * 2 * BLOCK, BLOCK)
        result = product_left(left[:, pl.ds(start, 2 * BLOCK)], rights).astype(BF)
        for y in range(2):
            emit(y, 0, 0, result[y * BLOCK : (y + 1) * BLOCK])


class Sender:
    def __init__(self, send, recv, partners):
        self.send, self.recv, self.partners = send, recv, partners
        self.copies = []

    def start(self, source, target, partner):
        index = len(self.copies)
        copy = pltpu.make_async_remote_copy(
            src_ref=source,
            dst_ref=target,
            send_sem=self.send.at[index],
            recv_sem=self.recv.at[index],
            device_id=self.partners[partner],
            device_id_type=MESH,
        )
        copy.start()
        self.copies.append(copy)
        return copy

    def finish(self):
        for copy in self.copies:
            copy.wait_send()


def finish_kernel(r):
    me = lax.axis_index("blk")
    x_at = lax.axis_index("grp")
    c_at, y_at, z0, z1 = [lax.rem(me // (1 << bit), 2) for bit in range(4)]
    partners = {"x": {"grp": 1 - x_at}}
    for bit, name in enumerate(("c", "y", "z0", "z1")):
        partners[name] = {"blk": me ^ (1 << bit)}
    barrier = pltpu.get_barrier_semaphore()
    for partner in partners.values():
        pl.semaphore_signal(barrier, 1, device_id=partner, device_id_type=MESH)
    mover = Mover(r.moves)
    early, later, weights = frame_loads(r, mover)
    pl.semaphore_wait(barrier, len(partners))
    sender = Sender(r.send, r.recv, partners)
    local = r.local
    rows = r.la1.shape[0]
    locals_ = []

    def load(source, target):
        copy = pltpu.make_async_copy(source, target, local.at[len(locals_)])
        copy.start()
        locals_.append(copy)
        return copy

    stores = []

    def store(source, target):
        stores.append(load(source, target))

    def ready(copies):
        for copy in copies:
            copy.wait_recv()

    def quarter(ref, start, cols, core):
        return ref.at[:, pl.ds(pl.multiple_of(start + core * cols, BLOCK), cols)]

    def own_right(ref, start, cols, target, to, index):
        here = slice(index * rows, (index + 1) * rows)
        there = slice((2 + index) * rows, (3 + index) * rows)
        return [
            load(quarter(ref, start, cols, c_at), target.at[here, to : to + cols]),
            sender.start(
                quarter(ref, start, cols, 1 - c_at), target.at[there, to : to + cols], "c"
            ),
        ]

    def own_left(ref, target, index):
        return [
            load(ref, target.at[index * rows : (index + 1) * rows]),
            sender.start(ref, target.at[(2 + index) * rows : (3 + index) * rows], "c"),
        ]

    right_a1, right_f0, right_a0 = r.right_a1, r.right_f0, r.right_a0
    left_a1, left_f0, left_a0 = r.left_a1, r.left_f0, r.left_a0
    qkv_cols, out_cols = right_a1.shape[1] * 3 // 4, right_a1.shape[1] // 4
    up_cols, down_cols = right_f0.shape[1] * 4 // 5, right_f0.shape[1] // 5
    width = left_a1.shape[1] // 2
    pg1_copy = sender.start(r.pg1_send, r.pg1_x, "x")
    rt0_copy = sender.start(r.rt0_send, r.rt0_x, "x")
    d1_loads = [load(r.stay_down, r.part_d1), load(r.came_down, r.y_d1)]
    u1_loads = [load(r.stay_up, r.part_u1), load(r.came_up, r.z0_u1)]
    a1_ready = (
        own_left(r.la1, left_a1, 0)
        + own_left(r.la1_x, left_a1, 1)
        + own_right(r.pg1, 0, qkv_cols, right_a1, 0, 0)
        + own_right(r.rt1, 0, out_cols, right_a1, qkv_cols, 0)
        + own_right(r.rt1_x, 0, out_cols, right_a1, qkv_cols, 1)
    )
    f0_ready = (
        own_left(r.lf0, left_f0, 0)
        + own_left(r.lf0_x, left_f0, 1)
        + own_right(r.rt0, 0, up_cols, right_f0, 0, 0)
        + own_right(r.rt0, 2 * up_cols, down_cols, right_f0, up_cols, 0)
    )
    a0_ready = own_left(r.la0, left_a0, 0) + own_left(r.la0_x, left_a0, 1)

    def rest_a1():
        pg1_copy.wait_recv()
        return own_right(r.pg1_x, 0, qkv_cols, right_a1, 0, 1)

    def rest_f0():
        rt0_copy.wait_recv()
        return own_right(r.rt0_x, 0, up_cols, right_f0, 0, 1) + own_right(
            r.rt0_x, 2 * up_cols, down_cols, right_f0, up_cols, 1
        )

    def rest_a0(copy):
        copies = own_right(r.pg_keep_sc, 0, qkv_cols, right_a0, 0, 0) + own_right(
            r.pg_keep_sc, 2 * qkv_cols, out_cols, right_a0, qkv_cols, 0
        )
        copy.wait_recv()
        return (
            copies
            + own_right(r.pm0_x, 0, qkv_cols, right_a0, 0, 1)
            + own_right(r.pm0_x, 2 * qkv_cols, out_cols, right_a0, qkv_cols, 1)
        )

    class Finish:
        def finish(self):
            half = BLOCK // 2
            other = self.own(3).at[pl.ds(pl.multiple_of((1 - c_at) * half, half), half)]
            self.c_copy = sender.start(other, self.fin.at[1], "c")
            self.fin[0] = self.own(3)[pl.ds(pl.multiple_of(c_at * half, half), half)]
            self.far_copies = [sender.start(self.fin.at[0], self.far.at[0], "x")]

        def fourth(self):
            self.c_copy.wait_recv()
            self.far_copies.append(sender.start(self.fin.at[1], self.far.at[1], "x"))
            store(self.fin, self.out.at[0:2, :, self.columns])

        def last(self):
            for copy in self.far_copies:
                copy.wait_recv()
            store(self.far, self.out.at[2:4, :, self.columns])

    class Group(Finish):
        def __init__(self, part, over, over_z0, over_z1, fin, far, out, columns, came=False):
            self.part, self.over, self.over_z0, self.over_z1 = part, over, over_z0, over_z1
            self.fin, self.far, self.out, self.columns = fin, far, out, columns
            self.came, self.copies, self.z0_copies = came, {}, {}

        def own(self, slot):
            return self.part.at[slot] if self.came else self.part.at[slot, y_at]

        def total(self, slot):
            return self.own(slot)[...].astype(F32) + self.over[slot].astype(F32)

        def made(self, slot):
            self.copies[slot] = sender.start(
                self.part.at[slot, 1 - y_at], self.over.at[slot], "y"
            )

        def step(self, slot):
            if not self.came:
                self.copies[slot].wait_recv()
            (lambda: self.first(0), lambda: self.first(1), self.second, self.third)[slot]()

        def first(self, slot):
            self.own(slot)[...] = self.total(slot).astype(BF)
            self.z0_copies[slot] = sender.start(self.own(slot), self.over_z0.at[slot], "z0")

        def second(self):
            value = self.total(2)
            self.z0_copies[0].wait_recv()
            self.own(2)[...] = (value + self.over_z0[0].astype(F32)).astype(BF)
            self.z1_copy = sender.start(self.own(2), self.over_z1, "z1")

        def third(self):
            value = self.total(3)
            self.z0_copies[1].wait_recv()
            value = value + self.over_z0[1].astype(F32)
            self.z1_copy.wait_recv()
            self.own(3)[...] = (value + self.over_z1[...].astype(F32)).astype(BF)
            self.finish()

    class Early(Finish):
        def __init__(self, part, came, over, over_z1, fin, far, out, columns, keep=None):
            self.part, self.came, self.over, self.over_z1 = part, came, over, over_z1
            self.keep = part if keep is None else keep
            self.fin, self.far, self.out, self.columns = fin, far, out, columns
            self.copies, self.z0_copies = {}, {}

        def own(self, slot):
            return self.keep.at[slot - 2, y_at]

        def total(self, slot, at):
            return self.keep[slot, at].astype(F32) + self.came[slot, at].astype(F32)

        def made(self, slot):
            if slot < 2:
                self.z0_copies[slot] = sender.start(
                    self.part.at[slot], self.came.at[slot], "z0"
                )

        def send(self, slot):
            if self.z0_copies:
                self.z0_copies[slot].wait_recv()
            self.keep[slot, 1 - y_at] = self.total(slot, 1 - y_at).astype(BF)
            self.copies[slot] = sender.start(
                self.keep.at[slot, 1 - y_at], self.over.at[slot], "y"
            )

        def step(self, slot):
            self.copies[slot].wait_recv()
            value = self.total(slot, y_at) + self.over[slot].astype(F32)
            if slot == 1:
                self.z1_copy.wait_recv()
                value = value + self.over_z1[...].astype(F32)
            self.keep[slot, y_at] = value.astype(BF)
            if slot == 0:
                self.z1_copy = sender.start(self.keep.at[0, y_at], self.over_z1, "z1")
            else:
                self.finish()

    every = slice(None)
    half_cols = r.part_u1.shape[3]
    u1 = Early(
        r.part_u1, r.z0_u1, r.y_u1, r.z1_u1, r.fin_u1, r.far_u1, r.f1_out, slice(0, half_cols)
    )
    d1 = Group(
        r.part_d1, r.y_d1, r.z0_d1, r.z1_d1, r.fin_d1, r.far_d1, r.f1_out,
        slice(half_cols, 2 * half_cols), True,
    )
    a1 = Early(
        r.part_a1, r.z0_a1, r.y_a1, r.z1_a1, r.fin_a1, r.far_a1, r.a1_out, every, r.part_a1.at[2:4]
    )
    f0 = Group(r.part_f0, r.y_f0, r.z0_f0, r.z1_f0, r.fin_f0, r.far_f0, r.f0_out, every)
    a0 = Group(r.part_a0, r.y_a0, r.z0_a0, r.z1_a0, r.fin_a0, r.far_a0, r.a0_out, every)

    def products(group, left, right, terms, slots=range(OUTER)):
        for slot in slots:
            at = slot_group(slot, z0, z1)
            base = 0
            for left_at, right_at, cols, tall in terms:

                def emit(y, row, col, values, slot=slot, base=base):
                    height, wide = values.shape
                    group.part[
                        slot, y, row : row + height, base + col : base + col + wide
                    ] = values

                slot_product(at, left, left_at, right, right_at, cols, tall, emit)
                base += cols * (4 if tall else 1)
            group.made(slot)

    att_terms = [(0, 0, qkv_cols, False), (width, qkv_cols, out_cols, False)]
    feed_terms = [(0, 0, up_cols, False), (width, up_cols, down_cols, True)]
    sums, sums_in, small_copies = r.sums, r.sums_in, []

    def small_step(name=None):
        index = len(small_copies)
        if index:
            small_copies[-1].wait_recv()
            sums[index] = sums[index - 1] + sums_in[index - 1]
        if name is not None:
            small_copies.append(sender.start(sums.at[index], sums_in.at[index], name))
        else:
            store(sums.at[index], r.small_out)

    backward = chain(frame_part(r, early, weights), input_part(r, later, weights, x_at))
    ready(d1_loads)
    d1.step(0)
    next(backward)
    d1.step(1)
    ready(u1_loads)
    u1.send(1)
    d1.step(2)
    a1_ready += rest_a1()
    next(backward)
    next(backward)
    next(backward)
    ready(a1_ready)
    products(a1, left_a1, right_a1, att_terms, (0,))
    u1.send(0)
    next(backward)
    f0_ready += rest_f0()
    ready(f0_ready)
    products(f0, left_f0, right_f0, feed_terms, (0,))
    next(backward)
    products(a1, left_a1, right_a1, att_terms, (1,))
    products(a1, left_a1, right_a1, att_terms, (2,))
    next(backward)
    products(f0, left_f0, right_f0, feed_terms, (1,))
    products(f0, left_f0, right_f0, feed_terms, (2,))
    d1.step(3)
    d1.fourth()
    f0.step(0)
    next(backward)
    a1.send(0)
    next(backward)
    next(backward)
    next(backward)
    u1.step(0)
    next(backward)
    next(backward)
    pm0_copy = sender.start(r.pg_send_sc, r.pm0_x, "x")
    store(r.input_grad_sc, r.input_grad)
    sums[0] = r.small_sc[...]
    small_step("x")
    products(a1, left_a1, right_a1, att_terms, (3,))
    a0_ready += rest_a0(pm0_copy)
    f0.step(1)
    f0.step(2)
    small_step("c")
    ready(a0_ready)
    products(a0, left_a0, right_a0, att_terms, (0,))
    a1.step(0)
    products(f0, left_f0, right_f0, feed_terms, (3,))
    small_step("y")
    products(a0, left_a0, right_a0, att_terms, (1,))
    a0.step(0)
    products(a0, left_a0, right_a0, att_terms, (2,))
    u1.step(1)
    small_step("z0")
    f0.step(3)
    f0.fourth()
    u1.fourth()
    a0.step(1)
    small_step("z1")
    a1.send(1)
    a0.step(2)
    products(a0, left_a0, right_a0, att_terms, (3,))
    a1.step(1)
    small_step()
    d1.last()
    a1.fourth()
    f0.last()
    u1.last()
    a0.step(3)
    a0.fourth()
    a1.last()
    a0.last()
    assert len(sender.copies) == r.send.shape[0]
    assert len(locals_) == local.shape[0]
    ready(stores)
    sender.finish()
    mover.finish()


def finish_all(frame, u1, d1, a1, f0, a0):
    rows, width = frame["tok"].shape
    wide, att = 2 * u1[0].shape[-1], u1[0].shape[-1]
    half = BLOCK // 2
    small_rows = 2 * frame["vectors"].shape[0] + 2 * frame["bias0"].shape[1] // width + 2
    loaded = dict(frame)
    out_weight, qkv_weight = loaded.pop("out_w"), loaded.pop("qkv_w")

    def piece(columns):
        return ((4, half, columns), BF, True)

    return named_call(
        finish_kernel,
        dict(
            **loaded, out_w=out_weight, qkv_w=qkv_weight, stay_up=u1[0], came_up=u1[1],
            stay_down=d1[0], came_down=d1[1], la1=a1[0], la1_x=a1[1], pg1=a1[2], pg1_send=a1[3],
            rt1=a1[4], rt1_x=a1[5], lf0=f0[0], lf0_x=f0[1], rt0=f0[2], rt0_send=f0[3], la0=a0[0],
            la0_x=a0[1],
        ),
        dict(
            f0_out=piece(wide), a0_out=piece(att), f1_out=piece(wide), a1_out=piece(att),
            small_out=((small_rows, width), F32, True), input_grad=((rows, width), BF, True),
        ),
        dict(
            **{key + "_sc": pltpu.VMEM(value.shape, value.dtype) for key, value in loaded.items()},
            pg_keep_sc=low(rows, 2 * width),
            pg_send_sc=low(rows, 2 * width),
            input_grad_sc=low(rows, width),
            small_sc=full(small_rows, width),
            w_out=low(width, width),
            w_qkv=low(width, 3 * width),
            dqkv_sc=full(rows, 3 * width),
            pg_sc=low(rows, 3 * width),
            rows_sc=full(8, width),
            heads_sc=full(8, WIDE),
            sems=pltpu.SemaphoreType.DMA((4,)),
            moves=pltpu.SemaphoreType.DMA((13,)),
            left_a1=low(4 * rows, 2 * width),
            right_a1=low(4 * rows, att),
            left_f0=low(4 * rows, f0[0].shape[1]),
            right_f0=low(4 * rows, wide * 5 // 8),
            left_a0=low(4 * rows, 2 * width),
            right_a0=low(4 * rows, att),
            pg1_x=low(rows, 3 * width // 2),
            rt0_x=low(*f0[2].shape),
            pm0_x=low(rows, 2 * width),
            part_u1=low(2, 2, BLOCK, att),
            part_d1=low(OUTER, BLOCK, att),
            part_a1=low(OUTER, 2, BLOCK, att),
            part_f0=low(OUTER, 2, BLOCK, wide),
            part_a0=low(OUTER, 2, BLOCK, att),
            y_u1=low(2, BLOCK, att),
            y_d1=low(OUTER, BLOCK, att),
            y_a1=low(2, BLOCK, att),
            y_f0=low(OUTER, BLOCK, wide),
            y_a0=low(OUTER, BLOCK, att),
            z0_u1=low(2, 2, BLOCK, att),
            z0_d1=low(2, BLOCK, att),
            z0_a1=low(2, 2, BLOCK, att),
            z0_f0=low(2, BLOCK, wide),
            z0_a0=low(2, BLOCK, att),
            z1_u1=low(BLOCK, att),
            z1_d1=low(BLOCK, att),
            z1_a1=low(BLOCK, att),
            z1_f0=low(BLOCK, wide),
            z1_a0=low(BLOCK, att),
            fin_u1=low(2, half, att),
            fin_d1=low(2, half, att),
            fin_a1=low(2, half, att),
            fin_f0=low(2, half, wide),
            fin_a0=low(2, half, att),
            far_u1=low(2, half, att),
            far_d1=low(2, half, att),
            far_a1=low(2, half, att),
            far_f0=low(2, half, wide),
            far_a0=low(2, half, att),
            sums=full(6, small_rows, width),
            sums_in=full(5, small_rows, width),
            local=pltpu.SemaphoreType.DMA((34,)),
            send=pltpu.SemaphoreType.DMA((66,)),
            recv=pltpu.SemaphoreType.DMA((66,)),
        ),
        60,
        pl.CostEstimate(
            flops=2 * rows * width * 4 * width + 2**33,
            bytes_accessed=2**26,
            transcendentals=HEADS * rows * rows,
        ),
        "finish_all",
        collective_id=3,
    )


PEERS = HEADS
FOLD = FRAME // 2
EXTRA = 16
GROUPS = 4
BACK_GROUPS = 4
MESH = pl.DeviceIdType.MESH


def fold_pair(values):
    lane = lax.broadcasted_iota(jnp.int32, (FOLD, LANES), 1)
    top, bottom = values[:FOLD], values[FOLD:]
    one = jnp.where(lane < HD, top, pltpu.roll(bottom, HD, 1))
    two = jnp.where(lane < HD, pltpu.roll(top, HD, 1), bottom)
    return one, two


def unfold_pair(one, two):
    lane = lax.broadcasted_iota(jnp.int32, (FOLD, LANES), 1)
    top = jnp.where(lane < HD, one, pltpu.roll(two, HD, 1))
    bottom = jnp.where(lane < HD, pltpu.roll(one, HD, 1), two)
    return top, bottom


def unfold_head(folded):
    lane = lax.broadcasted_iota(jnp.int32, (FOLD, LANES), 1)
    folded = folded.astype(F32)
    top = jnp.where(lane < HD, folded, 0.0)
    bottom = jnp.where(lane < HD, pltpu.roll(folded, HD, 1), 0.0)
    return top.astype(BF), bottom.astype(BF)


def fold_head(values):
    lane = lax.broadcasted_iota(jnp.int32, (FOLD, LANES), 1)
    return jnp.where(lane < HD, values[:FOLD], pltpu.roll(values[FOLD:], HD, 1))


def exchange(me, k, source, target, sems):
    return pltpu.make_async_remote_copy(
        src_ref=source,
        dst_ref=target,
        send_sem=sems.at[0, k],
        recv_sem=sems.at[1, k],
        device_id={"blk": me ^ k},
        device_id_type=MESH,
    )


def call_peers(me, partner):
    barrier = pltpu.get_barrier_semaphore()
    for k in range(1, PEERS):
        pl.semaphore_signal(barrier, 1, device_id={"blk": me ^ k}, device_id_type=MESH)
    pl.semaphore_signal(barrier, 1, device_id=partner, device_id_type=MESH)
    return lambda: pl.semaphore_wait(barrier, PEERS)


def all_to_all(me, source, target, sems, own_sem):
    copies = [exchange(me, k, source.at[me ^ k], target.at[me], sems) for k in range(PEERS - 1, 0, -1)]
    for copy in copies:
        copy.start()
    own = pltpu.make_async_copy(source.at[me], target.at[me], own_sem)
    own.start()
    return copies + [own]


def head_forward(me, qkv_ref, mark_copies, att_ref, r):
    width = att_ref.shape[1]
    for pair in range(width // LANES):
        for part in range(3):
            block = qkv_ref[:, part * width + pair * LANES : part * width + (pair + 1) * LANES]
            one, two = fold_pair(block.astype(F32) * (SCALE if part == 0 else 1.0))
            r.pack[2 * pair, part * FOLD : (part + 1) * FOLD] = one.astype(BF)
            r.pack[2 * pair + 1, part * FOLD : (part + 1) * FOLD] = two.astype(BF)
    for copy in all_to_all(me, r.pack, r.got, r.out_sems, r.own_sems.at[0]) + mark_copies:
        copy.wait()
    for s in range(PEERS):
        for part, target in enumerate((r.queries_sc, r.keys_sc, r.values_sc)):
            top, bottom = unfold_head(r.got[s, part * FOLD : (part + 1) * FOLD])
            target[s * FRAME : s * FRAME + FOLD] = top
            target[s * FRAME + FOLD : (s + 1) * FRAME] = bottom
        for index in range(2):
            at = index * PEERS + s
            r.marks_sc[at : at + 1] = r.marks_got[s, index : index + 1].astype(F32)
    keys, values = r.keys_sc[...], r.values_sc[...]
    tags = jnp.concatenate([r.marks_sc[s : s + 1] for s in range(PEERS)], axis=1)
    sends = []
    own = None
    per = PEERS // GROUPS
    for j in range(GROUPS - 1, -1, -1):
        block = (me // per) ^ j
        at = pl.ds(pl.multiple_of(block * per * FRAME, per * FRAME), per * FRAME)
        scores = product_right(r.queries_sc[at], keys)
        tops, totals, shares = [], [], []
        for i in range(per):
            scene = r.marks_sc[pl.ds(PEERS + block * per + i, 1)][:, :1]
            row = scores[i * FRAME : (i + 1) * FRAME] + jnp.where(tags == scene, 0.0, NEG)
            tops.append(jnp.max(row, axis=-1, keepdims=True))
            row = jnp.exp(row - tops[-1])
            totals.append(jnp.sum(row, axis=-1, keepdims=True))
            shares.append(row.astype(BF))
        top, total = jnp.concatenate(tops, axis=0), jnp.concatenate(totals, axis=0)
        result = product(jnp.concatenate(shares, axis=0), values) / total
        r.outs_sc[at] = result
        r.lse_sc[:, at] = as_row(top + jnp.log(total))
        for i in range(per):
            r.answers[block * per + i] = fold_head(result[i * FRAME : (i + 1) * FRAME]).astype(BF)
        for k in range(j * per, (j + 1) * per):
            if k:
                copy = exchange(me, k, r.answers.at[me ^ k], r.back.at[me], r.back_sems)
            else:
                copy = pltpu.make_async_copy(r.answers.at[me], r.back.at[me], r.own_sems.at[1])
            copy.start()
            sends.append(copy)
    for copy in sends:
        copy.wait()
    for pair in range(width // LANES):
        top, bottom = unfold_pair(r.back[2 * pair].astype(F32), r.back[2 * pair + 1].astype(F32))
        att_ref[:FOLD, pair * LANES : (pair + 1) * LANES] = top.astype(BF)
        att_ref[FOLD:, pair * LANES : (pair + 1) * LANES] = bottom.astype(BF)


def head_backward(me, grad_ref, dqkv_ref, r, meanwhile):
    width = grad_ref.shape[1]
    for pair in range(width // LANES):
        one, two = fold_pair(grad_ref[:, pair * LANES : (pair + 1) * LANES].astype(F32))
        r.pack[2 * pair] = one.astype(BF)
        r.pack[2 * pair + 1] = two.astype(BF)
    copies = all_to_all(me, r.pack, r.got, r.out_sems, r.own_sems.at[0])
    lane = lax.broadcasted_iota(jnp.int32, (1, LANES), 1)

    def lanes(terms, value):
        for index, term in enumerate(terms):
            value = jnp.where(lane == HD + index, term, value)
        return value

    for s in range(PEERS):
        at = slice(s * FRAME, (s + 1) * FRAME)
        tag = as_column(r.marks_sc[s : s + 1])
        scene = r.marks_sc[PEERS + s : PEERS + s + 1, :1]
        blocked = [jnp.where(tag == mark, NEG, 0.0) for mark in (0.0, 1.0, -1.0)]
        r.keys_sc[at] = lanes(blocked + [1.0] * 3, r.keys_sc[at].astype(F32)).astype(BF)
        other = [jnp.where(scene == mark, 0.0, 1.0) for mark in (0.0, 1.0)]
        less = [-term.astype(F32) for term in terms_of(as_column(r.lse_sc[:, at]))]
        r.queries_sc[at] = lanes(other + [1.0] + less, r.queries_sc[at].astype(F32)).astype(BF)
        r.values_sc[at] = lanes([1.0] * 3, r.values_sc[at].astype(F32)).astype(BF)
    for copy in copies:
        copy.wait()
    for s in range(PEERS):
        at = slice(s * FRAME, (s + 1) * FRAME)
        grads = jnp.concatenate(unfold_head(r.got[s]), axis=0).astype(F32)
        delta = jnp.sum(grads * r.outs_sc[at], axis=-1, keepdims=True)
        less = [-term.astype(F32) for term in terms_of(delta)]
        r.grads_sc[at] = lanes(less, grads).astype(BF)
    queries, outs = r.queries_sc[...], r.grads_sc[...]
    query_grad = None
    sends = []
    per = PEERS // BACK_GROUPS
    for j in range(BACK_GROUPS - 1, -1, -1):
        block = (me // per) ^ j
        at = pl.ds(pl.multiple_of(block * per * FRAME, per * FRAME), per * FRAME)
        keys, values = r.keys_sc[at], r.values_sc[at]
        shares = jnp.exp(product_right(keys, queries))
        score_grad = (shares * product_right(values, outs)).astype(BF)
        value_grad = product(shares.astype(BF), outs)
        key_grad = product(score_grad, queries)
        turned = jnp.transpose(keys.astype(F32)).astype(BF)[:HD]
        piece = product(turned, score_grad)
        query_grad = piece if query_grad is None else query_grad + piece
        for i in range(per):
            part = slice(i * FRAME, (i + 1) * FRAME)
            r.pairs[block * per + i, :FOLD] = fold_head(key_grad[part]).astype(BF)
            r.pairs[block * per + i, FOLD:] = fold_head(value_grad[part]).astype(BF)
        for k in range(j * per, (j + 1) * per):
            if k:
                copy = exchange(me, k, r.pairs.at[me ^ k], r.pairs_in.at[me], r.pair_sems)
            else:
                copy = pltpu.make_async_copy(r.pairs.at[me], r.pairs_in.at[me], r.own_sems.at[1])
            copy.start()
            sends.append(copy)
    padded = jnp.concatenate([query_grad * SCALE, jnp.zeros_like(query_grad)], axis=0)
    for s in range(PEERS):
        block = jnp.transpose(padded[:, s * FRAME : (s + 1) * FRAME])
        r.asked[s] = fold_head(block).astype(BF)
    sends += all_to_all(me, r.asked, r.asked_in, r.back_sems, r.own_sems.at[2])
    meanwhile()
    for copy in sends:
        copy.wait()
    for pair in range(width // LANES):
        for part in range(3):
            if part == 0:
                one, two = r.asked_in[2 * pair], r.asked_in[2 * pair + 1]
            else:
                rows = slice((part - 1) * FOLD, part * FOLD)
                one, two = r.pairs_in[2 * pair, rows], r.pairs_in[2 * pair + 1, rows]
            top, bottom = unfold_pair(one.astype(F32), two.astype(F32))
            cols = slice(part * width + pair * LANES, part * width + (pair + 1) * LANES)
            dqkv_ref[:FOLD, cols] = top.astype(BF)
            dqkv_ref[FOLD:, cols] = bottom.astype(BF)


def tile_heads(source, target):
    lane = lax.broadcasted_iota(jnp.int32, (1, WIDE), 1)
    for layer in range(2):
        every = jnp.concatenate(
            [source[layer : layer + 1], jnp.zeros((1, WIDE - 3 * HD), F32)], axis=1
        )
        for index in range(3):
            one = jnp.where((lane >= index * HD) & (lane < (index + 1) * HD), every, 0.0)
            two = one + pltpu.roll(one, HD, 1)
            target[layer, index : index + 1] = two + pltpu.roll(two, 2 * HD, 1)
        target[layer, 3:] = jnp.zeros((5, WIDE), F32)


def begin_kernel(r):
    me, x_at = lax.axis_index("blk"), lax.axis_index("grp")
    partner = {"grp": 1 - x_at}
    peers_here = call_peers(me, partner)
    width, units = r.tok.shape[1], r.up_w.shape[2]
    mover = Mover(r.moves)
    loads = [
        mover.start(*pair)
        for pair in (
            (r.tok, r.tok_sc), (r.vectors, r.vectors_sc), (r.head_norm, r.head_norm_sc),
            (r.up_bias, r.up_bias_sc), (r.valid, r.valid_sc),
        )
    ]
    copies = weight_copies(
        column_pieces(r.qkv_w.at[0], 3)
        + [r.out_w.at[0]]
        + interleaved(column_pieces(r.up_w.at[0], 4), row_pieces(r.down_w.at[0], 4)),
        column_pieces(r.w_qkv, 3)
        + [r.w_out]
        + interleaved(column_pieces(r.w_up, 4), row_pieces(r.w_down, 4)),
        r.sems,
    )
    for copy in loads:
        copy.wait()
    tile_heads(r.head_norm_sc, r.head_rows_sc)
    position = lax.broadcasted_iota(jnp.int32, (1, FRAME), 1)
    valid = jnp.where((r.valid_sc[...] == 1) | (position < SPECIAL), 1.0, 0.0)
    r.usable_sc[...] = valid
    scene = r.smem_scene[0].astype(F32)
    row = lax.broadcasted_iota(jnp.int32, (EXTRA, FRAME), 0)
    tags = jnp.where(valid > 0, scene, -1.0)
    r.marks_in_sc[...] = jnp.where(row == 0, tags, jnp.where(row == 1, scene, 0.0)).astype(BF)
    mover.flush(r.head_rows_sc, r.head_rows)
    mover.flush(r.usable_sc, r.usable)
    residual = r.tok_sc[...].astype(F32)
    normed0, att0 = r.leftatt0_sc.at[:, :width], r.leftatt0_sc.at[:, width:]
    project(
        0, residual, r.vectors_sc, r.head_rows_sc, r.w_qkv, copies[:3], normed0, r.pre0_sc,
        r.qkv0_sc,
    )
    mover.flush(r.pre0_sc, r.pre0)
    mover.flush(r.qkv0_sc, r.qkv0)
    frame_attend(r.usable_sc[...], r.qkv0_sc, att0)
    next_copies = weight_copies(
        column_pieces(r.qkv_w.at[1], 3), column_pieces(r.w_qkv, 3), r.next_sems
    )
    mover.flush(r.leftatt0_sc, r.leftatt0)
    peers_here()
    mark_copies = [
        exchange(me, k, r.marks_in_sc, r.marks_got.at[me], r.mark_sems) for k in range(1, PEERS)
    ]
    for copy in mark_copies:
        copy.start()
    r.marks_got[me] = r.marks_in_sc[...]
    sender = Sender(r.x_sems.at[0], r.x_sems.at[1], dict(x=partner))
    across = [sender.start(r.leftatt0_sc, r.leftatt0_x, "x")]
    lifted0, active0 = r.left0_sc.at[:, :width], r.left0_sc.at[:, width:]
    result = feed_forward(
        0, att0[...], residual, r.vectors_sc, r.up_bias_sc, r.w_out, r.w_up, r.w_down, copies[3:],
        r.mixed0_sc, r.middle0_sc, lifted0, r.slope0_sc, active0, r.feed0_sc,
    )
    r.res1_sc[...] = result
    for pair in (
        (r.left0_sc, r.left0), (r.mixed0_sc, r.mixed0), (r.middle0_sc, r.middle0),
        (r.slope0_sc, r.slope0), (r.feed0_sc, r.feed0), (r.res1_sc, r.res1),
    ):
        mover.flush(*pair)
    across.append(sender.start(r.left0_sc, r.left0_x, "x"))
    normed1, att1 = r.leftatt1_sc.at[:, :width], r.leftatt1_sc.at[:, width:]
    project(
        1, result, r.vectors_sc, r.head_rows_sc, r.w_qkv, next_copies, normed1, r.pre1_sc, r.qkv1_sc
    )
    mover.flush(r.pre1_sc, r.pre1)
    head_forward(me, r.qkv1_sc, mark_copies, att1, r)
    for pair in (
        (r.queries_sc, r.queries), (r.keys_sc, r.keys), (r.values_sc, r.values), (r.outs_sc, r.outs),
        (r.lse_sc, r.lse), (r.marks_sc, r.marks), (r.leftatt1_sc, r.leftatt1),
    ):
        mover.flush(*pair)
    for copy in across:
        copy.wait()
    mover.finish()


def begin(
    tokens, valid, scene, vectors, up_bias, head_norm, qkv_weight, out_weight, up_weight, down_weight
):
    rows, width = tokens.shape
    hidden = up_weight.shape[2]
    every = PEERS * FRAME
    loaded = dict(
        tok=tokens, vectors=vectors, head_norm=head_norm, up_bias=up_bias,
        valid=valid,
    )
    stored = dict(
        left0=((rows, hidden + width), BF),
        leftatt0=((rows, 2 * width), BF),
        pre0=((rows, 2 * width), F32),
        qkv0=((rows, 3 * width), BF),
        mixed0=((rows, width), F32),
        middle0=((rows, width), F32),
        slope0=((rows, hidden), F32),
        feed0=((rows, width), F32),
        res1=((rows, width), F32),
        leftatt1=((rows, 2 * width), BF),
        pre1=((rows, 2 * width), F32),
        queries=((every, LANES), BF),
        keys=((every, LANES), BF),
        values=((every, LANES), BF),
        outs=((every, LANES), F32),
        lse=((1, every), F32),
        marks=((2 * PEERS, LANES), F32),
        head_rows=((2, 8, WIDE), F32),
        usable=((1, rows), F32),
    )
    return named_call(
        begin_kernel,
        dict(
            smem_scene=scene, **loaded, qkv_w=qkv_weight, out_w=out_weight,
            up_w=up_weight, down_w=down_weight,
        ),
        dict(
            **{key: (*value, True) for key, value in stored.items()},
            leftatt0_x=((rows, 2 * width), BF, True),
            left0_x=((rows, hidden + width), BF, True),
        ),
        dict(
            **{key + "_sc": pltpu.VMEM(value.shape, value.dtype) for key, value in loaded.items()},
            **{key + "_sc": pltpu.VMEM(*value) for key, value in stored.items()},
            marks_in_sc=low(EXTRA, FRAME),
            qkv1_sc=low(rows, 3 * width),
            w_qkv=low(width, 3 * width),
            w_out=low(width, width),
            w_up=low(width, hidden),
            w_down=low(hidden, width),
            pack=low(PEERS, 3 * FOLD, LANES),
            got=low(PEERS, 3 * FOLD, LANES),
            marks_got=low(PEERS, EXTRA, LANES),
            mark_sems=pltpu.SemaphoreType.DMA((2, PEERS)),
            answers=low(PEERS, FOLD, LANES),
            back=low(PEERS, FOLD, LANES),
            sems=pltpu.SemaphoreType.DMA((12,)),
            next_sems=pltpu.SemaphoreType.DMA((3,)),
            moves=pltpu.SemaphoreType.DMA((5 + len(stored),)),
            own_sems=pltpu.SemaphoreType.DMA((2,)),
            out_sems=pltpu.SemaphoreType.DMA((2, PEERS)),
            back_sems=pltpu.SemaphoreType.DMA((2, PEERS)),
            x_sems=pltpu.SemaphoreType.DMA((2, 2)),
        ),
        60,
        pl.CostEstimate(
            flops=2 * rows * width * (7 * width + 2 * hidden) + 4 * every * every * LANES,
            bytes_accessed=2 * width * (7 * width + 2 * hidden),
            transcendentals=2 * rows * hidden + every * every,
        ),
        "begin",
        collective_id=1,
    )


def middle_kernel(r):
    me, x_at = lax.axis_index("blk"), lax.axis_index("grp")
    c_at, y_at, z0, z1 = [lax.rem(me // (1 << bit), 2) for bit in range(4)]
    partners = {"x": {"grp": 1 - x_at}, "c": {"blk": me ^ 1}}
    peers_here = call_peers(me, partners["x"])
    sender = Sender(r.ring_sems.at[0], r.ring_sems.at[1], partners)
    rows, width = r.res.shape
    units = r.up_w.shape[2]
    mover = Mover(r.moves)
    loads = [
        mover.start(*pair)
        for pair in (
            (r.vectors, r.vectors_sc), (r.leftatt1, r.leftatt1_sc), (r.res, r.res_sc),
            (r.up_bias, r.up_bias_sc), (r.cot, r.cot_sc),
        )
    ]
    copies = weight_copies(
        [r.out_w.at[1]]
        + interleaved(column_pieces(r.up_w.at[1], 4), row_pieces(r.down_w.at[1], 4)),
        [r.w_out] + interleaved(column_pieces(r.w_up, 4), row_pieces(r.w_down, 4)),
        r.sems,
    )
    late_loads = [
        mover.start(*pair)
        for pair in (
            (r.queries, r.queries_sc), (r.keys, r.keys_sc), (r.values, r.values_sc),
            (r.outs, r.outs_sc), (r.lse, r.lse_sc), (r.marks, r.marks_sc),
        )
    ]
    for copy in loads:
        copy.wait()
    own, mate = slice(0, rows), slice(rows, 2 * rows)
    quarter = units // 4
    lefts = []

    def done(j, active):
        for block in range(active.shape[1] // (2 * LANES)):
            for x in range(2):
                start = (2 * block + x) * LANES
                at = (j * active.shape[1] // 2) + block * LANES
                r.act_sc[x, :, at : at + LANES] = active[:, start : start + LANES]
        if j == 0:
            peers_here()
            lefts.append(
                sender.start(r.left_sc.at[own, :width], r.left_sc.at[mate, :width], "x")
            )
        filled = (j + 1) * active.shape[1] // 2
        if filled % quarter == 0:
            at = slice(filled - quarter, filled)
            to = slice(width + filled - quarter, width + filled)
            lefts.append(
                sender.start(r.act_sc.at[1 - x_at, :, at], r.left_sc.at[mate, to], "x")
            )

    result = feed_forward(
        1, r.leftatt1_sc[:, width:], r.res_sc[...], r.vectors_sc, r.up_bias_sc, r.w_out, r.w_up,
        r.w_down, copies, r.mixed_sc, r.middle_sc, r.left_sc.at[own, :width], r.slope_sc, None,
        r.feed_sc, done,
    )
    r.left_sc[own, width:] = r.act_sc[x_at]
    left_c = sender.start(r.left_sc.at[own], r.left_sc.at[2 * rows : 3 * rows], "c")
    r.output_sc[...] = result.astype(BF)
    mover.flush(r.output_sc, r.output)
    grad = feed_backward(
        1, r.cot_sc[...].astype(F32), r.feed_sc[...], r.middle_sc[...], r.mixed_sc[...],
        r.slope_sc, r.vectors_sc, r.w_up, r.w_down, None, r.fg_sc, r.hg_sc, r.mg_sc, r.bias_out,
        r.rows_out, 0,
    )
    half, part = units // 2, width // 2

    def columns(ref, start, count):
        return ref.at[:, pl.ds(pl.multiple_of(start, LANES), count)]

    rights = [
        sender.start(columns(r.hg_sc, (1 - x_at) * half, half), r.far_sc.at[:, :half], "x"),
        sender.start(r.fg_sc, r.far_sc.at[:, half:], "x"),
    ]
    mixed_x = sender.start(columns(r.mg_sc, (1 - x_at) * part, part), r.mixed1_x, "x")
    q_up, q_down = half // 2, part
    ready = [left_c]

    def place(up, down, up_at, down_at, index):
        here = slice(index * rows, (index + 1) * rows)
        there = slice((2 + index) * rows, (3 + index) * rows)
        for ref, start, count, to in ((up, up_at, q_up, 0), (down, down_at, q_down, q_up)):
            ready.append(
                mover.start(
                    columns(ref, start + c_at * count, count), r.right_sc.at[here, to : to + count]
                )
            )
            ready.append(
                sender.start(
                    columns(ref, start + (1 - c_at) * count, count),
                    r.right_sc.at[there, to : to + count],
                    "c",
                )
            )

    place(r.hg_sc, r.fg_sc, x_at * half, 0, 0)
    mover.flush(columns(r.mg_sc, x_at * part, part), r.mixed1)
    r.middle_grad_sc[...] = grad
    mover.flush(r.middle_grad_sc, r.middle_grad)
    r.att_grad_sc[...] = product_right(r.mg_sc[...], r.w_out[...]).astype(BF)
    for copy in late_loads:
        copy.wait()

    def meanwhile():
        for copy in lefts:
            copy.wait_recv()
        ready.append(
            sender.start(r.left_sc.at[mate], r.left_sc.at[3 * rows : 4 * rows], "c")
        )

    head_backward(me, r.att_grad_sc, r.dqkv_sc, r, meanwhile)
    mover.flush(r.dqkv_sc, r.dqkv)
    for copy in rights:
        copy.wait_recv()
    place(r.far_sc, r.far_sc, 0, half, 1)
    for copy in ready:
        copy.wait_recv()
    for slot in range(OUTER):
        target = (r.away_up_sc if slot < 2 else r.stay_up_sc).at[slot % 2]

        def emit(target, y, row, col, values):
            height, wide = values.shape
            target[y, row : row + height, col : col + wide] = values

        group = slot_group(slot, z0, z1)
        slot_product(
            group, r.left_sc, 0, r.right_sc, 0, q_up, False, functools.partial(emit, target)
        )
        for y in range(2):
            start = pl.multiple_of(width + (2 * group + y) * 2 * BLOCK, BLOCK)
            result = product_left(
                r.left_sc[:, pl.ds(start, 2 * BLOCK)], r.right_sc[:, q_up:]
            ).astype(BF)
            piece = BLOCK // 2
            for c in range(2):
                for t in range(2):
                    row = (2 * c + t) * piece
                    emit(r.down_sc.at[slot], y, c * piece, t * q_down, result[row : row + piece])
        if slot == 1:
            mover.flush(r.away_up_sc, r.away_up)
    mover.flush(r.down_sc.at[:, 1 - y_at], r.away_down)
    mover.flush(r.down_sc.at[:, y_at], r.stay_down)
    mover.flush(r.stay_up_sc, r.stay_up)
    mixed_x.wait_recv()
    assert len(sender.copies) == r.ring_sems.shape[1]
    sender.finish()
    mover.finish()


def middle(first, cotangent, vectors, up_bias, out_weight, up_weight, down_weight):
    rows, width = cotangent.shape
    hidden = up_weight.shape[2]
    every = PEERS * FRAME
    loaded = dict(
        vectors=vectors, leftatt1=first.leftatt1, res=first.res1, up_bias=up_bias,
        cot=cotangent, queries=first.queries, keys=first.keys, values=first.values,
        outs=first.outs, lse=first.lse, marks=first.marks,
    )
    columns = hidden // 4
    stored = dict(
        output=((rows, width), BF),
        middle_grad=((rows, width), F32),
        dqkv=((rows, 3 * width), BF),
        stay_up=((2, 2, BLOCK, columns), BF),
        away_up=((2, 2, BLOCK, columns), BF),
    )
    return named_call(
        middle_kernel,
        dict(
            **loaded, out_w=out_weight, up_w=up_weight, down_w=down_weight,
        ),
        dict(
            **{key: (*value, True) for key, value in stored.items()},
            stay_down=((OUTER, BLOCK, columns), BF, True),
            away_down=((OUTER, BLOCK, columns), BF, True),
            mixed1=((rows, width // 2), BF, True),
            mixed1_x=((rows, width // 2), BF, True),
            bias_out=((1, hidden), F32, False),
            rows_out=((8, width), F32, False),
        ),
        dict(
            **{key + "_sc": pltpu.VMEM(value.shape, value.dtype) for key, value in loaded.items()},
            **{key + "_sc": pltpu.VMEM(*value) for key, value in stored.items()},
            w_out=low(width, width),
            w_up=low(width, hidden),
            w_down=low(hidden, width),
            left_sc=low(4 * rows, hidden // 2 + width),
            act_sc=low(2, rows, hidden // 2),
            down_sc=low(OUTER, 2, BLOCK, columns),
            right_sc=low(4 * rows, hidden // 4 + width // 2),
            far_sc=low(rows, hidden // 2 + width),
            mixed_sc=full(rows, width),
            middle_sc=full(rows, width),
            slope_sc=full(rows, hidden),
            feed_sc=full(rows, width),
            fg_sc=low(rows, width),
            hg_sc=low(rows, hidden),
            mg_sc=low(rows, width),
            att_grad_sc=low(rows, width),
            grads_sc=low(every, LANES),
            pack=low(PEERS, FOLD, LANES),
            got=low(PEERS, FOLD, LANES),
            pairs=low(PEERS, 2 * FOLD, LANES),
            pairs_in=low(PEERS, 2 * FOLD, LANES),
            asked=low(PEERS, FOLD, LANES),
            asked_in=low(PEERS, FOLD, LANES),
            sems=pltpu.SemaphoreType.DMA((9,)),
            moves=pltpu.SemaphoreType.DMA((23,)),
            own_sems=pltpu.SemaphoreType.DMA((3,)),
            out_sems=pltpu.SemaphoreType.DMA((2, PEERS)),
            back_sems=pltpu.SemaphoreType.DMA((2, PEERS)),
            pair_sems=pltpu.SemaphoreType.DMA((2, PEERS)),
            ring_sems=pltpu.SemaphoreType.DMA((2, 12)),
        ),
        60,
        pl.CostEstimate(
            flops=4 * rows * width * (width + 2 * hidden) + 10 * every * every * LANES,
            bytes_accessed=2 * width * (width + 2 * hidden),
            transcendentals=2 * rows * hidden + every * every,
        ),
        "middle",
        collective_id=2,
    )


def per_device(
    tokens,
    qkv_weight,
    out_weight,
    up_weight,
    down_weight,
    vectors,
    up_bias,
    head_norm,
    token_valid,
    frame_scene,
    cotangent,
):
    count = lax.axis_size("blk")
    outer = count // 4
    me = lax.axis_index("blk")
    x_at = lax.axis_index("grp")
    c_at = lax.rem(me, 2)
    y_at = lax.rem(me // 2, 2)
    c_pairs = [(i, i ^ 1) for i in range(count)]
    y_pairs = [(i, i ^ 2) for i in range(count)]
    z_groups = [[4 * o + k for o in range(outer)] for k in range(4)]
    halves_at = jnp.stack([x_at, x_at]).astype(jnp.int32)
    places = jnp.stack(
        [c_at, y_at, x_at, lax.rem(me // 4, 2), lax.rem(me // 8, 2), halves_at[1], me]
    ).astype(jnp.int32)


    def swap_x(value):
        return lax.ppermute(value, "grp", [(0, 1), (1, 0)])

    def swap_c(value):
        return lax.ppermute(value, "blk", c_pairs)

    def swap_y(value):
        return lax.ppermute(value, "blk", y_pairs)

    def part(value, index, parts, axis):
        size = value.shape[axis] // parts
        return lax.dynamic_slice_in_dim(value, index * size, size, axis)

    def tied(value, *others):
        return lax.optimization_barrier((value, *others))

    def ready_sum(keep, arrived):
        return (keep.astype(F32) + arrived.astype(F32)).astype(BF)

    def scattered(own):
        return lax.psum_scatter(
            own, "blk", scatter_dimension=0, tiled=True, axis_index_groups=z_groups
        )

    def finished(total):
        pair = jnp.stack([part(total, c_at, 2, 0), swap_c(part(total, 1 - c_at, 2, 0))])
        return jnp.concatenate([pair, swap_x(pair)], axis=0)

    def total_of(value):
        value = value + swap_x(value)
        step = 1
        while step < count:
            pairs = [(i, i ^ step) for i in range(count)]
            value = value + lax.ppermute(value, "blk", pairs)
            step *= 2
        return value

    row_count, width = tokens.shape[1:]
    vector_count = vectors.shape[1]
    vectors = vectors.transpose(1, 0, 2)
    hidden = up_weight.shape[2]
    if count == HEADS:
        first = begin(
            tokens[0], token_valid[0], frame_scene[0], vectors, up_bias, head_norm, qkv_weight,
            out_weight, up_weight, down_weight,
        )
        head_rows, usable_row = first.head_rows, first.usable
        second = middle(
            first, cotangent[0], vectors, up_bias, out_weight, up_weight, down_weight
        )
        came_up = lax.ppermute(second.away_up, "blk", [(i, i ^ 4) for i in range(count)])
        came_down, leftatt1_x = swap_y(second.away_down), swap_x(first.leftatt1)
        pre0, qkv0, mixed0, middle0, slope0, feed0, res1, pre1 = (
            first.pre0, first.qkv0, first.mixed0, first.middle0, first.slope0, first.feed0,
            first.res1, first.pre1,
        )
        output, middle_grad1, dqkv1, bias1, rows1 = (
            second.output, second.middle_grad, second.dqkv, second.bias_out, second.rows_out
        )
    else:
        position = lax.broadcasted_iota(jnp.int32, (row_count,), 0)
        usable = (token_valid[0, 0] == 1) | (position < SPECIAL)
        usable_row = usable.astype(F32).reshape(1, row_count)
        scene = frame_scene[0, 0].astype(F32)
        tag_rows = jnp.where(usable, scene, -1.0)
        head_rows = jnp.tile(head_norm.reshape(2, 3, HD), (1, 1, WIDE // HD))
        head_rows = jnp.concatenate([head_rows, jnp.zeros((2, 5, WIDE), F32)], axis=1)
        left0, leftatt0, pre0, qkv0, mixed0, middle0, slope0, feed0, res1, normed1, pre1, qkv1 = (
            front(
                tokens[0], usable_row, vectors, up_bias, head_rows, qkv_weight, out_weight,
                up_weight, down_weight,
            )
        )
        att1, kept = gathered_forward(qkv1, tag_rows, scene)
        left1, leftatt1, output, right1, right1_send, att_grad1, middle_grad1, bias1, rows1 = turn(
            halves_at, att1, normed1, res1, cotangent[0], vectors, up_bias, out_weight, up_weight,
            down_weight,
        )
        dqkv1 = gathered_backward(att_grad1, kept, tag_rows, scene)
    third = back_one(
        dqkv1, pre1, res1, middle_grad1, feed0, middle0, mixed0, slope0, vectors,
        head_rows, qkv_weight, up_weight, down_weight,
    )
    frame = dict(
        mixed_grad=third.mixed_grad, grad=third.middle_grad, qkv=qkv0, pre=pre0, tok=tokens[0],
        usable=usable_row, vectors=vectors, head_rows=head_rows, rows10=third.rows_out, rows1=rows1,
        bias0=third.bias_out, bias1=bias1, heads1=third.head_out, out_w=out_weight, qkv_w=qkv_weight,
    )

    def feed_grads(name, lefts, rights):
        return weight_grads(
            name,
            outer,
            width,
            places,
            [
                (lefts, 0, width, rights, 0, hidden // 2, False),
                (lefts, width, hidden, rights, hidden // 2, width // 2, True),
            ],
        )

    def att_grads(name, lefts, projected, rights, at):
        return weight_grads(
            name,
            outer,
            width,
            places,
            [
                (lefts, 0, width, projected, 0, 3 * width // 2, False),
                (lefts, width, width, rights, at, width // 2, False),
            ],
        )

    def four(own, far):
        return (own, far, swap_c(own), swap_c(far))

    def reduce_apart(fourth):
        pg1_x, right0_far = swap_x(third.pg_send), swap_x(third.right_send)
        pg0_all = four(fourth.pg_keep, swap_x(fourth.pg_send))
        right1_all = four(right1, swap_x(right1_send))
        results = []
        for keep, send in (
            feed_grads(
                "feed_grads0", four(left0, swap_x(left0)), four(third.right_keep, right0_far)
            ),
            att_grads(
                "att_grads0", four(leftatt0, swap_x(leftatt0)), pg0_all, pg0_all, 3 * width // 2
            ),
            feed_grads("feed_grads1", four(left1, swap_x(left1)), right1_all),
            att_grads(
                "att_grads1", four(leftatt1, swap_x(leftatt1)), four(third.pg_keep, pg1_x),
                right1_all, (hidden + width) // 2,
            ),
        ):
            results.append(finished(scattered(ready_sum(keep, swap_y(send)))))
        return results

    if count == HEADS:
        fourth = finish_all(
            frame,
            (second.stay_up, came_up),
            (second.stay_down, came_down),
            (
                first.leftatt1, leftatt1_x, third.pg_keep, third.pg_send, second.mixed1,
                second.mixed1_x,
            ),
            (first.left0, first.left0_x, third.right_keep, third.right_send),
            (first.leftatt0, first.leftatt0_x),
        )
        pieces = [fourth.f0_out, fourth.a0_out, fourth.f1_out, fourth.a1_out]
        small = fourth.small_out
    else:
        fourth = back_two(halves_at, **frame)
        small = total_of(fourth.small)
        pieces = reduce_apart(fourth)
    weight_shapes = [
        (2, width // count, 3 * width),
        (2, width // count, width),
        (2, width // count, up_weight.shape[2]),
        (2, up_weight.shape[2] // count, width),
    ]
    if count == HEADS:
        small_shapes = [(vector_count, 2, HD), (2, hidden // count), (2, 3 * HD)]
        (
            qkv_grad, out_grad, up_grad, down_grad, vector_grad, bias_grad, head_grad, output,
            input_grad,
        ) = assemble(
            [*pieces, small], weight_shapes + small_shapes, [output, fourth.input_grad]
        )
        vector_grad = vector_grad.transpose(1, 0, 2)
    else:
        qkv_grad, out_grad, up_grad, down_grad = assemble(pieces, weight_shapes, [])
        input_grad = fourth.input_grad
        bias_rows = 2 * hidden // width
        vector_grad = part(small[: 2 * vector_count].reshape(2, -1, width), me, count, 2)
        bias_grad = small[2 * vector_count : 2 * vector_count + bias_rows].reshape(2, hidden)
        bias_grad = part(bias_grad, me, count, 1)
        head_grad = small[2 * vector_count + bias_rows, : 6 * HD].reshape(2, 3 * HD)
    return (
        output[None],
        input_grad[None],
        qkv_grad,
        out_grad,
        up_grad,
        down_grad,
        vector_grad,
        bias_grad,
        head_grad,
    )


def gathered_forward(qkv, tag_rows, scene):
    rows, width = qkv.shape[0], qkv.shape[1] // 3
    marks = jnp.zeros((KEEP, 2 * width), BF)
    marks = marks.at[0, :rows].set(tag_rows.astype(BF))
    marks = marks.at[1, :rows].set(jnp.full((rows,), scene).astype(BF))
    pairs = lax.all_gather(
        jnp.concatenate([qkv[:, width:], marks], axis=0), "blk", axis=0, tiled=False
    )
    tags = pairs[:, FRAME, :FRAME].astype(F32).reshape(1, -1)
    scenes = pairs[:, FRAME + 1, :FRAME].astype(F32).reshape(1, -1)
    queries = qkv[:, :width]
    attended, lse = global_attend(queries, pairs, tags, jnp.full((8, LANES), scene))
    every_query = lax.all_gather(
        with_rows(queries, lse.reshape(HEADS, rows)), "blk", axis=0, tiled=False
    )
    return attended.astype(BF), (qkv, pairs, tags, scenes, attended, lse, every_query)


def gathered_backward(attended_grad, kept, tag_rows, scene):
    qkv, pairs, tags, scenes, attended, lse, every_query = kept
    rows, width = attended_grad.shape
    delta = jnp.sum(
        (attended_grad.astype(F32) * attended).reshape(rows, HEADS, HD), axis=-1
    ).T
    every_grad = lax.all_gather(with_rows(attended_grad, delta), "blk", axis=0, tiled=False)
    query_grad = global_query_grad(
        qkv[:, :width],
        pairs,
        tags,
        jnp.full((8, LANES), scene),
        attended_grad,
        lse,
        delta.reshape(PAIRS, 2, rows),
    )
    key_grad, value_grad = global_key_grad(
        qkv[:, width : 2 * width],
        qkv[:, 2 * width :],
        tag_rows.reshape(1, rows),
        scenes,
        every_query,
        every_grad,
        rows_of(every_query, width),
        rows_of(every_grad, width),
    )
    return jnp.concatenate([query_grad, key_grad, value_grad], axis=1).astype(BF)


def solution(mesh):
    return jax.shard_map(
        per_device,
        mesh=mesh,
        in_specs=(
            P("grp", "blk", None),
            P(),
            P(),
            P(),
            P(),
            P(),
            P(),
            P(),
            P("grp", "blk", None),
            P("grp", "blk"),
            P("grp", "blk", None),
        ),
        out_specs=(
            P("grp", "blk", None),
            P("grp", "blk", None),
            P(None, "blk", None),
            P(None, "blk", None),
            P(None, "blk", None),
            P(None, "blk", None),
            P(None, None, "blk"),
            P(None, "blk"),
            P(),
        ),
        check_vma=False,
    )
```
